32 devices in a mesh: dp: 8 (over y, x, core), tensor: 4 (over z).
Axes of the slice: x: 2, y: 2, z: 4, core: 2. Of those that a mesh axis runs over, the one named last changes fastest.
Arguments:
- block_input: bfloat16 [16, 1024, 2048], P('dp', 'tensor'), may hold values from -6 to 6
- clip_lengths: int32 [16, 8], P('dp'), may hold values from 1 to 512, 896 in all within a row
- norm1_gain: bfloat16 [2048], P('dp'), may hold values from 0.5 to 1.5
- w_query: bfloat16 [2048, 2048], P('dp', 'tensor'), may hold values from -0.125 to 0.125
- w_key: bfloat16 [2048, 2048], P('dp', 'tensor'), may hold values from -0.125 to 0.125
- w_value: bfloat16 [2048, 2048], P('dp', 'tensor'), may hold values from -0.125 to 0.125
- w_out: bfloat16 [2048, 2048], P('tensor', 'dp'), may hold values from -0.5 to 0.5
- norm2_gain: bfloat16 [2048], P('dp'), may hold values from 0.5 to 1.5
- w_up: bfloat16 [2048, 8192], P('dp', 'tensor'), may hold values from -0.125 to 0.125
- w_down: bfloat16 [8192, 2048], P('tensor', 'dp'), may hold values from -0.0625 to 0.0625
- out_cotangent: bfloat16 [16, 1024, 2048], P('dp', 'tensor'), may hold values from -6 to 6
Outputs:
- block_output: bfloat16 [16, 1024, 2048], P('dp', 'tensor')
- input_grad: float32 [16, 1024, 2048], P('dp', 'tensor')
- norm1_gain_grad: float32 [2048], P('dp')
- w_query_grad: float32 [2048, 2048], P('dp', 'tensor')
- w_key_grad: float32 [2048, 2048], P('dp', 'tensor')
- w_value_grad: float32 [2048, 2048], P('dp', 'tensor')
- w_out_grad: float32 [2048, 2048], P('tensor', 'dp')
- norm2_gain_grad: float32 [2048], P('dp')
- w_up_grad: float32 [2048, 8192], P('dp', 'tensor')
- w_down_grad: float32 [8192, 2048], P('tensor', 'dp')
The draws below stay inside these ranges and needn't reach their ends.
Inputs may be any that keep to these rules, and one draw needn't show every extreme that they name: `clip_lengths`: in every buffer the 8 clip lengths sum to 896, and the longest clip has exactly 512 tokens.
All inputs are finite; a program needn't handle non-finite values.
Results may differ from the reference program's by a relative error of at most 0.018.
Values may be sent and summed in bfloat16 or wider, within the bound.
A program may use at most 256 MiB of HBM per device.

```python
import math
import jax
import jax.numpy as jnp
import numpy as np
from jax import lax

D = 2048
HEADS = 16
HEAD = 128
FF = 8192
SLOTS = 1024
CLIPS = 8
LONGEST = 512
FILLED = 896
BUFFERS = 16


def level_of(rng, dims, pieces, low, largest):
    loudness = 1.0
    for position, blocks in pieces:
        draws = jax.random.uniform(jax.random.fold_in(jax.random.fold_in(rng, 6), position), (blocks,), jnp.float32, low / len(pieces), largest / len(pieces))
        loudness = loudness * jnp.repeat(jnp.exp(draws), dims[position] // blocks).reshape((-1,) + (1,) * (len(dims) - 1 - position))
    return loudness


def split_up(amount, total, reach, skew):
    portions = [(1 << 20) // math.isqrt(rank ** skew) + 1 for rank in range(2, amount + 1)]
    spare, holding = total - reach - (amount - 1), [1] * (amount - 1)
    while spare > 0:
        free = [i for i in range(amount - 1) if holding[i] < reach]
        mass, left = sum([portions[i] for i in free]), spare
        for i in free:
            more = min(reach - holding[i], max(1, left * portions[i] // mass), spare)
            holding[i] = holding[i] + more
            spare = spare - more
    return np.array([reach] + holding)


def uneven(rng, amount, total, most, slope):
    if amount == 2:
        one = jax.random.randint(rng, (), max(1, total - most), min(most, total - 1) + 1)
        return jnp.stack([one, total - one])
    sizes = jnp.asarray(split_up(amount, total, most, slope), jnp.int32)
    twos = (amount - 1) // 2
    donor, sink = sizes[1:1 + 2 * twos:2], sizes[2:2 + 2 * twos:2]
    slack = jnp.minimum(donor - 1, most - sink)
    shifted = jax.random.randint(jax.random.fold_in(rng, 1), (twos,), 0, 1 << 20) % (slack + 1)
    sizes = sizes.at[1:1 + 2 * twos:2].set(donor - shifted).at[2:2 + 2 * twos:2].set(sink + shifted)
    return sizes[jax.random.permutation(jax.random.fold_in(rng, 2), amount)]


def scatter_about(stream_key, extent, width, most, split=(), kind=jnp.bfloat16):
    level = level_of(stream_key, extent, split, -0.22, 0.18) if split else 1.0
    values = jax.random.normal(stream_key, extent, jnp.float32) * width * level
    return jnp.minimum(jnp.maximum(values, -most), most).astype(kind)


def setup_inputs(seed: int = 0) -> dict:
    seeds = jax.random.split(jax.random.key(seed), 12)
    return {
        "block_input": scatter_about(seeds[0], (BUFFERS, SLOTS, D), 1.0, 6.0, ((0, 8), (1, 4))),
        "clip_lengths": jax.vmap(lambda own: uneven(own, CLIPS, FILLED, LONGEST, 2))(jax.random.split(seeds[1], BUFFERS)).reshape((BUFFERS, CLIPS)).astype(jnp.int32),
        "norm1_gain": jnp.clip(1.0 + 0.1 * jax.random.normal(seeds[2], (D,), jnp.float32), 0.5, 1.5).astype(jnp.bfloat16),
        "w_query": scatter_about(seeds[3], (D, D), D ** -0.5, 0.125, ((0, 8), (1, 4))),
        "w_key": scatter_about(seeds[4], (D, D), D ** -0.5, 0.125, ((0, 8), (1, 4))),
        "w_value": scatter_about(seeds[5], (D, D), D ** -0.5, 0.125, ((0, 8), (1, 4))),
        "w_out": scatter_about(seeds[6], (D, D), (D // 16) ** -0.5, 0.5, ((0, 4), (1, 8))),
        "norm2_gain": jnp.clip(1.0 + 0.1 * jax.random.normal(seeds[7], (D,), jnp.float32), 0.5, 1.5).astype(jnp.bfloat16),
        "w_up": scatter_about(seeds[8], (D, FF), D ** -0.5, 0.125, ((0, 8), (1, 4))),
        "w_down": scatter_about(seeds[9], (FF, D), FF ** -0.5, 0.0625, ((0, 4), (1, 8))),
        "out_cotangent": scatter_about(seeds[10], (BUFFERS, SLOTS, D), 1.0, 6.0, ((0, 8), (1, 4))),
    }


@jax.custom_vjp
def low(v):
    return lax.optimization_barrier(v.astype(jnp.bfloat16)).astype(jnp.float32)

@jax.custom_vjp
def low_back(v):
    return v

def low_keep(v):
    return (low(v), None)

def low_pass(kept, grad):
    return (grad,)

def back_keep(v):
    return (v, None)

def back_low(kept, grad):
    return (low(grad),)
low.defvjp(low_keep, low_pass)
low_back.defvjp(back_keep, back_low)
epsilon = 1e-05
masked_fill = -1000000000.0
highest = lax.Precision.HIGHEST

def matmul(left, right):
    return jnp.dot(left, right, precision=highest, preferred_element_type=jnp.float32)

def layer_norm(tokens, gain):
    centred = tokens - lax.optimization_barrier(jnp.mean(tokens, axis=-1, keepdims=True))
    inverse = lax.rsqrt(lax.optimization_barrier(jnp.mean(centred * centred, axis=-1, keepdims=True)) + epsilon)
    return centred * inverse * gain

def segments_of(lengths):
    places = jnp.arange(SLOTS, dtype=jnp.int32)
    ends = jnp.cumsum(lengths).astype(jnp.int32)
    return lax.optimization_barrier(jnp.sum((places[:, None] >= ends[None, :]).astype(jnp.int32), axis=1)).astype(jnp.int32)

def attention(query, key, value, segment):
    block_rows = min(512, SLOTS)
    places = jnp.arange(SLOTS, dtype=jnp.int32)

    def one_block(block_index):
        offset = (block_index * block_rows).astype(jnp.int32)
        q_rows = lax.dynamic_slice_in_dim(query, offset, block_rows, 0)
        q_segment = lax.dynamic_slice_in_dim(segment, offset, block_rows, 0)
        q_place = offset + jnp.arange(block_rows, dtype=jnp.int32)
        raw_scores = jnp.einsum('qhd,khd->hqk', q_rows, key, precision=highest)
        scores = low_back(raw_scores) * HEAD ** (-0.5)
        allowed = (q_segment[:, None] == segment[None, :]) & (places[None, :] <= q_place[:, None])
        scores = jnp.where(allowed[None], scores, masked_fill)
        weights = low(jax.nn.softmax(scores, axis=-1))
        return jnp.einsum('hqk,khd->qhd', weights, value, precision=highest)
    blocks = lax.map(jax.checkpoint(one_block), jnp.arange(SLOTS // block_rows, dtype=jnp.int32))
    return blocks.reshape(SLOTS, HEADS * HEAD)

def layer(tokens, segment, gain_one, query_w, key_w, value_w, out_w, gain_two, up_w, down_w):
    normed_one = low(layer_norm(tokens, gain_one))
    query = low(low_back(matmul(normed_one, query_w))).reshape(SLOTS, HEADS, HEAD)
    key = low(low_back(matmul(normed_one, key_w))).reshape(SLOTS, HEADS, HEAD)
    value = low(low_back(matmul(normed_one, value_w))).reshape(SLOTS, HEADS, HEAD)
    attended = low(low_back(attention(query, key, value, segment)))
    hidden = tokens + low_back(matmul(attended, out_w))
    normed_two = low(layer_norm(hidden, gain_two))
    pre_act = low_back(matmul(normed_two, up_w))
    activated = low(jax.nn.gelu(pre_act, approximate=True))
    return hidden + low_back(matmul(activated, down_w))

def reference(block_input, clip_lengths, norm1_gain, w_query, w_key, w_value, w_out, norm2_gain, w_up, w_down, out_cotangent):
    params = (norm1_gain.astype(jnp.float32), w_query.astype(jnp.float32), w_key.astype(jnp.float32), w_value.astype(jnp.float32), w_out.astype(jnp.float32), norm2_gain.astype(jnp.float32), w_up.astype(jnp.float32), w_down.astype(jnp.float32))

    def stepper(carried, buffer_in):
        tokens, lengths, cotangent = buffer_in
        segment = segments_of(lengths)
        valid_rows = (segment < CLIPS).astype(jnp.float32)

        def local_layer(*values):
            return layer(values[0], segment, *values[1:])
        output, pullback = jax.vjp(local_layer, tokens.astype(jnp.float32), *params)
        gradients = pullback(cotangent.astype(jnp.float32) * valid_rows[:, None])
        carried = tuple((summed + gradient for summed, gradient in zip(carried, gradients[1:])))
        return (carried, (output.astype(jnp.bfloat16), gradients[0]))
    initial = tuple((jnp.zeros_like(weight_in) for weight_in in params))
    summed, (outputs, input_grad) = lax.scan(stepper, initial, (block_input, clip_lengths, out_cotangent))
    return (outputs, input_grad, summed[0], summed[1], summed[2], summed[3], summed[4], summed[5], summed[6], summed[7])
```

```python
import functools

import jax
import jax.numpy as jnp
from jax import lax
from jax.experimental import pallas as pl
from jax.experimental.pallas import tpu as pltpu
from jax.sharding import PartitionSpec as P

HEAD = 128
LONGEST = 512
epsilon = 1e-05
masked_fill = -1000000000.0
bf16 = jnp.bfloat16
f32 = jnp.float32


def norm_rows(tokens, gain):
    centred = tokens - jnp.mean(tokens, axis=-1, keepdims=True)
    inverse = lax.rsqrt(jnp.mean(centred * centred, axis=-1, keepdims=True) + epsilon)
    unit_rows = centred * inverse
    return (unit_rows * gain, unit_rows, inverse)


def norm_back(grad_normed, unit_rows, inverse, gain):
    scaled = grad_normed * gain
    inner_sum = (
        scaled
        - jnp.mean(scaled, axis=-1, keepdims=True)
        - unit_rows * jnp.mean(scaled * unit_rows, axis=-1, keepdims=True)
    )
    return (inverse * inner_sum, jnp.sum(grad_normed * unit_rows, axis=0))


def gelu_tanh(values):
    return jax.nn.gelu(values, approximate=True)


def chunk_scores(q, k, start, s, c, rows):
    scores = lax.dot_general(
        q, k, (((1,), (1,)), ((), ())), preferred_element_type=f32
    ) * HEAD ** (-0.5)
    k_place = c * rows + lax.broadcasted_iota(jnp.int32, (rows, rows), 1)
    allowed = k_place >= start
    if c == s:
        q_place = s * rows + lax.broadcasted_iota(jnp.int32, (rows, rows), 0)
        allowed = jnp.logical_and(allowed, k_place <= q_place)
    return jnp.where(allowed, scores, masked_fill)


def clip_starts(ends_ref, buffer, clip_count, s, rows):
    place = s * rows + lax.broadcasted_iota(jnp.int32, (rows, 1), 0)
    start = jnp.zeros((rows, 1), jnp.int32)
    for clip in range(clip_count):
        end = ends_ref[buffer * clip_count + clip]
        start = jnp.where(place >= end, jnp.maximum(start, end), start)
    return start


def window(s, rows):
    back = -(-(LONGEST - 1) // rows)
    return range(max(0, s - back), s + 1)


def chunk_probs(q, keys, start, s, rows):
    cs = list(window(s, rows))
    scores = [chunk_scores(q, keys(c), start, s, c, rows) for c in cs]
    highest = functools.reduce(jnp.maximum, [jnp.max(v, axis=1, keepdims=True) for v in scores])
    shifted = [jnp.exp(v - highest) for v in scores]
    total = functools.reduce(jnp.add, [jnp.sum(v, axis=1, keepdims=True) for v in shifted])
    scale = 1.0 / total
    return cs, [v * scale for v in shifted]


def attend_kernel(clip_count, chunks, ends_ref, place_ref, qkv_ref, out_ref):
    buffer = pl.program_id(0)
    x_count = qkv_ref.shape[2]
    rows = qkv_ref.shape[3]

    def at(s):
        return (s // x_count) ^ place_ref[0], 0, (s % x_count) ^ place_ref[1]

    for s in range(chunks):
        q = qkv_ref[at(s)][:, :HEAD]
        start = clip_starts(ends_ref, buffer, clip_count, s, rows)
        cs, probs = chunk_probs(q, lambda c: qkv_ref[at(c)][:, HEAD : 2 * HEAD], start, s, rows)
        mixed = jnp.zeros((rows, HEAD), f32)
        for c, prob in zip(cs, probs):
            value = qkv_ref[at(c)][:, 2 * HEAD :]
            mixed = mixed + jnp.dot(prob.astype(bf16), value, preferred_element_type=f32)
        k_at, _, x_at = at(s)
        out_ref[k_at, 0, x_at] = mixed.astype(bf16)


def attend_back_kernel(
    clip_count, chunks, ends_ref, place_ref, qkv_ref, grad_ref, out_ref, key_sum, value_sum
):
    buffer = pl.program_id(0)
    x_count = qkv_ref.shape[2]
    rows = qkv_ref.shape[3]

    def at(s):
        return (s // x_count) ^ place_ref[0], 0, (s % x_count) ^ place_ref[1]

    key_sum[...] = jnp.zeros_like(key_sum)
    value_sum[...] = jnp.zeros_like(value_sum)
    for s in range(chunks):
        q = qkv_ref[at(s)][:, :HEAD]
        grad = grad_ref[at(s)]
        start = clip_starts(ends_ref, buffer, clip_count, s, rows)
        cs, probs = chunk_probs(q, lambda c: qkv_ref[at(c)][:, HEAD : 2 * HEAD], start, s, rows)
        grad_probs = [
            lax.dot_general(
                grad,
                qkv_ref[at(c)][:, 2 * HEAD :],
                (((1,), (1,)), ((), ())),
                preferred_element_type=f32,
            )
            for c in cs
        ]
        inner = functools.reduce(
            jnp.add,
            [jnp.sum(p * g, axis=1, keepdims=True) for p, g in zip(probs, grad_probs)],
        )
        grad_q = jnp.zeros((rows, HEAD), f32)
        for c, prob, grad_prob in zip(cs, probs, grad_probs):
            grad_score = (prob * (grad_prob - inner) * HEAD ** (-0.5)).astype(bf16)
            key = qkv_ref[at(c)][:, HEAD : 2 * HEAD]
            grad_q = grad_q + jnp.dot(grad_score, key, preferred_element_type=f32)
            key_sum[c] += lax.dot_general(
                grad_score, q, (((0,), (0,)), ((), ())), preferred_element_type=f32
            )
            value_sum[c] += lax.dot_general(
                prob.astype(bf16), grad, (((0,), (0,)), ((), ())), preferred_element_type=f32
            )
        k_at, _, x_at = at(s)
        out_ref[k_at, 0, x_at, :, :HEAD] = grad_q.astype(bf16)
    for s in range(chunks):
        k_at, _, x_at = at(s)
        out_ref[k_at, 0, x_at, :, HEAD : 2 * HEAD] = key_sum[s].astype(bf16)
        out_ref[k_at, 0, x_at, :, 2 * HEAD :] = value_sum[s].astype(bf16)


def attention_call(kernel, name, qkv, ends, place, width, scratch, matmuls, *more):
    two, buffers, x_count, rows, columns = qkv.shape
    heads = columns // (3 * HEAD)
    chunks = two * x_count
    clip_count = ends.shape[0] // buffers

    def spec(cols):
        return pl.BlockSpec((two, 1, x_count, rows, cols), lambda b, h, *_: (0, b, 0, 0, h))

    pairs = sum(len(window(s, rows)) for s in range(chunks)) * rows * rows * buffers * heads
    return pl.pallas_call(
        functools.partial(kernel, clip_count, chunks),
        out_shape=jax.ShapeDtypeStruct((two, buffers, x_count, rows, heads * width), bf16),
        grid_spec=pltpu.PrefetchScalarGridSpec(
            num_scalar_prefetch=2,
            grid=(buffers, heads),
            in_specs=[spec(3 * HEAD)] + [spec(HEAD) for _ in more],
            out_specs=spec(width),
            scratch_shapes=[pltpu.VMEM((chunks, rows, HEAD), f32) for _ in range(scratch)],
        ),
        compiler_params=pltpu.CompilerParams(
            dimension_semantics=("arbitrary", "arbitrary"), vmem_limit_bytes=32 << 20
        ),
        cost_estimate=pl.CostEstimate(
            flops=2 * matmuls * pairs * HEAD,
            transcendentals=pairs,
            bytes_accessed=qkv.size * 4,
        ),
        name=name,
    )(ends, place, qkv, *more)


def on_device(
    block_input,
    clip_lengths,
    norm1_gain,
    w_query,
    w_key,
    w_value,
    w_out,
    norm2_gain,
    w_up,
    w_down,
    out_cotangent,
):
    streams, rows, width = block_input.shape
    planes = lax.axis_size("tensor")
    lanes = lax.axis_size("dp")
    groups = lanes // planes
    x_count = planes // 2
    clip_count = clip_lengths.shape[1]
    own = lax.axis_index("dp")
    own_plane = lax.axis_index("tensor")
    direct = lanes == 8 and planes == 4
    heads = w_query.shape[1] * planes // (HEAD * lanes)

    def lane_chunk(lane):
        return lane // 2 + x_count * (lane % 2)

    chunk_lane = {lane_chunk(lane): lane for lane in range(planes)}
    there = [
        ((g * planes + l) * planes + s, (g * planes + chunk_lane[s]) * planes + lane_chunk(l))
        for g in range(groups)
        for l in range(planes)
        for s in range(planes)
    ]
    back = [(b, a) for a, b in there]

    def hop(value, mask):
        return lax.ppermute(value, "dp", [(i, i ^ mask) for i in range(lanes)])

    def gather_rows(value):
        if not direct:
            whole = lax.all_gather(value, "dp", axis=0, tiled=False)
            whole = whole.reshape(groups * x_count, 2, rows, width)
            return [whole[:, core].reshape(-1, width) for core in range(2)]
        half = rows // 2
        from_x = hop(value, 2)
        from_y = hop(value, 4)
        far_low = hop(from_y[:half], 2)
        far_high = hop(from_x[half:], 4)
        near = jnp.concatenate([value, from_x, from_y, far_low, far_high])
        return [near, hop(near, 1)]

    def sum_rows(term):
        if not direct:
            parts = jnp.stack([term(core).reshape(-1, rows, width) for core in range(2)], axis=1)
            return lax.psum_scatter(
                parts.reshape(-1, width).astype(bf16), "dp", scatter_dimension=0, tiled=True
            ).astype(f32)
        half = rows // 2
        other = hop(term(1).astype(bf16), 1)
        chip = (term(0) + other.astype(f32)).astype(bf16).reshape(4, rows, width)
        low = hop(chip[3, :half], 2)
        high = hop(chip[3, half:], 4)
        x_low = hop(chip[1, :half], 2)
        y_high = hop(chip[2, half:], 4)
        x_high = hop((chip[1, half:].astype(f32) + high.astype(f32)).astype(bf16), 2)
        y_low = hop((chip[2, :half].astype(f32) + low.astype(f32)).astype(bf16), 4)
        from_x = jnp.concatenate([x_low, x_high]).astype(f32)
        from_y = jnp.concatenate([y_low, y_high]).astype(f32)
        return chip[0].astype(f32) + from_x + from_y

    tokens_in = lax.ppermute(block_input, ("dp", "tensor"), there)

    attn_local = jnp.stack([w_query.T, w_key.T, w_value.T, w_out])
    attn_wide = lax.all_gather(attn_local, "tensor", axis=1, tiled=True)
    attn_w = lax.all_to_all(attn_wide, "dp", 1, 2, tiled=True)
    qkv_w = attn_w[:3].reshape(3, heads, HEAD, width).swapaxes(0, 1).reshape(-1, width)
    out_w = attn_w[3]
    up_part = lax.all_to_all(w_up.T, "dp", 0, 1, tiled=True)
    up_w = lax.all_gather(up_part, "tensor", axis=0, tiled=True)
    down_part = lax.all_to_all(w_down, "dp", 0, 1, tiled=True)
    down_w = lax.all_gather(down_part, "tensor", axis=0, tiled=True)
    gains = lax.all_gather(jnp.stack([norm1_gain, norm2_gain]), "dp", axis=1, tiled=True)
    gain_one = gains[0].astype(f32)
    gain_two = gains[1].astype(f32)

    cotangent = lax.ppermute(out_cotangent, ("dp", "tensor"), there)

    all_ends = jnp.cumsum(lax.all_gather(clip_lengths, "dp", axis=0, tiled=True), axis=1)
    own_group = own // planes
    own_lane = own % planes
    plane_lane = 2 * (own_plane % x_count) + own_plane // x_count
    group_ids = jnp.arange(groups, dtype=jnp.int32)
    if direct:
        group_ids = group_ids ^ own_group
        place = jnp.stack([own_lane % 2, own_lane // 2]).astype(jnp.int32)
    else:
        place = jnp.zeros((2,), jnp.int32)
    own_chunk = own_lane // 2 + x_count * (own_lane % 2)
    own_places = own_chunk * rows + jnp.arange(rows, dtype=jnp.int32)

    def rows_dot(left, right):
        return lax.dot_general(left, right, (((1,), (1,)), ((), ())), preferred_element_type=f32)

    def grad_dot(left, right):
        return lax.dot_general(left, right, (((0,), (0,)), ((), ())), preferred_element_type=f32)

    saved = []
    outputs = []
    for stream in range(streams):
        buffers = (group_ids * planes + plane_lane) * streams + stream
        ends = jnp.take(all_ends, buffers, axis=0).reshape(-1).astype(jnp.int32)
        own_buffer = (own_group * planes + plane_lane) * streams + stream
        last_end = lax.dynamic_index_in_dim(all_ends, own_buffer, 0, keepdims=False)[-1]
        valid = (own_places < last_end).astype(f32)
        tokens = tokens_in[stream].astype(f32)
        normed_one, unit_one, inverse_one = norm_rows(tokens, gain_one)
        features_one = gather_rows(normed_one.astype(bf16))
        qkv = jnp.stack([rows_dot(part, qkv_w).astype(bf16) for part in features_one])
        qkv = qkv.reshape(2, groups, x_count, rows, -1)
        mixed = attention_call(attend_kernel, "attend", qkv, ends, place, HEAD, 0, 2)
        mixed = mixed.reshape(2, groups * x_count * rows, heads * HEAD)
        hidden = tokens + sum_rows(
            lambda core: jnp.dot(mixed[core], out_w, preferred_element_type=f32)
        )
        normed_two, unit_two, inverse_two = norm_rows(hidden, gain_two)
        features_two = gather_rows(normed_two.astype(bf16))
        pre_act = [rows_dot(part, up_w) for part in features_two]
        activated = [gelu_tanh(part).astype(bf16) for part in pre_act]
        outputs.append(
            (
                hidden
                + sum_rows(
                    lambda core: jnp.dot(activated[core], down_w, preferred_element_type=f32)
                )
            ).astype(bf16)
        )
        grad_out = cotangent[stream].astype(f32) * valid[:, None]
        grad_branch = gather_rows(grad_out.astype(bf16))
        saved.append(
            (
                ends,
                features_one,
                unit_one,
                inverse_one,
                qkv,
                mixed,
                unit_two,
                inverse_two,
                features_two,
                pre_act,
                activated,
                grad_out,
                grad_branch,
            )
        )
    block_output = lax.ppermute(jnp.stack(outputs), ("dp", "tensor"), back)

    down_terms, up_terms, out_terms, qkv_terms = [], [], [], []
    gain_one_grad = 0.0
    gain_two_grad = 0.0
    input_grads = []
    middle = []
    for stream in range(streams):
        (ends, features_one, unit_one, inverse_one, qkv, mixed, unit_two, inverse_two) = saved[
            stream
        ][:8]
        features_two, pre_act, activated, grad_out, grad_branch = saved[stream][8:]
        grad_pre = []
        for core in range(2):
            grad_act = rows_dot(grad_branch[core], down_w)
            grad_pre.append(jax.vjp(gelu_tanh, pre_act[core])[1](grad_act)[0].astype(bf16))
        grad_normed_two = sum_rows(
            lambda core: jnp.dot(grad_pre[core], up_w, preferred_element_type=f32)
        )
        for core in range(2):
            down_terms.append(grad_dot(activated[core], grad_branch[core]))
            up_terms.append(grad_dot(grad_pre[core], features_two[core]))
        grad_from_two, gain_part = norm_back(grad_normed_two, unit_two, inverse_two, gain_two)
        gain_two_grad = gain_two_grad + gain_part
        middle.append(grad_out + grad_from_two)

    def summed(terms):
        return functools.reduce(jnp.add, terms).astype(bf16)

    def mlp_grad(terms):
        part = lax.psum_scatter(summed(terms), "tensor", scatter_dimension=0, tiled=True)
        return lax.all_to_all(part, "dp", 1, 0, tiled=True).astype(f32)

    down_grad = mlp_grad(down_terms)
    up_grad = mlp_grad(up_terms).T

    for stream in range(streams):
        (ends, features_one, unit_one, inverse_one, qkv, mixed, unit_two, inverse_two) = saved[
            stream
        ][:8]
        grad_hidden = middle[stream]
        grad_attn = gather_rows(grad_hidden.astype(bf16))
        grad_mixed = jnp.stack([rows_dot(part, out_w).astype(bf16) for part in grad_attn])
        for core in range(2):
            out_terms.append(grad_dot(mixed[core], grad_attn[core]))
        grad_qkv = attention_call(
            attend_back_kernel,
            "attend_back",
            qkv,
            ends,
            place,
            3 * HEAD,
            2,
            5,
            grad_mixed.reshape(2, groups, x_count, rows, heads * HEAD),
        ).reshape(2, groups * x_count * rows, -1)
        grad_normed_one = sum_rows(
            lambda core: jnp.dot(grad_qkv[core], qkv_w, preferred_element_type=f32)
        )
        for core in range(2):
            qkv_terms.append(grad_dot(grad_qkv[core], features_one[core]))
        grad_from_one, gain_part = norm_back(grad_normed_one, unit_one, inverse_one, gain_one)
        gain_one_grad = gain_one_grad + gain_part
        input_grads.append((grad_hidden + grad_from_one).astype(bf16))
    input_grad = lax.ppermute(jnp.stack(input_grads), ("dp", "tensor"), back).astype(f32)

    qkv_sum = summed(qkv_terms).reshape(heads, 3, HEAD, width).swapaxes(0, 1)
    attn_sum = jnp.concatenate([qkv_sum.reshape(3, -1, width), summed(out_terms)[None]])
    attn_part = lax.all_to_all(attn_sum, "dp", 2, 1, tiled=True)
    attn_grad = lax.psum_scatter(attn_part, "tensor", scatter_dimension=1, tiled=True).astype(f32)

    gain_grads = lax.psum_scatter(
        jnp.stack([gain_one_grad, gain_two_grad]), "dp", scatter_dimension=1, tiled=True
    )
    gain_grads = lax.psum(gain_grads, "tensor")
    return (
        block_output,
        input_grad,
        gain_grads[0],
        attn_grad[0].T,
        attn_grad[1].T,
        attn_grad[2].T,
        attn_grad[3],
        gain_grads[1],
        up_grad,
        down_grad,
    )


def solution(mesh):
    in_specs = (
        P("dp", "tensor", None),
        P("dp", None),
        P("dp"),
        P("dp", "tensor"),
        P("dp", "tensor"),
        P("dp", "tensor"),
        P("tensor", "dp"),
        P("dp"),
        P("dp", "tensor"),
        P("tensor", "dp"),
        P("dp", "tensor", None),
    )
    out_specs = (
        P("dp", "tensor", None),
        P("dp", "tensor", None),
        P("dp"),
        P("dp", "tensor"),
        P("dp", "tensor"),
        P("dp", "tensor"),
        P("tensor", "dp"),
        P("dp"),
        P("dp", "tensor"),
        P("tensor", "dp"),
    )
    return jax.shard_map(
        on_device, mesh=mesh, in_specs=in_specs, out_specs=out_specs, check_vma=False
    )
```

```python
import functools

import jax
import jax.numpy as jnp
import numpy as np
from jax import lax
from jax.experimental import pallas as pl
from jax.experimental.pallas import tpu as pltpu
from jax.sharding import PartitionSpec as P

HEAD = 128
LONGEST = 512
epsilon = 1e-05
masked_fill = -1000000000.0
bf16 = jnp.bfloat16
f32 = jnp.float32


def norm_rows(tokens, gain):
    centred = tokens - jnp.mean(tokens, axis=-1, keepdims=True)
    inverse = lax.rsqrt(jnp.mean(centred * centred, axis=-1, keepdims=True) + epsilon)
    unit_rows = centred * inverse
    return (unit_rows * gain, unit_rows, inverse)


def norm_back(grad_normed, unit_rows, inverse, gain):
    scaled = grad_normed * gain
    inner_sum = (
        scaled
        - jnp.mean(scaled, axis=-1, keepdims=True)
        - unit_rows * jnp.mean(scaled * unit_rows, axis=-1, keepdims=True)
    )
    return (inverse * inner_sum, jnp.sum(grad_normed * unit_rows, axis=0))


def gelu_tanh(values):
    return jax.nn.gelu(values, approximate=True)


def masked_scores(q_rows, keys_heads, segment, offset, block_rows):
    slot_count = keys_heads.shape[0]
    raw_scores = jnp.einsum(
        "qhd,khd->hqk", q_rows, keys_heads, preferred_element_type=jnp.float32
    ) * HEAD ** (-0.5)
    q_segment = lax.dynamic_slice_in_dim(segment, offset, block_rows, 0)
    q_place = offset + jnp.arange(block_rows, dtype=jnp.int32)
    places = jnp.arange(slot_count, dtype=jnp.int32)
    allowed = (q_segment[:, None] == segment[None, :]) & (places[None, :] <= q_place[:, None])
    return jnp.where(allowed[None], raw_scores, masked_fill)


def attend(query, key, value, segment, block_rows):
    slot_count = query.shape[0]
    head_count = query.shape[1] // HEAD
    keys_heads = key.reshape(slot_count, head_count, HEAD)
    values_heads = value.reshape(slot_count, head_count, HEAD)

    def one_block(block_index):
        offset = block_index * block_rows
        q_rows = lax.dynamic_slice_in_dim(query, offset, block_rows, 0).reshape(
            block_rows, head_count, HEAD
        )
        scores = masked_scores(q_rows, keys_heads, segment, offset, block_rows)
        highest = jnp.max(scores, axis=-1, keepdims=True)
        shifted = jnp.exp(scores - highest)
        totals = jnp.sum(shifted, axis=-1, keepdims=True)
        weights = (shifted / totals).astype(jnp.bfloat16)
        mixed_rows = jnp.einsum(
            "hqk,khd->qhd", weights, values_heads, preferred_element_type=jnp.float32
        )
        return (
            mixed_rows.reshape(block_rows, head_count * HEAD).astype(jnp.bfloat16),
            (highest + jnp.log(totals))[..., 0],
        )

    mixed_rows, log_norm = lax.map(one_block, jnp.arange(slot_count // block_rows, dtype=jnp.int32))
    return (mixed_rows.reshape(slot_count, head_count * HEAD), log_norm)


def attend_back(query, key, value, segment, log_norm, grad_mixed, block_rows):
    slot_count = query.shape[0]
    head_count = query.shape[1] // HEAD
    keys_heads = key.reshape(slot_count, head_count, HEAD)
    values_heads = value.reshape(slot_count, head_count, HEAD)

    def one_block(carried, block_index):
        grad_keys, grad_values = carried
        offset = block_index * block_rows
        q_rows = lax.dynamic_slice_in_dim(query, offset, block_rows, 0).reshape(
            block_rows, head_count, HEAD
        )
        g_rows = lax.dynamic_slice_in_dim(grad_mixed, offset, block_rows, 0).reshape(
            block_rows, head_count, HEAD
        )
        scores = masked_scores(q_rows, keys_heads, segment, offset, block_rows)
        prob_rows = jnp.exp(scores - log_norm[block_index][..., None])
        grad_values = grad_values + jnp.einsum(
            "hqk,qhd->khd",
            prob_rows.astype(jnp.bfloat16),
            g_rows,
            preferred_element_type=jnp.float32,
        )
        grad_probs = jnp.einsum(
            "qhd,khd->hqk", g_rows, values_heads, preferred_element_type=jnp.float32
        )
        inner_sum = jnp.sum(prob_rows * grad_probs, axis=-1, keepdims=True)
        grad_scores = (prob_rows * (grad_probs - inner_sum) * HEAD ** (-0.5)).astype(jnp.bfloat16)
        grad_query = jnp.einsum(
            "hqk,khd->qhd", grad_scores, keys_heads, preferred_element_type=jnp.float32
        )
        grad_keys = grad_keys + jnp.einsum(
            "hqk,qhd->khd", grad_scores, q_rows, preferred_element_type=jnp.float32
        )
        return (
            (grad_keys, grad_values),
            grad_query.reshape(block_rows, head_count * HEAD).astype(jnp.bfloat16),
        )

    zero_state = jnp.zeros((slot_count, head_count, HEAD), jnp.float32)
    (grad_keys, grad_values), grad_query = lax.scan(
        one_block, (zero_state, zero_state), jnp.arange(slot_count // block_rows, dtype=jnp.int32)
    )
    return (
        grad_query.reshape(slot_count, head_count * HEAD),
        grad_keys.reshape(slot_count, head_count * HEAD).astype(jnp.bfloat16),
        grad_values.reshape(slot_count, head_count * HEAD).astype(jnp.bfloat16),
    )


def on_device_any(
    block_input,
    clip_lengths,
    norm1_gain,
    w_query,
    w_key,
    w_value,
    w_out,
    norm2_gain,
    w_up,
    w_down,
    out_cotangent,
):
    micro_count = block_input.shape[0]
    local_rows = block_input.shape[1]
    tensor_size = lax.axis_size("tensor")
    slot_count = local_rows * tensor_size
    block_rows = min(512, slot_count)
    clip_count = clip_lengths.shape[1]
    row_offset = lax.axis_index("tensor") * local_rows
    places = jnp.arange(slot_count, dtype=jnp.int32)

    def fetch_weights():
        return (
            lax.all_gather(norm1_gain, "dp", axis=0, tiled=True),
            lax.all_gather(norm2_gain, "dp", axis=0, tiled=True),
            lax.all_gather(w_query, "dp", axis=0, tiled=True),
            lax.all_gather(w_key, "dp", axis=0, tiled=True),
            lax.all_gather(w_value, "dp", axis=0, tiled=True),
            lax.all_gather(w_up, "dp", axis=0, tiled=True),
            lax.all_gather(w_out, "dp", axis=1, tiled=True),
            lax.all_gather(w_down, "dp", axis=1, tiled=True),
        )

    def rows_forward(normed):
        return lax.all_gather(normed, "tensor", axis=0, tiled=True)

    def rows_backward(gradients):
        return lax.all_gather(gradients, "tensor", axis=0, tiled=True)

    def sum_forward(term_fn):
        return lax.psum_scatter(
            term_fn(jnp.int32(0), local_rows * lax.axis_size("tensor")),
            "tensor",
            scatter_dimension=0,
            tiled=True,
        )

    def sum_backward(term_fn):
        return lax.psum_scatter(
            term_fn(jnp.int32(0), local_rows * lax.axis_size("tensor")),
            "tensor",
            scatter_dimension=0,
            tiled=True,
        )

    grad_totals = None
    outputs = []
    input_grads = []
    for micro_index in range(micro_count):
        gathered = fetch_weights()
        gain_one = gathered[0].astype(jnp.float32)
        gain_two = gathered[1].astype(jnp.float32)
        query_w, key_w, value_w, up_w, out_w, down_w = (
            gathered[2],
            gathered[3],
            gathered[4],
            gathered[5],
            gathered[6],
            gathered[7],
        )
        tokens = block_input[micro_index].astype(jnp.float32)
        ends = jnp.cumsum(clip_lengths[micro_index])
        segment = jnp.sum((places[:, None] >= ends[None, :]).astype(jnp.int32), axis=1)
        own_segment = lax.dynamic_slice_in_dim(segment, row_offset, local_rows, 0)
        valid_rows = (own_segment < clip_count).astype(jnp.float32)
        normed_one, unit_one, inverse_one = norm_rows(tokens, gain_one)
        features_one = rows_forward(normed_one.astype(jnp.bfloat16))
        query = jnp.dot(features_one, query_w, preferred_element_type=jnp.float32).astype(
            jnp.bfloat16
        )
        key = jnp.dot(features_one, key_w, preferred_element_type=jnp.float32).astype(jnp.bfloat16)
        value = jnp.dot(features_one, value_w, preferred_element_type=jnp.float32).astype(
            jnp.bfloat16
        )
        mixed_rows, log_norm = attend(query, key, value, segment, block_rows)

        def attn_term(offset, row_count):
            return jnp.dot(mixed_rows, out_w, preferred_element_type=jnp.float32)

        hidden = tokens + sum_forward(attn_term)
        normed_two, unit_two, inverse_two = norm_rows(hidden, gain_two)
        features_two = rows_forward(normed_two.astype(jnp.bfloat16))
        pre_act = jnp.dot(features_two, up_w, preferred_element_type=jnp.float32)
        activated = gelu_tanh(pre_act).astype(jnp.bfloat16)

        def mlp_term(offset, row_count):
            return jnp.dot(activated, down_w, preferred_element_type=jnp.float32)

        outputs.append((hidden + sum_forward(mlp_term)).astype(jnp.bfloat16))
        regathered = fetch_weights()
        query_w, key_w, value_w, up_w, out_w, down_w = (
            regathered[2],
            regathered[3],
            regathered[4],
            regathered[5],
            regathered[6],
            regathered[7],
        )
        grad_out = out_cotangent[micro_index].astype(jnp.float32) * valid_rows[:, None]
        grad_branch = rows_backward(grad_out.astype(jnp.bfloat16))
        down_grad = jnp.einsum(
            "sf,sd->fd", activated, grad_branch, preferred_element_type=jnp.float32
        )
        grad_act = jnp.einsum("sd,fd->sf", grad_branch, down_w, preferred_element_type=jnp.float32)
        grad_pre = jax.vjp(gelu_tanh, pre_act)[1](grad_act)[0].astype(jnp.bfloat16)
        up_grad = jnp.einsum(
            "sd,sf->df", features_two, grad_pre, preferred_element_type=jnp.float32
        )

        def up_term(offset, row_count):
            return jnp.einsum("sf,df->sd", grad_pre, up_w, preferred_element_type=jnp.float32)

        grad_normed_two = sum_backward(up_term)
        grad_from_two, gain_two_grad = norm_back(grad_normed_two, unit_two, inverse_two, gain_two)
        grad_hidden = grad_out + grad_from_two
        grad_attn = rows_backward(grad_hidden.astype(jnp.bfloat16))
        out_grad = jnp.einsum(
            "sc,sd->cd", mixed_rows, grad_attn, preferred_element_type=jnp.float32
        )
        grad_mixed = jnp.einsum(
            "sd,cd->sc", grad_attn, out_w, preferred_element_type=jnp.float32
        ).astype(jnp.bfloat16)
        grad_query, grad_key, grad_value = attend_back(
            query, key, value, segment, log_norm, grad_mixed, block_rows
        )
        query_grad = jnp.einsum(
            "sd,sc->dc", features_one, grad_query, preferred_element_type=jnp.float32
        )
        key_grad = jnp.einsum(
            "sd,sc->dc", features_one, grad_key, preferred_element_type=jnp.float32
        )
        value_grad = jnp.einsum(
            "sd,sc->dc", features_one, grad_value, preferred_element_type=jnp.float32
        )

        def qkv_term(offset, row_count):
            part_query = jnp.einsum(
                "sc,dc->sd", grad_query, query_w, preferred_element_type=jnp.float32
            )
            part_key = jnp.einsum("sc,dc->sd", grad_key, key_w, preferred_element_type=jnp.float32)
            part_value = jnp.einsum(
                "sc,dc->sd", grad_value, value_w, preferred_element_type=jnp.float32
            )
            return part_query + part_key + part_value

        grad_normed_one = sum_backward(qkv_term)
        grad_from_one, gain_one_grad = norm_back(grad_normed_one, unit_one, inverse_one, gain_one)
        input_grads.append(grad_hidden + grad_from_one)
        micro_grads = (
            gain_one_grad,
            gain_two_grad,
            query_grad,
            key_grad,
            value_grad,
            up_grad,
            out_grad,
            down_grad,
        )
        if grad_totals is None:
            grad_totals = micro_grads
        else:
            grad_totals = jax.tree.map(jnp.add, grad_totals, micro_grads)
    grad_totals = (
        lax.psum_scatter(
            grad_totals[0].astype(jnp.bfloat16), "dp", scatter_dimension=0, tiled=True
        ).astype(jnp.float32),
        lax.psum_scatter(
            grad_totals[1].astype(jnp.bfloat16), "dp", scatter_dimension=0, tiled=True
        ).astype(jnp.float32),
        lax.psum_scatter(
            grad_totals[2].astype(jnp.bfloat16), "dp", scatter_dimension=0, tiled=True
        ).astype(jnp.float32),
        lax.psum_scatter(
            grad_totals[3].astype(jnp.bfloat16), "dp", scatter_dimension=0, tiled=True
        ).astype(jnp.float32),
        lax.psum_scatter(
            grad_totals[4].astype(jnp.bfloat16), "dp", scatter_dimension=0, tiled=True
        ).astype(jnp.float32),
        lax.psum_scatter(
            grad_totals[5].astype(jnp.bfloat16), "dp", scatter_dimension=0, tiled=True
        ).astype(jnp.float32),
        lax.psum_scatter(
            grad_totals[6].astype(jnp.bfloat16), "dp", scatter_dimension=1, tiled=True
        ).astype(jnp.float32),
        lax.psum_scatter(
            grad_totals[7].astype(jnp.bfloat16), "dp", scatter_dimension=1, tiled=True
        ).astype(jnp.float32),
    )
    gain_sums = lax.psum((grad_totals[0], grad_totals[1]), "tensor")
    return (
        jnp.stack(outputs),
        jnp.stack(input_grads),
        gain_sums[0],
        grad_totals[2],
        grad_totals[3],
        grad_totals[4],
        grad_totals[6],
        gain_sums[1],
        grad_totals[5],
        grad_totals[7],
    )


def chunk_scores(q, k, start, s, c, rows):
    scores = lax.dot_general(
        q, k, (((1,), (1,)), ((), ())), preferred_element_type=f32
    ) * HEAD ** (-0.5)
    k_place = c * rows + lax.broadcasted_iota(jnp.int32, (rows, rows), 1)
    allowed = k_place >= start
    if c == s:
        q_place = s * rows + lax.broadcasted_iota(jnp.int32, (rows, rows), 0)
        allowed = jnp.logical_and(allowed, k_place <= q_place)
    return jnp.where(allowed, scores, masked_fill)


def clip_starts(ends_ref, first, buffer, clip_count, s, rows):
    place = s * rows + lax.broadcasted_iota(jnp.int32, (rows, 1), 0)
    start = jnp.zeros((rows, 1), jnp.int32)
    for clip in range(clip_count):
        end = ends_ref[first + buffer * clip_count + clip]
        start = jnp.where(place >= end, jnp.maximum(start, end), start)
    return start


def window(s, rows):
    back = -(-(LONGEST - 1) // rows)
    return range(max(0, s - back), s + 1)


def chunk_probs(q, keys, start, s, rows):
    cs = list(window(s, rows))
    scores = [chunk_scores(q, keys(c), start, s, c, rows) for c in cs]
    highest = functools.reduce(jnp.maximum, [jnp.max(v, axis=1, keepdims=True) for v in scores])
    shifted = [jnp.exp(v - highest) for v in scores]
    total = functools.reduce(jnp.add, [jnp.sum(v, axis=1, keepdims=True) for v in shifted])
    scale = 1.0 / total
    return cs, [v * scale for v in shifted]


MESH = pl.DeviceIdType.MESH
N_TILE = 256


class Plane:
    def __init__(self, send_sems, recv_sems):
        me = lax.axis_index("dp")
        self.core = me % 2
        self.x = (me // 2) % 2
        self.peers = {
            "c": me + 1 - 2 * (me % 2),
            "x": me + 2 - 4 * ((me // 2) % 2),
            "y": me + 4 - 8 * ((me // 4) % 2),
        }
        self.send_sems, self.recv_sems = send_sems, recv_sems
        self.copies = []
        barrier = pltpu.get_barrier_semaphore()
        for peer in self.peers.values():
            pl.semaphore_signal(barrier, inc=1, device_id={"dp": peer}, device_id_type=MESH)
        pl.semaphore_wait(barrier, 3)

    def send(self, src, dst, way):
        index = len(self.copies)
        copy = pltpu.make_async_remote_copy(
            src_ref=src,
            dst_ref=dst,
            send_sem=self.send_sems.at[index],
            recv_sem=self.recv_sems.at[index],
            device_id={"dp": self.peers[way]},
            device_id_type=MESH,
        )
        copy.start()
        self.copies.append(copy)
        return copy

    def finish(self):
        for copy in self.copies:
            copy.wait_send()


class Gather:
    def __init__(self, plane, own, pieces):
        self.plane, self.own, self.pieces = plane, own, pieces
        self.half = own.shape[0] // 2

    def begin(self):
        send = self.plane.send
        self.x = send(self.own, self.pieces.at[1], "x")
        self.y = send(self.own, self.pieces.at[2], "y")
        self.c = [send(self.own, self.pieces.at[4], "c")]

    def middle(self):
        send, half, pieces = self.plane.send, self.half, self.pieces
        self.x.wait_recv()
        self.fy = send(pieces.at[1, pl.ds(half, half)], pieces.at[3, pl.ds(half, half)], "y")
        self.c.append(send(pieces.at[1], pieces.at[5], "c"))
        self.y.wait_recv()
        self.fx = send(pieces.at[2, pl.ds(0, half)], pieces.at[3, pl.ds(0, half)], "x")
        self.c.append(send(pieces.at[2], pieces.at[6], "c"))

    def end(self):
        self.fx.wait_recv()
        self.fy.wait_recv()
        self.c.append(self.plane.send(self.pieces.at[3], self.pieces.at[7], "c"))

    def core(self, index):
        self.c[index].wait_recv()


class Reduce:
    def __init__(self, plane, pieces, from_core, from_x, from_y):
        self.plane, self.pieces = plane, pieces
        self.from_core, self.from_x, self.from_y = from_core, from_x, from_y
        self.half = pieces.shape[1] // 2
        self.core = {}

    def give(self, m):
        self.core[m] = self.plane.send(self.pieces.at[4 + m], self.from_core.at[m], "c")

    def take(self, m):
        self.core[m].wait_recv()

    def chip_done(self, m):
        send, half, pieces = self.plane.send, self.half, self.pieces
        low, high = pl.ds(0, half), pl.ds(half, half)
        if m == 3:
            self.far_x = send(pieces.at[3, low], self.from_x.at[1], "x")
            self.far_y = send(pieces.at[3, high], self.from_y.at[1], "y")
        elif m == 1:
            self.near_x = send(pieces.at[1, low], self.from_x.at[0], "x")
        elif m == 2:
            self.near_y = send(pieces.at[2, high], self.from_y.at[0], "y")

    def late(self):
        half, pieces = self.half, self.pieces
        low, high = pl.ds(0, half), pl.ds(half, half)
        self.far_y.wait_recv()
        add_into(pieces.at[1, high], self.from_y.at[1])
        self.late_x = self.plane.send(pieces.at[1, high], self.from_x.at[2], "x")
        self.far_x.wait_recv()
        add_into(pieces.at[2, low], self.from_x.at[1])
        self.late_y = self.plane.send(pieces.at[2, low], self.from_y.at[2], "y")

    def total(self, out):
        half = self.half
        self.near_x.wait_recv()
        self.near_y.wait_recv()
        self.late_x.wait_recv()
        self.late_y.wait_recv()
        step = min(64, half)

        for base, x_part, y_part in ((0, 0, 2), (half, 2, 0)):

            def add(index, carry):
                at = pl.ds(pl.multiple_of(index * step, step), step)
                here = pl.ds(pl.multiple_of(base + index * step, step), step)
                out[here] = (
                    self.pieces[0, here].astype(f32)
                    + self.from_x[x_part, at].astype(f32)
                    + self.from_y[y_part, at].astype(f32)
                )
                return carry

            lax.fori_loop(0, half // step, add, 0)


def add_into(ref, other):
    step = min(64, ref.shape[0])

    def add(index, carry):
        at = pl.ds(pl.multiple_of(index * step, step), step)
        ref[at] = (ref[at].astype(f32) + other[at].astype(f32)).astype(bf16)
        return carry

    lax.fori_loop(0, ref.shape[0] // step, add, 0)


ORDER = (3, 1, 2, 0)


def tiles(count, tile, body):
    def step(index, carry):
        body(pl.ds(pl.multiple_of(index * tile, tile), tile))
        return carry

    lax.fori_loop(0, count // tile, step, 0)


def nn(left, right):
    return jnp.dot(left, right, preferred_element_type=f32)


def nt(left, right):
    return lax.dot_general(left, right, (((1,), (1,)), ((), ())), preferred_element_type=f32)


def tn(left, right):
    return lax.dot_general(left, right, (((0,), (0,)), ((), ())), preferred_element_type=f32)


class Feed:
    def __init__(self, source, slots, sems, order):
        self.source, self.slots, self.sems, self.order = source, slots, sems, list(order)

    def copy(self, index):
        slot = index % 2
        return pltpu.make_async_copy(
            self.source(self.order[index]), self.slots.at[slot], self.sems.at[slot]
        )

    def start(self, index):
        if index < len(self.order):
            self.copy(index).start()

    def get(self, index):
        self.copy(index).wait()
        return self.slots.at[index % 2]


def plane_call(kernel, name, collective_id, out_shape, in_spaces, out_spaces, scratch, copies, flops, args):
    spaces = {"any": pl.ANY, "vmem": pltpu.VMEM, "smem": pltpu.SMEM}
    return pl.pallas_call(
        kernel,
        out_shape=out_shape,
        in_specs=[pl.BlockSpec(memory_space=spaces[v]) for v in in_spaces],
        out_specs=[pl.BlockSpec(memory_space=spaces[v]) for v in out_spaces],
        scratch_shapes=list(scratch)
        + [pltpu.SemaphoreType.DMA((copies,)), pltpu.SemaphoreType.DMA((copies,))],
        compiler_params=pltpu.CompilerParams(
            collective_id=collective_id, has_side_effects=True, vmem_limit_bytes=60 << 20
        ),
        cost_estimate=pl.CostEstimate(flops=flops, bytes_accessed=64 << 20, transcendentals=0),
        name=name,
    )(*args)


def gather_kernel(own, pieces, own_sem, send_sems, recv_sems):
    plane = Plane(send_sems, recv_sems)
    streams = own.shape[0]
    gathers = [Gather(plane, own.at[s], pieces.at[s]) for s in range(streams)]
    keep = [pltpu.make_async_copy(own.at[s], pieces.at[s, 0], own_sem.at[s]) for s in range(streams)]
    for s in range(streams):
        gathers[s].begin()
        keep[s].start()
    for s in range(streams):
        gathers[s].middle()
    for s in range(streams):
        gathers[s].end()
    for s in range(streams):
        keep[s].wait()
        for index in range(4):
            gathers[s].core(index)
    plane.finish()


def gather_call(own, collective_id):
    streams, rows, width = own.shape
    return plane_call(
        gather_kernel,
        "gather",
        collective_id,
        [jax.ShapeDtypeStruct((streams, 8, rows, width), bf16)],
        ["any"],
        ["any"],
        [pltpu.SemaphoreType.DMA((streams,))],
        8 * streams,
        0,
        (own,),
    )[0]


def attend_piece(plane, qkv, b, h):
    first = pl.multiple_of(h * 3 * HEAD, HEAD)
    own_k, own_x = plane.core, plane.x

    def piece(chunk):
        k, x = 1 - chunk // 2, chunk % 2
        return (k + own_k - 2 * k * own_k) * 4 + 2 * b + (x + own_x - 2 * x * own_x)

    def part(chunk, which):
        return qkv[piece(chunk), :, pl.ds(pl.multiple_of(first + which * HEAD, HEAD), HEAD)]

    return piece, part


def attend_stream(plane, qkv, ends_ref, out, clip_count, end_at):
    rows = qkv.shape[1]
    heads = qkv.shape[2] // (3 * HEAD)

    def one(index, carry):
        b, h = index // heads, index % heads
        piece, part = attend_piece(plane, qkv, b, h)
        for s in range(4):
            start = clip_starts(ends_ref, end_at, b, clip_count, s, rows)
            cs, probs = chunk_probs(part(s, 0), lambda c: part(c, 1), start, s, rows)
            mixed = jnp.zeros((rows, HEAD), f32)
            for c, prob in zip(cs, probs):
                mixed = mixed + nn(prob.astype(bf16), part(c, 2))
            out[piece(s), :, pl.ds(pl.multiple_of(h * HEAD, HEAD), HEAD)] = mixed.astype(bf16)
        return carry

    lax.fori_loop(0, 2 * heads, one, 0)


def attend_back_stream(plane, qkv, grad, ends_ref, out, key_sum, value_sum, clip_count, end_at):
    rows = qkv.shape[1]
    heads = qkv.shape[2] // (3 * HEAD)

    def one(index, carry):
        b, h = index // heads, index % heads
        piece, part = attend_piece(plane, qkv, b, h)
        column = pl.ds(pl.multiple_of(h * HEAD, HEAD), HEAD)
        key_sum[...] = jnp.zeros_like(key_sum)
        value_sum[...] = jnp.zeros_like(value_sum)

        def put(s, which, value):
            at = pl.ds(pl.multiple_of(h * 3 * HEAD + which * HEAD, HEAD), HEAD)
            out[piece(s), :, at] = value.astype(bf16)

        for s in range(4):
            q = part(s, 0)
            g = grad[piece(s), :, column]
            start = clip_starts(ends_ref, end_at, b, clip_count, s, rows)
            cs, probs = chunk_probs(q, lambda c: part(c, 1), start, s, rows)
            grad_probs = [nt(g, part(c, 2)) for c in cs]
            inner = functools.reduce(
                jnp.add,
                [jnp.sum(p * v, axis=1, keepdims=True) for p, v in zip(probs, grad_probs)],
            )
            grad_q = jnp.zeros((rows, HEAD), f32)
            for c, prob, grad_prob in zip(cs, probs, grad_probs):
                grad_score = (prob * (grad_prob - inner) * HEAD ** (-0.5)).astype(bf16)
                grad_q = grad_q + nn(grad_score, part(c, 1))
                key_sum[c] += tn(grad_score, q)
                value_sum[c] += tn(prob.astype(bf16), g)
            put(s, 0, grad_q)
        for s in range(4):
            put(s, 1, key_sum[s])
            put(s, 2, value_sum[s])
        return carry

    lax.fori_loop(0, 2 * heads, one, 0)


def attention_kernel(
    clip_count, own, rows_in, weight, ends, pieces, qkv, mixed, slots, slot_sems, own_sem, send_sems, recv_sems
):
    plane = Plane(send_sems, recv_sems)
    streams = own.shape[0]
    gathers = [Gather(plane, own.at[s], pieces.at[s]) for s in range(streams)]
    keep = [pltpu.make_async_copy(own.at[s], pieces.at[s, 0], own_sem.at[s]) for s in range(streams)]
    for s in range(streams):
        gathers[s].begin()
        keep[s].start()
    total = weight.shape[0]
    feed = Feed(
        lambda at: rows_in.at[at[0], at[1]],
        slots,
        slot_sems,
        [(s, p) for s in range(streams) for p in range(8)],
    )
    feed.start(0)

    def project(s):
        for p in range(8):
            feed.start(s * 8 + p + 1)
            piece = feed.get(s * 8 + p)

            def tile(at):
                qkv[s, p, :, at] = nt(piece[...], weight[at]).astype(bf16)

            tiles(total, N_TILE, tile)

    def attend(s):
        attend_stream(plane, qkv.at[s], ends, mixed.at[s], clip_count, s * 2 * clip_count)

    project(0)
    attend(0)
    gathers[0].middle()
    project(1)
    gathers[1].middle()
    gathers[0].end()
    attend(1)
    gathers[1].end()
    for s in range(streams):
        keep[s].wait()
        for index in range(4):
            gathers[s].core(index)
    plane.finish()


def reduce_scratch(streams, rows, width):
    return [
        pltpu.VMEM((streams, 8, rows, width), bf16),
        pltpu.VMEM((streams, 4, rows, width), bf16),
        pltpu.VMEM((streams, 3, rows // 2, width), bf16),
        pltpu.VMEM((streams, 3, rows // 2, width), bf16),
    ]


def project_kernel(mixed, weight, out, parts, from_core, from_x, from_y, send_sems, recv_sems):
    plane = Plane(send_sems, recv_sems)
    streams = mixed.shape[0]
    width = weight.shape[1]
    sums = [
        Reduce(plane, parts.at[s], from_core.at[s], from_x.at[s], from_y.at[s])
        for s in range(streams)
    ]

    for s in range(streams):
        for m in ORDER:

            def other(at):
                parts[s, 4 + m, :, at] = nn(mixed[s, 4 + m], weight[:, at]).astype(bf16)

            tiles(width, N_TILE, other)
            sums[s].give(m)
        for m in ORDER:
            sums[s].take(m)

            def chip(at):
                here = nn(mixed[s, m], weight[:, at])
                parts[s, m, :, at] = (here + from_core[s, m, :, at].astype(f32)).astype(bf16)

            tiles(width, N_TILE, chip)
            sums[s].chip_done(m)
    for s in range(streams):
        sums[s].late()
    for s in range(streams):
        sums[s].total(out.at[s])
    plane.finish()


def gelu_pair(v):
    cubic = 0.044715 * (v * v) * v
    inner = (2.0 / np.pi) ** 0.5 * (v + cubic)
    th = jnp.tanh(inner)
    half = 0.5 * (1.0 + th)
    slope = (2.0 / np.pi) ** 0.5 * (1.0 + 3.0 * 0.044715 * (v * v))
    return v * half, half + 0.5 * v * (1.0 - th * th) * slope


def mlp_kernel(
    own, up_w, down_w, pieces, act_out, slope_out, out,
    parts, from_core, from_x, from_y, slots, act, slope, slot_sems, keep_sems, own_sem, send_sems, recv_sems,
):
    plane = Plane(send_sems, recv_sems)
    streams, rows, width = own.shape
    hidden = up_w.shape[1]
    gathers = [Gather(plane, own.at[s], pieces.at[s]) for s in range(streams)]
    sums = [
        Reduce(plane, parts.at[s], from_core.at[s], from_x.at[s], from_y.at[s])
        for s in range(streams)
    ]
    keep = [pltpu.make_async_copy(own.at[s], pieces.at[s, 0], own_sem.at[s]) for s in range(streams)]
    stores = []
    loads = [0]

    def load(s, p):
        slot = loads[0] % 2
        loads[0] += 1
        source = own.at[s] if p == 0 else pieces.at[s, p]
        copy = pltpu.make_async_copy(source, slots.at[slot], slot_sems.at[slot])
        copy.start()
        return copy, slots.at[slot]

    def work(s, p, loaded):
        copy, piece = loaded
        slot = len(stores) % 2
        if len(stores) >= 2:
            for store in stores[-2]:
                store.wait()
        copy.wait()

        def up(at):
            value, grad = gelu_pair(nn(piece[...], up_w[:, at]))
            act[slot, :, at] = value.astype(bf16)
            slope[slot, :, at] = grad.astype(bf16)

        tiles(hidden, N_TILE, up)
        pair = [
            pltpu.make_async_copy(act.at[slot], act_out.at[s, p], keep_sems.at[slot, 0]),
            pltpu.make_async_copy(slope.at[slot], slope_out.at[s, p], keep_sems.at[slot, 1]),
        ]
        for store in pair:
            store.start()
        stores.append(pair)
        if p < 4:
            sums[s].take(p)

        def down(at):
            here = nn(act[slot], down_w[:, at])
            if p < 4:
                here = here + from_core[s, p, :, at].astype(f32)
            parts[s, p, :, at] = here.astype(bf16)

        tiles(width, N_TILE, down)

    for s in range(streams):
        keep[s].start()
    gathers[0].begin()

    def pair_up(s, m):
        gathers[s].core(m)
        work(s, 4 + m, load(s, 4 + m))
        sums[s].give(m)
        work(s, m, load(s, m))
        sums[s].chip_done(m)

    for s in range(streams):
        pair_up(s, 0)
        gathers[s].middle()
        if s + 1 < streams:
            gathers[s + 1].begin()
        pair_up(s, 1)
        pair_up(s, 2)
        gathers[s].end()
        pair_up(s, 3)
        if s > 0:
            sums[s - 1].late()
    sums[streams - 1].late()
    for s in range(streams):
        sums[s].total(out.at[s])
        keep[s].wait()
    for pair in stores[-2:]:
        for store in pair:
            store.wait()
    plane.finish()


def mlp_back_kernel(
    grads, slope_in, up_w, down_w, pre_out, out,
    parts, from_core, from_x, from_y, slots, slopes, pre, slot_sems, slope_sems, keep_sems, send_sems, recv_sems,
):
    plane = Plane(send_sems, recv_sems)
    streams, _, rows, width = grads.shape
    hidden = up_w.shape[1]
    sums = [
        Reduce(plane, parts.at[s], from_core.at[s], from_x.at[s], from_y.at[s])
        for s in range(streams)
    ]
    order = [(s, p) for s in range(streams) for m in ORDER for p in (4 + m, m)]
    feed = Feed(lambda at: grads.at[at[0], at[1]], slots, slot_sems, order)
    feed_slope = Feed(lambda at: slope_in.at[at[0], at[1]], slopes, slope_sems, order)
    feed.start(0)
    feed_slope.start(0)
    stores = []
    for index, (s, p) in enumerate(order):
        feed.start(index + 1)
        feed_slope.start(index + 1)
        grad = feed.get(index)
        slope = feed_slope.get(index)
        slot = index % 2
        if index >= 2:
            stores[index - 2].wait()

        def back(at):
            value = nt(grad[...], down_w[at]) * slope[:, at].astype(f32)
            pre[slot, :, at] = value.astype(bf16)

        tiles(hidden, N_TILE, back)
        store = pltpu.make_async_copy(pre.at[slot], pre_out.at[s, p], keep_sems.at[slot])
        store.start()
        stores.append(store)
        if p < 4:
            sums[s].take(p)

        def through(at):
            here = nt(pre[slot], up_w[at])
            if p < 4:
                here = here + from_core[s, p, :, at].astype(f32)
            parts[s, p, :, at] = here.astype(bf16)

        tiles(width, N_TILE, through)
        if p >= 4:
            sums[s].give(p - 4)
        else:
            sums[s].chip_done(p)
        if s > 0 and p == 3:
            sums[s - 1].late()
    sums[streams - 1].late()
    for s in range(streams):
        sums[s].total(out.at[s])
    for store in stores[-2:]:
        store.wait()
    plane.finish()


def attention_back_kernel(
    clip_count, own, qkv, qkv_w, out_w, ends, pieces, grad_qkv, out,
    parts, from_core, from_x, from_y, slots, grad_mixed, key_sum, value_sum, slot_sems, own_sem, send_sems, recv_sems,
):
    plane = Plane(send_sems, recv_sems)
    streams, rows, width = own.shape
    inner = out_w.shape[0]
    gathers = [Gather(plane, own.at[s], pieces.at[s]) for s in range(streams)]
    sums = [
        Reduce(plane, parts.at[s], from_core.at[s], from_x.at[s], from_y.at[s])
        for s in range(streams)
    ]
    keep = [pltpu.make_async_copy(own.at[s], pieces.at[s, 0], own_sem.at[s]) for s in range(streams)]
    loads = [0]

    def mix(s, p):
        slot = loads[0] % 2
        loads[0] += 1
        source = own.at[s] if p == 0 else pieces.at[s, p]
        copy = pltpu.make_async_copy(source, slots.at[slot], slot_sems.at[slot])
        copy.start()
        copy.wait()
        grad_mixed[p] = nt(slots[slot], out_w[...]).astype(bf16)

    for s in range(streams):
        keep[s].start()
    gathers[0].begin()
    for s in range(streams):
        gather = gathers[s]
        mix(s, 0)
        gather.core(0)
        mix(s, 4)
        gather.middle()
        if s + 1 < streams:
            gathers[s + 1].begin()
        for index in (1, 2):
            mix(s, index)
            gather.core(index)
            mix(s, 4 + index)
        gather.end()
        mix(s, 3)
        gather.core(3)
        mix(s, 7)
        attend_back_stream(
            plane,
            qkv.at[s],
            grad_mixed,
            ends,
            grad_qkv.at[s],
            key_sum,
            value_sum,
            clip_count,
            s * 2 * clip_count,
        )
        for m in ORDER:

            def other(at):
                parts[s, 4 + m, :, at] = nn(grad_qkv[s, 4 + m], qkv_w[:, at]).astype(bf16)

            tiles(width, N_TILE, other)
            sums[s].give(m)
        for m in ORDER:
            sums[s].take(m)

            def chip(at):
                here = nn(grad_qkv[s, m], qkv_w[:, at])
                parts[s, m, :, at] = (here + from_core[s, m, :, at].astype(f32)).astype(bf16)

            tiles(width, N_TILE, chip)
            sums[s].chip_done(m)
        if s > 0:
            sums[s - 1].late()
    sums[streams - 1].late()
    for s in range(streams):
        sums[s].total(out.at[s])
        keep[s].wait()
    plane.finish()


def on_device(
    block_input,
    clip_lengths,
    norm1_gain,
    w_query,
    w_key,
    w_value,
    w_out,
    norm2_gain,
    w_up,
    w_down,
    out_cotangent,
):
    streams, rows, width = block_input.shape
    planes = lax.axis_size("tensor")
    lanes = lax.axis_size("dp")
    groups = lanes // planes
    x_count = planes // 2
    clip_count = clip_lengths.shape[1]
    own = lax.axis_index("dp")
    own_plane = lax.axis_index("tensor")
    own_core = own % 2
    heads = w_query.shape[1] * planes // (HEAD * lanes)
    depth = w_query.shape[0]
    hidden_part = w_up.shape[1] // lanes
    hidden_own = planes * hidden_part
    inner = heads * HEAD

    def lane_chunk(lane):
        return lane // 2 + x_count * (1 - lane % 2)

    def lane_plane(lane):
        return (lane // 2 + x_count * (lane % 2)) ^ 1

    chunk_lane = {lane_chunk(lane): lane for lane in range(planes)}
    there = [
        ((g * planes + l) * planes + s, (g * planes + chunk_lane[s]) * planes + lane_plane(l))
        for g in range(groups)
        for l in range(planes)
        for s in range(planes)
    ]
    back = [(b, a) for a, b in there]

    def hop(value, mask):
        return lax.ppermute(value, "dp", [(i, i ^ mask) for i in range(lanes)])

    def move(value, pairs):
        return lax.ppermute(value, ("dp", "tensor"), pairs)

    tokens_in = move(block_input, there)

    small = jnp.concatenate(
        [norm1_gain.astype(f32), norm2_gain.astype(f32), clip_lengths.reshape(-1).astype(f32)]
    )
    small = lax.all_gather(small, "dp", axis=0, tiled=False)
    gain_one = small[:, :depth].reshape(-1)
    gain_two = small[:, depth : 2 * depth].reshape(-1)
    lengths = small[:, 2 * depth :].reshape(-1, clip_count).astype(jnp.int32)

    chip_groups = [[i for i in range(lanes) if i % 2 == core] for core in range(2)]

    def swap(pair, axis):
        keep = lax.dynamic_index_in_dim(pair, own_core, axis, keepdims=False)
        give = lax.dynamic_index_in_dim(pair, 1 - own_core, axis, keepdims=False)
        got = hop(give, 1)
        return jnp.where(own_core == 0, jnp.stack([keep, got]), jnp.stack([got, keep]))

    def fetch_heads(parts):
        count = len(parts)
        local = jnp.stack(parts).reshape(count, 4, HEAD, depth).swapaxes(0, 1)
        chips = lax.all_to_all(local, "dp", 0, 0, axis_index_groups=chip_groups, tiled=True)
        wide = lax.all_gather(chips, "tensor", axis=0, tiled=False)
        both = swap(wide.reshape((2, 2) + chips.shape), 0)
        return both.transpose(1, 3, 4, 2, 0, 5).reshape(2, count, HEAD, width)

    def return_heads(grads):
        count = grads.shape[1]
        split = grads.reshape(2, count, HEAD, 4, 2, depth).transpose(4, 0, 3, 1, 2, 5)
        both = swap(split, 0).reshape((4,) + split.shape[2:])
        mine = lax.psum_scatter(both, "tensor", scatter_dimension=0, tiled=False)
        chips = lax.all_to_all(mine, "dp", 0, 0, axis_index_groups=chip_groups, tiled=True)
        return chips.swapaxes(0, 1).reshape(count, 4 * HEAD, depth)

    qkv_w = fetch_heads([w_query.T, w_key.T, w_value.T]).reshape(-1, width)
    out_w = fetch_heads([w_out]).reshape(-1, width)

    up_part = lax.all_to_all(
        w_up.reshape(depth, lanes, hidden_part).swapaxes(0, 1), "dp", 0, 0, tiled=True
    ).reshape(width, hidden_part)
    down_part = lax.all_to_all(
        w_down.reshape(lanes, hidden_part, depth), "dp", 0, 0, tiled=True
    ).swapaxes(0, 1).reshape(hidden_part, width)
    up_w = lax.all_gather(up_part, "tensor", axis=0, tiled=False).swapaxes(0, 1)
    up_w = up_w.reshape(width, hidden_own)
    down_w = lax.all_gather(down_part, "tensor", axis=0, tiled=True)

    cotangent = move(out_cotangent, there)

    all_ends = jnp.cumsum(lengths, axis=1)
    own_group = own // planes
    own_lane = own % planes
    plane_lane = 2 * ((own_plane ^ 1) % x_count) + (own_plane ^ 1) // x_count
    stream_ids = jnp.arange(streams, dtype=jnp.int32)
    group_ids = jnp.arange(groups, dtype=jnp.int32) ^ own_group
    buffers = ((group_ids[None] * planes + plane_lane) * streams + stream_ids[:, None]).reshape(-1)
    ends = jnp.take(all_ends, buffers, axis=0)
    own_places = lane_chunk(own_lane) * rows + jnp.arange(rows, dtype=jnp.int32)
    last_ends = ends.reshape(streams, groups, clip_count)[:, 0, -1]
    valid = (own_places[None] < last_ends[:, None]).astype(f32)
    ends = ends.reshape(-1).astype(jnp.int32)

    pieces = jax.ShapeDtypeStruct((streams, 8, rows, width), bf16)
    sums = jax.ShapeDtypeStruct((streams, rows, width), f32)
    row_count = streams * 8 * rows
    slots = pltpu.VMEM((2, rows, width), bf16)
    dma = pltpu.SemaphoreType.DMA

    def piece_shape(columns):
        return jax.ShapeDtypeStruct((streams, 8, rows, columns), bf16)

    tokens = tokens_in.astype(f32)
    normed_one, unit_one, inverse_one = norm_rows(tokens, gain_one)
    features_one = gather_call(normed_one.astype(bf16), 0)
    grad_out = cotangent.astype(f32) * valid[:, :, None]
    grad_branch, qkv, mixed = plane_call(
        functools.partial(attention_kernel, clip_count),
        "attention",
        1,
        [pieces, piece_shape(3 * inner), piece_shape(inner)],
        ["any", "any", "vmem", "smem"],
        ["any", "vmem", "vmem"],
        [slots, dma((2,)), dma((streams,))],
        8 * streams,
        2 * row_count * width * 3 * inner,
        (grad_out.astype(bf16), features_one, qkv_w, ends),
    )
    attn_sum = plane_call(
        project_kernel,
        "project",
        2,
        [sums],
        ["vmem", "vmem"],
        ["vmem"],
        reduce_scratch(streams, rows, width),
        10 * streams,
        2 * row_count * width * inner,
        (mixed, out_w),
    )[0]
    hidden = tokens + attn_sum
    normed_two, unit_two, inverse_two = norm_rows(hidden, gain_two)
    part = pltpu.VMEM((2, rows, hidden_own), bf16)
    features_two, activated, slope, mlp_sum = plane_call(
        mlp_kernel,
        "mlp",
        3,
        [pieces, piece_shape(hidden_own), piece_shape(hidden_own), sums],
        ["any", "vmem", "vmem"],
        ["any", "any", "any", "vmem"],
        reduce_scratch(streams, rows, width)
        + [slots, part, part, dma((2,)), dma((2, 2)), dma((streams,))],
        18 * streams,
        4 * row_count * width * hidden_own,
        (normed_two.astype(bf16), up_w, down_w),
    )
    output = move((hidden + mlp_sum).astype(bf16), back)

    grad_pre, back_sum = plane_call(
        mlp_back_kernel,
        "mlp_back",
        4,
        [piece_shape(hidden_own), sums],
        ["any", "any", "vmem", "vmem"],
        ["any", "vmem"],
        reduce_scratch(streams, rows, width)
        + [slots, part, part, dma((2,)), dma((2,)), dma((2,))],
        10 * streams,
        4 * row_count * width * hidden_own,
        (grad_branch, slope, up_w, down_w),
    )
    from_two, gain_two_grad = norm_back(back_sum, unit_two, inverse_two, gain_two)
    grad_hidden = grad_out + from_two

    def grad_dot(left, right):
        return lax.dot_general(
            left.reshape(row_count, -1),
            right.reshape(row_count, -1),
            (((0,), (0,)), ((), ())),
            preferred_element_type=f32,
        ).astype(bf16)

    down_sum = lax.psum_scatter(
        grad_dot(activated, grad_branch), "tensor", scatter_dimension=0, tiled=True
    )
    down_sum = down_sum.reshape(hidden_part, lanes, depth).swapaxes(0, 1)
    down_grad = lax.all_to_all(down_sum, "dp", 0, 0, tiled=True).reshape(-1, depth).astype(f32)
    up_sum = grad_dot(features_two, grad_pre).reshape(width, planes, hidden_part).swapaxes(0, 1)
    up_sum = lax.psum_scatter(up_sum, "tensor", scatter_dimension=0, tiled=False)
    up_grad = lax.all_to_all(up_sum.reshape(lanes, depth, hidden_part), "dp", 0, 0, tiled=True)
    up_grad = up_grad.swapaxes(0, 1).reshape(depth, -1).astype(f32)

    chunk = pltpu.VMEM((4, rows, HEAD), f32)
    grad_attn, grad_qkv, input_sum = plane_call(
        functools.partial(attention_back_kernel, clip_count),
        "attention_back",
        5,
        [pieces, piece_shape(3 * inner), sums],
        ["any", "vmem", "vmem", "vmem", "smem"],
        ["any", "vmem", "vmem"],
        reduce_scratch(streams, rows, width)
        + [slots, pltpu.VMEM((8, rows, inner), bf16), chunk, chunk, dma((2,)), dma((streams,))],
        18 * streams,
        2 * row_count * width * 4 * inner,
        (grad_hidden.astype(bf16), qkv, qkv_w, out_w, ends),
    )
    from_one, gain_one_grad = norm_back(input_sum, unit_one, inverse_one, gain_one)
    input_grad = move((grad_hidden + from_one).astype(bf16), back).astype(f32)

    out_grad = return_heads(grad_dot(mixed, grad_attn).reshape(heads, 1, HEAD, width))[0]
    qkv_grad = return_heads(grad_dot(grad_qkv, features_one).reshape(heads, 3, HEAD, width))

    gain_grads = jnp.stack([gain_one_grad.sum(0), gain_two_grad.sum(0)])
    for mask in (1, 2, 4):
        gain_grads = gain_grads + hop(gain_grads, mask)
    for mask in (1, 2):
        gain_grads = gain_grads + lax.ppermute(
            gain_grads, "tensor", [(i, i ^ mask) for i in range(planes)]
        )
    gain_grads = lax.dynamic_slice_in_dim(gain_grads, own * depth, depth, 1)
    return (
        output,
        input_grad,
        gain_grads[0],
        qkv_grad[0].T.astype(f32),
        qkv_grad[1].T.astype(f32),
        qkv_grad[2].T.astype(f32),
        out_grad.astype(f32),
        gain_grads[1],
        up_grad,
        down_grad,
    )


def solution(mesh):
    in_specs = (
        P("dp", "tensor", None),
        P("dp", None),
        P("dp"),
        P("dp", "tensor"),
        P("dp", "tensor"),
        P("dp", "tensor"),
        P("tensor", "dp"),
        P("dp"),
        P("dp", "tensor"),
        P("tensor", "dp"),
        P("dp", "tensor", None),
    )
    out_specs = (
        P("dp", "tensor", None),
        P("dp", "tensor", None),
        P("dp"),
        P("dp", "tensor"),
        P("dp", "tensor"),
        P("dp", "tensor"),
        P("tensor", "dp"),
        P("dp"),
        P("dp", "tensor"),
        P("tensor", "dp"),
    )
    own_form = mesh.shape["dp"] == 8 and mesh.shape["tensor"] == 4
    return jax.shard_map(
        on_device if own_form else on_device_any, mesh=mesh, in_specs=in_specs, out_specs=out_specs, check_vma=False
    )
```

```python
import functools

import jax
import jax.numpy as jnp
import numpy as np
from jax import lax
from jax.experimental import pallas as pl
from jax.experimental.pallas import tpu as pltpu
from jax.sharding import PartitionSpec as P

HEAD = 128
LONGEST = 512
epsilon = 1e-05
masked_fill = -1000000000.0
bf16 = jnp.bfloat16
f32 = jnp.float32


def norm_rows(tokens, gain):
    centred = tokens - jnp.mean(tokens, axis=-1, keepdims=True)
    inverse = lax.rsqrt(jnp.mean(centred * centred, axis=-1, keepdims=True) + epsilon)
    unit_rows = centred * inverse
    return (unit_rows * gain, unit_rows, inverse)


def norm_back(grad_normed, unit_rows, inverse, gain):
    scaled = grad_normed * gain
    inner_sum = (
        scaled
        - jnp.mean(scaled, axis=-1, keepdims=True)
        - unit_rows * jnp.mean(scaled * unit_rows, axis=-1, keepdims=True)
    )
    return (inverse * inner_sum, jnp.sum(grad_normed * unit_rows, axis=0))


def gelu_tanh(values):
    return jax.nn.gelu(values, approximate=True)


def masked_scores(q_rows, keys_heads, segment, offset, block_rows):
    slot_count = keys_heads.shape[0]
    raw_scores = jnp.einsum(
        "qhd,khd->hqk", q_rows, keys_heads, preferred_element_type=jnp.float32
    ) * HEAD ** (-0.5)
    q_segment = lax.dynamic_slice_in_dim(segment, offset, block_rows, 0)
    q_place = offset + jnp.arange(block_rows, dtype=jnp.int32)
    places = jnp.arange(slot_count, dtype=jnp.int32)
    allowed = (q_segment[:, None] == segment[None, :]) & (places[None, :] <= q_place[:, None])
    return jnp.where(allowed[None], raw_scores, masked_fill)


def attend(query, key, value, segment, block_rows):
    slot_count = query.shape[0]
    head_count = query.shape[1] // HEAD
    keys_heads = key.reshape(slot_count, head_count, HEAD)
    values_heads = value.reshape(slot_count, head_count, HEAD)

    def one_block(block_index):
        offset = block_index * block_rows
        q_rows = lax.dynamic_slice_in_dim(query, offset, block_rows, 0).reshape(
            block_rows, head_count, HEAD
        )
        scores = masked_scores(q_rows, keys_heads, segment, offset, block_rows)
        highest = jnp.max(scores, axis=-1, keepdims=True)
        shifted = jnp.exp(scores - highest)
        totals = jnp.sum(shifted, axis=-1, keepdims=True)
        weights = (shifted / totals).astype(jnp.bfloat16)
        mixed_rows = jnp.einsum(
            "hqk,khd->qhd", weights, values_heads, preferred_element_type=jnp.float32
        )
        return (
            mixed_rows.reshape(block_rows, head_count * HEAD).astype(jnp.bfloat16),
            (highest + jnp.log(totals))[..., 0],
        )

    mixed_rows, log_norm = lax.map(one_block, jnp.arange(slot_count // block_rows, dtype=jnp.int32))
    return (mixed_rows.reshape(slot_count, head_count * HEAD), log_norm)


def attend_back(query, key, value, segment, log_norm, grad_mixed, block_rows):
    slot_count = query.shape[0]
    head_count = query.shape[1] // HEAD
    keys_heads = key.reshape(slot_count, head_count, HEAD)
    values_heads = value.reshape(slot_count, head_count, HEAD)

    def one_block(carried, block_index):
        grad_keys, grad_values = carried
        offset = block_index * block_rows
        q_rows = lax.dynamic_slice_in_dim(query, offset, block_rows, 0).reshape(
            block_rows, head_count, HEAD
        )
        g_rows = lax.dynamic_slice_in_dim(grad_mixed, offset, block_rows, 0).reshape(
            block_rows, head_count, HEAD
        )
        scores = masked_scores(q_rows, keys_heads, segment, offset, block_rows)
        prob_rows = jnp.exp(scores - log_norm[block_index][..., None])
        grad_values = grad_values + jnp.einsum(
            "hqk,qhd->khd",
            prob_rows.astype(jnp.bfloat16),
            g_rows,
            preferred_element_type=jnp.float32,
        )
        grad_probs = jnp.einsum(
            "qhd,khd->hqk", g_rows, values_heads, preferred_element_type=jnp.float32
        )
        inner_sum = jnp.sum(prob_rows * grad_probs, axis=-1, keepdims=True)
        grad_scores = (prob_rows * (grad_probs - inner_sum) * HEAD ** (-0.5)).astype(jnp.bfloat16)
        grad_query = jnp.einsum(
            "hqk,khd->qhd", grad_scores, keys_heads, preferred_element_type=jnp.float32
        )
        grad_keys = grad_keys + jnp.einsum(
            "hqk,qhd->khd", grad_scores, q_rows, preferred_element_type=jnp.float32
        )
        return (
            (grad_keys, grad_values),
            grad_query.reshape(block_rows, head_count * HEAD).astype(jnp.bfloat16),
        )

    zero_state = jnp.zeros((slot_count, head_count, HEAD), jnp.float32)
    (grad_keys, grad_values), grad_query = lax.scan(
        one_block, (zero_state, zero_state), jnp.arange(slot_count // block_rows, dtype=jnp.int32)
    )
    return (
        grad_query.reshape(slot_count, head_count * HEAD),
        grad_keys.reshape(slot_count, head_count * HEAD).astype(jnp.bfloat16),
        grad_values.reshape(slot_count, head_count * HEAD).astype(jnp.bfloat16),
    )


def on_device_any(
    block_input,
    clip_lengths,
    norm1_gain,
    w_query,
    w_key,
    w_value,
    w_out,
    norm2_gain,
    w_up,
    w_down,
    out_cotangent,
):
    micro_count = block_input.shape[0]
    local_rows = block_input.shape[1]
    tensor_size = lax.axis_size("tensor")
    slot_count = local_rows * tensor_size
    block_rows = min(512, slot_count)
    clip_count = clip_lengths.shape[1]
    row_offset = lax.axis_index("tensor") * local_rows
    places = jnp.arange(slot_count, dtype=jnp.int32)

    def fetch_weights():
        return (
            lax.all_gather(norm1_gain, "dp", axis=0, tiled=True),
            lax.all_gather(norm2_gain, "dp", axis=0, tiled=True),
            lax.all_gather(w_query, "dp", axis=0, tiled=True),
            lax.all_gather(w_key, "dp", axis=0, tiled=True),
            lax.all_gather(w_value, "dp", axis=0, tiled=True),
            lax.all_gather(w_up, "dp", axis=0, tiled=True),
            lax.all_gather(w_out, "dp", axis=1, tiled=True),
            lax.all_gather(w_down, "dp", axis=1, tiled=True),
        )

    def rows_forward(normed):
        return lax.all_gather(normed, "tensor", axis=0, tiled=True)

    def rows_backward(gradients):
        return lax.all_gather(gradients, "tensor", axis=0, tiled=True)

    def sum_forward(term_fn):
        return lax.psum_scatter(
            term_fn(jnp.int32(0), local_rows * lax.axis_size("tensor")),
            "tensor",
            scatter_dimension=0,
            tiled=True,
        )

    def sum_backward(term_fn):
        return lax.psum_scatter(
            term_fn(jnp.int32(0), local_rows * lax.axis_size("tensor")),
            "tensor",
            scatter_dimension=0,
            tiled=True,
        )

    grad_totals = None
    outputs = []
    input_grads = []
    for micro_index in range(micro_count):
        gathered = fetch_weights()
        gain_one = gathered[0].astype(jnp.float32)
        gain_two = gathered[1].astype(jnp.float32)
        query_w, key_w, value_w, up_w, out_w, down_w = (
            gathered[2],
            gathered[3],
            gathered[4],
            gathered[5],
            gathered[6],
            gathered[7],
        )
        tokens = block_input[micro_index].astype(jnp.float32)
        ends = jnp.cumsum(clip_lengths[micro_index])
        segment = jnp.sum((places[:, None] >= ends[None, :]).astype(jnp.int32), axis=1)
        own_segment = lax.dynamic_slice_in_dim(segment, row_offset, local_rows, 0)
        valid_rows = (own_segment < clip_count).astype(jnp.float32)
        normed_one, unit_one, inverse_one = norm_rows(tokens, gain_one)
        features_one = rows_forward(normed_one.astype(jnp.bfloat16))
        query = jnp.dot(features_one, query_w, preferred_element_type=jnp.float32).astype(
            jnp.bfloat16
        )
        key = jnp.dot(features_one, key_w, preferred_element_type=jnp.float32).astype(jnp.bfloat16)
        value = jnp.dot(features_one, value_w, preferred_element_type=jnp.float32).astype(
            jnp.bfloat16
        )
        mixed_rows, log_norm = attend(query, key, value, segment, block_rows)

        def attn_term(offset, row_count):
            return jnp.dot(mixed_rows, out_w, preferred_element_type=jnp.float32)

        hidden = tokens + sum_forward(attn_term)
        normed_two, unit_two, inverse_two = norm_rows(hidden, gain_two)
        features_two = rows_forward(normed_two.astype(jnp.bfloat16))
        pre_act = jnp.dot(features_two, up_w, preferred_element_type=jnp.float32)
        activated = gelu_tanh(pre_act).astype(jnp.bfloat16)

        def mlp_term(offset, row_count):
            return jnp.dot(activated, down_w, preferred_element_type=jnp.float32)

        outputs.append((hidden + sum_forward(mlp_term)).astype(jnp.bfloat16))
        regathered = fetch_weights()
        query_w, key_w, value_w, up_w, out_w, down_w = (
            regathered[2],
            regathered[3],
            regathered[4],
            regathered[5],
            regathered[6],
            regathered[7],
        )
        grad_out = out_cotangent[micro_index].astype(jnp.float32) * valid_rows[:, None]
        grad_branch = rows_backward(grad_out.astype(jnp.bfloat16))
        down_grad = jnp.einsum(
            "sf,sd->fd", activated, grad_branch, preferred_element_type=jnp.float32
        )
        grad_act = jnp.einsum("sd,fd->sf", grad_branch, down_w, preferred_element_type=jnp.float32)
        grad_pre = jax.vjp(gelu_tanh, pre_act)[1](grad_act)[0].astype(jnp.bfloat16)
        up_grad = jnp.einsum(
            "sd,sf->df", features_two, grad_pre, preferred_element_type=jnp.float32
        )

        def up_term(offset, row_count):
            return jnp.einsum("sf,df->sd", grad_pre, up_w, preferred_element_type=jnp.float32)

        grad_normed_two = sum_backward(up_term)
        grad_from_two, gain_two_grad = norm_back(grad_normed_two, unit_two, inverse_two, gain_two)
        grad_hidden = grad_out + grad_from_two
        grad_attn = rows_backward(grad_hidden.astype(jnp.bfloat16))
        out_grad = jnp.einsum(
            "sc,sd->cd", mixed_rows, grad_attn, preferred_element_type=jnp.float32
        )
        grad_mixed = jnp.einsum(
            "sd,cd->sc", grad_attn, out_w, preferred_element_type=jnp.float32
        ).astype(jnp.bfloat16)
        grad_query, grad_key, grad_value = attend_back(
            query, key, value, segment, log_norm, grad_mixed, block_rows
        )
        query_grad = jnp.einsum(
            "sd,sc->dc", features_one, grad_query, preferred_element_type=jnp.float32
        )
        key_grad = jnp.einsum(
            "sd,sc->dc", features_one, grad_key, preferred_element_type=jnp.float32
        )
        value_grad = jnp.einsum(
            "sd,sc->dc", features_one, grad_value, preferred_element_type=jnp.float32
        )

        def qkv_term(offset, row_count):
            part_query = jnp.einsum(
                "sc,dc->sd", grad_query, query_w, preferred_element_type=jnp.float32
            )
            part_key = jnp.einsum("sc,dc->sd", grad_key, key_w, preferred_element_type=jnp.float32)
            part_value = jnp.einsum(
                "sc,dc->sd", grad_value, value_w, preferred_element_type=jnp.float32
            )
            return part_query + part_key + part_value

        grad_normed_one = sum_backward(qkv_term)
        grad_from_one, gain_one_grad = norm_back(grad_normed_one, unit_one, inverse_one, gain_one)
        input_grads.append(grad_hidden + grad_from_one)
        micro_grads = (
            gain_one_grad,
            gain_two_grad,
            query_grad,
            key_grad,
            value_grad,
            up_grad,
            out_grad,
            down_grad,
        )
        if grad_totals is None:
            grad_totals = micro_grads
        else:
            grad_totals = jax.tree.map(jnp.add, grad_totals, micro_grads)
    grad_totals = (
        lax.psum_scatter(
            grad_totals[0].astype(jnp.bfloat16), "dp", scatter_dimension=0, tiled=True
        ).astype(jnp.float32),
        lax.psum_scatter(
            grad_totals[1].astype(jnp.bfloat16), "dp", scatter_dimension=0, tiled=True
        ).astype(jnp.float32),
        lax.psum_scatter(
            grad_totals[2].astype(jnp.bfloat16), "dp", scatter_dimension=0, tiled=True
        ).astype(jnp.float32),
        lax.psum_scatter(
            grad_totals[3].astype(jnp.bfloat16), "dp", scatter_dimension=0, tiled=True
        ).astype(jnp.float32),
        lax.psum_scatter(
            grad_totals[4].astype(jnp.bfloat16), "dp", scatter_dimension=0, tiled=True
        ).astype(jnp.float32),
        lax.psum_scatter(
            grad_totals[5].astype(jnp.bfloat16), "dp", scatter_dimension=0, tiled=True
        ).astype(jnp.float32),
        lax.psum_scatter(
            grad_totals[6].astype(jnp.bfloat16), "dp", scatter_dimension=1, tiled=True
        ).astype(jnp.float32),
        lax.psum_scatter(
            grad_totals[7].astype(jnp.bfloat16), "dp", scatter_dimension=1, tiled=True
        ).astype(jnp.float32),
    )
    gain_sums = lax.psum((grad_totals[0], grad_totals[1]), "tensor")
    return (
        jnp.stack(outputs),
        jnp.stack(input_grads),
        gain_sums[0],
        grad_totals[2],
        grad_totals[3],
        grad_totals[4],
        grad_totals[6],
        gain_sums[1],
        grad_totals[5],
        grad_totals[7],
    )


def chunk_scores(q, k, start, s, c, rows):
    scores = lax.dot_general(
        q, k, (((1,), (1,)), ((), ())), preferred_element_type=f32
    ) * HEAD ** (-0.5)
    k_place = c * rows + lax.broadcasted_iota(jnp.int32, (rows, rows), 1)
    allowed = k_place >= start
    if c == s:
        q_place = s * rows + lax.broadcasted_iota(jnp.int32, (rows, rows), 0)
        allowed = jnp.logical_and(allowed, k_place <= q_place)
    return jnp.where(allowed, scores, masked_fill)


def clip_starts(ends_ref, first, buffer, clip_count, s, rows):
    place = s * rows + lax.broadcasted_iota(jnp.int32, (rows, 1), 0)
    start = jnp.zeros((rows, 1), jnp.int32)
    for clip in range(clip_count):
        end = ends_ref[first + buffer * clip_count + clip]
        start = jnp.where(place >= end, jnp.maximum(start, end), start)
    return start


def window(s, rows):
    back = -(-(LONGEST - 1) // rows)
    return range(max(0, s - back), s + 1)


def chunk_probs(q, keys, start, s, rows):
    cs = list(window(s, rows))
    scores = [chunk_scores(q, keys(c), start, s, c, rows) for c in cs]
    highest = functools.reduce(jnp.maximum, [jnp.max(v, axis=1, keepdims=True) for v in scores])
    shifted = [jnp.exp(v - highest) for v in scores]
    total = functools.reduce(jnp.add, [jnp.sum(v, axis=1, keepdims=True) for v in shifted])
    scale = 1.0 / total
    return cs, [v * scale for v in shifted]


MESH = pl.DeviceIdType.MESH
N_TILE = 256


class Plane:
    def __init__(self, send_sems, recv_sems, more=()):
        me = lax.axis_index("dp")
        self.core = me % 2
        self.x = (me // 2) % 2
        self.peers = {
            "c": me + 1 - 2 * (me % 2),
            "x": me + 2 - 4 * ((me // 2) % 2),
            "y": me + 4 - 8 * ((me // 4) % 2),
        }
        self.send_sems, self.recv_sems = send_sems, recv_sems
        self.copies = []
        barrier = pltpu.get_barrier_semaphore()
        for peer in self.peers.values():
            pl.semaphore_signal(barrier, inc=1, device_id={"dp": peer}, device_id_type=MESH)
        for place in more:
            pl.semaphore_signal(barrier, inc=1, device_id=at_device(place), device_id_type=MESH)
        pl.semaphore_wait(barrier, 3 + len(more))

    def send(self, src, dst, way):
        return self.send_to(src, dst, {"dp": self.peers[way]})

    def send_to(self, src, dst, device):
        index = len(self.copies)
        copy = pltpu.make_async_remote_copy(
            src_ref=src,
            dst_ref=dst,
            send_sem=self.send_sems.at[index],
            recv_sem=self.recv_sems.at[index],
            device_id=device,
            device_id_type=MESH,
        )
        copy.start()
        self.copies.append(copy)
        return copy

    def finish(self):
        for copy in self.copies:
            copy.wait_send()


class Gather:
    def __init__(self, plane, own, pieces):
        self.plane, self.own, self.pieces = plane, own, pieces
        self.half = own.shape[0] // 2

    def begin(self):
        send = self.plane.send
        self.x = send(self.own, self.pieces.at[1], "x")
        self.y = send(self.own, self.pieces.at[2], "y")
        self.c = [send(self.own, self.pieces.at[4], "c")]

    def middle(self):
        send, half, pieces = self.plane.send, self.half, self.pieces
        self.x.wait_recv()
        self.fy = send(pieces.at[1, pl.ds(half, half)], pieces.at[3, pl.ds(half, half)], "y")
        self.c.append(send(pieces.at[1], pieces.at[5], "c"))
        self.y.wait_recv()
        self.fx = send(pieces.at[2, pl.ds(0, half)], pieces.at[3, pl.ds(0, half)], "x")
        self.c.append(send(pieces.at[2], pieces.at[6], "c"))

    def end(self):
        self.fx.wait_recv()
        self.fy.wait_recv()
        self.c.append(self.plane.send(self.pieces.at[3], self.pieces.at[7], "c"))

    def core(self, index):
        self.c[index].wait_recv()


class Reduce:
    def __init__(self, plane, pieces, from_core, from_x, from_y):
        self.plane, self.pieces = plane, pieces
        self.from_core, self.from_x, self.from_y = from_core, from_x, from_y
        self.half = pieces.shape[1] // 2
        self.core = {}

    def give(self, m):
        self.core[m] = self.plane.send(self.pieces.at[4 + m], self.from_core.at[m], "c")

    def take(self, m):
        self.core[m].wait_recv()

    def chip_done(self, m):
        send, half, pieces = self.plane.send, self.half, self.pieces
        low, high = pl.ds(0, half), pl.ds(half, half)
        if m == 3:
            self.far_x = send(pieces.at[3, low], self.from_x.at[1], "x")
            self.far_y = send(pieces.at[3, high], self.from_y.at[1], "y")
        elif m == 1:
            self.near_x = send(pieces.at[1, low], self.from_x.at[0], "x")
        elif m == 2:
            self.near_y = send(pieces.at[2, high], self.from_y.at[0], "y")

    def late(self):
        half, pieces = self.half, self.pieces
        low, high = pl.ds(0, half), pl.ds(half, half)
        self.far_y.wait_recv()
        add_into(pieces.at[1, high], self.from_y.at[1])
        self.late_x = self.plane.send(pieces.at[1, high], self.from_x.at[2], "x")
        self.far_x.wait_recv()
        add_into(pieces.at[2, low], self.from_x.at[1])
        self.late_y = self.plane.send(pieces.at[2, low], self.from_y.at[2], "y")

    def total(self, out):
        half = self.half
        self.near_x.wait_recv()
        self.near_y.wait_recv()
        self.late_x.wait_recv()
        self.late_y.wait_recv()
        step = min(64, half)

        for base, x_part, y_part in ((0, 0, 2), (half, 2, 0)):

            def add(index, carry):
                at = pl.ds(pl.multiple_of(index * step, step), step)
                here = pl.ds(pl.multiple_of(base + index * step, step), step)
                out[here] = (
                    self.pieces[0, here].astype(f32)
                    + self.from_x[x_part, at].astype(f32)
                    + self.from_y[y_part, at].astype(f32)
                )
                return carry

            lax.fori_loop(0, half // step, add, 0)


def add_into(ref, other):
    step = min(64, ref.shape[0])

    def add(index, carry):
        at = pl.ds(pl.multiple_of(index * step, step), step)
        ref[at] = (ref[at].astype(f32) + other[at].astype(f32)).astype(bf16)
        return carry

    lax.fori_loop(0, ref.shape[0] // step, add, 0)


ORDER = (3, 1, 2, 0)


def tiles(count, tile, body):
    def step(index, carry):
        body(pl.ds(pl.multiple_of(index * tile, tile), tile))
        return carry

    lax.fori_loop(0, count // tile, step, 0)


def nn(left, right):
    return jnp.dot(left, right, preferred_element_type=f32)


def nt(left, right):
    return lax.dot_general(left, right, (((1,), (1,)), ((), ())), preferred_element_type=f32)


def tn(left, right):
    return lax.dot_general(left, right, (((0,), (0,)), ((), ())), preferred_element_type=f32)


class Feed:
    def __init__(self, source, slots, sems, order):
        self.source, self.slots, self.sems, self.order = source, slots, sems, list(order)

    def copy(self, index):
        slot = index % 2
        return pltpu.make_async_copy(
            self.source(self.order[index]), self.slots.at[slot], self.sems.at[slot]
        )

    def start(self, index):
        if index < len(self.order):
            self.copy(index).start()

    def get(self, index):
        self.copy(index).wait()
        return self.slots.at[index % 2]


def plane_call(kernel, name, collective_id, out_shape, in_spaces, out_spaces, scratch, copies, flops, args):
    spaces = {"any": pl.ANY, "vmem": pltpu.VMEM, "smem": pltpu.SMEM}
    return pl.pallas_call(
        kernel,
        out_shape=out_shape,
        in_specs=[pl.BlockSpec(memory_space=spaces[v]) for v in in_spaces],
        out_specs=[pl.BlockSpec(memory_space=spaces[v]) for v in out_spaces],
        scratch_shapes=list(scratch)
        + [pltpu.SemaphoreType.DMA((copies,)), pltpu.SemaphoreType.DMA((copies,))],
        compiler_params=pltpu.CompilerParams(
            collective_id=collective_id, has_side_effects=True, vmem_limit_bytes=60 << 20
        ),
        cost_estimate=pl.CostEstimate(flops=flops, bytes_accessed=64 << 20, transcendentals=0),
        name=name,
    )(*args)


def row_target():
    me, plane = lax.axis_index("dp"), lax.axis_index("tensor")
    group, lane = me // 4, me % 4
    turn = lane // 2 + 2 * (lane % 2)
    target = (group * 4 + 2 * (plane % 2) + 1 - plane // 2, turn + 1 - 2 * (turn % 2))
    turn = plane + 1 - 2 * (plane % 2)
    source = (group * 4 + 2 * (turn % 2) + turn // 2, lane // 2 + 2 * (1 - lane % 2))
    return target, source


def at_device(place):
    return {"dp": place[0], "tensor": place[1]}


def start_kernel(
    tokens, w_query, w_key, w_value, w_out, w_up, w_down, small,
    tokens_out, qkv_out, out_out, up_out, down_out, small_out,
    local_sems, send_sems, recv_sems,
):
    me, plane = lax.axis_index("dp"), lax.axis_index("tensor")
    chip, core = me // 2, me % 2
    depth = w_query.shape[0]
    part = up_out.shape[1]
    target, source = row_target()
    peers = [lax.rem(me + j, 8) for j in range(1, 8)]
    barrier = pltpu.get_barrier_semaphore()
    for peer in peers:
        pl.semaphore_signal(barrier, inc=1, device_id={"dp": peer}, device_id_type=MESH)
    for place in (target, source):
        pl.semaphore_signal(barrier, inc=1, device_id=at_device(place), device_id_type=MESH)
    pl.semaphore_wait(barrier, 9)
    copies, locals_ = [], []

    def send(src, dst, device):
        copy = pltpu.make_async_remote_copy(
            src_ref=src,
            dst_ref=dst,
            send_sem=send_sems.at[len(copies)],
            recv_sem=recv_sems.at[len(copies)],
            device_id=device,
            device_id_type=MESH,
        )
        copy.start()
        copies.append(copy)

    def keep(src, dst):
        copy = pltpu.make_async_copy(src, dst, local_sems.at[len(locals_)])
        copy.start()
        locals_.append(copy)

    def block(index, size):
        return pl.ds(pl.multiple_of(index * size, size), size)

    send(tokens, tokens_out, at_device(target))
    for peer in peers:
        send(small, small_out.at[me], {"dp": peer})
    keep(small, small_out.at[me])
    heads = [(w_query, 0), (w_key, 1), (w_value, 2)]
    for j in range(1, 4):
        other = lax.rem(chip + j, 4)
        device = {"dp": 2 * other + core}
        for weight, which in heads:
            send(weight.at[:, block(other, HEAD)], qkv_out.at[which, chip], device)
    for weight, which in heads:
        keep(weight.at[:, block(chip, HEAD)], qkv_out.at[which, chip])
    for j in range(1, 4):
        other = lax.rem(chip + j, 4)
        send(w_out.at[block(other, HEAD)], out_out.at[chip], {"dp": 2 * other + core})
    keep(w_out.at[block(chip, HEAD)], out_out.at[chip])
    for peer in peers:
        send(w_up.at[:, block(peer, part)], up_out.at[block(me, depth)], {"dp": peer})
        send(w_down.at[block(peer, part)], down_out.at[:, block(me, depth)], {"dp": peer})
    keep(w_up.at[:, block(me, part)], up_out.at[block(me, depth)])
    keep(w_down.at[block(me, part)], down_out.at[:, block(me, depth)])
    for copy in locals_:
        copy.wait()
    for copy in copies:
        copy.wait()


def gather_kernel(own, rows_in, pieces, rows_out, own_sem, send_sems, recv_sems):
    target, source = row_target()
    plane = Plane(send_sems, recv_sems, [target, source])
    streams = own.shape[0]
    moved = plane.send_to(rows_in, rows_out, at_device(target))
    gathers = [Gather(plane, own.at[s], pieces.at[s]) for s in range(streams)]
    keep = [pltpu.make_async_copy(own.at[s], pieces.at[s, 0], own_sem.at[s]) for s in range(streams)]
    for s in range(streams):
        gathers[s].begin()
        keep[s].start()
    for s in range(streams):
        gathers[s].middle()
    for s in range(streams):
        gathers[s].end()
    for s in range(streams):
        keep[s].wait()
        for index in range(4):
            gathers[s].core(index)
    moved.wait_recv()
    plane.finish()


def attend_piece(plane, qkv, b, h):
    first = pl.multiple_of(h * 3 * HEAD, HEAD)
    own_k, own_x = plane.core, plane.x

    def piece(chunk):
        k, x = 1 - chunk // 2, chunk % 2
        return (k + own_k - 2 * k * own_k) * 4 + 2 * b + (x + own_x - 2 * x * own_x)

    def part(chunk, which):
        return qkv[piece(chunk), :, pl.ds(pl.multiple_of(first + which * HEAD, HEAD), HEAD)]

    return piece, part


def attend_stream(plane, qkv, ends_ref, out, clip_count, end_at):
    rows = qkv.shape[1]
    heads = qkv.shape[2] // (3 * HEAD)

    def one(index, carry):
        b, h = index // heads, index % heads
        piece, part = attend_piece(plane, qkv, b, h)
        for s in range(4):
            start = clip_starts(ends_ref, end_at, b, clip_count, s, rows)
            cs, probs = chunk_probs(part(s, 0), lambda c: part(c, 1), start, s, rows)
            mixed = jnp.zeros((rows, HEAD), f32)
            for c, prob in zip(cs, probs):
                mixed = mixed + nn(prob.astype(bf16), part(c, 2))
            out[piece(s), :, pl.ds(pl.multiple_of(h * HEAD, HEAD), HEAD)] = mixed.astype(bf16)
        return carry

    lax.fori_loop(0, 2 * heads, one, 0)


def attend_back_stream(plane, qkv, grad, ends_ref, out, key_sum, value_sum, clip_count, end_at):
    rows = qkv.shape[1]
    heads = qkv.shape[2] // (3 * HEAD)

    def one(index, carry):
        b, h = index // heads, index % heads
        piece, part = attend_piece(plane, qkv, b, h)
        column = pl.ds(pl.multiple_of(h * HEAD, HEAD), HEAD)
        key_sum[...] = jnp.zeros_like(key_sum)
        value_sum[...] = jnp.zeros_like(value_sum)

        def put(s, which, value):
            at = pl.ds(pl.multiple_of(h * 3 * HEAD + which * HEAD, HEAD), HEAD)
            out[piece(s), :, at] = value.astype(bf16)

        for s in range(4):
            q = part(s, 0)
            g = grad[piece(s), :, column]
            start = clip_starts(ends_ref, end_at, b, clip_count, s, rows)
            cs, probs = chunk_probs(q, lambda c: part(c, 1), start, s, rows)
            grad_probs = [nt(g, part(c, 2)) for c in cs]
            inner = functools.reduce(
                jnp.add,
                [jnp.sum(p * v, axis=1, keepdims=True) for p, v in zip(probs, grad_probs)],
            )
            grad_q = jnp.zeros((rows, HEAD), f32)
            for c, prob, grad_prob in zip(cs, probs, grad_probs):
                grad_score = (prob * (grad_prob - inner) * HEAD ** (-0.5)).astype(bf16)
                grad_q = grad_q + nn(grad_score, part(c, 1))
                key_sum[c] += tn(grad_score, q)
                value_sum[c] += tn(prob.astype(bf16), g)
            put(s, 0, grad_q)
        for s in range(4):
            put(s, 1, key_sum[s])
            put(s, 2, value_sum[s])
        return carry

    lax.fori_loop(0, 2 * heads, one, 0)


def attention_kernel(
    clip_count, own, rows_in, wide, ends, pieces, qkv, mixed, weight, slots, slot_sems, own_sem, wide_sems, send_sems, recv_sems
):
    plane = Plane(send_sems, recv_sems)
    streams = own.shape[0]
    gathers = [Gather(plane, own.at[s], pieces.at[s]) for s in range(streams)]
    keep = [pltpu.make_async_copy(own.at[s], pieces.at[s, 0], own_sem.at[s]) for s in range(streams)]
    traded, kept = [], []
    for head in range(2):
        for which in range(3):
            column = pl.ds((head * 3 + which) * HEAD, HEAD)
            here = weight.at[:, plane.core, :, column]
            traded.append(plane.send(wide.at[2 * (1 - plane.core) + head, which], here, "c"))
            copy = pltpu.make_async_copy(
                wide.at[2 * plane.core + head, which], here, wide_sems.at[len(kept)]
            )
            copy.start()
            kept.append(copy)
    for s in range(streams):
        gathers[s].begin()
        keep[s].start()
    total = weight.shape[3]
    feed = Feed(
        lambda at: rows_in.at[at[0], at[1]],
        slots,
        slot_sems,
        [(s, p) for s in range(streams) for p in range(8)],
    )
    feed.start(0)

    def project(s):
        for p in range(8):
            feed.start(s * 8 + p + 1)
            piece = feed.get(s * 8 + p)

            def tile(at):
                columns = weight[:, :, :, at].reshape(width, N_TILE)
                qkv[s, p, :, at] = nn(piece[...], columns).astype(bf16)

            tiles(total, N_TILE, tile)

    for copy in traded:
        copy.wait_recv()
    for copy in kept:
        copy.wait()
    width = own.shape[2]

    def attend(s):
        attend_stream(plane, qkv.at[s], ends, mixed.at[s], clip_count, s * 2 * clip_count)

    project(0)
    attend(0)
    gathers[0].middle()
    project(1)
    gathers[1].middle()
    gathers[0].end()
    attend(1)
    gathers[1].end()
    for s in range(streams):
        keep[s].wait()
        for index in range(4):
            gathers[s].core(index)
    plane.finish()


def reduce_scratch(streams, rows, width):
    return [
        pltpu.VMEM((streams, 8, rows, width), bf16),
        pltpu.VMEM((streams, 4, rows, width), bf16),
        pltpu.VMEM((streams, 3, rows // 2, width), bf16),
        pltpu.VMEM((streams, 3, rows // 2, width), bf16),
    ]


def project_kernel(
    mixed, wide, out, weight, parts, from_core, from_x, from_y, wide_sems, send_sems, recv_sems
):
    plane = Plane(send_sems, recv_sems)
    streams = mixed.shape[0]
    width = weight.shape[1]
    depth = wide.shape[3]
    traded, kept = [], []
    for head in range(2):
        for chip in range(4):
            column = pl.ds(pl.multiple_of((2 * chip + plane.core) * depth, depth), depth)
            here = weight.at[pl.ds(head * HEAD, HEAD), column]
            traded.append(plane.send(wide.at[2 * (1 - plane.core) + head, chip], here, "c"))
            copy = pltpu.make_async_copy(
                wide.at[2 * plane.core + head, chip], here, wide_sems.at[len(kept)]
            )
            copy.start()
            kept.append(copy)
    for copy in traded:
        copy.wait_recv()
    for copy in kept:
        copy.wait()
    sums = [
        Reduce(plane, parts.at[s], from_core.at[s], from_x.at[s], from_y.at[s])
        for s in range(streams)
    ]

    for s in range(streams):
        for m in ORDER:

            def other(at):
                parts[s, 4 + m, :, at] = nn(mixed[s, 4 + m], weight[:, at]).astype(bf16)

            tiles(width, N_TILE, other)
            sums[s].give(m)
        for m in ORDER:
            sums[s].take(m)

            def chip(at):
                here = nn(mixed[s, m], weight[:, at])
                parts[s, m, :, at] = (here + from_core[s, m, :, at].astype(f32)).astype(bf16)

            tiles(width, N_TILE, chip)
            sums[s].chip_done(m)
    for s in range(streams):
        sums[s].late()
    for s in range(streams):
        sums[s].total(out.at[s])
    plane.finish()


def gelu_pair(v):
    cubic = 0.044715 * (v * v) * v
    inner = (2.0 / np.pi) ** 0.5 * (v + cubic)
    th = jnp.tanh(inner)
    half = 0.5 * (1.0 + th)
    slope = (2.0 / np.pi) ** 0.5 * (1.0 + 3.0 * 0.044715 * (v * v))
    return v * half, half + 0.5 * v * (1.0 - th * th) * slope


def mlp_kernel(
    own, up_w, down_w, pieces, act_out, slope_out, out,
    parts, from_core, from_x, from_y, slots, act, slope, slot_sems, keep_sems, own_sem, send_sems, recv_sems,
):
    plane = Plane(send_sems, recv_sems)
    streams, rows, width = own.shape
    hidden = up_w.shape[1]
    gathers = [Gather(plane, own.at[s], pieces.at[s]) for s in range(streams)]
    sums = [
        Reduce(plane, parts.at[s], from_core.at[s], from_x.at[s], from_y.at[s])
        for s in range(streams)
    ]
    keep = [pltpu.make_async_copy(own.at[s], pieces.at[s, 0], own_sem.at[s]) for s in range(streams)]
    stores = []
    loads = [0]

    def load(s, p):
        slot = loads[0] % 2
        loads[0] += 1
        source = own.at[s] if p == 0 else pieces.at[s, p]
        copy = pltpu.make_async_copy(source, slots.at[slot], slot_sems.at[slot])
        copy.start()
        return copy, slots.at[slot]

    def work(s, p, loaded):
        copy, piece = loaded
        slot = len(stores) % 2
        if len(stores) >= 2:
            for store in stores[-2]:
                store.wait()
        copy.wait()

        def up(at):
            value, grad = gelu_pair(nn(piece[...], up_w[:, at]))
            act[slot, :, at] = value.astype(bf16)
            slope[slot, :, at] = grad.astype(bf16)

        tiles(hidden, N_TILE, up)
        pair = [
            pltpu.make_async_copy(act.at[slot], act_out.at[s, p], keep_sems.at[slot, 0]),
            pltpu.make_async_copy(slope.at[slot], slope_out.at[s, p], keep_sems.at[slot, 1]),
        ]
        for store in pair:
            store.start()
        stores.append(pair)
        if p < 4:
            sums[s].take(p)

        def down(at):
            here = nn(act[slot], down_w[:, at])
            if p < 4:
                here = here + from_core[s, p, :, at].astype(f32)
            parts[s, p, :, at] = here.astype(bf16)

        tiles(width, N_TILE, down)

    for s in range(streams):
        keep[s].start()
    gathers[0].begin()

    def pair_up(s, m):
        gathers[s].core(m)
        work(s, 4 + m, load(s, 4 + m))
        sums[s].give(m)
        work(s, m, load(s, m))
        sums[s].chip_done(m)

    for s in range(streams):
        pair_up(s, 0)
        gathers[s].middle()
        if s + 1 < streams:
            gathers[s + 1].begin()
        pair_up(s, 1)
        pair_up(s, 2)
        gathers[s].end()
        pair_up(s, 3)
        if s > 0:
            sums[s - 1].late()
    sums[streams - 1].late()
    for s in range(streams):
        sums[s].total(out.at[s])
        keep[s].wait()
    for pair in stores[-2:]:
        for store in pair:
            store.wait()
    plane.finish()


def mlp_back_kernel(
    grads, slope_in, up_w, down_w, pre_out, out,
    parts, from_core, from_x, from_y, slots, slopes, pre, slot_sems, slope_sems, keep_sems, send_sems, recv_sems,
):
    plane = Plane(send_sems, recv_sems)
    streams, _, rows, width = grads.shape
    hidden = up_w.shape[1]
    sums = [
        Reduce(plane, parts.at[s], from_core.at[s], from_x.at[s], from_y.at[s])
        for s in range(streams)
    ]
    order = [(s, p) for s in range(streams) for m in ORDER for p in (4 + m, m)]
    feed = Feed(lambda at: grads.at[at[0], at[1]], slots, slot_sems, order)
    feed_slope = Feed(lambda at: slope_in.at[at[0], at[1]], slopes, slope_sems, order)
    feed.start(0)
    feed_slope.start(0)
    stores = []
    for index, (s, p) in enumerate(order):
        feed.start(index + 1)
        feed_slope.start(index + 1)
        grad = feed.get(index)
        slope = feed_slope.get(index)
        slot = index % 2
        if index >= 2:
            stores[index - 2].wait()

        def back(at):
            value = nt(grad[...], down_w[at]) * slope[:, at].astype(f32)
            pre[slot, :, at] = value.astype(bf16)

        tiles(hidden, N_TILE, back)
        store = pltpu.make_async_copy(pre.at[slot], pre_out.at[s, p], keep_sems.at[slot])
        store.start()
        stores.append(store)
        if p < 4:
            sums[s].take(p)

        def through(at):
            here = nt(pre[slot], up_w[at])
            if p < 4:
                here = here + from_core[s, p, :, at].astype(f32)
            parts[s, p, :, at] = here.astype(bf16)

        tiles(width, N_TILE, through)
        if p >= 4:
            sums[s].give(p - 4)
        else:
            sums[s].chip_done(p)
        if s > 0 and p == 3:
            sums[s - 1].late()
    sums[streams - 1].late()
    for s in range(streams):
        sums[s].total(out.at[s])
    for store in stores[-2:]:
        store.wait()
    plane.finish()


def attention_back_kernel(
    clip_count, own, qkv, qkv_w, out_w, ends, pieces, grad_qkv, out,
    parts, from_core, from_x, from_y, slots, grad_mixed, key_sum, value_sum, slot_sems, own_sem, send_sems, recv_sems,
):
    plane = Plane(send_sems, recv_sems)
    streams, rows, width = own.shape
    inner = out_w.shape[0]
    gathers = [Gather(plane, own.at[s], pieces.at[s]) for s in range(streams)]
    sums = [
        Reduce(plane, parts.at[s], from_core.at[s], from_x.at[s], from_y.at[s])
        for s in range(streams)
    ]
    keep = [pltpu.make_async_copy(own.at[s], pieces.at[s, 0], own_sem.at[s]) for s in range(streams)]
    loads = [0]

    def mix(s, p):
        slot = loads[0] % 2
        loads[0] += 1
        source = own.at[s] if p == 0 else pieces.at[s, p]
        copy = pltpu.make_async_copy(source, slots.at[slot], slot_sems.at[slot])
        copy.start()
        copy.wait()
        grad_mixed[p] = nt(slots[slot], out_w[...]).astype(bf16)

    for s in range(streams):
        keep[s].start()
    gathers[0].begin()
    for s in range(streams):
        gather = gathers[s]
        mix(s, 0)
        gather.core(0)
        mix(s, 4)
        gather.middle()
        if s + 1 < streams:
            gathers[s + 1].begin()
        for index in (1, 2):
            mix(s, index)
            gather.core(index)
            mix(s, 4 + index)
        gather.end()
        mix(s, 3)
        gather.core(3)
        mix(s, 7)
        attend_back_stream(
            plane,
            qkv.at[s],
            grad_mixed,
            ends,
            grad_qkv.at[s],
            key_sum,
            value_sum,
            clip_count,
            s * 2 * clip_count,
        )
        for m in ORDER:

            def other(at):
                parts[s, 4 + m, :, at] = nt(grad_qkv[s, 4 + m], qkv_w[at]).astype(bf16)

            tiles(width, N_TILE, other)
            sums[s].give(m)
        for m in ORDER:
            sums[s].take(m)

            def chip(at):
                here = nt(grad_qkv[s, m], qkv_w[at])
                parts[s, m, :, at] = (here + from_core[s, m, :, at].astype(f32)).astype(bf16)

            tiles(width, N_TILE, chip)
            sums[s].chip_done(m)
        if s > 0:
            sums[s - 1].late()
    sums[streams - 1].late()
    for s in range(streams):
        sums[s].total(out.at[s])
        keep[s].wait()
    plane.finish()


def on_device(
    block_input,
    clip_lengths,
    norm1_gain,
    w_query,
    w_key,
    w_value,
    w_out,
    norm2_gain,
    w_up,
    w_down,
    out_cotangent,
):
    streams, rows, width = block_input.shape
    planes = lax.axis_size("tensor")
    lanes = lax.axis_size("dp")
    groups = lanes // planes
    x_count = planes // 2
    clip_count = clip_lengths.shape[1]
    own = lax.axis_index("dp")
    own_plane = lax.axis_index("tensor")
    own_core = own % 2
    heads = w_query.shape[1] * planes // (HEAD * lanes)
    depth = w_query.shape[0]
    hidden_part = w_up.shape[1] // lanes
    hidden_own = planes * hidden_part
    inner = heads * HEAD

    def lane_chunk(lane):
        return lane // 2 + x_count * (1 - lane % 2)

    def lane_plane(lane):
        return (lane // 2 + x_count * (lane % 2)) ^ 1

    chunk_lane = {lane_chunk(lane): lane for lane in range(planes)}
    back = [
        ((g * planes + chunk_lane[s]) * planes + lane_plane(l), (g * planes + l) * planes + s)
        for g in range(groups)
        for l in range(planes)
        for s in range(planes)
    ]

    def hop(value, mask):
        return lax.ppermute(value, "dp", [(i, i ^ mask) for i in range(lanes)])

    def move(value, pairs):
        return lax.ppermute(value, ("dp", "tensor"), pairs)

    small = jnp.zeros((8, depth), f32)
    small = small.at[0].set(norm1_gain.astype(f32)).at[1].set(norm2_gain.astype(f32))
    small = small.at[2, : streams * clip_count].set(clip_lengths.reshape(-1).astype(f32))
    tokens_in, qkv_part, out_part, up_part, down_part, small = plane_call(
        start_kernel,
        "start",
        6,
        [
            jax.ShapeDtypeStruct(block_input.shape, bf16),
            jax.ShapeDtypeStruct((3, 4, depth, HEAD), bf16),
            jax.ShapeDtypeStruct((4, HEAD, depth), bf16),
            jax.ShapeDtypeStruct((width, hidden_part), bf16),
            jax.ShapeDtypeStruct((hidden_part, width), bf16),
            jax.ShapeDtypeStruct((lanes, 8, depth), f32),
        ],
        ["any"] * 8,
        ["any"] * 6,
        [pltpu.SemaphoreType.DMA((7,))],
        34,
        0,
        (block_input, w_query, w_key, w_value, w_out, w_up, w_down, small),
    )
    gain_one = small[:, 0].reshape(-1)
    gain_two = small[:, 1].reshape(-1)
    lengths = small[:, 2, : streams * clip_count].reshape(-1, clip_count).astype(jnp.int32)

    qkv_wide = lax.all_gather(qkv_part, "tensor", axis=0, tiled=False)
    out_wide = lax.all_gather(out_part, "tensor", axis=0, tiled=False)
    up_w = lax.all_gather(up_part, "tensor", axis=0, tiled=False).swapaxes(0, 1)
    up_w = up_w.reshape(width, hidden_own)
    down_w = lax.all_gather(down_part, "tensor", axis=0, tiled=True)

    chip_groups = [[i for i in range(lanes) if i % 2 == core] for core in range(2)]

    def return_heads(split):
        keep = lax.dynamic_index_in_dim(split, own_core, 1, keepdims=False)
        give = lax.dynamic_index_in_dim(split, 1 - own_core, 1, keepdims=False)
        got = hop(give, 1)
        both = jnp.where(
            own_core == 0, jnp.concatenate([keep, got]), jnp.concatenate([got, keep])
        )
        mine = lax.psum_scatter(both, "tensor", scatter_dimension=0, tiled=False)
        return lax.all_to_all(mine, "dp", 0, 0, axis_index_groups=chip_groups, tiled=True)

    all_ends = jnp.cumsum(lengths, axis=1)
    own_group = own // planes
    own_lane = own % planes
    plane_lane = 2 * ((own_plane ^ 1) % x_count) + (own_plane ^ 1) // x_count
    stream_ids = jnp.arange(streams, dtype=jnp.int32)
    group_ids = jnp.arange(groups, dtype=jnp.int32) ^ own_group
    buffers = ((group_ids[None] * planes + plane_lane) * streams + stream_ids[:, None]).reshape(-1)
    ends = jnp.take(all_ends, buffers, axis=0)
    own_places = lane_chunk(own_lane) * rows + jnp.arange(rows, dtype=jnp.int32)
    last_ends = ends.reshape(streams, groups, clip_count)[:, 0, -1]
    valid = (own_places[None] < last_ends[:, None]).astype(f32)
    ends = ends.reshape(-1).astype(jnp.int32)

    pieces = jax.ShapeDtypeStruct((streams, 8, rows, width), bf16)
    sums = jax.ShapeDtypeStruct((streams, rows, width), f32)
    row_count = streams * 8 * rows
    slots = pltpu.VMEM((2, rows, width), bf16)
    dma = pltpu.SemaphoreType.DMA

    def piece_shape(columns):
        return jax.ShapeDtypeStruct((streams, 8, rows, columns), bf16)

    tokens = tokens_in.astype(f32)
    normed_one, unit_one, inverse_one = norm_rows(tokens, gain_one)
    features_one, cotangent = plane_call(
        gather_kernel,
        "gather",
        0,
        [pieces, jax.ShapeDtypeStruct(block_input.shape, bf16)],
        ["any", "any"],
        ["any", "any"],
        [dma((streams,))],
        8 * streams + 1,
        0,
        (normed_one.astype(bf16), out_cotangent),
    )
    grad_out = cotangent.astype(f32) * valid[:, :, None]
    grad_branch, qkv, mixed, qkv_w = plane_call(
        functools.partial(attention_kernel, clip_count),
        "attention",
        1,
        [
            pieces,
            piece_shape(3 * inner),
            piece_shape(inner),
            jax.ShapeDtypeStruct((4, 2, depth, 3 * inner), bf16),
        ],
        ["any", "any", "any", "smem"],
        ["any", "vmem", "vmem", "vmem"],
        [slots, dma((2,)), dma((streams,)), dma((6,))],
        8 * streams + 6,
        2 * row_count * width * 3 * inner,
        (grad_out.astype(bf16), features_one, qkv_wide, ends),
    )
    attn_sum, out_w = plane_call(
        project_kernel,
        "project",
        2,
        [sums, jax.ShapeDtypeStruct((inner, width), bf16)],
        ["vmem", "any"],
        ["vmem", "vmem"],
        reduce_scratch(streams, rows, width) + [dma((8,))],
        10 * streams + 8,
        2 * row_count * width * inner,
        (mixed, out_wide),
    )
    hidden = tokens + attn_sum
    normed_two, unit_two, inverse_two = norm_rows(hidden, gain_two)
    part = pltpu.VMEM((2, rows, hidden_own), bf16)
    features_two, activated, slope, mlp_sum = plane_call(
        mlp_kernel,
        "mlp",
        3,
        [pieces, piece_shape(hidden_own), piece_shape(hidden_own), sums],
        ["any", "vmem", "vmem"],
        ["any", "any", "any", "vmem"],
        reduce_scratch(streams, rows, width)
        + [slots, part, part, dma((2,)), dma((2, 2)), dma((streams,))],
        18 * streams,
        4 * row_count * width * hidden_own,
        (normed_two.astype(bf16), up_w, down_w),
    )
    output = move((hidden + mlp_sum).astype(bf16), back)

    grad_pre, back_sum = plane_call(
        mlp_back_kernel,
        "mlp_back",
        4,
        [piece_shape(hidden_own), sums],
        ["any", "any", "vmem", "vmem"],
        ["any", "vmem"],
        reduce_scratch(streams, rows, width)
        + [slots, part, part, dma((2,)), dma((2,)), dma((2,))],
        10 * streams,
        4 * row_count * width * hidden_own,
        (grad_branch, slope, up_w, down_w),
    )
    from_two, gain_two_grad = norm_back(back_sum, unit_two, inverse_two, gain_two)
    grad_hidden = grad_out + from_two

    def grad_dot(left, right):
        return lax.dot_general(
            left.reshape(row_count, -1),
            right.reshape(row_count, -1),
            (((0,), (0,)), ((), ())),
            preferred_element_type=f32,
        ).astype(bf16)

    down_dot = grad_dot(activated, grad_branch)
    up_dot = grad_dot(features_two, grad_pre)
    grad_attn_own, down_dot, up_dot = lax.optimization_barrier(
        (grad_hidden.astype(bf16), down_dot, up_dot)
    )
    down_sum = lax.psum_scatter(down_dot, "tensor", scatter_dimension=0, tiled=True)
    down_sum = down_sum.reshape(hidden_part, lanes, depth).swapaxes(0, 1)
    down_grad = lax.all_to_all(down_sum, "dp", 0, 0, tiled=True).reshape(-1, depth).astype(f32)
    up_sum = up_dot.reshape(width, planes, hidden_part).swapaxes(0, 1)
    up_sum = lax.psum_scatter(up_sum, "tensor", scatter_dimension=0, tiled=False)
    up_grad = lax.all_to_all(up_sum.reshape(lanes, depth, hidden_part), "dp", 0, 0, tiled=True)
    up_grad = up_grad.swapaxes(0, 1).reshape(depth, -1).astype(f32)

    chunk = pltpu.VMEM((4, rows, HEAD), f32)
    grad_attn, grad_qkv, input_sum = plane_call(
        functools.partial(attention_back_kernel, clip_count),
        "attention_back",
        5,
        [pieces, piece_shape(3 * inner), sums],
        ["any", "vmem", "vmem", "vmem", "smem"],
        ["any", "vmem", "vmem"],
        reduce_scratch(streams, rows, width)
        + [slots, pltpu.VMEM((8, rows, inner), bf16), chunk, chunk, dma((2,)), dma((streams,))],
        18 * streams,
        2 * row_count * width * 4 * inner,
        (grad_attn_own, qkv, qkv_w.reshape(width, 3 * inner), out_w, ends),
    )
    from_one, gain_one_grad = norm_back(input_sum, unit_one, inverse_one, gain_one)
    input_grad = move((grad_hidden + from_one).astype(bf16), back).astype(f32)

    out_sum = grad_dot(mixed, grad_attn).reshape(heads, HEAD, 4, 2, depth)
    out_grad = return_heads(out_sum.transpose(0, 3, 2, 1, 4)).reshape(-1, depth)
    qkv_sum = grad_dot(features_one, grad_qkv).reshape(4, 2, depth, heads, 3, HEAD)
    qkv_grad = return_heads(qkv_sum.transpose(3, 1, 0, 4, 2, 5))
    qkv_grad = qkv_grad.transpose(1, 2, 0, 3).reshape(3, depth, -1).astype(f32)

    gain_grads = jnp.stack([gain_one_grad.sum(0), gain_two_grad.sum(0)])
    for mask in (1, 2, 4):
        gain_grads = gain_grads + hop(gain_grads, mask)
    for mask in (1, 2):
        gain_grads = gain_grads + lax.ppermute(
            gain_grads, "tensor", [(i, i ^ mask) for i in range(planes)]
        )
    gain_grads = lax.dynamic_slice_in_dim(gain_grads, own * depth, depth, 1)
    return (
        output,
        input_grad,
        gain_grads[0],
        qkv_grad[0],
        qkv_grad[1],
        qkv_grad[2],
        out_grad.astype(f32),
        gain_grads[1],
        up_grad,
        down_grad,
    )


def solution(mesh):
    in_specs = (
        P("dp", "tensor", None),
        P("dp", None),
        P("dp"),
        P("dp", "tensor"),
        P("dp", "tensor"),
        P("dp", "tensor"),
        P("tensor", "dp"),
        P("dp"),
        P("dp", "tensor"),
        P("tensor", "dp"),
        P("dp", "tensor", None),
    )
    out_specs = (
        P("dp", "tensor", None),
        P("dp", "tensor", None),
        P("dp"),
        P("dp", "tensor"),
        P("dp", "tensor"),
        P("dp", "tensor"),
        P("tensor", "dp"),
        P("dp"),
        P("dp", "tensor"),
        P("tensor", "dp"),
    )
    own_form = mesh.shape["dp"] == 8 and mesh.shape["tensor"] == 4
    return jax.shard_map(
        on_device if own_form else on_device_any, mesh=mesh, in_specs=in_specs, out_specs=out_specs, check_vma=False
    )
```

```python
import functools

import jax
import jax.numpy as jnp
import numpy as np
from jax import lax
from jax.experimental import pallas as pl
from jax.experimental.pallas import tpu as pltpu
from jax.sharding import PartitionSpec as P

HEAD = 128
LONGEST = 512
epsilon = 1e-05
masked_fill = -1000000000.0
bf16 = jnp.bfloat16
f32 = jnp.float32


def norm_rows(tokens, gain):
    centred = tokens - jnp.mean(tokens, axis=-1, keepdims=True)
    inverse = lax.rsqrt(jnp.mean(centred * centred, axis=-1, keepdims=True) + epsilon)
    unit_rows = centred * inverse
    return (unit_rows * gain, unit_rows, inverse)


def norm_back(grad_normed, unit_rows, inverse, gain):
    scaled = grad_normed * gain
    inner_sum = (
        scaled
        - jnp.mean(scaled, axis=-1, keepdims=True)
        - unit_rows * jnp.mean(scaled * unit_rows, axis=-1, keepdims=True)
    )
    return (inverse * inner_sum, jnp.sum(grad_normed * unit_rows, axis=0))


def gelu_tanh(values):
    return jax.nn.gelu(values, approximate=True)


def masked_scores(q_rows, keys_heads, segment, offset, block_rows):
    slot_count = keys_heads.shape[0]
    raw_scores = jnp.einsum(
        "qhd,khd->hqk", q_rows, keys_heads, preferred_element_type=jnp.float32
    ) * HEAD ** (-0.5)
    q_segment = lax.dynamic_slice_in_dim(segment, offset, block_rows, 0)
    q_place = offset + jnp.arange(block_rows, dtype=jnp.int32)
    places = jnp.arange(slot_count, dtype=jnp.int32)
    allowed = (q_segment[:, None] == segment[None, :]) & (places[None, :] <= q_place[:, None])
    return jnp.where(allowed[None], raw_scores, masked_fill)


def attend(query, key, value, segment, block_rows):
    slot_count = query.shape[0]
    head_count = query.shape[1] // HEAD
    keys_heads = key.reshape(slot_count, head_count, HEAD)
    values_heads = value.reshape(slot_count, head_count, HEAD)

    def one_block(block_index):
        offset = block_index * block_rows
        q_rows = lax.dynamic_slice_in_dim(query, offset, block_rows, 0).reshape(
            block_rows, head_count, HEAD
        )
        scores = masked_scores(q_rows, keys_heads, segment, offset, block_rows)
        highest = jnp.max(scores, axis=-1, keepdims=True)
        shifted = jnp.exp(scores - highest)
        totals = jnp.sum(shifted, axis=-1, keepdims=True)
        weights = (shifted / totals).astype(jnp.bfloat16)
        mixed_rows = jnp.einsum(
            "hqk,khd->qhd", weights, values_heads, preferred_element_type=jnp.float32
        )
        return (
            mixed_rows.reshape(block_rows, head_count * HEAD).astype(jnp.bfloat16),
            (highest + jnp.log(totals))[..., 0],
        )

    mixed_rows, log_norm = lax.map(one_block, jnp.arange(slot_count // block_rows, dtype=jnp.int32))
    return (mixed_rows.reshape(slot_count, head_count * HEAD), log_norm)


def attend_back(query, key, value, segment, log_norm, grad_mixed, block_rows):
    slot_count = query.shape[0]
    head_count = query.shape[1] // HEAD
    keys_heads = key.reshape(slot_count, head_count, HEAD)
    values_heads = value.reshape(slot_count, head_count, HEAD)

    def one_block(carried, block_index):
        grad_keys, grad_values = carried
        offset = block_index * block_rows
        q_rows = lax.dynamic_slice_in_dim(query, offset, block_rows, 0).reshape(
            block_rows, head_count, HEAD
        )
        g_rows = lax.dynamic_slice_in_dim(grad_mixed, offset, block_rows, 0).reshape(
            block_rows, head_count, HEAD
        )
        scores = masked_scores(q_rows, keys_heads, segment, offset, block_rows)
        prob_rows = jnp.exp(scores - log_norm[block_index][..., None])
        grad_values = grad_values + jnp.einsum(
            "hqk,qhd->khd",
            prob_rows.astype(jnp.bfloat16),
            g_rows,
            preferred_element_type=jnp.float32,
        )
        grad_probs = jnp.einsum(
            "qhd,khd->hqk", g_rows, values_heads, preferred_element_type=jnp.float32
        )
        inner_sum = jnp.sum(prob_rows * grad_probs, axis=-1, keepdims=True)
        grad_scores = (prob_rows * (grad_probs - inner_sum) * HEAD ** (-0.5)).astype(jnp.bfloat16)
        grad_query = jnp.einsum(
            "hqk,khd->qhd", grad_scores, keys_heads, preferred_element_type=jnp.float32
        )
        grad_keys = grad_keys + jnp.einsum(
            "hqk,qhd->khd", grad_scores, q_rows, preferred_element_type=jnp.float32
        )
        return (
            (grad_keys, grad_values),
            grad_query.reshape(block_rows, head_count * HEAD).astype(jnp.bfloat16),
        )

    zero_state = jnp.zeros((slot_count, head_count, HEAD), jnp.float32)
    (grad_keys, grad_values), grad_query = lax.scan(
        one_block, (zero_state, zero_state), jnp.arange(slot_count // block_rows, dtype=jnp.int32)
    )
    return (
        grad_query.reshape(slot_count, head_count * HEAD),
        grad_keys.reshape(slot_count, head_count * HEAD).astype(jnp.bfloat16),
        grad_values.reshape(slot_count, head_count * HEAD).astype(jnp.bfloat16),
    )


def on_device_any(
    block_input,
    clip_lengths,
    norm1_gain,
    w_query,
    w_key,
    w_value,
    w_out,
    norm2_gain,
    w_up,
    w_down,
    out_cotangent,
):
    micro_count = block_input.shape[0]
    local_rows = block_input.shape[1]
    tensor_size = lax.axis_size("tensor")
    slot_count = local_rows * tensor_size
    block_rows = min(512, slot_count)
    clip_count = clip_lengths.shape[1]
    row_offset = lax.axis_index("tensor") * local_rows
    places = jnp.arange(slot_count, dtype=jnp.int32)

    def fetch_weights():
        return (
            lax.all_gather(norm1_gain, "dp", axis=0, tiled=True),
            lax.all_gather(norm2_gain, "dp", axis=0, tiled=True),
            lax.all_gather(w_query, "dp", axis=0, tiled=True),
            lax.all_gather(w_key, "dp", axis=0, tiled=True),
            lax.all_gather(w_value, "dp", axis=0, tiled=True),
            lax.all_gather(w_up, "dp", axis=0, tiled=True),
            lax.all_gather(w_out, "dp", axis=1, tiled=True),
            lax.all_gather(w_down, "dp", axis=1, tiled=True),
        )

    def rows_forward(normed):
        return lax.all_gather(normed, "tensor", axis=0, tiled=True)

    def rows_backward(gradients):
        return lax.all_gather(gradients, "tensor", axis=0, tiled=True)

    def sum_forward(term_fn):
        return lax.psum_scatter(
            term_fn(jnp.int32(0), local_rows * lax.axis_size("tensor")),
            "tensor",
            scatter_dimension=0,
            tiled=True,
        )

    def sum_backward(term_fn):
        return lax.psum_scatter(
            term_fn(jnp.int32(0), local_rows * lax.axis_size("tensor")),
            "tensor",
            scatter_dimension=0,
            tiled=True,
        )

    grad_totals = None
    outputs = []
    input_grads = []
    for micro_index in range(micro_count):
        gathered = fetch_weights()
        gain_one = gathered[0].astype(jnp.float32)
        gain_two = gathered[1].astype(jnp.float32)
        query_w, key_w, value_w, up_w, out_w, down_w = (
            gathered[2],
            gathered[3],
            gathered[4],
            gathered[5],
            gathered[6],
            gathered[7],
        )
        tokens = block_input[micro_index].astype(jnp.float32)
        ends = jnp.cumsum(clip_lengths[micro_index])
        segment = jnp.sum((places[:, None] >= ends[None, :]).astype(jnp.int32), axis=1)
        own_segment = lax.dynamic_slice_in_dim(segment, row_offset, local_rows, 0)
        valid_rows = (own_segment < clip_count).astype(jnp.float32)
        normed_one, unit_one, inverse_one = norm_rows(tokens, gain_one)
        features_one = rows_forward(normed_one.astype(jnp.bfloat16))
        query = jnp.dot(features_one, query_w, preferred_element_type=jnp.float32).astype(
            jnp.bfloat16
        )
        key = jnp.dot(features_one, key_w, preferred_element_type=jnp.float32).astype(jnp.bfloat16)
        value = jnp.dot(features_one, value_w, preferred_element_type=jnp.float32).astype(
            jnp.bfloat16
        )
        mixed_rows, log_norm = attend(query, key, value, segment, block_rows)

        def attn_term(offset, row_count):
            return jnp.dot(mixed_rows, out_w, preferred_element_type=jnp.float32)

        hidden = tokens + sum_forward(attn_term)
        normed_two, unit_two, inverse_two = norm_rows(hidden, gain_two)
        features_two = rows_forward(normed_two.astype(jnp.bfloat16))
        pre_act = jnp.dot(features_two, up_w, preferred_element_type=jnp.float32)
        activated = gelu_tanh(pre_act).astype(jnp.bfloat16)

        def mlp_term(offset, row_count):
            return jnp.dot(activated, down_w, preferred_element_type=jnp.float32)

        outputs.append((hidden + sum_forward(mlp_term)).astype(jnp.bfloat16))
        regathered = fetch_weights()
        query_w, key_w, value_w, up_w, out_w, down_w = (
            regathered[2],
            regathered[3],
            regathered[4],
            regathered[5],
            regathered[6],
            regathered[7],
        )
        grad_out = out_cotangent[micro_index].astype(jnp.float32) * valid_rows[:, None]
        grad_branch = rows_backward(grad_out.astype(jnp.bfloat16))
        down_grad = jnp.einsum(
            "sf,sd->fd", activated, grad_branch, preferred_element_type=jnp.float32
        )
        grad_act = jnp.einsum("sd,fd->sf", grad_branch, down_w, preferred_element_type=jnp.float32)
        grad_pre = jax.vjp(gelu_tanh, pre_act)[1](grad_act)[0].astype(jnp.bfloat16)
        up_grad = jnp.einsum(
            "sd,sf->df", features_two, grad_pre, preferred_element_type=jnp.float32
        )

        def up_term(offset, row_count):
            return jnp.einsum("sf,df->sd", grad_pre, up_w, preferred_element_type=jnp.float32)

        grad_normed_two = sum_backward(up_term)
        grad_from_two, gain_two_grad = norm_back(grad_normed_two, unit_two, inverse_two, gain_two)
        grad_hidden = grad_out + grad_from_two
        grad_attn = rows_backward(grad_hidden.astype(jnp.bfloat16))
        out_grad = jnp.einsum(
            "sc,sd->cd", mixed_rows, grad_attn, preferred_element_type=jnp.float32
        )
        grad_mixed = jnp.einsum(
            "sd,cd->sc", grad_attn, out_w, preferred_element_type=jnp.float32
        ).astype(jnp.bfloat16)
        grad_query, grad_key, grad_value = attend_back(
            query, key, value, segment, log_norm, grad_mixed, block_rows
        )
        query_grad = jnp.einsum(
            "sd,sc->dc", features_one, grad_query, preferred_element_type=jnp.float32
        )
        key_grad = jnp.einsum(
            "sd,sc->dc", features_one, grad_key, preferred_element_type=jnp.float32
        )
        value_grad = jnp.einsum(
            "sd,sc->dc", features_one, grad_value, preferred_element_type=jnp.float32
        )

        def qkv_term(offset, row_count):
            part_query = jnp.einsum(
                "sc,dc->sd", grad_query, query_w, preferred_element_type=jnp.float32
            )
            part_key = jnp.einsum("sc,dc->sd", grad_key, key_w, preferred_element_type=jnp.float32)
            part_value = jnp.einsum(
                "sc,dc->sd", grad_value, value_w, preferred_element_type=jnp.float32
            )
            return part_query + part_key + part_value

        grad_normed_one = sum_backward(qkv_term)
        grad_from_one, gain_one_grad = norm_back(grad_normed_one, unit_one, inverse_one, gain_one)
        input_grads.append(grad_hidden + grad_from_one)
        micro_grads = (
            gain_one_grad,
            gain_two_grad,
            query_grad,
            key_grad,
            value_grad,
            up_grad,
            out_grad,
            down_grad,
        )
        if grad_totals is None:
            grad_totals = micro_grads
        else:
            grad_totals = jax.tree.map(jnp.add, grad_totals, micro_grads)
    grad_totals = (
        lax.psum_scatter(
            grad_totals[0].astype(jnp.bfloat16), "dp", scatter_dimension=0, tiled=True
        ).astype(jnp.float32),
        lax.psum_scatter(
            grad_totals[1].astype(jnp.bfloat16), "dp", scatter_dimension=0, tiled=True
        ).astype(jnp.float32),
        lax.psum_scatter(
            grad_totals[2].astype(jnp.bfloat16), "dp", scatter_dimension=0, tiled=True
        ).astype(jnp.float32),
        lax.psum_scatter(
            grad_totals[3].astype(jnp.bfloat16), "dp", scatter_dimension=0, tiled=True
        ).astype(jnp.float32),
        lax.psum_scatter(
            grad_totals[4].astype(jnp.bfloat16), "dp", scatter_dimension=0, tiled=True
        ).astype(jnp.float32),
        lax.psum_scatter(
            grad_totals[5].astype(jnp.bfloat16), "dp", scatter_dimension=0, tiled=True
        ).astype(jnp.float32),
        lax.psum_scatter(
            grad_totals[6].astype(jnp.bfloat16), "dp", scatter_dimension=1, tiled=True
        ).astype(jnp.float32),
        lax.psum_scatter(
            grad_totals[7].astype(jnp.bfloat16), "dp", scatter_dimension=1, tiled=True
        ).astype(jnp.float32),
    )
    gain_sums = lax.psum((grad_totals[0], grad_totals[1]), "tensor")
    return (
        jnp.stack(outputs),
        jnp.stack(input_grads),
        gain_sums[0],
        grad_totals[2],
        grad_totals[3],
        grad_totals[4],
        grad_totals[6],
        gain_sums[1],
        grad_totals[5],
        grad_totals[7],
    )


def chunk_scores(q, k, start, s, c, rows):
    scores = lax.dot_general(
        q, k, (((1,), (1,)), ((), ())), preferred_element_type=f32
    ) * HEAD ** (-0.5)
    k_place = c * rows + lax.broadcasted_iota(jnp.int32, (rows, rows), 1)
    allowed = k_place >= start
    if c == s:
        q_place = s * rows + lax.broadcasted_iota(jnp.int32, (rows, rows), 0)
        allowed = jnp.logical_and(allowed, k_place <= q_place)
    return jnp.where(allowed, scores, masked_fill)


def clip_starts(ends_ref, first, buffer, clip_count, s, rows):
    place = s * rows + lax.broadcasted_iota(jnp.int32, (rows, 1), 0)
    start = jnp.zeros((rows, 1), jnp.int32)
    for clip in range(clip_count):
        end = ends_ref[first + buffer * clip_count + clip]
        start = jnp.where(place >= end, jnp.maximum(start, end), start)
    return start


def window(s, rows):
    back = -(-(LONGEST - 1) // rows)
    return range(max(0, s - back), s + 1)


def chunk_probs(q, keys, start, s, rows):
    cs = list(window(s, rows))
    scores = [chunk_scores(q, keys(c), start, s, c, rows) for c in cs]
    highest = functools.reduce(jnp.maximum, [jnp.max(v, axis=1, keepdims=True) for v in scores])
    shifted = [jnp.exp(v - highest) for v in scores]
    total = functools.reduce(jnp.add, [jnp.sum(v, axis=1, keepdims=True) for v in shifted])
    scale = 1.0 / total
    return cs, [v * scale for v in shifted]


MESH = pl.DeviceIdType.MESH
N_TILE = 1024


class Plane:
    def __init__(self, send_sems, recv_sems, more=()):
        me = lax.axis_index("dp")
        self.core = me % 2
        self.x = (me // 2) % 2
        self.peers = {
            "c": me + 1 - 2 * (me % 2),
            "x": me + 2 - 4 * ((me // 2) % 2),
            "y": me + 4 - 8 * ((me // 4) % 2),
        }
        self.send_sems, self.recv_sems = send_sems, recv_sems
        self.copies = []
        barrier = pltpu.get_barrier_semaphore()
        for peer in self.peers.values():
            pl.semaphore_signal(barrier, inc=1, device_id={"dp": peer}, device_id_type=MESH)
        for place in more:
            pl.semaphore_signal(barrier, inc=1, device_id=at_device(place), device_id_type=MESH)
        pl.semaphore_wait(barrier, 3 + len(more))

    def send(self, src, dst, way):
        return self.send_to(src, dst, {"dp": self.peers[way]})

    def send_to(self, src, dst, device):
        index = len(self.copies)
        copy = pltpu.make_async_remote_copy(
            src_ref=src,
            dst_ref=dst,
            send_sem=self.send_sems.at[index],
            recv_sem=self.recv_sems.at[index],
            device_id=device,
            device_id_type=MESH,
        )
        copy.start()
        self.copies.append(copy)
        return copy

    def finish(self):
        for copy in self.copies:
            copy.wait_send()


class Gather:
    def __init__(self, plane, own, pieces):
        self.plane, self.own, self.pieces = plane, own, pieces
        self.half = own.shape[0] // 2

    def begin(self):
        send = self.plane.send
        self.x = send(self.own, self.pieces.at[1], "x")
        self.y = send(self.own, self.pieces.at[2], "y")
        self.c = [send(self.own, self.pieces.at[4], "c")]

    def middle(self):
        send, half, pieces = self.plane.send, self.half, self.pieces
        self.x.wait_recv()
        self.fy = send(pieces.at[1, pl.ds(half, half)], pieces.at[3, pl.ds(half, half)], "y")
        self.c.append(send(pieces.at[1], pieces.at[5], "c"))
        self.y.wait_recv()
        self.fx = send(pieces.at[2, pl.ds(0, half)], pieces.at[3, pl.ds(0, half)], "x")
        self.c.append(send(pieces.at[2], pieces.at[6], "c"))

    def end(self):
        self.fx.wait_recv()
        self.fy.wait_recv()
        self.c.append(self.plane.send(self.pieces.at[3], self.pieces.at[7], "c"))

    def core(self, index):
        self.c[index].wait_recv()


class Reduce:
    def __init__(self, plane, pieces, from_core, from_x, from_y):
        self.plane, self.pieces = plane, pieces
        self.from_core, self.from_x, self.from_y = from_core, from_x, from_y
        self.half = pieces.shape[1] // 2
        self.core = {}

    def give(self, m):
        self.core[m] = self.plane.send(self.pieces.at[4 + m], self.from_core.at[m], "c")

    def take(self, m):
        self.core[m].wait_recv()

    def chip_done(self, m):
        send, half, pieces = self.plane.send, self.half, self.pieces
        low, high = pl.ds(0, half), pl.ds(half, half)
        if m == 3:
            self.far_x = send(pieces.at[3, low], self.from_x.at[1], "x")
            self.far_y = send(pieces.at[3, high], self.from_y.at[1], "y")
        elif m == 1:
            self.near_x = send(pieces.at[1, low], self.from_x.at[0], "x")
        elif m == 2:
            self.near_y = send(pieces.at[2, high], self.from_y.at[0], "y")

    def late(self):
        half, pieces = self.half, self.pieces
        low, high = pl.ds(0, half), pl.ds(half, half)
        self.far_y.wait_recv()
        add_into(pieces.at[1, high], self.from_y.at[1])
        self.late_x = self.plane.send(pieces.at[1, high], self.from_x.at[2], "x")
        self.far_x.wait_recv()
        add_into(pieces.at[2, low], self.from_x.at[1])
        self.late_y = self.plane.send(pieces.at[2, low], self.from_y.at[2], "y")

    def total(self, out):
        half = self.half
        self.near_x.wait_recv()
        self.near_y.wait_recv()
        self.late_x.wait_recv()
        self.late_y.wait_recv()
        step = min(64, half)

        for base, x_part, y_part in ((0, 0, 2), (half, 2, 0)):

            def add(index, carry):
                at = pl.ds(pl.multiple_of(index * step, step), step)
                here = pl.ds(pl.multiple_of(base + index * step, step), step)
                out[here] = (
                    self.pieces[0, here].astype(f32)
                    + self.from_x[x_part, at].astype(f32)
                    + self.from_y[y_part, at].astype(f32)
                )
                return carry

            lax.fori_loop(0, half // step, add, 0)


def add_into(ref, other):
    step = min(64, ref.shape[0])

    def add(index, carry):
        at = pl.ds(pl.multiple_of(index * step, step), step)
        ref[at] = (ref[at].astype(f32) + other[at].astype(f32)).astype(bf16)
        return carry

    lax.fori_loop(0, ref.shape[0] // step, add, 0)


ORDER = (3, 1, 2, 0)


def tiles(count, tile, body):
    tile = min(tile, count)

    def step(index, carry):
        body(pl.ds(pl.multiple_of(index * tile, tile), tile))
        return carry

    lax.fori_loop(0, count // tile, step, 0)


def nn(left, right):
    return jnp.dot(left, right, preferred_element_type=f32)


def nt(left, right):
    return lax.dot_general(left, right, (((1,), (1,)), ((), ())), preferred_element_type=f32)


def tn(left, right):
    return lax.dot_general(left, right, (((0,), (0,)), ((), ())), preferred_element_type=f32)


class Feed:
    def __init__(self, source, slots, sems, order):
        self.source, self.slots, self.sems, self.order = source, slots, sems, list(order)

    def copy(self, index):
        slot = index % 2
        return pltpu.make_async_copy(
            self.source(self.order[index]), self.slots.at[slot], self.sems.at[slot]
        )

    def start(self, index):
        if index < len(self.order):
            self.copy(index).start()

    def get(self, index):
        self.copy(index).wait()
        return self.slots.at[index % 2]


def plane_call(kernel, name, collective_id, out_shape, in_spaces, out_spaces, scratch, copies, flops, args):
    spaces = {"any": pl.ANY, "vmem": pltpu.VMEM, "smem": pltpu.SMEM}
    return pl.pallas_call(
        kernel,
        out_shape=out_shape,
        in_specs=[pl.BlockSpec(memory_space=spaces[v]) for v in in_spaces],
        out_specs=[pl.BlockSpec(memory_space=spaces[v]) for v in out_spaces],
        scratch_shapes=list(scratch)
        + [pltpu.SemaphoreType.DMA((copies,)), pltpu.SemaphoreType.DMA((copies,))],
        compiler_params=pltpu.CompilerParams(
            collective_id=collective_id, has_side_effects=True, vmem_limit_bytes=60 << 20
        ),
        cost_estimate=pl.CostEstimate(flops=flops, bytes_accessed=64 << 20, transcendentals=0),
        name=name,
    )(*args)


def row_places():
    me, plane = lax.axis_index("dp"), lax.axis_index("tensor")
    chip, core = 2 * (me // 2), me % 2
    outward = [(chip + 1 - plane // 2, 2 * core + j) for j in range(2)]
    inward = [(chip + plane // 2, 2 * (1 - core) + i) for i in range(2)]
    return outward, inward


def at_device(place):
    return {"dp": place[0], "tensor": place[1]}


class RowMove:
    def __init__(self, src, dst, sems):
        self.src, self.dst, self.sems = src, dst, sems
        self.copies = []

    def copy(self, here, there, place):
        return pltpu.make_async_remote_copy(
            src_ref=self.src.at[here],
            dst_ref=self.dst.at[there],
            send_sem=self.sems.at[0, here],
            recv_sem=self.sems.at[1, there],
            device_id=at_device(place),
            device_id_type=MESH,
        )

    def start(self, places, there):
        for here in range(2):
            copy = self.copy(here, there, places[here])
            copy.start()
            self.copies.append(copy)
        self.arrivals = [self.copy(index, index, places[index]) for index in range(2)]

    def outward(self):
        self.start(row_places()[0], lax.axis_index("tensor") % 2)

    def back(self):
        self.start(row_places()[1], lax.axis_index("tensor") % 2)

    def wait(self):
        for copy in self.copies:
            copy.wait_send()
        for copy in self.arrivals:
            copy.wait_recv()


def start_kernel(
    tokens, w_query, w_key, w_value, w_out, w_up, w_down, small,
    tokens_out, qkv_out, out_out, up_out, down_out, small_out,
    local_sems, row_sems, send_sems, recv_sems,
):
    me, plane = lax.axis_index("dp"), lax.axis_index("tensor")
    chip, core = me // 2, me % 2
    depth = w_query.shape[0]
    part = up_out.shape[1]
    outward, inward = row_places()
    peers = [lax.rem(me + j, 8) for j in range(1, 8)]
    barrier = pltpu.get_barrier_semaphore()
    for peer in peers:
        pl.semaphore_signal(barrier, inc=1, device_id={"dp": peer}, device_id_type=MESH)
    for place in outward + inward:
        pl.semaphore_signal(barrier, inc=1, device_id=at_device(place), device_id_type=MESH)
    pl.semaphore_wait(barrier, 11)
    copies, locals_ = [], []

    def send(src, dst, device):
        copy = pltpu.make_async_remote_copy(
            src_ref=src,
            dst_ref=dst,
            send_sem=send_sems.at[len(copies)],
            recv_sem=recv_sems.at[len(copies)],
            device_id=device,
            device_id_type=MESH,
        )
        copy.start()
        copies.append(copy)

    def keep(src, dst):
        copy = pltpu.make_async_copy(src, dst, local_sems.at[len(locals_)])
        copy.start()
        locals_.append(copy)

    def block(index, size):
        return pl.ds(pl.multiple_of(index * size, size), size)

    rows_move = RowMove(tokens, tokens_out, row_sems)
    rows_move.outward()
    for peer in peers:
        send(small, small_out.at[me], {"dp": peer})
    keep(small, small_out.at[me])
    heads = [(w_query, 0), (w_key, 1), (w_value, 2)]
    for j in range(1, 4):
        other = lax.rem(chip + j, 4)
        device = {"dp": 2 * other + core}
        for weight, which in heads:
            send(weight.at[:, block(other, HEAD)], qkv_out.at[which, chip], device)
    for weight, which in heads:
        keep(weight.at[:, block(chip, HEAD)], qkv_out.at[which, chip])
    for j in range(1, 4):
        other = lax.rem(chip + j, 4)
        send(w_out.at[block(other, HEAD)], out_out.at[chip], {"dp": 2 * other + core})
    keep(w_out.at[block(chip, HEAD)], out_out.at[chip])
    for peer in peers:
        send(w_up.at[:, block(peer, part)], up_out.at[block(me, depth)], {"dp": peer})
        send(w_down.at[block(peer, part)], down_out.at[:, block(me, depth)], {"dp": peer})
    keep(w_up.at[:, block(me, part)], up_out.at[block(me, depth)])
    keep(w_down.at[block(me, part)], down_out.at[:, block(me, depth)])
    for copy in locals_:
        copy.wait()
    for copy in copies:
        copy.wait()
    rows_move.wait()


def gather_kernel(own, rows_in, pieces, rows_out, own_sem, row_sems, send_sems, recv_sems):
    outward, inward = row_places()
    plane = Plane(send_sems, recv_sems, outward + inward)
    streams = own.shape[0]
    rows_move = RowMove(rows_in, rows_out, row_sems)
    rows_move.outward()
    gathers = [Gather(plane, own.at[s], pieces.at[s]) for s in range(streams)]
    keep = [pltpu.make_async_copy(own.at[s], pieces.at[s, 0], own_sem.at[s]) for s in range(streams)]
    for s in range(streams):
        gathers[s].begin()
        keep[s].start()
    for s in range(streams):
        gathers[s].middle()
    for s in range(streams):
        gathers[s].end()
    for s in range(streams):
        keep[s].wait()
        for index in range(4):
            gathers[s].core(index)
    rows_move.wait()
    plane.finish()


def chunk_at(plane, chip, s):
    k = 1 - s // 2
    return s % 2, (k + plane.core - 2 * k * plane.core) * 4 + chip


def chunk_part(plane, qkv, chip, head):
    def part(s, which):
        column = pl.multiple_of((head * 3 + which) * HEAD, HEAD)
        stream, piece = chunk_at(plane, chip, s)
        return qkv[stream, piece, :, pl.ds(column, HEAD)]

    return part


def attend_all(plane, qkv, ends_ref, out, clip_count):
    rows = qkv.shape[2]
    heads = qkv.shape[3] // (3 * HEAD)

    def one(index, carry):
        chip, head = index // heads, index % heads
        part = chunk_part(plane, qkv, chip, head)
        column = pl.ds(pl.multiple_of(head * HEAD, HEAD), HEAD)
        for s in range(4):
            start = clip_starts(ends_ref, 0, chip, clip_count, s, rows)
            cs, probs = chunk_probs(part(s, 0), lambda c: part(c, 1), start, s, rows)
            mixed = jnp.zeros((rows, HEAD), f32)
            for c, prob in zip(cs, probs):
                mixed = mixed + nn(prob.astype(bf16), part(c, 2))
            stream, piece = chunk_at(plane, chip, s)
            out[stream, piece, :, column] = mixed.astype(bf16)
        return carry

    return one


def attend_back_chip(plane, qkv, grad_mixed, ends_ref, out, key_sum, value_sum, clip_count, chip):
    rows = qkv.shape[2]
    heads = qkv.shape[3] // (3 * HEAD)

    def one(head, carry):
        part = chunk_part(plane, qkv, chip, head)
        column = pl.ds(pl.multiple_of(head * HEAD, HEAD), HEAD)
        key_sum[...] = jnp.zeros_like(key_sum)
        value_sum[...] = jnp.zeros_like(value_sum)

        def put(s, which, value):
            at = pl.ds(pl.multiple_of((head * 3 + which) * HEAD, HEAD), HEAD)
            stream, piece = chunk_at(plane, chip, s)
            out[stream, piece, :, at] = value.astype(bf16)

        for s in range(4):
            q = part(s, 0)
            stream, piece = chunk_at(plane, chip, s)
            g = grad_mixed[stream, piece, :, column]
            start = clip_starts(ends_ref, 0, chip, clip_count, s, rows)
            cs, probs = chunk_probs(q, lambda c: part(c, 1), start, s, rows)
            grad_probs = [nt(g, part(c, 2)) for c in cs]
            inner = functools.reduce(
                jnp.add,
                [jnp.sum(p * v, axis=1, keepdims=True) for p, v in zip(probs, grad_probs)],
            )
            grad_q = jnp.zeros((rows, HEAD), f32)
            for c, prob, grad_prob in zip(cs, probs, grad_probs):
                grad_score = (prob * (grad_prob - inner) * HEAD ** (-0.5)).astype(bf16)
                grad_q = grad_q + nn(grad_score, part(c, 1))
                key_sum[c] += tn(grad_score, q)
                value_sum[c] += tn(prob.astype(bf16), g)
            put(s, 0, grad_q)
        for s in range(4):
            put(s, 1, key_sum[s])
            put(s, 2, value_sum[s])
        return carry

    lax.fori_loop(0, heads, one, 0)


def attention_kernel(
    clip_count, own, rows_in, wide, ends, pieces, qkv, mixed, weight, slots, slot_sems, own_sem, wide_sems, send_sems, recv_sems
):
    plane = Plane(send_sems, recv_sems)
    streams = own.shape[0]
    gathers = [Gather(plane, own.at[s], pieces.at[s]) for s in range(streams)]
    keep = [pltpu.make_async_copy(own.at[s], pieces.at[s, 0], own_sem.at[s]) for s in range(streams)]
    traded, kept = [], []
    for head in range(2):
        for which in range(3):
            column = pl.ds((head * 3 + which) * HEAD, HEAD)
            here = weight.at[:, plane.core, :, column]
            traded.append(plane.send(wide.at[2 * (1 - plane.core) + head, which], here, "c"))
            copy = pltpu.make_async_copy(
                wide.at[2 * plane.core + head, which], here, wide_sems.at[len(kept)]
            )
            copy.start()
            kept.append(copy)
    for s in range(streams):
        gathers[s].begin()
        keep[s].start()
    total = weight.shape[3]
    feed = Feed(
        lambda at: rows_in.at[at[0], at[1]],
        slots,
        slot_sems,
        [(s, p) for s in range(streams) for p in range(8)],
    )
    feed.start(0)

    def project(s):
        for p in range(8):
            feed.start(s * 8 + p + 1)
            piece = feed.get(s * 8 + p)

            def tile(at):
                columns = weight[:, :, :, at].reshape(width, -1)
                qkv[s, p, :, at] = nn(piece[...], columns).astype(bf16)

            tiles(total, N_TILE, tile)

    for copy in traded:
        copy.wait_recv()
    for copy in kept:
        copy.wait()
    width = own.shape[2]

    attend = attend_all(plane, qkv, ends, mixed, clip_count)
    heads = total // (3 * HEAD)
    project(0)
    gathers[0].middle()
    project(1)
    gathers[1].middle()
    gathers[0].end()
    lax.fori_loop(0, 2 * heads, attend, 0)
    gathers[1].end()
    lax.fori_loop(2 * heads, 4 * heads, attend, 0)
    for s in range(streams):
        keep[s].wait()
        for index in range(4):
            gathers[s].core(index)
    plane.finish()


def reduce_scratch(streams, rows, width):
    return [
        pltpu.VMEM((streams, 8, rows, width), bf16),
        pltpu.VMEM((streams, 4, rows, width), bf16),
        pltpu.VMEM((streams, 3, rows // 2, width), bf16),
        pltpu.VMEM((streams, 3, rows // 2, width), bf16),
    ]


def project_kernel(
    mixed, wide, out, weight, parts, from_core, from_x, from_y, wide_sems, send_sems, recv_sems
):
    plane = Plane(send_sems, recv_sems)
    streams = mixed.shape[0]
    width = weight.shape[1]
    depth = wide.shape[3]
    traded, kept = [], []
    for head in range(2):
        for chip in range(4):
            column = pl.ds(pl.multiple_of((2 * chip + plane.core) * depth, depth), depth)
            here = weight.at[pl.ds(head * HEAD, HEAD), column]
            traded.append(plane.send(wide.at[2 * (1 - plane.core) + head, chip], here, "c"))
            copy = pltpu.make_async_copy(
                wide.at[2 * plane.core + head, chip], here, wide_sems.at[len(kept)]
            )
            copy.start()
            kept.append(copy)
    for copy in traded:
        copy.wait_recv()
    for copy in kept:
        copy.wait()
    sums = [
        Reduce(plane, parts.at[s], from_core.at[s], from_x.at[s], from_y.at[s])
        for s in range(streams)
    ]

    for s in range(streams):
        for m in ORDER:

            def other(at):
                parts[s, 4 + m, :, at] = nn(mixed[s, 4 + m], weight[:, at]).astype(bf16)

            tiles(width, N_TILE, other)
            sums[s].give(m)
        for m in ORDER:
            sums[s].take(m)

            def chip(at):
                here = nn(mixed[s, m], weight[:, at])
                parts[s, m, :, at] = (here + from_core[s, m, :, at].astype(f32)).astype(bf16)

            tiles(width, N_TILE, chip)
            sums[s].chip_done(m)
    for s in range(streams):
        sums[s].late()
    for s in range(streams):
        sums[s].total(out.at[s])
    plane.finish()


def gelu_pair(v):
    cubic = 0.044715 * (v * v) * v
    inner = (2.0 / np.pi) ** 0.5 * (v + cubic)
    th = jnp.tanh(inner)
    half = 0.5 * (1.0 + th)
    slope = (2.0 / np.pi) ** 0.5 * (1.0 + 3.0 * 0.044715 * (v * v))
    return v * half, half + 0.5 * v * (1.0 - th * th) * slope


def mlp_kernel(
    own, up_w, down_w, grads, pieces, slope_out, down_grad, out,
    parts, from_core, from_x, from_y, slots, act, slope, total, grad_slots,
    slot_sems, keep_sems, own_sem, grad_sems, send_sems, recv_sems,
):
    plane = Plane(send_sems, recv_sems)
    streams, rows, width = own.shape
    hidden = up_w.shape[1]
    gathers = [Gather(plane, own.at[s], pieces.at[s]) for s in range(streams)]
    sums = [
        Reduce(plane, parts.at[s], from_core.at[s], from_x.at[s], from_y.at[s])
        for s in range(streams)
    ]
    keep = [pltpu.make_async_copy(own.at[s], pieces.at[s, 0], own_sem.at[s]) for s in range(streams)]
    stores = []
    loads = [0]

    def load(s, p):
        slot = loads[0] % 2
        loads[0] += 1
        source = own.at[s] if p == 0 else pieces.at[s, p]
        copy = pltpu.make_async_copy(source, slots.at[slot], slot_sems.at[slot])
        copy.start()
        return copy, slots.at[slot]

    def work(s, p, loaded):
        copy, piece = loaded
        slot = len(stores) % 2
        index = len(stores)
        feed.start(index + 1)
        if index >= 2:
            stores[index - 2].wait()
        copy.wait()

        def up(at):
            value, grad = gelu_pair(nn(piece[...], up_w[:, at]))
            act[slot, :, at] = value.astype(bf16)
            slope[slot, :, at] = grad.astype(bf16)

        tiles(hidden, N_TILE, up)
        store = pltpu.make_async_copy(slope.at[slot], slope_out.at[s, p], keep_sems.at[slot])
        store.start()
        stores.append(store)
        if p < 4:
            sums[s].take(p)

        def down(at):
            here = nn(act[slot], down_w[:, at])
            if p < 4:
                here = here + from_core[s, p, :, at].astype(f32)
            parts[s, p, :, at] = here.astype(bf16)

        tiles(width, N_TILE, down)
        if p >= 4:
            sums[s].give(p - 4)
        else:
            sums[s].chip_done(p)
        grad = feed.get(index)

        def weigh(at):
            term = tn(act[slot], grad[:, at])
            total[:, at] = term if index == 0 else total[:, at] + term

        tiles(width, 512, weigh)

    order = [(s, p) for s in range(streams) for m in range(4) for p in (4 + m, m)]
    feed = Feed(lambda at: grads.at[at[0], at[1]], grad_slots, grad_sems, order)
    feed.start(0)
    for s in range(streams):
        keep[s].start()
    gathers[0].begin()

    def pair_up(s, m):
        gathers[s].core(m)
        work(s, 4 + m, load(s, 4 + m))
        work(s, m, load(s, m))

    for s in range(streams):
        pair_up(s, 0)
        gathers[s].middle()
        if s + 1 < streams:
            gathers[s + 1].begin()
        pair_up(s, 1)
        pair_up(s, 2)
        gathers[s].end()
        pair_up(s, 3)
        if s > 0:
            sums[s - 1].late()
    sums[streams - 1].late()
    for s in range(streams):
        sums[s].total(out.at[s])
        keep[s].wait()
    for store in stores[-2:]:
        store.wait()
    stores = []
    for index in range(hidden // rows):
        if index >= 2:
            stores[index - 2].wait()
        here = pl.ds(index * rows, rows)
        slots[index % 2] = total[here].astype(bf16)
        store = pltpu.make_async_copy(
            slots.at[index % 2], down_grad.at[here], keep_sems.at[index % 2]
        )
        store.start()
        stores.append(store)
    for store in stores[-2:]:
        store.wait()
    plane.finish()


def mlp_back_kernel(
    grads, slope_in, up_w, down_w, rows_in, pre_out, out, rows_out,
    parts, from_core, from_x, from_y, slots, slopes, pre,
    slot_sems, slope_sems, keep_sems, row_sems, send_sems, recv_sems,
):
    outward, inward = row_places()
    plane = Plane(send_sems, recv_sems, outward + inward)
    rows_move = RowMove(rows_in, rows_out, row_sems)
    rows_move.back()
    streams, _, rows, width = grads.shape
    hidden = up_w.shape[1]
    sums = [
        Reduce(plane, parts.at[s], from_core.at[s], from_x.at[s], from_y.at[s])
        for s in range(streams)
    ]
    order = [(s, p) for s in range(streams) for m in ORDER for p in (4 + m, m)]
    feed = Feed(lambda at: grads.at[at[0], at[1]], slots, slot_sems, order)
    feed_slope = Feed(lambda at: slope_in.at[at[0], at[1]], slopes, slope_sems, order)
    feed.start(0)
    feed_slope.start(0)
    stores = []
    for index, (s, p) in enumerate(order):
        feed.start(index + 1)
        feed_slope.start(index + 1)
        grad = feed.get(index)
        slope = feed_slope.get(index)
        slot = index % 2
        if index >= 2:
            stores[index - 2].wait()

        def back(at):
            value = nt(grad[...], down_w[at]) * slope[:, at].astype(f32)
            pre[slot, :, at] = value.astype(bf16)

        tiles(hidden, N_TILE, back)
        store = pltpu.make_async_copy(pre.at[slot], pre_out.at[s, p], keep_sems.at[slot])
        store.start()
        stores.append(store)
        if p < 4:
            sums[s].take(p)

        def through(at):
            here = nt(pre[slot], up_w[at])
            if p < 4:
                here = here + from_core[s, p, :, at].astype(f32)
            parts[s, p, :, at] = here.astype(bf16)

        tiles(width, N_TILE, through)
        if p >= 4:
            sums[s].give(p - 4)
        else:
            sums[s].chip_done(p)
        if s > 0 and p == 3:
            sums[s - 1].late()
    sums[streams - 1].late()
    for s in range(streams):
        sums[s].total(out.at[s])
    for store in stores[-2:]:
        store.wait()
    rows_move.wait()
    plane.finish()


def attention_back_kernel(
    clip_count, own, qkv, qkv_w, out_w, ends, pieces, grad_qkv, out,
    parts, from_core, from_x, from_y, slots, grad_mixed, key_sum, value_sum, slot_sems, own_sem, send_sems, recv_sems,
):
    plane = Plane(send_sems, recv_sems)
    streams, rows, width = own.shape
    inner = out_w.shape[0]
    gathers = [Gather(plane, own.at[s], pieces.at[s]) for s in range(streams)]
    sums = [
        Reduce(plane, parts.at[s], from_core.at[s], from_x.at[s], from_y.at[s])
        for s in range(streams)
    ]
    keep = [pltpu.make_async_copy(own.at[s], pieces.at[s, 0], own_sem.at[s]) for s in range(streams)]
    loads = [0]

    def mix(s, p):
        slot = loads[0] % 2
        loads[0] += 1
        source = own.at[s] if p == 0 else pieces.at[s, p]
        copy = pltpu.make_async_copy(source, slots.at[slot], slot_sems.at[slot])
        copy.start()
        copy.wait()
        grad_mixed[s, p] = nt(slots[slot], out_w[...]).astype(bf16)

    for s in range(streams):
        keep[s].start()
    gathers[0].begin()
    for s in range(streams):
        gather = gathers[s]
        mix(s, 0)
        gather.core(0)
        mix(s, 4)
        gather.middle()
        if s + 1 < streams:
            gathers[s + 1].begin()
        for index in (1, 2):
            mix(s, index)
            gather.core(index)
            mix(s, 4 + index)
        gather.end()
        mix(s, 3)
        gather.core(3)
        mix(s, 7)
    for m in ORDER:
        attend_back_chip(
            plane, qkv, grad_mixed, ends, grad_qkv, key_sum, value_sum, clip_count, m
        )
        for s in range(streams):

            def other(at):
                parts[s, 4 + m, :, at] = nt(grad_qkv[s, 4 + m], qkv_w[at]).astype(bf16)

            tiles(width, N_TILE, other)
            sums[s].give(m)
        for s in range(streams):
            sums[s].take(m)

            def chip(at):
                here = nt(grad_qkv[s, m], qkv_w[at])
                parts[s, m, :, at] = (here + from_core[s, m, :, at].astype(f32)).astype(bf16)

            tiles(width, N_TILE, chip)
            sums[s].chip_done(m)
    for s in range(streams):
        sums[s].late()
    for s in range(streams):
        sums[s].total(out.at[s])
        keep[s].wait()
    plane.finish()


def on_device(
    block_input,
    clip_lengths,
    norm1_gain,
    w_query,
    w_key,
    w_value,
    w_out,
    norm2_gain,
    w_up,
    w_down,
    out_cotangent,
):
    streams, rows, width = block_input.shape
    planes = lax.axis_size("tensor")
    lanes = lax.axis_size("dp")
    clip_count = clip_lengths.shape[1]
    own = lax.axis_index("dp")
    own_plane = lax.axis_index("tensor")
    own_core = own % 2
    heads = w_query.shape[1] * planes // (HEAD * lanes)
    depth = w_query.shape[0]
    hidden_part = w_up.shape[1] // lanes
    hidden_own = planes * hidden_part
    inner = heads * HEAD

    def hop(value, mask):
        return lax.ppermute(value, "dp", [(i, i ^ mask) for i in range(lanes)])

    def rows_back(value):
        got = []
        for turn in range(streams):
            pairs = [
                (
                    (2 * chip + core) * planes + plane,
                    (2 * chip + plane // 2) * planes + 2 * (1 - core) + (plane + turn) % 2,
                )
                for chip in range(lanes // 2)
                for core in range(2)
                for plane in range(planes)
            ]
            mine = lax.dynamic_index_in_dim(value, (own_plane + turn) % 2, 0, keepdims=False)
            got.append(lax.ppermute(mine, ("dp", "tensor"), pairs))
        even = own_plane % 2 == 0
        return jnp.where(even, jnp.stack(got), jnp.stack(got[::-1]))

    small = jnp.zeros((8, depth), f32)
    small = small.at[0].set(norm1_gain.astype(f32)).at[1].set(norm2_gain.astype(f32))
    small = small.at[2, : streams * clip_count].set(clip_lengths.reshape(-1).astype(f32))
    tokens_in, qkv_part, out_part, up_part, down_part, small = plane_call(
        start_kernel,
        "start",
        6,
        [
            jax.ShapeDtypeStruct(block_input.shape, bf16),
            jax.ShapeDtypeStruct((3, 4, depth, HEAD), bf16),
            jax.ShapeDtypeStruct((4, HEAD, depth), bf16),
            jax.ShapeDtypeStruct((width, hidden_part), bf16),
            jax.ShapeDtypeStruct((hidden_part, width), bf16),
            jax.ShapeDtypeStruct((lanes, 8, depth), f32),
        ],
        ["any"] * 8,
        ["any"] * 6,
        [pltpu.SemaphoreType.DMA((7,)), pltpu.SemaphoreType.DMA((2, 2))],
        33,
        0,
        (block_input, w_query, w_key, w_value, w_out, w_up, w_down, small),
    )
    gain_one = small[:, 0].reshape(-1)
    gain_two = small[:, 1].reshape(-1)
    lengths = small[:, 2, : streams * clip_count].reshape(-1, clip_count).astype(jnp.int32)

    qkv_wide = lax.all_gather(qkv_part, "tensor", axis=0, tiled=False)
    out_wide = lax.all_gather(out_part, "tensor", axis=0, tiled=False)
    up_w = lax.all_gather(up_part, "tensor", axis=0, tiled=False).swapaxes(0, 1)
    up_w = up_w.reshape(width, hidden_own)
    down_w = lax.all_gather(down_part, "tensor", axis=0, tiled=True)

    chip_groups = [[i for i in range(lanes) if i % 2 == core] for core in range(2)]

    def return_heads(split):
        keep = lax.dynamic_index_in_dim(split, own_core, 1, keepdims=False)
        give = lax.dynamic_index_in_dim(split, 1 - own_core, 1, keepdims=False)
        got = hop(give, 1)
        both = jnp.where(
            own_core == 0, jnp.concatenate([keep, got]), jnp.concatenate([got, keep])
        )
        mine = lax.psum_scatter(both, "tensor", scatter_dimension=0, tiled=False)
        return lax.all_to_all(mine, "dp", 0, 0, axis_index_groups=chip_groups, tiled=True)

    all_ends = jnp.cumsum(lengths, axis=1)
    buffers = 4 * (own // 2 ^ jnp.arange(4, dtype=jnp.int32)) + own_plane
    ends = jnp.take(all_ends, buffers, axis=0)
    chunks = 2 * (1 - own_core) + jnp.arange(streams, dtype=jnp.int32)
    places = chunks[:, None] * rows + jnp.arange(rows, dtype=jnp.int32)
    valid = (places < ends[0, -1]).astype(f32)
    ends = ends.reshape(-1).astype(jnp.int32)

    pieces = jax.ShapeDtypeStruct((streams, 8, rows, width), bf16)
    sums = jax.ShapeDtypeStruct((streams, rows, width), f32)
    row_count = streams * 8 * rows
    slots = pltpu.VMEM((2, rows, width), bf16)
    dma = pltpu.SemaphoreType.DMA

    def piece_shape(columns):
        return jax.ShapeDtypeStruct((streams, 8, rows, columns), bf16)

    tokens = tokens_in.astype(f32)
    normed_one, unit_one, inverse_one = norm_rows(tokens, gain_one)
    features_one, cotangent = plane_call(
        gather_kernel,
        "gather",
        0,
        [pieces, jax.ShapeDtypeStruct(block_input.shape, bf16)],
        ["any", "any"],
        ["any", "any"],
        [dma((streams,)), dma((2, 2))],
        8 * streams,
        0,
        (normed_one.astype(bf16), out_cotangent),
    )
    grad_out = cotangent.astype(f32) * valid[:, :, None]
    grad_branch, qkv, mixed, qkv_w = plane_call(
        functools.partial(attention_kernel, clip_count),
        "attention",
        1,
        [
            pieces,
            piece_shape(3 * inner),
            piece_shape(inner),
            jax.ShapeDtypeStruct((4, 2, depth, 3 * inner), bf16),
        ],
        ["any", "any", "any", "smem"],
        ["any", "vmem", "vmem", "vmem"],
        [slots, dma((2,)), dma((streams,)), dma((6,))],
        8 * streams + 6,
        2 * row_count * width * 3 * inner,
        (grad_out.astype(bf16), features_one, qkv_wide, ends),
    )
    attn_sum, out_w = plane_call(
        project_kernel,
        "project",
        2,
        [sums, jax.ShapeDtypeStruct((inner, width), bf16)],
        ["vmem", "any"],
        ["vmem", "vmem"],
        reduce_scratch(streams, rows, width) + [dma((8,))],
        10 * streams + 8,
        2 * row_count * width * inner,
        (mixed, out_wide),
    )
    hidden = tokens + attn_sum
    normed_two, unit_two, inverse_two = norm_rows(hidden, gain_two)
    part = pltpu.VMEM((2, rows, hidden_own), bf16)
    features_two, slope, down_dot, mlp_sum = plane_call(
        mlp_kernel,
        "mlp",
        3,
        [
            pieces,
            piece_shape(hidden_own),
            jax.ShapeDtypeStruct((hidden_own, width), bf16),
            sums,
        ],
        ["any", "vmem", "vmem", "any"],
        ["any", "any", "any", "vmem"],
        reduce_scratch(streams, rows, width)
        + [slots, part, part, pltpu.VMEM((hidden_own, width), f32), slots]
        + [dma((2,)), dma((2,)), dma((streams,)), dma((2,))],
        18 * streams,
        6 * row_count * width * hidden_own,
        (normed_two.astype(bf16), up_w, down_w, grad_branch),
    )

    grad_pre, back_sum, output = plane_call(
        mlp_back_kernel,
        "mlp_back",
        4,
        [piece_shape(hidden_own), sums, jax.ShapeDtypeStruct(block_input.shape, bf16)],
        ["any", "any", "vmem", "vmem", "any"],
        ["any", "vmem", "any"],
        reduce_scratch(streams, rows, width)
        + [slots, part, part, dma((2,)), dma((2,)), dma((2,)), dma((2, 2))],
        10 * streams,
        4 * row_count * width * hidden_own,
        (grad_branch, slope, up_w, down_w, (hidden + mlp_sum).astype(bf16)),
    )
    from_two, gain_two_grad = norm_back(back_sum, unit_two, inverse_two, gain_two)
    grad_hidden = grad_out + from_two

    def grad_dot(left, right):
        return lax.dot_general(
            left.reshape(row_count, -1),
            right.reshape(row_count, -1),
            (((0,), (0,)), ((), ())),
            preferred_element_type=f32,
        ).astype(bf16)

    up_dot = grad_dot(features_two, grad_pre)
    grad_attn_own, up_dot = lax.optimization_barrier((grad_hidden.astype(bf16), up_dot))
    down_sum = lax.psum_scatter(down_dot, "tensor", scatter_dimension=0, tiled=True)
    up_sum = up_dot.reshape(width, planes, hidden_part).swapaxes(0, 1)
    up_sum = lax.psum_scatter(up_sum, "tensor", scatter_dimension=0, tiled=False)

    chunk = pltpu.VMEM((4, rows, HEAD), f32)
    grad_attn, grad_qkv, input_sum = plane_call(
        functools.partial(attention_back_kernel, clip_count),
        "attention_back",
        5,
        [pieces, piece_shape(3 * inner), sums],
        ["any", "vmem", "vmem", "vmem", "smem"],
        ["any", "vmem", "vmem"],
        reduce_scratch(streams, rows, width)
        + [slots, pltpu.VMEM((streams, 8, rows, inner), bf16), chunk, chunk, dma((2,)), dma((streams,))],
        18 * streams,
        2 * row_count * width * 4 * inner,
        (grad_attn_own, qkv, qkv_w.reshape(width, 3 * inner), out_w, ends),
    )
    input_sum, grad_qkv, grad_attn, down_sum, up_sum = lax.optimization_barrier(
        (input_sum, grad_qkv, grad_attn, down_sum, up_sum)
    )
    down_sum = down_sum.reshape(hidden_part, lanes, depth).swapaxes(0, 1)
    down_grad = lax.all_to_all(down_sum, "dp", 0, 0, tiled=True).reshape(-1, depth).astype(f32)
    up_grad = lax.all_to_all(up_sum.reshape(lanes, depth, hidden_part), "dp", 0, 0, tiled=True)
    up_grad = up_grad.swapaxes(0, 1).reshape(depth, -1).astype(f32)
    from_one, gain_one_grad = norm_back(input_sum, unit_one, inverse_one, gain_one)
    input_grad = rows_back((grad_hidden + from_one).astype(bf16)).astype(f32)

    out_sum = grad_dot(mixed, grad_attn).reshape(heads, HEAD, 4, 2, depth)
    out_grad = return_heads(out_sum.transpose(0, 3, 2, 1, 4)).reshape(-1, depth)
    qkv_sum = grad_dot(features_one, grad_qkv).reshape(4, 2, depth, heads, 3, HEAD)
    qkv_grad = return_heads(qkv_sum.transpose(3, 1, 0, 4, 2, 5))
    qkv_grad = qkv_grad.transpose(1, 2, 0, 3).reshape(3, depth, -1).astype(f32)

    gain_grads = jnp.stack([gain_one_grad.sum(0), gain_two_grad.sum(0)])
    for mask in (1, 2, 4):
        gain_grads = gain_grads + hop(gain_grads, mask)
    for mask in (1, 2):
        gain_grads = gain_grads + lax.ppermute(
            gain_grads, "tensor", [(i, i ^ mask) for i in range(planes)]
        )
    gain_grads = lax.dynamic_slice_in_dim(gain_grads, own * depth, depth, 1)
    return (
        output,
        input_grad,
        gain_grads[0],
        qkv_grad[0],
        qkv_grad[1],
        qkv_grad[2],
        out_grad.astype(f32),
        gain_grads[1],
        up_grad,
        down_grad,
    )


def solution(mesh):
    in_specs = (
        P("dp", "tensor", None),
        P("dp", None),
        P("dp"),
        P("dp", "tensor"),
        P("dp", "tensor"),
        P("dp", "tensor"),
        P("tensor", "dp"),
        P("dp"),
        P("dp", "tensor"),
        P("tensor", "dp"),
        P("dp", "tensor", None),
    )
    out_specs = (
        P("dp", "tensor", None),
        P("dp", "tensor", None),
        P("dp"),
        P("dp", "tensor"),
        P("dp", "tensor"),
        P("dp", "tensor"),
        P("tensor", "dp"),
        P("dp"),
        P("dp", "tensor"),
        P("tensor", "dp"),
    )
    own_form = mesh.shape["dp"] == 8 and mesh.shape["tensor"] == 4
    return jax.shard_map(
        on_device if own_form else on_device_any, mesh=mesh, in_specs=in_specs, out_specs=out_specs, check_vma=False
    )
```

```python
import functools

import jax
import jax.numpy as jnp
import numpy as np
from jax import lax
from jax.experimental import pallas as pl
from jax.experimental.pallas import tpu as pltpu
from jax.sharding import PartitionSpec as P

HEAD = 128
LONGEST = 512
epsilon = 1e-05
masked_fill = -1000000000.0
bf16 = jnp.bfloat16
f32 = jnp.float32


def norm_rows(tokens, gain):
    centred = tokens - jnp.mean(tokens, axis=-1, keepdims=True)
    inverse = lax.rsqrt(jnp.mean(centred * centred, axis=-1, keepdims=True) + epsilon)
    unit_rows = centred * inverse
    return (unit_rows * gain, unit_rows, inverse)


def norm_back(grad_normed, unit_rows, inverse, gain):
    scaled = grad_normed * gain
    inner_sum = (
        scaled
        - jnp.mean(scaled, axis=-1, keepdims=True)
        - unit_rows * jnp.mean(scaled * unit_rows, axis=-1, keepdims=True)
    )
    return (inverse * inner_sum, jnp.sum(grad_normed * unit_rows, axis=0))


def gelu_tanh(values):
    return jax.nn.gelu(values, approximate=True)


def masked_scores(q_rows, keys_heads, segment, offset, block_rows):
    slot_count = keys_heads.shape[0]
    raw_scores = jnp.einsum(
        "qhd,khd->hqk", q_rows, keys_heads, preferred_element_type=jnp.float32
    ) * HEAD ** (-0.5)
    q_segment = lax.dynamic_slice_in_dim(segment, offset, block_rows, 0)
    q_place = offset + jnp.arange(block_rows, dtype=jnp.int32)
    places = jnp.arange(slot_count, dtype=jnp.int32)
    allowed = (q_segment[:, None] == segment[None, :]) & (places[None, :] <= q_place[:, None])
    return jnp.where(allowed[None], raw_scores, masked_fill)


def attend(query, key, value, segment, block_rows):
    slot_count = query.shape[0]
    head_count = query.shape[1] // HEAD
    keys_heads = key.reshape(slot_count, head_count, HEAD)
    values_heads = value.reshape(slot_count, head_count, HEAD)

    def one_block(block_index):
        offset = block_index * block_rows
        q_rows = lax.dynamic_slice_in_dim(query, offset, block_rows, 0).reshape(
            block_rows, head_count, HEAD
        )
        scores = masked_scores(q_rows, keys_heads, segment, offset, block_rows)
        highest = jnp.max(scores, axis=-1, keepdims=True)
        shifted = jnp.exp(scores - highest)
        totals = jnp.sum(shifted, axis=-1, keepdims=True)
        weights = (shifted / totals).astype(jnp.bfloat16)
        mixed_rows = jnp.einsum(
            "hqk,khd->qhd", weights, values_heads, preferred_element_type=jnp.float32
        )
        return (
            mixed_rows.reshape(block_rows, head_count * HEAD).astype(jnp.bfloat16),
            (highest + jnp.log(totals))[..., 0],
        )

    mixed_rows, log_norm = lax.map(one_block, jnp.arange(slot_count // block_rows, dtype=jnp.int32))
    return (mixed_rows.reshape(slot_count, head_count * HEAD), log_norm)


def attend_back(query, key, value, segment, log_norm, grad_mixed, block_rows):
    slot_count = query.shape[0]
    head_count = query.shape[1] // HEAD
    keys_heads = key.reshape(slot_count, head_count, HEAD)
    values_heads = value.reshape(slot_count, head_count, HEAD)

    def one_block(carried, block_index):
        grad_keys, grad_values = carried
        offset = block_index * block_rows
        q_rows = lax.dynamic_slice_in_dim(query, offset, block_rows, 0).reshape(
            block_rows, head_count, HEAD
        )
        g_rows = lax.dynamic_slice_in_dim(grad_mixed, offset, block_rows, 0).reshape(
            block_rows, head_count, HEAD
        )
        scores = masked_scores(q_rows, keys_heads, segment, offset, block_rows)
        prob_rows = jnp.exp(scores - log_norm[block_index][..., None])
        grad_values = grad_values + jnp.einsum(
            "hqk,qhd->khd",
            prob_rows.astype(jnp.bfloat16),
            g_rows,
            preferred_element_type=jnp.float32,
        )
        grad_probs = jnp.einsum(
            "qhd,khd->hqk", g_rows, values_heads, preferred_element_type=jnp.float32
        )
        inner_sum = jnp.sum(prob_rows * grad_probs, axis=-1, keepdims=True)
        grad_scores = (prob_rows * (grad_probs - inner_sum) * HEAD ** (-0.5)).astype(jnp.bfloat16)
        grad_query = jnp.einsum(
            "hqk,khd->qhd", grad_scores, keys_heads, preferred_element_type=jnp.float32
        )
        grad_keys = grad_keys + jnp.einsum(
            "hqk,qhd->khd", grad_scores, q_rows, preferred_element_type=jnp.float32
        )
        return (
            (grad_keys, grad_values),
            grad_query.reshape(block_rows, head_count * HEAD).astype(jnp.bfloat16),
        )

    zero_state = jnp.zeros((slot_count, head_count, HEAD), jnp.float32)
    (grad_keys, grad_values), grad_query = lax.scan(
        one_block, (zero_state, zero_state), jnp.arange(slot_count // block_rows, dtype=jnp.int32)
    )
    return (
        grad_query.reshape(slot_count, head_count * HEAD),
        grad_keys.reshape(slot_count, head_count * HEAD).astype(jnp.bfloat16),
        grad_values.reshape(slot_count, head_count * HEAD).astype(jnp.bfloat16),
    )


def on_device_any(
    block_input,
    clip_lengths,
    norm1_gain,
    w_query,
    w_key,
    w_value,
    w_out,
    norm2_gain,
    w_up,
    w_down,
    out_cotangent,
):
    micro_count = block_input.shape[0]
    local_rows = block_input.shape[1]
    tensor_size = lax.axis_size("tensor")
    slot_count = local_rows * tensor_size
    block_rows = min(512, slot_count)
    clip_count = clip_lengths.shape[1]
    row_offset = lax.axis_index("tensor") * local_rows
    places = jnp.arange(slot_count, dtype=jnp.int32)

    def fetch_weights():
        return (
            lax.all_gather(norm1_gain, "dp", axis=0, tiled=True),
            lax.all_gather(norm2_gain, "dp", axis=0, tiled=True),
            lax.all_gather(w_query, "dp", axis=0, tiled=True),
            lax.all_gather(w_key, "dp", axis=0, tiled=True),
            lax.all_gather(w_value, "dp", axis=0, tiled=True),
            lax.all_gather(w_up, "dp", axis=0, tiled=True),
            lax.all_gather(w_out, "dp", axis=1, tiled=True),
            lax.all_gather(w_down, "dp", axis=1, tiled=True),
        )

    def rows_forward(normed):
        return lax.all_gather(normed, "tensor", axis=0, tiled=True)

    def rows_backward(gradients):
        return lax.all_gather(gradients, "tensor", axis=0, tiled=True)

    def sum_forward(term_fn):
        return lax.psum_scatter(
            term_fn(jnp.int32(0), local_rows * lax.axis_size("tensor")),
            "tensor",
            scatter_dimension=0,
            tiled=True,
        )

    def sum_backward(term_fn):
        return lax.psum_scatter(
            term_fn(jnp.int32(0), local_rows * lax.axis_size("tensor")),
            "tensor",
            scatter_dimension=0,
            tiled=True,
        )

    grad_totals = None
    outputs = []
    input_grads = []
    for micro_index in range(micro_count):
        gathered = fetch_weights()
        gain_one = gathered[0].astype(jnp.float32)
        gain_two = gathered[1].astype(jnp.float32)
        query_w, key_w, value_w, up_w, out_w, down_w = (
            gathered[2],
            gathered[3],
            gathered[4],
            gathered[5],
            gathered[6],
            gathered[7],
        )
        tokens = block_input[micro_index].astype(jnp.float32)
        ends = jnp.cumsum(clip_lengths[micro_index])
        segment = jnp.sum((places[:, None] >= ends[None, :]).astype(jnp.int32), axis=1)
        own_segment = lax.dynamic_slice_in_dim(segment, row_offset, local_rows, 0)
        valid_rows = (own_segment < clip_count).astype(jnp.float32)
        normed_one, unit_one, inverse_one = norm_rows(tokens, gain_one)
        features_one = rows_forward(normed_one.astype(jnp.bfloat16))
        query = jnp.dot(features_one, query_w, preferred_element_type=jnp.float32).astype(
            jnp.bfloat16
        )
        key = jnp.dot(features_one, key_w, preferred_element_type=jnp.float32).astype(jnp.bfloat16)
        value = jnp.dot(features_one, value_w, preferred_element_type=jnp.float32).astype(
            jnp.bfloat16
        )
        mixed_rows, log_norm = attend(query, key, value, segment, block_rows)

        def attn_term(offset, row_count):
            return jnp.dot(mixed_rows, out_w, preferred_element_type=jnp.float32)

        hidden = tokens + sum_forward(attn_term)
        normed_two, unit_two, inverse_two = norm_rows(hidden, gain_two)
        features_two = rows_forward(normed_two.astype(jnp.bfloat16))
        pre_act = jnp.dot(features_two, up_w, preferred_element_type=jnp.float32)
        activated = gelu_tanh(pre_act).astype(jnp.bfloat16)

        def mlp_term(offset, row_count):
            return jnp.dot(activated, down_w, preferred_element_type=jnp.float32)

        outputs.append((hidden + sum_forward(mlp_term)).astype(jnp.bfloat16))
        regathered = fetch_weights()
        query_w, key_w, value_w, up_w, out_w, down_w = (
            regathered[2],
            regathered[3],
            regathered[4],
            regathered[5],
            regathered[6],
            regathered[7],
        )
        grad_out = out_cotangent[micro_index].astype(jnp.float32) * valid_rows[:, None]
        grad_branch = rows_backward(grad_out.astype(jnp.bfloat16))
        down_grad = jnp.einsum(
            "sf,sd->fd", activated, grad_branch, preferred_element_type=jnp.float32
        )
        grad_act = jnp.einsum("sd,fd->sf", grad_branch, down_w, preferred_element_type=jnp.float32)
        grad_pre = jax.vjp(gelu_tanh, pre_act)[1](grad_act)[0].astype(jnp.bfloat16)
        up_grad = jnp.einsum(
            "sd,sf->df", features_two, grad_pre, preferred_element_type=jnp.float32
        )

        def up_term(offset, row_count):
            return jnp.einsum("sf,df->sd", grad_pre, up_w, preferred_element_type=jnp.float32)

        grad_normed_two = sum_backward(up_term)
        grad_from_two, gain_two_grad = norm_back(grad_normed_two, unit_two, inverse_two, gain_two)
        grad_hidden = grad_out + grad_from_two
        grad_attn = rows_backward(grad_hidden.astype(jnp.bfloat16))
        out_grad = jnp.einsum(
            "sc,sd->cd", mixed_rows, grad_attn, preferred_element_type=jnp.float32
        )
        grad_mixed = jnp.einsum(
            "sd,cd->sc", grad_attn, out_w, preferred_element_type=jnp.float32
        ).astype(jnp.bfloat16)
        grad_query, grad_key, grad_value = attend_back(
            query, key, value, segment, log_norm, grad_mixed, block_rows
        )
        query_grad = jnp.einsum(
            "sd,sc->dc", features_one, grad_query, preferred_element_type=jnp.float32
        )
        key_grad = jnp.einsum(
            "sd,sc->dc", features_one, grad_key, preferred_element_type=jnp.float32
        )
        value_grad = jnp.einsum(
            "sd,sc->dc", features_one, grad_value, preferred_element_type=jnp.float32
        )

        def qkv_term(offset, row_count):
            part_query = jnp.einsum(
                "sc,dc->sd", grad_query, query_w, preferred_element_type=jnp.float32
            )
            part_key = jnp.einsum("sc,dc->sd", grad_key, key_w, preferred_element_type=jnp.float32)
            part_value = jnp.einsum(
                "sc,dc->sd", grad_value, value_w, preferred_element_type=jnp.float32
            )
            return part_query + part_key + part_value

        grad_normed_one = sum_backward(qkv_term)
        grad_from_one, gain_one_grad = norm_back(grad_normed_one, unit_one, inverse_one, gain_one)
        input_grads.append(grad_hidden + grad_from_one)
        micro_grads = (
            gain_one_grad,
            gain_two_grad,
            query_grad,
            key_grad,
            value_grad,
            up_grad,
            out_grad,
            down_grad,
        )
        if grad_totals is None:
            grad_totals = micro_grads
        else:
            grad_totals = jax.tree.map(jnp.add, grad_totals, micro_grads)
    grad_totals = (
        lax.psum_scatter(
            grad_totals[0].astype(jnp.bfloat16), "dp", scatter_dimension=0, tiled=True
        ).astype(jnp.float32),
        lax.psum_scatter(
            grad_totals[1].astype(jnp.bfloat16), "dp", scatter_dimension=0, tiled=True
        ).astype(jnp.float32),
        lax.psum_scatter(
            grad_totals[2].astype(jnp.bfloat16), "dp", scatter_dimension=0, tiled=True
        ).astype(jnp.float32),
        lax.psum_scatter(
            grad_totals[3].astype(jnp.bfloat16), "dp", scatter_dimension=0, tiled=True
        ).astype(jnp.float32),
        lax.psum_scatter(
            grad_totals[4].astype(jnp.bfloat16), "dp", scatter_dimension=0, tiled=True
        ).astype(jnp.float32),
        lax.psum_scatter(
            grad_totals[5].astype(jnp.bfloat16), "dp", scatter_dimension=0, tiled=True
        ).astype(jnp.float32),
        lax.psum_scatter(
            grad_totals[6].astype(jnp.bfloat16), "dp", scatter_dimension=1, tiled=True
        ).astype(jnp.float32),
        lax.psum_scatter(
            grad_totals[7].astype(jnp.bfloat16), "dp", scatter_dimension=1, tiled=True
        ).astype(jnp.float32),
    )
    gain_sums = lax.psum((grad_totals[0], grad_totals[1]), "tensor")
    return (
        jnp.stack(outputs),
        jnp.stack(input_grads),
        gain_sums[0],
        grad_totals[2],
        grad_totals[3],
        grad_totals[4],
        grad_totals[6],
        gain_sums[1],
        grad_totals[5],
        grad_totals[7],
    )


def chunk_scores(q, k, start, s, c, rows):
    scores = lax.dot_general(
        q, k, (((1,), (1,)), ((), ())), preferred_element_type=f32
    ) * HEAD ** (-0.5)
    k_place = c * rows + lax.broadcasted_iota(jnp.int32, (rows, rows), 1)
    allowed = k_place >= start
    if c == s:
        q_place = s * rows + lax.broadcasted_iota(jnp.int32, (rows, rows), 0)
        allowed = jnp.logical_and(allowed, k_place <= q_place)
    return jnp.where(allowed, scores, masked_fill)


def clip_starts(ends_ref, first, buffer, clip_count, s, rows):
    place = s * rows + lax.broadcasted_iota(jnp.int32, (rows, 1), 0)
    start = jnp.zeros((rows, 1), jnp.int32)
    for clip in range(clip_count):
        end = ends_ref[first + buffer * clip_count + clip]
        start = jnp.where(place >= end, jnp.maximum(start, end), start)
    return start


def window(s, rows):
    back = -(-(LONGEST - 1) // rows)
    return range(max(0, s - back), s + 1)


def chunk_probs(q, keys, start, s, rows):
    cs = list(window(s, rows))
    scores = [chunk_scores(q, keys(c), start, s, c, rows) for c in cs]
    highest = functools.reduce(jnp.maximum, [jnp.max(v, axis=1, keepdims=True) for v in scores])
    shifted = [jnp.exp(v - highest) for v in scores]
    total = functools.reduce(jnp.add, [jnp.sum(v, axis=1, keepdims=True) for v in shifted])
    scale = 1.0 / total
    return cs, [v * scale for v in shifted]


MESH = pl.DeviceIdType.MESH
N_TILE = 1024


class Plane:
    def __init__(self, send_sems, recv_sems, more=()):
        me = lax.axis_index("dp")
        self.core = me % 2
        self.x = (me // 2) % 2
        self.peers = {
            "c": me + 1 - 2 * (me % 2),
            "x": me + 2 - 4 * ((me // 2) % 2),
            "y": me + 4 - 8 * ((me // 4) % 2),
        }
        self.send_sems, self.recv_sems = send_sems, recv_sems
        self.copies = []
        barrier = pltpu.get_barrier_semaphore()
        for peer in self.peers.values():
            pl.semaphore_signal(barrier, inc=1, device_id={"dp": peer}, device_id_type=MESH)
        for place in more:
            pl.semaphore_signal(barrier, inc=1, device_id=at_device(place), device_id_type=MESH)
        pl.semaphore_wait(barrier, 3 + len(more))

    def send(self, src, dst, way):
        return self.send_to(src, dst, {"dp": self.peers[way]})

    def send_to(self, src, dst, device):
        index = len(self.copies)
        copy = pltpu.make_async_remote_copy(
            src_ref=src,
            dst_ref=dst,
            send_sem=self.send_sems.at[index],
            recv_sem=self.recv_sems.at[index],
            device_id=device,
            device_id_type=MESH,
        )
        copy.start()
        self.copies.append(copy)
        return copy

    def finish(self):
        for copy in self.copies:
            copy.wait_send()


class Gather:
    def __init__(self, plane, own, pieces):
        self.plane, self.own, self.pieces = plane, own, pieces
        self.half = own.shape[0] // 2

    def begin(self):
        send = self.plane.send
        self.x = send(self.own, self.pieces.at[1], "x")
        self.y = send(self.own, self.pieces.at[2], "y")
        self.c = [send(self.own, self.pieces.at[4], "c")]

    def middle(self):
        send, half, pieces = self.plane.send, self.half, self.pieces
        self.x.wait_recv()
        self.fy = send(pieces.at[1, pl.ds(half, half)], pieces.at[3, pl.ds(half, half)], "y")
        self.c.append(send(pieces.at[1], pieces.at[5], "c"))
        self.y.wait_recv()
        self.fx = send(pieces.at[2, pl.ds(0, half)], pieces.at[3, pl.ds(0, half)], "x")
        self.c.append(send(pieces.at[2], pieces.at[6], "c"))

    def end(self):
        self.fx.wait_recv()
        self.fy.wait_recv()
        self.c.append(self.plane.send(self.pieces.at[3], self.pieces.at[7], "c"))

    def core(self, index):
        self.c[index].wait_recv()


class Reduce:
    def __init__(self, plane, pieces, from_core, from_x, from_y):
        self.plane, self.pieces = plane, pieces
        self.from_core, self.from_x, self.from_y = from_core, from_x, from_y
        self.half = pieces.shape[1] // 2
        self.core = {}

    def give(self, m):
        self.core[m] = self.plane.send(self.pieces.at[4 + m], self.from_core.at[m], "c")

    def take(self, m):
        self.core[m].wait_recv()

    def chip_done(self, m):
        send, half, pieces = self.plane.send, self.half, self.pieces
        low, high = pl.ds(0, half), pl.ds(half, half)
        if m == 3:
            self.far_x = send(pieces.at[3, low], self.from_x.at[1], "x")
            self.far_y = send(pieces.at[3, high], self.from_y.at[1], "y")
        elif m == 1:
            self.near_x = send(pieces.at[1, low], self.from_x.at[0], "x")
        elif m == 2:
            self.near_y = send(pieces.at[2, high], self.from_y.at[0], "y")

    def late_x(self):
        high = pl.ds(self.half, self.half)
        self.far_y.wait_recv()
        add_into(self.pieces.at[1, high], self.from_y.at[1])
        self.late_x_copy = self.plane.send(self.pieces.at[1, high], self.from_x.at[2], "x")

    def late_y(self):
        low = pl.ds(0, self.half)
        self.far_x.wait_recv()
        add_into(self.pieces.at[2, low], self.from_x.at[1])
        self.late_y_copy = self.plane.send(self.pieces.at[2, low], self.from_y.at[2], "y")

    def late(self):
        self.late_x()
        self.late_y()

    def total(self, out):
        half = self.half
        self.near_x.wait_recv()
        self.near_y.wait_recv()
        self.late_x_copy.wait_recv()
        self.late_y_copy.wait_recv()
        step = min(64, half)

        for base, x_part, y_part in ((0, 0, 2), (half, 2, 0)):

            def add(index, carry):
                at = pl.ds(pl.multiple_of(index * step, step), step)
                here = pl.ds(pl.multiple_of(base + index * step, step), step)
                out[here] = (
                    self.pieces[0, here].astype(f32)
                    + self.from_x[x_part, at].astype(f32)
                    + self.from_y[y_part, at].astype(f32)
                )
                return carry

            lax.fori_loop(0, half // step, add, 0)


def add_into(ref, other):
    step = min(64, ref.shape[0])

    def add(index, carry):
        at = pl.ds(pl.multiple_of(index * step, step), step)
        ref[at] = (ref[at].astype(f32) + other[at].astype(f32)).astype(bf16)
        return carry

    lax.fori_loop(0, ref.shape[0] // step, add, 0)


ORDER = (3, 1, 2, 0)


def tiles(count, tile, body):
    tile = min(tile, count)

    def step(index, carry):
        body(pl.ds(pl.multiple_of(index * tile, tile), tile))
        return carry

    lax.fori_loop(0, count // tile, step, 0)


def nn(left, right):
    return jnp.dot(left, right, preferred_element_type=f32)


def nt(left, right):
    return lax.dot_general(left, right, (((1,), (1,)), ((), ())), preferred_element_type=f32)


def tn(left, right):
    return lax.dot_general(left, right, (((0,), (0,)), ((), ())), preferred_element_type=f32)


class Feed:
    def __init__(self, source, slots, sems, order):
        self.source, self.slots, self.sems, self.order = source, slots, sems, list(order)

    def copy(self, index):
        slot = index % 2
        return pltpu.make_async_copy(
            self.source(self.order[index]), self.slots.at[slot], self.sems.at[slot]
        )

    def start(self, index):
        if index < len(self.order):
            self.copy(index).start()

    def get(self, index):
        self.copy(index).wait()
        return self.slots.at[index % 2]


def plane_call(kernel, name, collective_id, out_shape, in_spaces, out_spaces, scratch, copies, flops, args):
    spaces = {"any": pl.ANY, "vmem": pltpu.VMEM, "smem": pltpu.SMEM}
    return pl.pallas_call(
        kernel,
        out_shape=out_shape,
        in_specs=[pl.BlockSpec(memory_space=spaces[v]) for v in in_spaces],
        out_specs=[pl.BlockSpec(memory_space=spaces[v]) for v in out_spaces],
        scratch_shapes=list(scratch)
        + [pltpu.SemaphoreType.DMA((copies,)), pltpu.SemaphoreType.DMA((copies,))],
        compiler_params=pltpu.CompilerParams(
            collective_id=collective_id, has_side_effects=True, vmem_limit_bytes=60 << 20
        ),
        cost_estimate=pl.CostEstimate(flops=flops, bytes_accessed=64 << 20, transcendentals=0),
        name=name,
    )(*args)


def row_places():
    me, plane = lax.axis_index("dp"), lax.axis_index("tensor")
    chip, core = 2 * (me // 2), me % 2
    outward = [(chip + 1 - plane // 2, 2 * core + j) for j in range(2)]
    inward = [(chip + plane // 2, 2 * (1 - core) + i) for i in range(2)]
    return outward, inward


def at_device(place):
    return {"dp": place[0], "tensor": place[1]}


class RowMove:
    def __init__(self, src, dst, sems):
        self.src, self.dst, self.sems = src, dst, sems
        self.copies = []

    def copy(self, here, there, place):
        return pltpu.make_async_remote_copy(
            src_ref=self.src.at[here],
            dst_ref=self.dst.at[there],
            send_sem=self.sems.at[0, here],
            recv_sem=self.sems.at[1, there],
            device_id=at_device(place),
            device_id_type=MESH,
        )

    def start(self, places, there):
        for here in range(2):
            copy = self.copy(here, there, places[here])
            copy.start()
            self.copies.append(copy)
        self.arrivals = [self.copy(index, index, places[index]) for index in range(2)]

    def outward(self):
        self.start(row_places()[0], lax.axis_index("tensor") % 2)

    def back(self):
        self.start(row_places()[1], lax.axis_index("tensor") % 2)

    def wait(self):
        for copy in self.copies:
            copy.wait_send()
        for copy in self.arrivals:
            copy.wait_recv()


def start_kernel(
    tokens, w_query, w_key, w_value, w_out, w_up, w_down, small,
    tokens_out, qkv_out, out_out, up_out, down_out, small_out,
    local_sems, row_sems, send_sems, recv_sems,
):
    me, plane = lax.axis_index("dp"), lax.axis_index("tensor")
    chip, core = me // 2, me % 2
    depth = w_query.shape[0]
    part = up_out.shape[1]
    outward, inward = row_places()
    peers = [lax.rem(me + j, 8) for j in range(1, 8)]
    barrier = pltpu.get_barrier_semaphore()
    for peer in peers:
        pl.semaphore_signal(barrier, inc=1, device_id={"dp": peer}, device_id_type=MESH)
    for place in outward + inward:
        pl.semaphore_signal(barrier, inc=1, device_id=at_device(place), device_id_type=MESH)
    pl.semaphore_wait(barrier, 11)
    copies, locals_ = [], []

    def send(src, dst, device):
        copy = pltpu.make_async_remote_copy(
            src_ref=src,
            dst_ref=dst,
            send_sem=send_sems.at[len(copies)],
            recv_sem=recv_sems.at[len(copies)],
            device_id=device,
            device_id_type=MESH,
        )
        copy.start()
        copies.append(copy)

    def keep(src, dst):
        copy = pltpu.make_async_copy(src, dst, local_sems.at[len(locals_)])
        copy.start()
        locals_.append(copy)

    def block(index, size):
        return pl.ds(pl.multiple_of(index * size, size), size)

    rows_move = RowMove(tokens, tokens_out, row_sems)
    rows_move.outward()
    for peer in peers:
        send(small, small_out.at[me], {"dp": peer})
    keep(small, small_out.at[me])
    heads = [(w_query, 0), (w_key, 1), (w_value, 2)]
    for j in range(1, 4):
        other = lax.rem(chip + j, 4)
        device = {"dp": 2 * other + core}
        for weight, which in heads:
            send(weight.at[:, block(other, HEAD)], qkv_out.at[which, chip], device)
    for weight, which in heads:
        keep(weight.at[:, block(chip, HEAD)], qkv_out.at[which, chip])
    for j in range(1, 4):
        other = lax.rem(chip + j, 4)
        send(w_out.at[block(other, HEAD)], out_out.at[chip], {"dp": 2 * other + core})
    keep(w_out.at[block(chip, HEAD)], out_out.at[chip])
    for peer in peers:
        send(w_up.at[:, block(peer, part)], up_out.at[block(me, depth)], {"dp": peer})
        send(w_down.at[block(peer, part)], down_out.at[:, block(me, depth)], {"dp": peer})
    keep(w_up.at[:, block(me, part)], up_out.at[block(me, depth)])
    keep(w_down.at[block(me, part)], down_out.at[:, block(me, depth)])
    for copy in locals_:
        copy.wait()
    for copy in copies:
        copy.wait()
    rows_move.wait()


def gather_kernel(own, rows_in, pieces, rows_out, own_sem, row_sems, send_sems, recv_sems):
    outward, inward = row_places()
    plane = Plane(send_sems, recv_sems, outward + inward)
    streams = own.shape[0]
    rows_move = RowMove(rows_in, rows_out, row_sems)
    rows_move.outward()
    gathers = [Gather(plane, own.at[s], pieces.at[s]) for s in range(streams)]
    keep = [pltpu.make_async_copy(own.at[s], pieces.at[s, 0], own_sem.at[s]) for s in range(streams)]
    for s in range(streams):
        gathers[s].begin()
        keep[s].start()
    for s in range(streams):
        gathers[s].middle()
    for s in range(streams):
        gathers[s].end()
    for s in range(streams):
        keep[s].wait()
        for index in range(4):
            gathers[s].core(index)
    rows_move.wait()
    plane.finish()


def chunk_at(plane, s):
    k = 1 - s // 2
    return s % 2, k + plane.core - 2 * k * plane.core


def chunk_part(plane, qkv, chip, head):
    def part(s, which):
        column = pl.multiple_of((head * 3 + which) * HEAD, HEAD)
        stream, core = chunk_at(plane, s)
        piece = core * (qkv.shape[1] // 2) + chip
        return qkv[stream, piece, :, pl.ds(column, HEAD)]

    return part


def attend_all(plane, qkv, ends_ref, out, clip_count):
    rows = qkv.shape[2]
    heads = qkv.shape[3] // (3 * HEAD)

    def one(index, carry):
        chip, head = index // heads, index % heads
        part = chunk_part(plane, qkv, chip, head)
        column = pl.ds(pl.multiple_of(head * HEAD, HEAD), HEAD)
        for s in range(4):
            start = clip_starts(ends_ref, 0, chip, clip_count, s, rows)
            cs, probs = chunk_probs(part(s, 0), lambda c: part(c, 1), start, s, rows)
            mixed = jnp.zeros((rows, HEAD), f32)
            for c, prob in zip(cs, probs):
                mixed = mixed + nn(prob.astype(bf16), part(c, 2))
            stream, core = chunk_at(plane, s)
            out[stream, core * 4 + chip, :, column] = mixed.astype(bf16)
        return carry

    return one


def attend_back_chip(plane, qkv, grad_mixed, ends_ref, out, key_sum, value_sum, clip_count, chip):
    rows = qkv.shape[2]
    heads = qkv.shape[3] // (3 * HEAD)

    def one(head, carry):
        part = chunk_part(plane, qkv, 0, head)
        column = pl.ds(pl.multiple_of(head * HEAD, HEAD), HEAD)
        key_sum[...] = jnp.zeros_like(key_sum)
        value_sum[...] = jnp.zeros_like(value_sum)

        def put(s, which, value):
            at = pl.ds(pl.multiple_of((head * 3 + which) * HEAD, HEAD), HEAD)
            stream, core = chunk_at(plane, s)
            out[stream, core, :, at] = value.astype(bf16)

        for s in range(4):
            q = part(s, 0)
            stream, core = chunk_at(plane, s)
            g = grad_mixed[stream, core * 4 + chip, :, column]
            start = clip_starts(ends_ref, 0, chip, clip_count, s, rows)
            cs, probs = chunk_probs(q, lambda c: part(c, 1), start, s, rows)
            grad_probs = [nt(g, part(c, 2)) for c in cs]
            inner = functools.reduce(
                jnp.add,
                [jnp.sum(p * v, axis=1, keepdims=True) for p, v in zip(probs, grad_probs)],
            )
            grad_q = jnp.zeros((rows, HEAD), f32)
            for c, prob, grad_prob in zip(cs, probs, grad_probs):
                grad_score = (prob * (grad_prob - inner) * HEAD ** (-0.5)).astype(bf16)
                grad_q = grad_q + nn(grad_score, part(c, 1))
                key_sum[c] += tn(grad_score, q)
                value_sum[c] += tn(prob.astype(bf16), g)
            put(s, 0, grad_q)
        for s in range(4):
            put(s, 1, key_sum[s])
            put(s, 2, value_sum[s])
        return carry

    lax.fori_loop(0, heads, one, 0)


def attention_kernel(
    clip_count, own, rows_in, wide, ends, pieces, qkv, mixed, weight, slots, slot_sems, own_sem, wide_sems, send_sems, recv_sems
):
    plane = Plane(send_sems, recv_sems)
    streams = own.shape[0]
    gathers = [Gather(plane, own.at[s], pieces.at[s]) for s in range(streams)]
    keep = [pltpu.make_async_copy(own.at[s], pieces.at[s, 0], own_sem.at[s]) for s in range(streams)]
    traded, kept = [], []
    for head in range(2):
        for which in range(3):
            column = pl.ds((head * 3 + which) * HEAD, HEAD)
            here = weight.at[:, plane.core, :, column]
            traded.append(plane.send(wide.at[2 * (1 - plane.core) + head, which], here, "c"))
            copy = pltpu.make_async_copy(
                wide.at[2 * plane.core + head, which], here, wide_sems.at[len(kept)]
            )
            copy.start()
            kept.append(copy)
    for s in range(streams):
        gathers[s].begin()
        keep[s].start()
    total = weight.shape[3]
    feed = Feed(
        lambda at: rows_in.at[at[0], at[1]],
        slots,
        slot_sems,
        [(s, p) for s in range(streams) for p in range(8)],
    )
    feed.start(0)

    def project(s):
        for p in range(8):
            feed.start(s * 8 + p + 1)
            piece = feed.get(s * 8 + p)

            def tile(at):
                columns = weight[:, :, :, at].reshape(width, -1)
                qkv[s, p, :, at] = nn(piece[...], columns).astype(bf16)

            tiles(total, N_TILE, tile)

    for copy in traded:
        copy.wait_recv()
    for copy in kept:
        copy.wait()
    width = own.shape[2]

    attend = attend_all(plane, qkv, ends, mixed, clip_count)
    heads = total // (3 * HEAD)
    project(0)
    project(1)
    gathers[0].middle()
    lax.fori_loop(0, heads, attend, 0)
    gathers[0].end()
    lax.fori_loop(heads, 2 * heads, attend, 0)
    gathers[1].middle()
    lax.fori_loop(2 * heads, 3 * heads, attend, 0)
    gathers[1].end()
    lax.fori_loop(3 * heads, 4 * heads, attend, 0)
    for s in range(streams):
        keep[s].wait()
        for index in range(4):
            gathers[s].core(index)
    plane.finish()


def reduce_scratch(streams, rows, width):
    return [
        pltpu.VMEM((streams, 8, rows, width), bf16),
        pltpu.VMEM((streams, 4, rows, width), bf16),
        pltpu.VMEM((streams, 3, rows // 2, width), bf16),
        pltpu.VMEM((streams, 3, rows // 2, width), bf16),
    ]


def project_kernel(
    mixed, wide, out, weight, parts, from_core, from_x, from_y, wide_sems, send_sems, recv_sems
):
    plane = Plane(send_sems, recv_sems)
    streams = mixed.shape[0]
    width = weight.shape[1]
    depth = wide.shape[3]
    traded, kept = [], []
    for head in range(2):
        for chip in range(4):
            column = pl.ds(pl.multiple_of((2 * chip + plane.core) * depth, depth), depth)
            here = weight.at[pl.ds(head * HEAD, HEAD), column]
            traded.append(plane.send(wide.at[2 * (1 - plane.core) + head, chip], here, "c"))
            copy = pltpu.make_async_copy(
                wide.at[2 * plane.core + head, chip], here, wide_sems.at[len(kept)]
            )
            copy.start()
            kept.append(copy)
    for copy in traded:
        copy.wait_recv()
    for copy in kept:
        copy.wait()
    sums = [
        Reduce(plane, parts.at[s], from_core.at[s], from_x.at[s], from_y.at[s])
        for s in range(streams)
    ]

    for s in range(streams):
        for m in ORDER:

            def other(at):
                parts[s, 4 + m, :, at] = nn(mixed[s, 4 + m], weight[:, at]).astype(bf16)

            tiles(width, N_TILE, other)
            sums[s].give(m)
        for m in ORDER:
            sums[s].take(m)

            def chip(at):
                here = nn(mixed[s, m], weight[:, at])
                parts[s, m, :, at] = (here + from_core[s, m, :, at].astype(f32)).astype(bf16)

            tiles(width, N_TILE, chip)
            sums[s].chip_done(m)
        if s > 0:
            sums[s - 1].late()
    sums[streams - 1].late()
    for s in range(streams):
        sums[s].total(out.at[s])
    plane.finish()


def gelu_pair(v):
    cubic = 0.044715 * (v * v) * v
    inner = (2.0 / np.pi) ** 0.5 * (v + cubic)
    th = jnp.tanh(inner)
    half = 0.5 * (1.0 + th)
    slope = (2.0 / np.pi) ** 0.5 * (1.0 + 3.0 * 0.044715 * (v * v))
    return v * half, half + 0.5 * v * (1.0 - th * th) * slope


def lay_out(wide, flat, sems):
    copies = []
    part = wide.shape[2]
    for plane in range(wide.shape[0]):
        copy = pltpu.make_async_copy(
            wide.at[plane], flat.at[:, pl.ds(plane * part, part)], sems.at[plane]
        )
        copy.start()
        copies.append(copy)
    return copies


def mlp_kernel(
    own, up_wide, down_w, grads, pieces, slope_out, down_grad, out,
    parts, from_core, from_x, from_y, up_w, slots, act, slope, total, grad_slots,
    up_sems, slot_sems, keep_sems, own_sem, grad_sems, send_sems, recv_sems,
):
    plane = Plane(send_sems, recv_sems)
    streams, rows, width = own.shape
    hidden = up_w.shape[1]
    up_copies = lay_out(up_wide, up_w, up_sems)
    gathers = [Gather(plane, own.at[s], pieces.at[s]) for s in range(streams)]
    sums = [
        Reduce(plane, parts.at[s], from_core.at[s], from_x.at[s], from_y.at[s])
        for s in range(streams)
    ]
    keep = [pltpu.make_async_copy(own.at[s], pieces.at[s, 0], own_sem.at[s]) for s in range(streams)]
    stores = []
    loads = [0]

    def load(s, p):
        slot = loads[0] % 2
        loads[0] += 1
        source = own.at[s] if p == 0 else pieces.at[s, p]
        copy = pltpu.make_async_copy(source, slots.at[slot], slot_sems.at[slot])
        copy.start()
        return copy, slots.at[slot]

    def work(s, p, loaded):
        copy, piece = loaded
        slot = len(stores) % 2
        index = len(stores)
        feed.start(index + 1)
        if index >= 2:
            stores[index - 2].wait()
        copy.wait()

        def up(at):
            value, grad = gelu_pair(nn(piece[...], up_w[:, at]))
            act[slot, :, at] = value.astype(bf16)
            slope[slot, :, at] = grad.astype(bf16)

        tiles(hidden, N_TILE, up)
        store = pltpu.make_async_copy(slope.at[slot], slope_out.at[s, p], keep_sems.at[slot])
        store.start()
        stores.append(store)
        if p < 4:
            sums[s].take(p)

        def down(at):
            here = nn(act[slot], down_w[:, at])
            if p < 4:
                here = here + from_core[s, p, :, at].astype(f32)
            parts[s, p, :, at] = here.astype(bf16)

        tiles(width, N_TILE, down)
        if p >= 4:
            sums[s].give(p - 4)
        else:
            sums[s].chip_done(p)
        grad = feed.get(index)

        def weigh(at):
            term = tn(act[slot], grad[:, at])
            total[:, at] = term if index == 0 else total[:, at] + term

        tiles(width, 512, weigh)

    order = [
        (s, p)
        for s in range(streams)
        for m in ((0, 1, 2, 3) if s == 0 else (0, 1, 3, 2))
        for p in (4 + m, m)
    ]
    feed = Feed(lambda at: grads.at[at[0], at[1]], grad_slots, grad_sems, order)
    feed.start(0)
    for s in range(streams):
        keep[s].start()
    gathers[0].begin()

    def pair_up(s, m):
        gathers[s].core(m)
        work(s, 4 + m, load(s, 4 + m))
        work(s, m, load(s, m))

    for s in range(streams):
        if s == 0:
            for copy in up_copies:
                copy.wait()
        pair_up(s, 0)
        gathers[s].middle()
        if s + 1 < streams:
            gathers[s + 1].begin()
        if s > 0:
            sums[s - 1].late()
        pair_up(s, 1)
        gathers[s].end()
        if s == 0:
            pair_up(s, 2)
        pair_up(s, 3)
        if s > 0:
            sums[s].late_x()
            pair_up(s, 2)
            sums[s].late_y()
    for s in range(streams):
        sums[s].total(out.at[s])
        keep[s].wait()
    for store in stores[-2:]:
        store.wait()
    stores = []
    for index in range(hidden // rows):
        if index >= 2:
            stores[index - 2].wait()
        here = pl.ds(index * rows, rows)
        slots[index % 2] = total[here].astype(bf16)
        store = pltpu.make_async_copy(
            slots.at[index % 2], down_grad.at[here], keep_sems.at[index % 2]
        )
        store.start()
        stores.append(store)
    for store in stores[-2:]:
        store.wait()
    plane.finish()


def mlp_back_kernel(
    grads, slope_in, up_wide, down_w, rows_in, pre_out, out, rows_out,
    parts, from_core, from_x, from_y, up_w, slots, slopes, pre,
    up_sems, slot_sems, slope_sems, keep_sems, row_sems, send_sems, recv_sems,
):
    outward, inward = row_places()
    plane = Plane(send_sems, recv_sems, outward + inward)
    rows_move = RowMove(rows_in, rows_out, row_sems)
    rows_move.back()
    streams, _, rows, width = grads.shape
    hidden = up_w.shape[1]
    up_copies = lay_out(up_wide, up_w, up_sems)
    sums = [
        Reduce(plane, parts.at[s], from_core.at[s], from_x.at[s], from_y.at[s])
        for s in range(streams)
    ]
    order = [(s, p) for s in range(streams) for m in ORDER for p in (4 + m, m)]
    feed = Feed(lambda at: grads.at[at[0], at[1]], slots, slot_sems, order)
    feed_slope = Feed(lambda at: slope_in.at[at[0], at[1]], slopes, slope_sems, order)
    feed.start(0)
    feed_slope.start(0)
    stores = []
    for index, (s, p) in enumerate(order):
        feed.start(index + 1)
        feed_slope.start(index + 1)
        grad = feed.get(index)
        slope = feed_slope.get(index)
        slot = index % 2
        if index >= 2:
            stores[index - 2].wait()

        def back(at):
            value = nt(grad[...], down_w[at]) * slope[:, at].astype(f32)
            pre[slot, :, at] = value.astype(bf16)

        tiles(hidden, N_TILE, back)
        if index == 0:
            for copy in up_copies:
                copy.wait()
        store = pltpu.make_async_copy(pre.at[slot], pre_out.at[s, p], keep_sems.at[slot])
        store.start()
        stores.append(store)
        if p < 4:
            sums[s].take(p)

        def through(at):
            here = nt(pre[slot], up_w[at])
            if p < 4:
                here = here + from_core[s, p, :, at].astype(f32)
            parts[s, p, :, at] = here.astype(bf16)

        tiles(width, N_TILE, through)
        if p >= 4:
            sums[s].give(p - 4)
        else:
            sums[s].chip_done(p)
            if p == 1:
                sums[s].late_x()
            if p == 2:
                sums[s].late_y()
    for s in range(streams):
        sums[s].total(out.at[s])
    for store in stores[-2:]:
        store.wait()
    rows_move.wait()
    plane.finish()


def attention_back_kernel(
    clip_count, own, qkv, mixed, features, qkv_w, out_w, ends,
    pieces, qkv_grad, out_grad, out,
    parts, from_core, from_x, from_y, slots, mixed_slots, grad_mixed, qkv_chip, grad_chip, key_sum, value_sum,
    qkv_sum, out_sum, slot_sems, mixed_sems, chip_sems, own_sem, send_sems, recv_sems,
):
    plane = Plane(send_sems, recv_sems)
    streams, rows, width = own.shape
    gathers = [Gather(plane, own.at[s], pieces.at[s]) for s in range(streams)]
    sums = [
        Reduce(plane, parts.at[s], from_core.at[s], from_x.at[s], from_y.at[s])
        for s in range(streams)
    ]
    keep = [pltpu.make_async_copy(own.at[s], pieces.at[s, 0], own_sem.at[s]) for s in range(streams)]
    order = [(s, p) for s in range(streams) for p in (0, 4, 1, 5, 2, 6, 3, 7)]
    feed_mixed = Feed(lambda at: mixed.at[at[0], at[1]], mixed_slots, mixed_sems, order)
    feed_mixed.start(0)
    done = [0]

    def mix(s, p):
        index = done[0]
        done[0] += 1
        feed_mixed.start(index + 1)
        slot = index % 2
        source = own.at[s] if p == 0 else pieces.at[s, p]
        copy = pltpu.make_async_copy(source, slots.at[slot], slot_sems.at[slot])
        copy.start()
        left = feed_mixed.get(index)
        copy.wait()
        grad_mixed[s, p] = nt(slots[slot], out_w[...]).astype(bf16)

        def weigh(at):
            term = tn(left[...], slots[slot, :, at])
            out_sum[:, at] = term if index == 0 else out_sum[:, at] + term

        tiles(width, N_TILE, weigh)

    def load_chip(m):
        copies = [
            pltpu.make_async_copy(
                qkv.at[s, core * 4 + m], qkv_chip.at[s, core], chip_sems.at[s * 2 + core]
            )
            for s in range(streams)
            for core in range(2)
        ]
        for copy in copies:
            copy.start()
        return copies

    for s in range(streams):
        keep[s].start()
    gathers[0].begin()
    for s in range(streams):
        gather = gathers[s]
        mix(s, 0)
        gather.core(0)
        mix(s, 4)
        gather.middle()
        if s + 1 < streams:
            gathers[s + 1].begin()
        for index in (1, 2):
            mix(s, index)
            gather.core(index)
            mix(s, 4 + index)
        gather.end()
        mix(s, 3)
        gather.core(3)
        mix(s, 7)
    for index in range(out_sum.shape[0] // rows):
        here = pl.ds(index * rows, rows)
        slots[0] = out_sum[here].astype(bf16)
        out_store = pltpu.make_async_copy(slots.at[0], out_grad.at[here], slot_sems.at[0])
        out_store.start()
        out_store.wait()
    feed = Feed(
        lambda at: features.at[at[0], at[1]],
        slots,
        slot_sems,
        [(s, p) for m in ORDER for s in range(streams) for p in (4 + m, m)],
    )
    feed.start(0)
    for copy in load_chip(ORDER[0]):
        copy.wait()
    for place, m in enumerate(ORDER):
        attend_back_chip(
            plane, qkv_chip, grad_mixed, ends, grad_chip, key_sum, value_sum, clip_count, m
        )
        coming = load_chip(ORDER[place + 1]) if place < 3 else []
        for s in range(streams):

            def other(at):
                parts[s, 4 + m, :, at] = nt(grad_chip[s, 1], qkv_w[at]).astype(bf16)

            tiles(width, N_TILE, other)
            sums[s].give(m)
        for s in range(streams):
            sums[s].take(m)

            def chip(at):
                here = nt(grad_chip[s, 0], qkv_w[at])
                parts[s, m, :, at] = (here + from_core[s, m, :, at].astype(f32)).astype(bf16)

            tiles(width, N_TILE, chip)
            sums[s].chip_done(m)
        for s in range(streams):
            for core in (1, 0):
                index = place * 2 * streams + 2 * s + 1 - core
                feed.start(index + 1)
                left = feed.get(index)

                def weigh(at):
                    term = tn(left[:, at], grad_chip[s, core])
                    qkv_sum[at] = term if index == 0 else qkv_sum[at] + term

                tiles(width, 512, weigh)
        for s in range(streams):
            if m == 1:
                sums[s].late_x()
            if m == 2:
                sums[s].late_y()
        for copy in coming:
            copy.wait()
    stores = []
    for index in range(width // rows):
        if index >= 4:
            stores[index - 4].wait()
        here = pl.ds(index * rows, rows)
        stage = grad_chip.at[index // 2 % 2, index % 2]
        stage[...] = qkv_sum[here].astype(bf16)
        store = pltpu.make_async_copy(stage, qkv_grad.at[here], chip_sems.at[index % 4])
        store.start()
        stores.append(store)
    for s in range(streams):
        sums[s].total(out.at[s])
        keep[s].wait()
    for store in stores[-4:]:
        store.wait()
    plane.finish()


def end_kernel(
    rows_in, qkv_grad, out_grad, gains,
    rows_out, qkv_out, out_out, gains_out,
    qkv_part, out_part, qkv_come, out_come, gain_come, gain_sum, gain_all,
    local_sems, row_sems, send_sems, recv_sems,
):
    me, z = lax.axis_index("dp"), lax.axis_index("tensor")
    chip, core = me // 2, me % 2
    depth = qkv_grad.shape[2]
    outward, inward = row_places()
    peers = [lax.rem(me + j, 8) for j in range(1, 8)]
    planes = [lax.rem(z + j, 4) for j in range(1, 4)]
    barrier = pltpu.get_barrier_semaphore()
    for peer in peers:
        pl.semaphore_signal(barrier, inc=1, device_id={"dp": peer}, device_id_type=MESH)
    for plane in planes:
        pl.semaphore_signal(barrier, inc=1, device_id={"tensor": plane}, device_id_type=MESH)
    for place in outward + inward:
        pl.semaphore_signal(barrier, inc=1, device_id=at_device(place), device_id_type=MESH)
    pl.semaphore_wait(barrier, 14)
    copies, locals_ = [], []

    def send(src, dst, device):
        copy = pltpu.make_async_remote_copy(
            src_ref=src,
            dst_ref=dst,
            send_sem=send_sems.at[len(copies)],
            recv_sem=recv_sems.at[len(copies)],
            device_id=device,
            device_id_type=MESH,
        )
        copy.start()
        copies.append(copy)
        return copy

    def keep(src, dst):
        copy = pltpu.make_async_copy(src, dst, local_sems.at[len(locals_)])
        copy.start()
        locals_.append(copy)

    def block(index, size):
        return pl.ds(pl.multiple_of(index * size, size), size)

    other = {"dp": me + 1 - 2 * core}
    traded = []
    for head in range(2):
        mine = 2 * core + head
        for which in range(3):
            column = pl.ds((head * 3 + which) * HEAD, HEAD)
            traded.append(
                send(qkv_grad.at[:, 1 - core, :, column], qkv_part.at[mine, which], other)
            )
            keep(qkv_grad.at[:, core, :, column], qkv_part.at[mine, which])
        here = pl.ds(head * HEAD, HEAD)
        for c in range(4):
            theirs = pl.ds(pl.multiple_of((2 * c + 1 - core) * depth, depth), depth)
            own = pl.ds(pl.multiple_of((2 * c + core) * depth, depth), depth)
            traded.append(send(out_grad.at[here, theirs], out_part.at[mine, c], other))
            keep(out_grad.at[here, own], out_part.at[mine, c])
    gain_first = [send(gains.at[peer], gain_come.at[me], {"dp": peer}) for peer in peers]
    gain_come[me] = gains[me]
    for copy in traded:
        copy.wait_recv()
    for copy in locals_:
        copy.wait()
    after = {"tensor": planes[0]}
    for step in range(3):
        part = lax.rem(z + 3 - step, 4)
        ring = [
            send(qkv_part.at[part], qkv_come.at[step], after),
            send(out_part.at[part], out_come.at[step], after),
        ]
        if step == 0:
            rows_move = RowMove(rows_in, rows_out, row_sems)
            rows_move.back()
            for copy in gain_first:
                copy.wait_recv()
            gain_sum[...] = functools.reduce(jnp.add, [gain_come[i] for i in range(8)])
            gain_second = [
                send(gain_sum, gain_all.at[z], {"tensor": plane}) for plane in planes
            ]
            gain_all[z] = gain_sum[...]
        for copy in ring:
            copy.wait_recv()
        part = lax.rem(z + 2 - step, 4) if step < 2 else z
        for which in range(3):
            for c in range(4):
                here = qkv_part.at[part, which, c]
                here[...] = (
                    here[...].astype(f32) + qkv_come[step, which, c].astype(f32)
                ).astype(bf16)
        for c in range(4):
            here = out_part.at[part, c]
            here[...] = (here[...].astype(f32) + out_come[step, c].astype(f32)).astype(bf16)
    last = []
    for j in range(1, 4):
        to = lax.rem(chip + j, 4)
        device = {"dp": 2 * to + core}
        last.append(send(qkv_part.at[z, :, to], qkv_out.at[:, :, block(chip, HEAD)], device))
        last.append(send(out_part.at[z, to], out_out.at[block(chip, HEAD)], device))
    start = len(locals_)
    keep(qkv_part.at[z, :, chip], qkv_out.at[:, :, block(chip, HEAD)])
    keep(out_part.at[z, chip], out_out.at[block(chip, HEAD)])
    for copy in gain_second:
        copy.wait_recv()
    gains_out[...] = functools.reduce(jnp.add, [gain_all[i] for i in range(4)])
    for copy in last:
        copy.wait_recv()
    for copy in locals_[start:]:
        copy.wait()
    rows_move.wait()
    for copy in copies:
        copy.wait_send()


def on_device(
    block_input,
    clip_lengths,
    norm1_gain,
    w_query,
    w_key,
    w_value,
    w_out,
    norm2_gain,
    w_up,
    w_down,
    out_cotangent,
):
    streams, rows, width = block_input.shape
    planes = lax.axis_size("tensor")
    lanes = lax.axis_size("dp")
    clip_count = clip_lengths.shape[1]
    own = lax.axis_index("dp")
    own_plane = lax.axis_index("tensor")
    own_core = own % 2
    heads = w_query.shape[1] * planes // (HEAD * lanes)
    depth = w_query.shape[0]
    hidden_part = w_up.shape[1] // lanes
    hidden_own = planes * hidden_part
    inner = heads * HEAD

    small = jnp.zeros((8, depth), f32)
    small = small.at[0].set(norm1_gain.astype(f32)).at[1].set(norm2_gain.astype(f32))
    small = small.at[2, : streams * clip_count].set(clip_lengths.reshape(-1).astype(f32))
    tokens_in, qkv_part, out_part, up_part, down_part, small = plane_call(
        start_kernel,
        "start",
        6,
        [
            jax.ShapeDtypeStruct(block_input.shape, bf16),
            jax.ShapeDtypeStruct((3, 4, depth, HEAD), bf16),
            jax.ShapeDtypeStruct((4, HEAD, depth), bf16),
            jax.ShapeDtypeStruct((width, hidden_part), bf16),
            jax.ShapeDtypeStruct((hidden_part, width), bf16),
            jax.ShapeDtypeStruct((lanes, 8, depth), f32),
        ],
        ["any"] * 8,
        ["any"] * 6,
        [pltpu.SemaphoreType.DMA((7,)), pltpu.SemaphoreType.DMA((2, 2))],
        33,
        0,
        (block_input, w_query, w_key, w_value, w_out, w_up, w_down, small),
    )
    gain_one = small[:, 0].reshape(-1)
    gain_two = small[:, 1].reshape(-1)
    lengths = small[:, 2, : streams * clip_count].reshape(-1, clip_count).astype(jnp.int32)

    qkv_wide = lax.all_gather(qkv_part, "tensor", axis=0, tiled=False)
    out_wide = lax.all_gather(out_part, "tensor", axis=0, tiled=False)
    up_wide = lax.all_gather(up_part, "tensor", axis=0, tiled=False)
    down_w = lax.all_gather(down_part, "tensor", axis=0, tiled=True)

    all_ends = jnp.cumsum(lengths, axis=1)
    buffers = 4 * (own // 2 ^ jnp.arange(4, dtype=jnp.int32)) + own_plane
    ends = jnp.take(all_ends, buffers, axis=0)
    chunks = 2 * (1 - own_core) + jnp.arange(streams, dtype=jnp.int32)
    places = chunks[:, None] * rows + jnp.arange(rows, dtype=jnp.int32)
    valid = (places < ends[0, -1]).astype(f32)
    ends = ends.reshape(-1).astype(jnp.int32)

    pieces = jax.ShapeDtypeStruct((streams, 8, rows, width), bf16)
    sums = jax.ShapeDtypeStruct((streams, rows, width), f32)
    row_count = streams * 8 * rows
    slots = pltpu.VMEM((2, rows, width), bf16)
    dma = pltpu.SemaphoreType.DMA

    def piece_shape(columns):
        return jax.ShapeDtypeStruct((streams, 8, rows, columns), bf16)

    tokens = tokens_in.astype(f32)
    normed_one, unit_one, inverse_one = norm_rows(tokens, gain_one)
    features_one, cotangent = plane_call(
        gather_kernel,
        "gather",
        0,
        [pieces, jax.ShapeDtypeStruct(block_input.shape, bf16)],
        ["any", "any"],
        ["any", "any"],
        [dma((streams,)), dma((2, 2))],
        8 * streams,
        0,
        (normed_one.astype(bf16), out_cotangent),
    )
    grad_out = cotangent.astype(f32) * valid[:, :, None]
    grad_branch, qkv, mixed, qkv_w = plane_call(
        functools.partial(attention_kernel, clip_count),
        "attention",
        1,
        [
            pieces,
            piece_shape(3 * inner),
            piece_shape(inner),
            jax.ShapeDtypeStruct((4, 2, depth, 3 * inner), bf16),
        ],
        ["any", "any", "any", "smem"],
        ["any", "vmem", "vmem", "vmem"],
        [slots, dma((2,)), dma((streams,)), dma((6,))],
        8 * streams + 6,
        2 * row_count * width * 3 * inner,
        (grad_out.astype(bf16), features_one, qkv_wide, ends),
    )
    attn_sum, out_w = plane_call(
        project_kernel,
        "project",
        2,
        [sums, jax.ShapeDtypeStruct((inner, width), bf16)],
        ["vmem", "any"],
        ["vmem", "vmem"],
        reduce_scratch(streams, rows, width) + [dma((8,))],
        10 * streams + 8,
        2 * row_count * width * inner,
        (mixed, out_wide),
    )
    hidden = tokens + attn_sum
    normed_two, unit_two, inverse_two = norm_rows(hidden, gain_two)
    part = pltpu.VMEM((2, rows, hidden_own), bf16)
    up_flat = pltpu.VMEM((width, hidden_own), bf16)
    features_two, slope, down_dot, mlp_sum = plane_call(
        mlp_kernel,
        "mlp",
        3,
        [
            pieces,
            piece_shape(hidden_own),
            jax.ShapeDtypeStruct((hidden_own, width), bf16),
            sums,
        ],
        ["any", "any", "vmem", "any"],
        ["any", "any", "any", "vmem"],
        reduce_scratch(streams, rows, width)
        + [up_flat, slots, part, part, pltpu.VMEM((hidden_own, width), f32), slots]
        + [dma((planes,)), dma((2,)), dma((2,)), dma((streams,)), dma((2,))],
        18 * streams,
        6 * row_count * width * hidden_own,
        (normed_two.astype(bf16), up_wide, down_w, grad_branch),
    )

    grad_pre, back_sum, output = plane_call(
        mlp_back_kernel,
        "mlp_back",
        4,
        [piece_shape(hidden_own), sums, jax.ShapeDtypeStruct(block_input.shape, bf16)],
        ["any", "any", "any", "vmem", "any"],
        ["any", "vmem", "any"],
        reduce_scratch(streams, rows, width)
        + [up_flat, slots, part, part, dma((planes,)), dma((2,)), dma((2,)), dma((2,)), dma((2, 2))],
        10 * streams,
        4 * row_count * width * hidden_own,
        (grad_branch, slope, up_wide, down_w, (hidden + mlp_sum).astype(bf16)),
    )
    from_two, gain_two_grad = norm_back(back_sum, unit_two, inverse_two, gain_two)
    grad_hidden = grad_out + from_two

    def grad_dot(left, right):
        return lax.dot_general(
            left.reshape(row_count, -1),
            right.reshape(row_count, -1),
            (((0,), (0,)), ((), ())),
            preferred_element_type=f32,
        ).astype(bf16)

    up_dot = grad_dot(features_two, grad_pre)
    grad_attn_own, up_dot = lax.optimization_barrier((grad_hidden.astype(bf16), up_dot))
    down_sum = lax.psum_scatter(down_dot, "tensor", scatter_dimension=0, tiled=True)
    up_sum = up_dot.reshape(width, planes, hidden_part).swapaxes(0, 1)
    up_sum = lax.psum_scatter(up_sum, "tensor", scatter_dimension=0, tiled=False)

    chunk = pltpu.VMEM((4, rows, HEAD), f32)
    chip_rows = pltpu.VMEM((streams, 2, rows, 3 * inner), bf16)
    _, qkv_dot, out_dot, input_sum = plane_call(
        functools.partial(attention_back_kernel, clip_count),
        "attention_back",
        5,
        [
            pieces,
            jax.ShapeDtypeStruct((width, 3 * inner), bf16),
            jax.ShapeDtypeStruct((inner, width), bf16),
            sums,
        ],
        ["any", "any", "any", "any", "vmem", "vmem", "smem"],
        ["any", "any", "any", "vmem"],
        reduce_scratch(streams, rows, width)
        + [slots, pltpu.VMEM((2, rows, inner), bf16)]
        + [pltpu.VMEM((streams, 8, rows, inner), bf16), chip_rows, chip_rows, chunk, chunk]
        + [pltpu.VMEM((width, 3 * inner), f32), pltpu.VMEM((inner, width), f32)]
        + [dma((2,)), dma((2,)), dma((4,)), dma((streams,))],
        18 * streams,
        2 * row_count * width * 8 * inner,
        (
            grad_attn_own,
            qkv,
            mixed,
            features_one,
            qkv_w.reshape(width, 3 * inner),
            out_w,
            ends,
        ),
    )
    input_sum, down_sum, up_sum = lax.optimization_barrier((input_sum, down_sum, up_sum))
    down_sum = down_sum.reshape(hidden_part, lanes, depth).swapaxes(0, 1)
    down_grad = lax.all_to_all(down_sum, "dp", 0, 0, tiled=True).reshape(-1, depth).astype(f32)
    up_grad = lax.all_to_all(up_sum.reshape(lanes, depth, hidden_part), "dp", 0, 0, tiled=True)
    up_grad = up_grad.swapaxes(0, 1).reshape(depth, -1).astype(f32)
    from_one, gain_one_grad = norm_back(input_sum, unit_one, inverse_one, gain_one)
    gains = jnp.stack([gain_one_grad.sum(0), gain_two_grad.sum(0)]).reshape(2, lanes, depth)
    gains = jnp.zeros((lanes, 8, depth), f32).at[:, :2].set(gains.swapaxes(0, 1))
    small_sum = pltpu.VMEM((8, depth), f32)
    input_grad, qkv_grad, out_grad, gains = plane_call(
        end_kernel,
        "end",
        7,
        [
            jax.ShapeDtypeStruct(block_input.shape, bf16),
            jax.ShapeDtypeStruct((3, depth, 4 * HEAD), bf16),
            jax.ShapeDtypeStruct((4 * HEAD, depth), bf16),
            jax.ShapeDtypeStruct((8, depth), f32),
        ],
        ["any", "any", "any", "vmem"],
        ["any", "any", "any", "vmem"],
        [
            pltpu.VMEM((4, 3, 4, depth, HEAD), bf16),
            pltpu.VMEM((4, 4, HEAD, depth), bf16),
            pltpu.VMEM((3, 3, 4, depth, HEAD), bf16),
            pltpu.VMEM((3, 4, HEAD, depth), bf16),
            pltpu.VMEM((8, 8, depth), f32),
            small_sum,
            pltpu.VMEM((4, 8, depth), f32),
            dma((16,)),
            dma((2, 2)),
        ],
        36,
        0,
        (
            (grad_hidden + from_one).astype(bf16),
            qkv_dot.reshape(4, 2, depth, 3 * inner),
            out_dot,
            gains,
        ),
    )
    qkv_grad = qkv_grad.astype(f32)
    return (
        output,
        input_grad.astype(f32),
        gains[0],
        qkv_grad[0],
        qkv_grad[1],
        qkv_grad[2],
        out_grad.astype(f32),
        gains[1],
        up_grad,
        down_grad,
    )


def solution(mesh):
    in_specs = (
        P("dp", "tensor", None),
        P("dp", None),
        P("dp"),
        P("dp", "tensor"),
        P("dp", "tensor"),
        P("dp", "tensor"),
        P("tensor", "dp"),
        P("dp"),
        P("dp", "tensor"),
        P("tensor", "dp"),
        P("dp", "tensor", None),
    )
    out_specs = (
        P("dp", "tensor", None),
        P("dp", "tensor", None),
        P("dp"),
        P("dp", "tensor"),
        P("dp", "tensor"),
        P("dp", "tensor"),
        P("tensor", "dp"),
        P("dp"),
        P("dp", "tensor"),
        P("tensor", "dp"),
    )
    own_form = mesh.shape["dp"] == 8 and mesh.shape["tensor"] == 4
    return jax.shard_map(
        on_device if own_form else on_device_any, mesh=mesh, in_specs=in_specs, out_specs=out_specs, check_vma=False
    )
```

```python
import functools

import jax
import jax.numpy as jnp
import numpy as np
from jax import lax
from jax.experimental import pallas as pl
from jax.experimental.pallas import tpu as pltpu
from jax.sharding import PartitionSpec as P

HEAD = 128
LONGEST = 512
epsilon = 1e-05
masked_fill = -1000000000.0
bf16 = jnp.bfloat16
f32 = jnp.float32


def norm_rows(tokens, gain):
    centred = tokens - jnp.mean(tokens, axis=-1, keepdims=True)
    inverse = lax.rsqrt(jnp.mean(centred * centred, axis=-1, keepdims=True) + epsilon)
    unit_rows = centred * inverse
    return (unit_rows * gain, unit_rows, inverse)


def norm_back(grad_normed, unit_rows, inverse, gain):
    scaled = grad_normed * gain
    inner_sum = (
        scaled
        - jnp.mean(scaled, axis=-1, keepdims=True)
        - unit_rows * jnp.mean(scaled * unit_rows, axis=-1, keepdims=True)
    )
    return (inverse * inner_sum, jnp.sum(grad_normed * unit_rows, axis=0))


def gelu_tanh(values):
    return jax.nn.gelu(values, approximate=True)


def masked_scores(q_rows, keys_heads, segment, offset, block_rows):
    slot_count = keys_heads.shape[0]
    raw_scores = jnp.einsum(
        "qhd,khd->hqk", q_rows, keys_heads, preferred_element_type=jnp.float32
    ) * HEAD ** (-0.5)
    q_segment = lax.dynamic_slice_in_dim(segment, offset, block_rows, 0)
    q_place = offset + jnp.arange(block_rows, dtype=jnp.int32)
    places = jnp.arange(slot_count, dtype=jnp.int32)
    allowed = (q_segment[:, None] == segment[None, :]) & (places[None, :] <= q_place[:, None])
    return jnp.where(allowed[None], raw_scores, masked_fill)


def attend(query, key, value, segment, block_rows):
    slot_count = query.shape[0]
    head_count = query.shape[1] // HEAD
    keys_heads = key.reshape(slot_count, head_count, HEAD)
    values_heads = value.reshape(slot_count, head_count, HEAD)

    def one_block(block_index):
        offset = block_index * block_rows
        q_rows = lax.dynamic_slice_in_dim(query, offset, block_rows, 0).reshape(
            block_rows, head_count, HEAD
        )
        scores = masked_scores(q_rows, keys_heads, segment, offset, block_rows)
        highest = jnp.max(scores, axis=-1, keepdims=True)
        shifted = jnp.exp(scores - highest)
        totals = jnp.sum(shifted, axis=-1, keepdims=True)
        weights = (shifted / totals).astype(jnp.bfloat16)
        mixed_rows = jnp.einsum(
            "hqk,khd->qhd", weights, values_heads, preferred_element_type=jnp.float32
        )
        return (
            mixed_rows.reshape(block_rows, head_count * HEAD).astype(jnp.bfloat16),
            (highest + jnp.log(totals))[..., 0],
        )

    mixed_rows, log_norm = lax.map(one_block, jnp.arange(slot_count // block_rows, dtype=jnp.int32))
    return (mixed_rows.reshape(slot_count, head_count * HEAD), log_norm)


def attend_back(query, key, value, segment, log_norm, grad_mixed, block_rows):
    slot_count = query.shape[0]
    head_count = query.shape[1] // HEAD
    keys_heads = key.reshape(slot_count, head_count, HEAD)
    values_heads = value.reshape(slot_count, head_count, HEAD)

    def one_block(carried, block_index):
        grad_keys, grad_values = carried
        offset = block_index * block_rows
        q_rows = lax.dynamic_slice_in_dim(query, offset, block_rows, 0).reshape(
            block_rows, head_count, HEAD
        )
        g_rows = lax.dynamic_slice_in_dim(grad_mixed, offset, block_rows, 0).reshape(
            block_rows, head_count, HEAD
        )
        scores = masked_scores(q_rows, keys_heads, segment, offset, block_rows)
        prob_rows = jnp.exp(scores - log_norm[block_index][..., None])
        grad_values = grad_values + jnp.einsum(
            "hqk,qhd->khd",
            prob_rows.astype(jnp.bfloat16),
            g_rows,
            preferred_element_type=jnp.float32,
        )
        grad_probs = jnp.einsum(
            "qhd,khd->hqk", g_rows, values_heads, preferred_element_type=jnp.float32
        )
        inner_sum = jnp.sum(prob_rows * grad_probs, axis=-1, keepdims=True)
        grad_scores = (prob_rows * (grad_probs - inner_sum) * HEAD ** (-0.5)).astype(jnp.bfloat16)
        grad_query = jnp.einsum(
            "hqk,khd->qhd", grad_scores, keys_heads, preferred_element_type=jnp.float32
        )
        grad_keys = grad_keys + jnp.einsum(
            "hqk,qhd->khd", grad_scores, q_rows, preferred_element_type=jnp.float32
        )
        return (
            (grad_keys, grad_values),
            grad_query.reshape(block_rows, head_count * HEAD).astype(jnp.bfloat16),
        )

    zero_state = jnp.zeros((slot_count, head_count, HEAD), jnp.float32)
    (grad_keys, grad_values), grad_query = lax.scan(
        one_block, (zero_state, zero_state), jnp.arange(slot_count // block_rows, dtype=jnp.int32)
    )
    return (
        grad_query.reshape(slot_count, head_count * HEAD),
        grad_keys.reshape(slot_count, head_count * HEAD).astype(jnp.bfloat16),
        grad_values.reshape(slot_count, head_count * HEAD).astype(jnp.bfloat16),
    )


def on_device_any(
    block_input,
    clip_lengths,
    norm1_gain,
    w_query,
    w_key,
    w_value,
    w_out,
    norm2_gain,
    w_up,
    w_down,
    out_cotangent,
):
    micro_count = block_input.shape[0]
    local_rows = block_input.shape[1]
    tensor_size = lax.axis_size("tensor")
    slot_count = local_rows * tensor_size
    block_rows = min(512, slot_count)
    clip_count = clip_lengths.shape[1]
    row_offset = lax.axis_index("tensor") * local_rows
    places = jnp.arange(slot_count, dtype=jnp.int32)

    def fetch_weights():
        return (
            lax.all_gather(norm1_gain, "dp", axis=0, tiled=True),
            lax.all_gather(norm2_gain, "dp", axis=0, tiled=True),
            lax.all_gather(w_query, "dp", axis=0, tiled=True),
            lax.all_gather(w_key, "dp", axis=0, tiled=True),
            lax.all_gather(w_value, "dp", axis=0, tiled=True),
            lax.all_gather(w_up, "dp", axis=0, tiled=True),
            lax.all_gather(w_out, "dp", axis=1, tiled=True),
            lax.all_gather(w_down, "dp", axis=1, tiled=True),
        )

    def rows_forward(normed):
        return lax.all_gather(normed, "tensor", axis=0, tiled=True)

    def rows_backward(gradients):
        return lax.all_gather(gradients, "tensor", axis=0, tiled=True)

    def sum_forward(term_fn):
        return lax.psum_scatter(
            term_fn(jnp.int32(0), local_rows * lax.axis_size("tensor")),
            "tensor",
            scatter_dimension=0,
            tiled=True,
        )

    def sum_backward(term_fn):
        return lax.psum_scatter(
            term_fn(jnp.int32(0), local_rows * lax.axis_size("tensor")),
            "tensor",
            scatter_dimension=0,
            tiled=True,
        )

    grad_totals = None
    outputs = []
    input_grads = []
    for micro_index in range(micro_count):
        gathered = fetch_weights()
        gain_one = gathered[0].astype(jnp.float32)
        gain_two = gathered[1].astype(jnp.float32)
        query_w, key_w, value_w, up_w, out_w, down_w = (
            gathered[2],
            gathered[3],
            gathered[4],
            gathered[5],
            gathered[6],
            gathered[7],
        )
        tokens = block_input[micro_index].astype(jnp.float32)
        ends = jnp.cumsum(clip_lengths[micro_index])
        segment = jnp.sum((places[:, None] >= ends[None, :]).astype(jnp.int32), axis=1)
        own_segment = lax.dynamic_slice_in_dim(segment, row_offset, local_rows, 0)
        valid_rows = (own_segment < clip_count).astype(jnp.float32)
        normed_one, unit_one, inverse_one = norm_rows(tokens, gain_one)
        features_one = rows_forward(normed_one.astype(jnp.bfloat16))
        query = jnp.dot(features_one, query_w, preferred_element_type=jnp.float32).astype(
            jnp.bfloat16
        )
        key = jnp.dot(features_one, key_w, preferred_element_type=jnp.float32).astype(jnp.bfloat16)
        value = jnp.dot(features_one, value_w, preferred_element_type=jnp.float32).astype(
            jnp.bfloat16
        )
        mixed_rows, log_norm = attend(query, key, value, segment, block_rows)

        def attn_term(offset, row_count):
            return jnp.dot(mixed_rows, out_w, preferred_element_type=jnp.float32)

        hidden = tokens + sum_forward(attn_term)
        normed_two, unit_two, inverse_two = norm_rows(hidden, gain_two)
        features_two = rows_forward(normed_two.astype(jnp.bfloat16))
        pre_act = jnp.dot(features_two, up_w, preferred_element_type=jnp.float32)
        activated = gelu_tanh(pre_act).astype(jnp.bfloat16)

        def mlp_term(offset, row_count):
            return jnp.dot(activated, down_w, preferred_element_type=jnp.float32)

        outputs.append((hidden + sum_forward(mlp_term)).astype(jnp.bfloat16))
        regathered = fetch_weights()
        query_w, key_w, value_w, up_w, out_w, down_w = (
            regathered[2],
            regathered[3],
            regathered[4],
            regathered[5],
            regathered[6],
            regathered[7],
        )
        grad_out = out_cotangent[micro_index].astype(jnp.float32) * valid_rows[:, None]
        grad_branch = rows_backward(grad_out.astype(jnp.bfloat16))
        down_grad = jnp.einsum(
            "sf,sd->fd", activated, grad_branch, preferred_element_type=jnp.float32
        )
        grad_act = jnp.einsum("sd,fd->sf", grad_branch, down_w, preferred_element_type=jnp.float32)
        grad_pre = jax.vjp(gelu_tanh, pre_act)[1](grad_act)[0].astype(jnp.bfloat16)
        up_grad = jnp.einsum(
            "sd,sf->df", features_two, grad_pre, preferred_element_type=jnp.float32
        )

        def up_term(offset, row_count):
            return jnp.einsum("sf,df->sd", grad_pre, up_w, preferred_element_type=jnp.float32)

        grad_normed_two = sum_backward(up_term)
        grad_from_two, gain_two_grad = norm_back(grad_normed_two, unit_two, inverse_two, gain_two)
        grad_hidden = grad_out + grad_from_two
        grad_attn = rows_backward(grad_hidden.astype(jnp.bfloat16))
        out_grad = jnp.einsum(
            "sc,sd->cd", mixed_rows, grad_attn, preferred_element_type=jnp.float32
        )
        grad_mixed = jnp.einsum(
            "sd,cd->sc", grad_attn, out_w, preferred_element_type=jnp.float32
        ).astype(jnp.bfloat16)
        grad_query, grad_key, grad_value = attend_back(
            query, key, value, segment, log_norm, grad_mixed, block_rows
        )
        query_grad = jnp.einsum(
            "sd,sc->dc", features_one, grad_query, preferred_element_type=jnp.float32
        )
        key_grad = jnp.einsum(
            "sd,sc->dc", features_one, grad_key, preferred_element_type=jnp.float32
        )
        value_grad = jnp.einsum(
            "sd,sc->dc", features_one, grad_value, preferred_element_type=jnp.float32
        )

        def qkv_term(offset, row_count):
            part_query = jnp.einsum(
                "sc,dc->sd", grad_query, query_w, preferred_element_type=jnp.float32
            )
            part_key = jnp.einsum("sc,dc->sd", grad_key, key_w, preferred_element_type=jnp.float32)
            part_value = jnp.einsum(
                "sc,dc->sd", grad_value, value_w, preferred_element_type=jnp.float32
            )
            return part_query + part_key + part_value

        grad_normed_one = sum_backward(qkv_term)
        grad_from_one, gain_one_grad = norm_back(grad_normed_one, unit_one, inverse_one, gain_one)
        input_grads.append(grad_hidden + grad_from_one)
        micro_grads = (
            gain_one_grad,
            gain_two_grad,
            query_grad,
            key_grad,
            value_grad,
            up_grad,
            out_grad,
            down_grad,
        )
        if grad_totals is None:
            grad_totals = micro_grads
        else:
            grad_totals = jax.tree.map(jnp.add, grad_totals, micro_grads)
    grad_totals = (
        lax.psum_scatter(
            grad_totals[0].astype(jnp.bfloat16), "dp", scatter_dimension=0, tiled=True
        ).astype(jnp.float32),
        lax.psum_scatter(
            grad_totals[1].astype(jnp.bfloat16), "dp", scatter_dimension=0, tiled=True
        ).astype(jnp.float32),
        lax.psum_scatter(
            grad_totals[2].astype(jnp.bfloat16), "dp", scatter_dimension=0, tiled=True
        ).astype(jnp.float32),
        lax.psum_scatter(
            grad_totals[3].astype(jnp.bfloat16), "dp", scatter_dimension=0, tiled=True
        ).astype(jnp.float32),
        lax.psum_scatter(
            grad_totals[4].astype(jnp.bfloat16), "dp", scatter_dimension=0, tiled=True
        ).astype(jnp.float32),
        lax.psum_scatter(
            grad_totals[5].astype(jnp.bfloat16), "dp", scatter_dimension=0, tiled=True
        ).astype(jnp.float32),
        lax.psum_scatter(
            grad_totals[6].astype(jnp.bfloat16), "dp", scatter_dimension=1, tiled=True
        ).astype(jnp.float32),
        lax.psum_scatter(
            grad_totals[7].astype(jnp.bfloat16), "dp", scatter_dimension=1, tiled=True
        ).astype(jnp.float32),
    )
    gain_sums = lax.psum((grad_totals[0], grad_totals[1]), "tensor")
    return (
        jnp.stack(outputs),
        jnp.stack(input_grads),
        gain_sums[0],
        grad_totals[2],
        grad_totals[3],
        grad_totals[4],
        grad_totals[6],
        gain_sums[1],
        grad_totals[5],
        grad_totals[7],
    )


def chunk_scores(q, k, start, s, c, rows):
    scores = lax.dot_general(
        q, k, (((1,), (1,)), ((), ())), preferred_element_type=f32
    ) * HEAD ** (-0.5)
    k_place = c * rows + lax.broadcasted_iota(jnp.int32, (rows, rows), 1)
    allowed = k_place >= start
    if c == s:
        q_place = s * rows + lax.broadcasted_iota(jnp.int32, (rows, rows), 0)
        allowed = jnp.logical_and(allowed, k_place <= q_place)
    return jnp.where(allowed, scores, masked_fill)


def clip_starts(ends_ref, first, buffer, clip_count, s, rows):
    place = s * rows + lax.broadcasted_iota(jnp.int32, (rows, 1), 0)
    start = jnp.zeros((rows, 1), jnp.int32)
    for clip in range(clip_count):
        end = ends_ref[first + buffer * clip_count + clip]
        start = jnp.where(place >= end, jnp.maximum(start, end), start)
    return start


def window(s, rows):
    back = -(-(LONGEST - 1) // rows)
    return range(max(0, s - back), s + 1)


def chunk_probs(q, keys, start, s, rows):
    cs = list(window(s, rows))
    scores = [chunk_scores(q, keys(c), start, s, c, rows) for c in cs]
    highest = functools.reduce(jnp.maximum, [jnp.max(v, axis=1, keepdims=True) for v in scores])
    shifted = [jnp.exp(v - highest) for v in scores]
    total = functools.reduce(jnp.add, [jnp.sum(v, axis=1, keepdims=True) for v in shifted])
    scale = 1.0 / total
    return cs, [v * scale for v in shifted]


MESH = pl.DeviceIdType.MESH
N_TILE = 1024


class Plane:
    def __init__(self, send_sems, recv_sems, more=()):
        me = lax.axis_index("dp")
        self.core = me % 2
        self.x = (me // 2) % 2
        self.peers = {
            "c": me + 1 - 2 * (me % 2),
            "x": me + 2 - 4 * ((me // 2) % 2),
            "y": me + 4 - 8 * ((me // 4) % 2),
        }
        self.send_sems, self.recv_sems = send_sems, recv_sems
        self.copies = []
        barrier = pltpu.get_barrier_semaphore()
        for peer in self.peers.values():
            pl.semaphore_signal(barrier, inc=1, device_id={"dp": peer}, device_id_type=MESH)
        for place in more:
            pl.semaphore_signal(barrier, inc=1, device_id=at_device(place), device_id_type=MESH)
        pl.semaphore_wait(barrier, 3 + len(more))

    def send(self, src, dst, way):
        return self.send_to(src, dst, {"dp": self.peers[way]})

    def send_to(self, src, dst, device):
        index = len(self.copies)
        copy = pltpu.make_async_remote_copy(
            src_ref=src,
            dst_ref=dst,
            send_sem=self.send_sems.at[index],
            recv_sem=self.recv_sems.at[index],
            device_id=device,
            device_id_type=MESH,
        )
        copy.start()
        self.copies.append(copy)
        return copy

    def finish(self):
        for copy in self.copies:
            copy.wait_send()


class Gather:
    def __init__(self, plane, own, pieces):
        self.plane, self.own, self.pieces = plane, own, pieces
        self.half = own.shape[0] // 2

    def begin(self):
        send = self.plane.send
        self.x = send(self.own, self.pieces.at[1], "x")
        self.y = send(self.own, self.pieces.at[2], "y")
        self.c = [send(self.own, self.pieces.at[4], "c")]

    def middle(self):
        send, half, pieces = self.plane.send, self.half, self.pieces
        self.x.wait_recv()
        self.fy = send(pieces.at[1, pl.ds(half, half)], pieces.at[3, pl.ds(half, half)], "y")
        self.c.append(send(pieces.at[1], pieces.at[5], "c"))
        self.y.wait_recv()
        self.fx = send(pieces.at[2, pl.ds(0, half)], pieces.at[3, pl.ds(0, half)], "x")
        self.c.append(send(pieces.at[2], pieces.at[6], "c"))

    def end(self):
        self.fx.wait_recv()
        self.fy.wait_recv()
        self.c.append(self.plane.send(self.pieces.at[3], self.pieces.at[7], "c"))

    def core(self, index):
        self.c[index].wait_recv()


class Reduce:
    def __init__(self, plane, pieces, from_core, from_x, from_y):
        self.plane, self.pieces = plane, pieces
        self.from_core, self.from_x, self.from_y = from_core, from_x, from_y
        self.half = pieces.shape[1] // 2
        self.core = {}

    def give(self, m):
        self.core[m] = self.plane.send(self.pieces.at[4 + m], self.from_core.at[m], "c")

    def take(self, m):
        self.core[m].wait_recv()

    def chip_done(self, m):
        send, half, pieces = self.plane.send, self.half, self.pieces
        low, high = pl.ds(0, half), pl.ds(half, half)
        if m == 3:
            self.far_x = send(pieces.at[3, low], self.from_x.at[1], "x")
            self.far_y = send(pieces.at[3, high], self.from_y.at[1], "y")
        elif m == 1:
            self.near_x = send(pieces.at[1, low], self.from_x.at[0], "x")
        elif m == 2:
            self.near_y = send(pieces.at[2, high], self.from_y.at[0], "y")

    def late_x(self):
        high = pl.ds(self.half, self.half)
        self.far_y.wait_recv()
        add_into(self.pieces.at[1, high], self.from_y.at[1])
        self.late_x_copy = self.plane.send(self.pieces.at[1, high], self.from_x.at[2], "x")

    def late_y(self):
        low = pl.ds(0, self.half)
        self.far_x.wait_recv()
        add_into(self.pieces.at[2, low], self.from_x.at[1])
        self.late_y_copy = self.plane.send(self.pieces.at[2, low], self.from_y.at[2], "y")

    def late(self):
        self.late_x()
        self.late_y()

    def total(self, out):
        half = self.half
        self.near_x.wait_recv()
        self.near_y.wait_recv()
        self.late_x_copy.wait_recv()
        self.late_y_copy.wait_recv()
        step = min(64, half)

        for base, x_part, y_part in ((0, 0, 2), (half, 2, 0)):

            def add(index, carry):
                at = pl.ds(pl.multiple_of(index * step, step), step)
                here = pl.ds(pl.multiple_of(base + index * step, step), step)
                out[here] = (
                    self.pieces[0, here].astype(f32)
                    + self.from_x[x_part, at].astype(f32)
                    + self.from_y[y_part, at].astype(f32)
                )
                return carry

            lax.fori_loop(0, half // step, add, 0)


def add_into(ref, other):
    step = min(64, ref.shape[0])

    def add(index, carry):
        at = pl.ds(pl.multiple_of(index * step, step), step)
        ref[at] = (ref[at].astype(f32) + other[at].astype(f32)).astype(bf16)
        return carry

    lax.fori_loop(0, ref.shape[0] // step, add, 0)


ORDER = (3, 1, 2, 0)


def tiles(count, tile, body):
    tile = min(tile, count)

    def step(index, carry):
        body(pl.ds(pl.multiple_of(index * tile, tile), tile))
        return carry

    lax.fori_loop(0, count // tile, step, 0)


def nn(left, right):
    return jnp.dot(left, right, preferred_element_type=f32)


def nt(left, right):
    return lax.dot_general(left, right, (((1,), (1,)), ((), ())), preferred_element_type=f32)


def tn(left, right):
    return lax.dot_general(left, right, (((0,), (0,)), ((), ())), preferred_element_type=f32)


class Feed:
    def __init__(self, source, slots, sems, order):
        self.source, self.slots, self.sems, self.order = source, slots, sems, list(order)

    def copy(self, index):
        slot = index % 2
        return pltpu.make_async_copy(
            self.source(self.order[index]), self.slots.at[slot], self.sems.at[slot]
        )

    def start(self, index):
        if index < len(self.order):
            self.copy(index).start()

    def get(self, index):
        self.copy(index).wait()
        return self.slots.at[index % 2]


def plane_call(kernel, name, collective_id, out_shape, in_spaces, out_spaces, scratch, copies, flops, args):
    spaces = {"any": pl.ANY, "vmem": pltpu.VMEM, "smem": pltpu.SMEM}
    return pl.pallas_call(
        kernel,
        out_shape=out_shape,
        in_specs=[pl.BlockSpec(memory_space=spaces[v]) for v in in_spaces],
        out_specs=[pl.BlockSpec(memory_space=spaces[v]) for v in out_spaces],
        scratch_shapes=list(scratch)
        + [pltpu.SemaphoreType.DMA((copies,)), pltpu.SemaphoreType.DMA((copies,))],
        compiler_params=pltpu.CompilerParams(
            collective_id=collective_id, has_side_effects=True, vmem_limit_bytes=61 << 20
        ),
        cost_estimate=pl.CostEstimate(flops=flops, bytes_accessed=64 << 20, transcendentals=0),
        name=name,
    )(*args)


def row_places():
    me, plane = lax.axis_index("dp"), lax.axis_index("tensor")
    chip, core = 2 * (me // 2), me % 2
    outward = [(chip + 1 - plane // 2, 2 * core + j) for j in range(2)]
    inward = [(chip + plane // 2, 2 * (1 - core) + i) for i in range(2)]
    return outward, inward


def at_device(place):
    return {"dp": place[0], "tensor": place[1]}


class RowMove:
    def __init__(self, src, dst, sems):
        self.src, self.dst, self.sems = src, dst, sems
        self.copies = []

    def copy(self, here, there, place):
        return pltpu.make_async_remote_copy(
            src_ref=self.src.at[here],
            dst_ref=self.dst.at[there],
            send_sem=self.sems.at[0, here],
            recv_sem=self.sems.at[1, there],
            device_id=at_device(place),
            device_id_type=MESH,
        )

    def start(self, places, there):
        for here in range(2):
            copy = self.copy(here, there, places[here])
            copy.start()
            self.copies.append(copy)
        self.arrivals = [self.copy(index, index, places[index]) for index in range(2)]

    def outward(self):
        self.start(row_places()[0], lax.axis_index("tensor") % 2)

    def back(self):
        self.start(row_places()[1], lax.axis_index("tensor") % 2)

    def wait(self):
        for copy in self.copies:
            copy.wait_send()
        for copy in self.arrivals:
            copy.wait_recv()


def start_kernel(
    tokens, w_query, w_key, w_value, w_out, w_up, w_down, small,
    tokens_out, qkv_out, out_out, up_out, down_out, small_out,
    local_sems, row_sems, send_sems, recv_sems,
):
    me, plane = lax.axis_index("dp"), lax.axis_index("tensor")
    chip, core = me // 2, me % 2
    depth = w_query.shape[0]
    part = up_out.shape[1]
    outward, inward = row_places()
    peers = [lax.rem(me + j, 8) for j in range(1, 8)]
    barrier = pltpu.get_barrier_semaphore()
    for peer in peers:
        pl.semaphore_signal(barrier, inc=1, device_id={"dp": peer}, device_id_type=MESH)
    for place in outward + inward:
        pl.semaphore_signal(barrier, inc=1, device_id=at_device(place), device_id_type=MESH)
    pl.semaphore_wait(barrier, 11)
    copies, locals_ = [], []

    def send(src, dst, device):
        copy = pltpu.make_async_remote_copy(
            src_ref=src,
            dst_ref=dst,
            send_sem=send_sems.at[len(copies)],
            recv_sem=recv_sems.at[len(copies)],
            device_id=device,
            device_id_type=MESH,
        )
        copy.start()
        copies.append(copy)

    def keep(src, dst):
        copy = pltpu.make_async_copy(src, dst, local_sems.at[len(locals_)])
        copy.start()
        locals_.append(copy)

    def block(index, size):
        return pl.ds(pl.multiple_of(index * size, size), size)

    rows_move = RowMove(tokens, tokens_out, row_sems)
    rows_move.outward()
    for peer in peers:
        send(small, small_out.at[me], {"dp": peer})
    keep(small, small_out.at[me])
    heads = [(w_query, 0), (w_key, 1), (w_value, 2)]
    for j in range(1, 4):
        other = lax.rem(chip + j, 4)
        device = {"dp": 2 * other + core}
        for weight, which in heads:
            send(weight.at[:, block(other, HEAD)], qkv_out.at[which, chip], device)
    for weight, which in heads:
        keep(weight.at[:, block(chip, HEAD)], qkv_out.at[which, chip])
    for j in range(1, 4):
        other = lax.rem(chip + j, 4)
        send(w_out.at[block(other, HEAD)], out_out.at[chip], {"dp": 2 * other + core})
    keep(w_out.at[block(chip, HEAD)], out_out.at[chip])
    for peer in peers:
        send(w_up.at[:, block(peer, part)], up_out.at[block(me, depth)], {"dp": peer})
        send(w_down.at[block(peer, part)], down_out.at[:, block(me, depth)], {"dp": peer})
    keep(w_up.at[:, block(me, part)], up_out.at[block(me, depth)])
    keep(w_down.at[block(me, part)], down_out.at[:, block(me, depth)])
    for copy in locals_:
        copy.wait()
    for copy in copies:
        copy.wait()
    rows_move.wait()


def gather_kernel(own, rows_in, pieces, rows_out, own_sem, row_sems, send_sems, recv_sems):
    outward, inward = row_places()
    plane = Plane(send_sems, recv_sems, outward + inward)
    streams = own.shape[0]
    rows_move = RowMove(rows_in, rows_out, row_sems)
    rows_move.outward()
    gathers = [Gather(plane, own.at[s], pieces.at[s]) for s in range(streams)]
    keep = [pltpu.make_async_copy(own.at[s], pieces.at[s, 0], own_sem.at[s]) for s in range(streams)]
    for s in range(streams):
        gathers[s].begin()
        keep[s].start()
    for s in range(streams):
        gathers[s].middle()
    for s in range(streams):
        gathers[s].end()
    for s in range(streams):
        keep[s].wait()
        for index in range(4):
            gathers[s].core(index)
    rows_move.wait()
    plane.finish()


def chunk_at(plane, s):
    k = 1 - s // 2
    return s % 2, k + plane.core - 2 * k * plane.core


def chunk_part(plane, qkv, chip, head):
    def part(s, which):
        column = pl.multiple_of((head * 3 + which) * HEAD, HEAD)
        stream, core = chunk_at(plane, s)
        piece = core * (qkv.shape[1] // 2) + chip
        return qkv[stream, piece, :, pl.ds(column, HEAD)]

    return part


def attend_all(plane, qkv, ends_ref, out, clip_count):
    rows = qkv.shape[2]
    heads = qkv.shape[3] // (3 * HEAD)

    def one(index, carry):
        chip, head = index // heads, index % heads
        part = chunk_part(plane, qkv, chip, head)
        column = pl.ds(pl.multiple_of(head * HEAD, HEAD), HEAD)
        for s in range(4):
            start = clip_starts(ends_ref, 0, chip, clip_count, s, rows)
            cs, probs = chunk_probs(part(s, 0), lambda c: part(c, 1), start, s, rows)
            mixed = jnp.zeros((rows, HEAD), f32)
            for c, prob in zip(cs, probs):
                mixed = mixed + nn(prob.astype(bf16), part(c, 2))
            stream, core = chunk_at(plane, s)
            out[stream, core * 4 + chip, :, column] = mixed.astype(bf16)
        return carry

    return one


def attend_back_chip(plane, qkv, grad_mixed, ends_ref, out, key_sum, value_sum, clip_count, chip):
    rows = qkv.shape[2]
    heads = qkv.shape[3] // (3 * HEAD)

    def one(head, carry):
        part = chunk_part(plane, qkv, 0, head)
        column = pl.ds(pl.multiple_of(head * HEAD, HEAD), HEAD)
        key_sum[...] = jnp.zeros_like(key_sum)
        value_sum[...] = jnp.zeros_like(value_sum)

        def put(s, which, value):
            at = pl.ds(pl.multiple_of((head * 3 + which) * HEAD, HEAD), HEAD)
            stream, core = chunk_at(plane, s)
            out[stream, core, :, at] = value.astype(bf16)

        for s in range(4):
            q = part(s, 0)
            stream, core = chunk_at(plane, s)
            g = grad_mixed[stream, core * 4 + chip, :, column]
            start = clip_starts(ends_ref, 0, chip, clip_count, s, rows)
            cs, probs = chunk_probs(q, lambda c: part(c, 1), start, s, rows)
            grad_probs = [nt(g, part(c, 2)) for c in cs]
            inner = functools.reduce(
                jnp.add,
                [jnp.sum(p * v, axis=1, keepdims=True) for p, v in zip(probs, grad_probs)],
            )
            grad_q = jnp.zeros((rows, HEAD), f32)
            for c, prob, grad_prob in zip(cs, probs, grad_probs):
                grad_score = (prob * (grad_prob - inner) * HEAD ** (-0.5)).astype(bf16)
                grad_q = grad_q + nn(grad_score, part(c, 1))
                key_sum[c] += tn(grad_score, q)
                value_sum[c] += tn(prob.astype(bf16), g)
            put(s, 0, grad_q)
        for s in range(4):
            put(s, 1, key_sum[s])
            put(s, 2, value_sum[s])
        return carry

    lax.fori_loop(0, heads, one, 0)


def attention_kernel(
    clip_count, own, rows_in, wide, ends, pieces, qkv, mixed, weight, slots, slot_sems, own_sem, wide_sems, send_sems, recv_sems
):
    plane = Plane(send_sems, recv_sems)
    streams = own.shape[0]
    gathers = [Gather(plane, own.at[s], pieces.at[s]) for s in range(streams)]
    keep = [pltpu.make_async_copy(own.at[s], pieces.at[s, 0], own_sem.at[s]) for s in range(streams)]
    traded, kept = [], []
    for head in range(2):
        for which in range(3):
            column = pl.ds((head * 3 + which) * HEAD, HEAD)
            here = weight.at[:, plane.core, :, column]
            traded.append(plane.send(wide.at[2 * (1 - plane.core) + head, which], here, "c"))
            copy = pltpu.make_async_copy(
                wide.at[2 * plane.core + head, which], here, wide_sems.at[len(kept)]
            )
            copy.start()
            kept.append(copy)
    for s in range(streams):
        gathers[s].begin()
        keep[s].start()
    total = weight.shape[3]
    feed = Feed(
        lambda at: rows_in.at[at[0], at[1]],
        slots,
        slot_sems,
        [(s, p) for s in range(streams) for p in range(8)],
    )
    feed.start(0)

    def project(s):
        for p in range(8):
            feed.start(s * 8 + p + 1)
            piece = feed.get(s * 8 + p)

            def tile(at):
                columns = weight[:, :, :, at].reshape(width, -1)
                qkv[s, p, :, at] = nn(piece[...], columns).astype(bf16)

            tiles(total, N_TILE, tile)

    for copy in traded:
        copy.wait_recv()
    for copy in kept:
        copy.wait()
    width = own.shape[2]

    attend = attend_all(plane, qkv, ends, mixed, clip_count)
    heads = total // (3 * HEAD)
    project(0)
    project(1)
    lax.fori_loop(0, 2 * heads, attend, 0)
    gathers[0].middle()
    gathers[1].middle()
    lax.fori_loop(2 * heads, 4 * heads, attend, 0)
    gathers[0].end()
    gathers[1].end()
    for s in range(streams):
        keep[s].wait()
        for index in range(4):
            gathers[s].core(index)
    plane.finish()


def reduce_scratch(streams, rows, width):
    return [
        pltpu.VMEM((streams, 8, rows, width), bf16),
        pltpu.VMEM((streams, 4, rows, width), bf16),
        pltpu.VMEM((streams, 3, rows // 2, width), bf16),
        pltpu.VMEM((streams, 3, rows // 2, width), bf16),
    ]


def project_kernel(
    mixed, wide, out, weight, parts, from_core, from_x, from_y, wide_sems, send_sems, recv_sems
):
    plane = Plane(send_sems, recv_sems)
    streams = mixed.shape[0]
    width = weight.shape[1]
    depth = wide.shape[3]
    traded, kept = [], []
    for head in range(2):
        for chip in range(4):
            column = pl.ds(pl.multiple_of((2 * chip + plane.core) * depth, depth), depth)
            here = weight.at[pl.ds(head * HEAD, HEAD), column]
            traded.append(plane.send(wide.at[2 * (1 - plane.core) + head, chip], here, "c"))
            copy = pltpu.make_async_copy(
                wide.at[2 * plane.core + head, chip], here, wide_sems.at[len(kept)]
            )
            copy.start()
            kept.append(copy)
    for copy in traded:
        copy.wait_recv()
    for copy in kept:
        copy.wait()
    sums = [
        Reduce(plane, parts.at[s], from_core.at[s], from_x.at[s], from_y.at[s])
        for s in range(streams)
    ]

    for s in range(streams):
        for m in ORDER:

            def other(at):
                parts[s, 4 + m, :, at] = nn(mixed[s, 4 + m], weight[:, at]).astype(bf16)

            tiles(width, N_TILE, other)
            sums[s].give(m)
        for m in ORDER:
            sums[s].take(m)

            def chip(at):
                here = nn(mixed[s, m], weight[:, at])
                parts[s, m, :, at] = (here + from_core[s, m, :, at].astype(f32)).astype(bf16)

            tiles(width, N_TILE, chip)
            sums[s].chip_done(m)
        if s > 0:
            sums[s - 1].late()
    sums[streams - 1].late()
    for s in range(streams):
        sums[s].total(out.at[s])
    plane.finish()


def gelu_pair(v):
    cubic = 0.044715 * (v * v) * v
    inner = (2.0 / np.pi) ** 0.5 * (v + cubic)
    th = jnp.tanh(inner)
    half = 0.5 * (1.0 + th)
    slope = (2.0 / np.pi) ** 0.5 * (1.0 + 3.0 * 0.044715 * (v * v))
    return v * half, half + 0.5 * v * (1.0 - th * th) * slope


def lay_out(wide, flat, sems):
    copies = []
    part = wide.shape[2]
    for plane in range(wide.shape[0]):
        copy = pltpu.make_async_copy(
            wide.at[plane], flat.at[:, pl.ds(plane * part, part)], sems.at[plane]
        )
        copy.start()
        copies.append(copy)
    return copies


def mlp_kernel(
    own, up_wide, down_w, grads, pieces, slope_out, down_grad, out,
    parts, from_core, from_x, from_y, up_w, slots, act, slope, total, grad_slots,
    up_sems, slot_sems, keep_sems, own_sem, grad_sems, send_sems, recv_sems,
):
    plane = Plane(send_sems, recv_sems)
    streams, rows, width = own.shape
    hidden = up_w.shape[1]
    up_copies = lay_out(up_wide, up_w, up_sems)
    gathers = [Gather(plane, own.at[s], pieces.at[s]) for s in range(streams)]
    sums = [
        Reduce(plane, parts.at[s], from_core.at[s], from_x.at[s], from_y.at[s])
        for s in range(streams)
    ]
    keep = [pltpu.make_async_copy(own.at[s], pieces.at[s, 0], own_sem.at[s]) for s in range(streams)]
    stores = []
    loads = [0]

    def load(s, p):
        slot = loads[0] % 2
        loads[0] += 1
        source = own.at[s] if p == 0 else pieces.at[s, p]
        copy = pltpu.make_async_copy(source, slots.at[slot], slot_sems.at[slot])
        copy.start()
        return copy, slots.at[slot]

    def work(s, p, loaded):
        copy, piece = loaded
        slot = len(stores) % 2
        index = len(stores)
        if index >= 2:
            stores[index - 2].wait()
        copy.wait()

        def up(at):
            value, grad = gelu_pair(nn(piece[...], up_w[:, at]))
            act[slot, :, at] = value.astype(bf16)
            slope[slot, :, at] = grad.astype(bf16)

        tiles(hidden, N_TILE, up)
        store = pltpu.make_async_copy(slope.at[slot], slope_out.at[s, p], keep_sems.at[slot])
        store.start()
        stores.append(store)
        if p < 4:
            sums[s].take(p)

        def down(at):
            here = nn(act[slot], down_w[:, at])
            if p < 4:
                here = here + from_core[s, p, :, at].astype(f32)
            parts[s, p, :, at] = here.astype(bf16)

        tiles(width, N_TILE, down)
        if p >= 4:
            sums[s].give(p - 4)
        else:
            sums[s].chip_done(p)

    for s in range(streams):
        keep[s].start()
    gathers[0].begin()

    def pair_up(s, m):
        coming = [
            pltpu.make_async_copy(grads.at[s, p], grad_slots.at[i], grad_sems.at[i])
            for i, p in enumerate((4 + m, m))
        ]
        for copy in coming:
            copy.start()
        gathers[s].core(m)
        first = not stores
        work(s, 4 + m, load(s, 4 + m))
        work(s, m, load(s, m))
        for copy in coming:
            copy.wait()
        left = act[...].reshape(2 * rows, hidden)

        def weigh(at):
            term = tn(left, grad_slots[:, :, at].reshape(2 * rows, -1))
            total[:, at] = term if first else total[:, at] + term

        tiles(width, 512, weigh)

    for s in range(streams):
        if s == 0:
            for copy in up_copies:
                copy.wait()
        else:
            gathers[s].middle()
        pair_up(s, 0)
        if s == 0:
            gathers[s].middle()
        if s + 1 < streams:
            gathers[s + 1].begin()
        if s > 0:
            sums[s - 1].late()
        pair_up(s, 1)
        gathers[s].end()
        if s == 0:
            pair_up(s, 2)
        pair_up(s, 3)
        if s > 0:
            sums[s].late_x()
            pair_up(s, 2)
            sums[s].late_y()
    for s in range(streams):
        sums[s].total(out.at[s])
        keep[s].wait()
    for store in stores[-2:]:
        store.wait()
    stores = []
    for index in range(hidden // rows):
        if index >= 2:
            stores[index - 2].wait()
        here = pl.ds(index * rows, rows)
        slots[index % 2] = total[here].astype(bf16)
        store = pltpu.make_async_copy(
            slots.at[index % 2], down_grad.at[here], keep_sems.at[index % 2]
        )
        store.start()
        stores.append(store)
    for store in stores[-2:]:
        store.wait()
    plane.finish()


def mlp_back_kernel(
    grads, slope_in, features, up_wide, down_w, up_grad, out,
    parts, from_core, from_x, from_y, up_w, slots, slopes, pre, rows_two, total,
    up_sems, slot_sems, slope_sems, row_sems, keep_sems, send_sems, recv_sems,
):
    plane = Plane(send_sems, recv_sems)
    streams, _, rows, width = grads.shape
    hidden = up_w.shape[1]
    part = up_wide.shape[2]
    up_copies = lay_out(up_wide, up_w, up_sems)
    sums = [
        Reduce(plane, parts.at[s], from_core.at[s], from_x.at[s], from_y.at[s])
        for s in range(streams)
    ]
    order = [(s, p) for s in range(streams) for m in ORDER for p in (4 + m, m)]
    feed = Feed(lambda at: grads.at[at[0], at[1]], slots, slot_sems, order)
    feed_slope = Feed(lambda at: slope_in.at[at[0], at[1]], slopes, slope_sems, order)
    feed_rows = Feed(lambda at: features.at[at[0], at[1]], rows_two, row_sems, order)
    feed.start(0)
    feed_slope.start(0)
    for index, (s, p) in enumerate(order):
        feed.start(index + 1)
        feed_slope.start(index + 1)
        feed_rows.start(index)
        grad = feed.get(index)
        slope = feed_slope.get(index)
        slot = index % 2

        def back(at):
            value = nt(grad[...], down_w[at]) * slope[:, at].astype(f32)
            pre[slot, :, at] = value.astype(bf16)

        tiles(hidden, N_TILE, back)
        if index == 0:
            for copy in up_copies:
                copy.wait()
        if p < 4:
            sums[s].take(p)

        def through(at):
            here = nt(pre[slot], up_w[at])
            if p < 4:
                here = here + from_core[s, p, :, at].astype(f32)
            parts[s, p, :, at] = here.astype(bf16)

        tiles(width, N_TILE, through)
        if p >= 4:
            sums[s].give(p - 4)
            continue
        sums[s].chip_done(p)
        if p == 1:
            sums[s].late_x()
        if p == 2:
            sums[s].late_y()
        feed_rows.get(index - 1)
        feed_rows.get(index)
        right = pre[...].reshape(2 * rows, hidden)

        def weigh(at):
            term = tn(rows_two[:, :, at].reshape(2 * rows, -1), right)
            total[at] = term if index == 1 else total[at] + term

        tiles(width, 512, weigh)
    stores = []
    for index in range(width // rows):
        slot = index % 2
        for store in stores[index - 2] if index >= 2 else []:
            store.wait()
        here = pl.ds(index * rows, rows)
        pre[slot] = total[here].astype(bf16)
        stores.append([])
        for at in range(hidden // part):
            store = pltpu.make_async_copy(
                pre.at[slot, :, pl.ds(at * part, part)], up_grad.at[at, here], keep_sems.at[slot, at]
            )
            store.start()
            stores[-1].append(store)
    for s in range(streams):
        sums[s].total(out.at[s])
    for pair in stores[-2:]:
        for store in pair:
            store.wait()
    plane.finish()


def attention_back_kernel(
    clip_count, own, qkv, mixed, features, rows_in, qkv_w, out_w, ends,
    pieces, qkv_grad, out_grad, rows_out, out,
    parts, from_core, from_x, from_y, slots, mixed_slots, grad_mixed, qkv_chip, grad_chip, key_sum, value_sum,
    qkv_sum, out_sum, slot_sems, mixed_sems, chip_sems, store_sems, row_sems, own_sem, send_sems, recv_sems,
):
    outward, inward = row_places()
    plane = Plane(send_sems, recv_sems, outward + inward)
    rows_move = RowMove(rows_in, rows_out, row_sems)
    rows_move.back()
    streams, rows, width = own.shape
    gathers = [Gather(plane, own.at[s], pieces.at[s]) for s in range(streams)]
    sums = [
        Reduce(plane, parts.at[s], from_core.at[s], from_x.at[s], from_y.at[s])
        for s in range(streams)
    ]
    keep = [pltpu.make_async_copy(own.at[s], pieces.at[s, 0], own_sem.at[s]) for s in range(streams)]
    order = [(s, p) for s in range(streams) for p in (0, 4, 1, 5, 2, 6, 3, 7)]
    feed_mixed = Feed(lambda at: mixed.at[at[0], at[1]], mixed_slots, mixed_sems, order)
    feed_mixed.start(0)
    done = [0]

    def mix(s, p):
        index = done[0]
        done[0] += 1
        feed_mixed.start(index + 1)
        slot = index % 2
        source = own.at[s] if p == 0 else pieces.at[s, p]
        copy = pltpu.make_async_copy(source, slots.at[slot], slot_sems.at[slot])
        copy.start()
        left = feed_mixed.get(index)
        copy.wait()
        grad_mixed[s, p] = nt(slots[slot], out_w[...]).astype(bf16)

        def weigh(at):
            term = tn(left[...], slots[slot, :, at])
            out_sum[:, at] = term if index == 0 else out_sum[:, at] + term

        tiles(width, N_TILE, weigh)

    def load_chip(m):
        copies = [
            pltpu.make_async_copy(
                qkv.at[s, core * 4 + m], qkv_chip.at[s, core], chip_sems.at[s * 2 + core]
            )
            for s in range(streams)
            for core in range(2)
        ]
        for copy in copies:
            copy.start()
        return copies

    for s in range(streams):
        keep[s].start()
    gathers[0].begin()
    for s in range(streams):
        gather = gathers[s]
        mix(s, 0)
        gather.core(0)
        mix(s, 4)
        gather.middle()
        if s + 1 < streams:
            gathers[s + 1].begin()
        for index in (1, 2):
            mix(s, index)
            gather.core(index)
            mix(s, 4 + index)
        gather.end()
        mix(s, 3)
        gather.core(3)
        mix(s, 7)
    for index in range(out_sum.shape[0] // rows):
        here = pl.ds(index * rows, rows)
        slots[0] = out_sum[here].astype(bf16)
        out_store = pltpu.make_async_copy(slots.at[0], out_grad.at[here], slot_sems.at[0])
        out_store.start()
        out_store.wait()

    def load_rows(m):
        copies = [
            pltpu.make_async_copy(
                features.at[s, core * 4 + m], slots.at[s * 2 + core], slot_sems.at[s * 2 + core]
            )
            for s in range(streams)
            for core in range(2)
        ]
        for copy in copies:
            copy.start()
        return copies

    def weigh_chip(place, copies):
        for copy in copies:
            copy.wait()
        right = grad_chip[place % 2].reshape(4 * rows, -1)

        def weigh(at):
            term = tn(slots[:, :, at].reshape(4 * rows, -1), right)
            qkv_sum[at] = term if place == 0 else qkv_sum[at] + term

        tiles(width, 512, weigh)

    coming_rows = load_rows(ORDER[0])
    for copy in load_chip(ORDER[0]):
        copy.wait()
    for place, m in enumerate(ORDER):
        grad_here = grad_chip.at[place % 2]
        attend_back_chip(
            plane, qkv_chip, grad_mixed, ends, grad_here, key_sum, value_sum, clip_count, m
        )
        coming = load_chip(ORDER[place + 1]) if place < 3 else []
        for s in range(streams):

            def other(at):
                parts[s, 4 + m, :, at] = nt(grad_here[s, 1], qkv_w[at]).astype(bf16)

            tiles(width, N_TILE, other)
            sums[s].give(m)
        for s in range(streams):
            sums[s].take(m)

            def chip(at):
                here = nt(grad_here[s, 0], qkv_w[at])
                parts[s, m, :, at] = (here + from_core[s, m, :, at].astype(f32)).astype(bf16)

            tiles(width, N_TILE, chip)
            sums[s].chip_done(m)
        if place > 0:
            weigh_chip(place - 1, coming_rows)
            coming_rows = load_rows(m)
        for s in range(streams):
            if m == 1:
                sums[s].late_x()
            if m == 2:
                sums[s].late_y()
        for copy in coming:
            copy.wait()
    weigh_chip(3, coming_rows)
    stores = []
    for index in range(width // rows):
        if index >= 4:
            stores[index - 4].wait()
        here = pl.ds(index * rows, rows)
        stage = grad_chip.at[0, index // 2 % 2, index % 2]
        stage[...] = qkv_sum[here].astype(bf16)
        store = pltpu.make_async_copy(stage, qkv_grad.at[here], store_sems.at[index % 4])
        store.start()
        stores.append(store)
    for s in range(streams):
        sums[s].total(out.at[s])
        keep[s].wait()
    for store in stores[-4:]:
        store.wait()
    rows_move.wait()
    plane.finish()


def end_kernel(
    rows_in, qkv_grad, out_grad, up_sum, down_sum, gains,
    rows_out, qkv_out, out_out, up_out, down_out, gains_out,
    qkv_part, out_part, qkv_come, out_come, gain_come, gain_sum, gain_all,
    local_sems, row_sems, send_sems, recv_sems,
):
    me, z = lax.axis_index("dp"), lax.axis_index("tensor")
    chip, core = me // 2, me % 2
    depth = qkv_grad.shape[2]
    outward, inward = row_places()
    peers = [lax.rem(me + j, 8) for j in range(1, 8)]
    planes = [lax.rem(z + j, 4) for j in range(1, 4)]
    barrier = pltpu.get_barrier_semaphore()
    for peer in peers:
        pl.semaphore_signal(barrier, inc=1, device_id={"dp": peer}, device_id_type=MESH)
    for plane in planes:
        pl.semaphore_signal(barrier, inc=1, device_id={"tensor": plane}, device_id_type=MESH)
    for place in outward + inward:
        pl.semaphore_signal(barrier, inc=1, device_id=at_device(place), device_id_type=MESH)
    pl.semaphore_wait(barrier, 14)
    copies, locals_ = [], []

    def send(src, dst, device):
        copy = pltpu.make_async_remote_copy(
            src_ref=src,
            dst_ref=dst,
            send_sem=send_sems.at[len(copies)],
            recv_sem=recv_sems.at[len(copies)],
            device_id=device,
            device_id_type=MESH,
        )
        copy.start()
        copies.append(copy)
        return copy

    def keep(src, dst):
        copy = pltpu.make_async_copy(src, dst, local_sems.at[len(locals_)])
        copy.start()
        locals_.append(copy)

    def block(index, size):
        return pl.ds(pl.multiple_of(index * size, size), size)

    other = {"dp": me + 1 - 2 * core}
    traded = []
    for head in range(2):
        mine = 2 * core + head
        for which in range(3):
            column = pl.ds((head * 3 + which) * HEAD, HEAD)
            traded.append(
                send(qkv_grad.at[:, 1 - core, :, column], qkv_part.at[mine, which], other)
            )
            keep(qkv_grad.at[:, core, :, column], qkv_part.at[mine, which])
        here = pl.ds(head * HEAD, HEAD)
        for c in range(4):
            theirs = pl.ds(pl.multiple_of((2 * c + 1 - core) * depth, depth), depth)
            own = pl.ds(pl.multiple_of((2 * c + core) * depth, depth), depth)
            traded.append(send(out_grad.at[here, theirs], out_part.at[mine, c], other))
            keep(out_grad.at[here, own], out_part.at[mine, c])
    gain_first = [send(gains.at[peer], gain_come.at[me], {"dp": peer}) for peer in peers]
    gain_come[me] = gains[me]
    begun = len(locals_)
    part = up_sum.shape[1]
    shards = []
    for peer in peers:
        shards.append(send(up_sum.at[block(peer, depth)], up_out.at[:, block(me, part)], {"dp": peer}))
        shards.append(send(down_sum.at[:, block(peer, depth)], down_out.at[block(me, part)], {"dp": peer}))
    keep(up_sum.at[block(me, depth)], up_out.at[:, block(me, part)])
    keep(down_sum.at[:, block(me, depth)], down_out.at[block(me, part)])
    for copy in traded:
        copy.wait_recv()
    for copy in locals_[:begun]:
        copy.wait()
    after = {"tensor": planes[0]}
    for step in range(3):
        part = lax.rem(z + 3 - step, 4)
        ring = [
            send(qkv_part.at[part], qkv_come.at[step], after),
            send(out_part.at[part], out_come.at[step], after),
        ]
        if step == 0:
            rows_move = RowMove(rows_in, rows_out, row_sems)
            rows_move.back()
            for copy in gain_first:
                copy.wait_recv()
            gain_sum[...] = functools.reduce(jnp.add, [gain_come[i] for i in range(8)])
            gain_second = [
                send(gain_sum, gain_all.at[z], {"tensor": plane}) for plane in planes
            ]
            gain_all[z] = gain_sum[...]
        for copy in ring:
            copy.wait_recv()
        part = lax.rem(z + 2 - step, 4) if step < 2 else z
        for which in range(3):
            for c in range(4):
                here = qkv_part.at[part, which, c]
                here[...] = (
                    here[...].astype(f32) + qkv_come[step, which, c].astype(f32)
                ).astype(bf16)
        for c in range(4):
            here = out_part.at[part, c]
            here[...] = (here[...].astype(f32) + out_come[step, c].astype(f32)).astype(bf16)
    last = []
    for j in range(1, 4):
        to = lax.rem(chip + j, 4)
        device = {"dp": 2 * to + core}
        last.append(send(qkv_part.at[z, :, to], qkv_out.at[:, :, block(chip, HEAD)], device))
        last.append(send(out_part.at[z, to], out_out.at[block(chip, HEAD)], device))
    keep(qkv_part.at[z, :, chip], qkv_out.at[:, :, block(chip, HEAD)])
    keep(out_part.at[z, chip], out_out.at[block(chip, HEAD)])
    for copy in gain_second:
        copy.wait_recv()
    gains_out[...] = functools.reduce(jnp.add, [gain_all[i] for i in range(4)])
    for copy in last + shards:
        copy.wait_recv()
    for copy in locals_[begun:]:
        copy.wait()
    rows_move.wait()
    for copy in copies:
        copy.wait_send()


def on_device(
    block_input,
    clip_lengths,
    norm1_gain,
    w_query,
    w_key,
    w_value,
    w_out,
    norm2_gain,
    w_up,
    w_down,
    out_cotangent,
):
    streams, rows, width = block_input.shape
    planes = lax.axis_size("tensor")
    lanes = lax.axis_size("dp")
    clip_count = clip_lengths.shape[1]
    own = lax.axis_index("dp")
    own_plane = lax.axis_index("tensor")
    own_core = own % 2
    heads = w_query.shape[1] * planes // (HEAD * lanes)
    depth = w_query.shape[0]
    hidden_part = w_up.shape[1] // lanes
    hidden_own = planes * hidden_part
    inner = heads * HEAD

    small = jnp.zeros((8, depth), f32)
    small = small.at[0].set(norm1_gain.astype(f32)).at[1].set(norm2_gain.astype(f32))
    small = small.at[2, : streams * clip_count].set(clip_lengths.reshape(-1).astype(f32))
    tokens_in, qkv_part, out_part, up_part, down_part, small = plane_call(
        start_kernel,
        "start",
        6,
        [
            jax.ShapeDtypeStruct(block_input.shape, bf16),
            jax.ShapeDtypeStruct((3, 4, depth, HEAD), bf16),
            jax.ShapeDtypeStruct((4, HEAD, depth), bf16),
            jax.ShapeDtypeStruct((width, hidden_part), bf16),
            jax.ShapeDtypeStruct((hidden_part, width), bf16),
            jax.ShapeDtypeStruct((lanes, 8, depth), f32),
        ],
        ["any"] * 8,
        ["any"] * 6,
        [pltpu.SemaphoreType.DMA((7,)), pltpu.SemaphoreType.DMA((2, 2))],
        33,
        0,
        (block_input, w_query, w_key, w_value, w_out, w_up, w_down, small),
    )
    gain_one = small[:, 0].reshape(-1)
    gain_two = small[:, 1].reshape(-1)
    lengths = small[:, 2, : streams * clip_count].reshape(-1, clip_count).astype(jnp.int32)

    qkv_wide = lax.all_gather(qkv_part, "tensor", axis=0, tiled=False)
    out_wide = lax.all_gather(out_part, "tensor", axis=0, tiled=False)
    up_wide = lax.all_gather(up_part, "tensor", axis=0, tiled=False)
    down_w = lax.all_gather(down_part, "tensor", axis=0, tiled=True)

    all_ends = jnp.cumsum(lengths, axis=1)
    buffers = 4 * (own // 2 ^ jnp.arange(4, dtype=jnp.int32)) + own_plane
    ends = jnp.take(all_ends, buffers, axis=0)
    chunks = 2 * (1 - own_core) + jnp.arange(streams, dtype=jnp.int32)
    places = chunks[:, None] * rows + jnp.arange(rows, dtype=jnp.int32)
    valid = (places < ends[0, -1]).astype(f32)
    ends = ends.reshape(-1).astype(jnp.int32)

    pieces = jax.ShapeDtypeStruct((streams, 8, rows, width), bf16)
    sums = jax.ShapeDtypeStruct((streams, rows, width), f32)
    row_count = streams * 8 * rows
    slots = pltpu.VMEM((2, rows, width), bf16)
    dma = pltpu.SemaphoreType.DMA

    def piece_shape(columns):
        return jax.ShapeDtypeStruct((streams, 8, rows, columns), bf16)

    tokens = tokens_in.astype(f32)
    normed_one, unit_one, inverse_one = norm_rows(tokens, gain_one)
    features_one, cotangent = plane_call(
        gather_kernel,
        "gather",
        0,
        [pieces, jax.ShapeDtypeStruct(block_input.shape, bf16)],
        ["any", "any"],
        ["any", "any"],
        [dma((streams,)), dma((2, 2))],
        8 * streams,
        0,
        (normed_one.astype(bf16), out_cotangent),
    )
    grad_out = cotangent.astype(f32) * valid[:, :, None]
    grad_branch, qkv, mixed, qkv_w = plane_call(
        functools.partial(attention_kernel, clip_count),
        "attention",
        1,
        [
            pieces,
            piece_shape(3 * inner),
            piece_shape(inner),
            jax.ShapeDtypeStruct((4, 2, depth, 3 * inner), bf16),
        ],
        ["any", "any", "any", "smem"],
        ["any", "vmem", "vmem", "vmem"],
        [slots, dma((2,)), dma((streams,)), dma((6,))],
        8 * streams + 6,
        2 * row_count * width * 3 * inner,
        (grad_out.astype(bf16), features_one, qkv_wide, ends),
    )
    attn_sum, out_w = plane_call(
        project_kernel,
        "project",
        2,
        [sums, jax.ShapeDtypeStruct((inner, width), bf16)],
        ["vmem", "any"],
        ["vmem", "vmem"],
        reduce_scratch(streams, rows, width) + [dma((8,))],
        10 * streams + 8,
        2 * row_count * width * inner,
        (mixed, out_wide),
    )
    hidden = tokens + attn_sum
    normed_two, unit_two, inverse_two = norm_rows(hidden, gain_two)
    part = pltpu.VMEM((2, rows, hidden_own), bf16)
    up_flat = pltpu.VMEM((width, hidden_own), bf16)
    features_two, slope, down_dot, mlp_sum = plane_call(
        mlp_kernel,
        "mlp",
        3,
        [
            pieces,
            piece_shape(hidden_own),
            jax.ShapeDtypeStruct((hidden_own, width), bf16),
            sums,
        ],
        ["any", "any", "vmem", "any"],
        ["any", "any", "any", "vmem"],
        reduce_scratch(streams, rows, width)
        + [up_flat, slots, part, part, pltpu.VMEM((hidden_own, width), f32), slots]
        + [dma((planes,)), dma((2,)), dma((2,)), dma((streams,)), dma((2,))],
        18 * streams,
        6 * row_count * width * hidden_own,
        (normed_two.astype(bf16), up_wide, down_w, grad_branch),
    )

    up_dot, back_sum = plane_call(
        mlp_back_kernel,
        "mlp_back",
        4,
        [jax.ShapeDtypeStruct((planes, width, hidden_part), bf16), sums],
        ["any", "any", "any", "any", "vmem"],
        ["any", "vmem"],
        reduce_scratch(streams, rows, width)
        + [up_flat, slots, part, part, slots, pltpu.VMEM((width, hidden_own), f32)]
        + [dma((planes,)), dma((2,)), dma((2,)), dma((2,)), dma((2, planes))],
        10 * streams,
        6 * row_count * width * hidden_own,
        (grad_branch, slope, features_two, up_wide, down_w),
    )
    from_two, gain_two_grad = norm_back(back_sum, unit_two, inverse_two, gain_two)
    grad_hidden = grad_out + from_two
    down_sum = lax.psum_scatter(down_dot, "tensor", scatter_dimension=0, tiled=True)
    up_sum = lax.psum_scatter(up_dot, "tensor", scatter_dimension=0, tiled=False)
    chunk = pltpu.VMEM((4, rows, HEAD), f32)
    chip_rows = pltpu.VMEM((streams, 2, rows, 3 * inner), bf16)
    _, qkv_dot, out_dot, output, input_sum = plane_call(
        functools.partial(attention_back_kernel, clip_count),
        "attention_back",
        5,
        [
            pieces,
            jax.ShapeDtypeStruct((width, 3 * inner), bf16),
            jax.ShapeDtypeStruct((inner, width), bf16),
            jax.ShapeDtypeStruct(block_input.shape, bf16),
            sums,
        ],
        ["any", "any", "any", "any", "any", "vmem", "vmem", "smem"],
        ["any", "any", "any", "any", "vmem"],
        reduce_scratch(streams, rows, width)
        + [pltpu.VMEM((4, rows, width), bf16), pltpu.VMEM((2, rows, inner), bf16)]
        + [pltpu.VMEM((streams, 8, rows, inner), bf16), chip_rows]
        + [pltpu.VMEM((2, streams, 2, rows, 3 * inner), bf16), chunk, chunk]
        + [pltpu.VMEM((width, 3 * inner), f32), pltpu.VMEM((inner, width), f32)]
        + [dma((4,)), dma((2,)), dma((4,)), dma((4,)), dma((2, 2)), dma((streams,))],
        18 * streams,
        2 * row_count * width * 8 * inner,
        (
            grad_hidden.astype(bf16),
            qkv,
            mixed,
            features_one,
            (hidden + mlp_sum).astype(bf16),
            qkv_w.reshape(width, 3 * inner),
            out_w,
            ends,
        ),
    )
    input_sum, down_sum, up_sum = lax.optimization_barrier((input_sum, down_sum, up_sum))
    from_one, gain_one_grad = norm_back(input_sum, unit_one, inverse_one, gain_one)
    gains = jnp.stack([gain_one_grad.sum(0), gain_two_grad.sum(0)]).reshape(2, lanes, depth)
    gains = jnp.zeros((lanes, 8, depth), f32).at[:, :2].set(gains.swapaxes(0, 1))
    small_sum = pltpu.VMEM((8, depth), f32)
    input_grad, qkv_grad, out_grad, up_grad, down_grad, gains = plane_call(
        end_kernel,
        "end",
        7,
        [
            jax.ShapeDtypeStruct(block_input.shape, bf16),
            jax.ShapeDtypeStruct((3, depth, 4 * HEAD), bf16),
            jax.ShapeDtypeStruct((4 * HEAD, depth), bf16),
            jax.ShapeDtypeStruct(w_up.shape, bf16),
            jax.ShapeDtypeStruct(w_down.shape, bf16),
            jax.ShapeDtypeStruct((8, depth), f32),
        ],
        ["any", "any", "any", "any", "any", "vmem"],
        ["any", "any", "any", "any", "any", "vmem"],
        [
            pltpu.VMEM((4, 3, 4, depth, HEAD), bf16),
            pltpu.VMEM((4, 4, HEAD, depth), bf16),
            pltpu.VMEM((3, 3, 4, depth, HEAD), bf16),
            pltpu.VMEM((3, 4, HEAD, depth), bf16),
            pltpu.VMEM((8, 8, depth), f32),
            small_sum,
            pltpu.VMEM((4, 8, depth), f32),
            dma((18,)),
            dma((2, 2)),
        ],
        50,
        0,
        (
            (grad_hidden + from_one).astype(bf16),
            qkv_dot.reshape(4, 2, depth, 3 * inner),
            out_dot,
            up_sum,
            down_sum,
            gains,
        ),
    )
    qkv_grad = qkv_grad.astype(f32)
    return (
        output,
        input_grad.astype(f32),
        gains[0],
        qkv_grad[0],
        qkv_grad[1],
        qkv_grad[2],
        out_grad.astype(f32),
        gains[1],
        up_grad.astype(f32),
        down_grad.astype(f32),
    )


def solution(mesh):
    in_specs = (
        P("dp", "tensor", None),
        P("dp", None),
        P("dp"),
        P("dp", "tensor"),
        P("dp", "tensor"),
        P("dp", "tensor"),
        P("tensor", "dp"),
        P("dp"),
        P("dp", "tensor"),
        P("tensor", "dp"),
        P("dp", "tensor", None),
    )
    out_specs = (
        P("dp", "tensor", None),
        P("dp", "tensor", None),
        P("dp"),
        P("dp", "tensor"),
        P("dp", "tensor"),
        P("dp", "tensor"),
        P("tensor", "dp"),
        P("dp"),
        P("dp", "tensor"),
        P("tensor", "dp"),
    )
    own_form = mesh.shape["dp"] == 8 and mesh.shape["tensor"] == 4
    return jax.shard_map(
        on_device if own_form else on_device_any, mesh=mesh, in_specs=in_specs, out_specs=out_specs, check_vma=False
    )
```

```python
import functools

import jax
import jax.numpy as jnp
import numpy as np
from jax import lax
from jax.experimental import pallas as pl
from jax.experimental.pallas import tpu as pltpu
from jax.sharding import PartitionSpec as P

HEAD = 128
LONGEST = 512
epsilon = 1e-05
masked_fill = -1000000000.0
bf16 = jnp.bfloat16
f32 = jnp.float32


def norm_rows(tokens, gain):
    centred = tokens - jnp.mean(tokens, axis=-1, keepdims=True)
    inverse = lax.rsqrt(jnp.mean(centred * centred, axis=-1, keepdims=True) + epsilon)
    unit_rows = centred * inverse
    return (unit_rows * gain, unit_rows, inverse)


def norm_back(grad_normed, unit_rows, inverse, gain):
    scaled = grad_normed * gain
    inner_sum = (
        scaled
        - jnp.mean(scaled, axis=-1, keepdims=True)
        - unit_rows * jnp.mean(scaled * unit_rows, axis=-1, keepdims=True)
    )
    return (inverse * inner_sum, jnp.sum(grad_normed * unit_rows, axis=0))


def gelu_tanh(values):
    return jax.nn.gelu(values, approximate=True)


def masked_scores(q_rows, keys_heads, segment, offset, block_rows):
    slot_count = keys_heads.shape[0]
    raw_scores = jnp.einsum(
        "qhd,khd->hqk", q_rows, keys_heads, preferred_element_type=jnp.float32
    ) * HEAD ** (-0.5)
    q_segment = lax.dynamic_slice_in_dim(segment, offset, block_rows, 0)
    q_place = offset + jnp.arange(block_rows, dtype=jnp.int32)
    places = jnp.arange(slot_count, dtype=jnp.int32)
    allowed = (q_segment[:, None] == segment[None, :]) & (places[None, :] <= q_place[:, None])
    return jnp.where(allowed[None], raw_scores, masked_fill)


def attend(query, key, value, segment, block_rows):
    slot_count = query.shape[0]
    head_count = query.shape[1] // HEAD
    keys_heads = key.reshape(slot_count, head_count, HEAD)
    values_heads = value.reshape(slot_count, head_count, HEAD)

    def one_block(block_index):
        offset = block_index * block_rows
        q_rows = lax.dynamic_slice_in_dim(query, offset, block_rows, 0).reshape(
            block_rows, head_count, HEAD
        )
        scores = masked_scores(q_rows, keys_heads, segment, offset, block_rows)
        highest = jnp.max(scores, axis=-1, keepdims=True)
        shifted = jnp.exp(scores - highest)
        totals = jnp.sum(shifted, axis=-1, keepdims=True)
        weights = (shifted / totals).astype(jnp.bfloat16)
        mixed_rows = jnp.einsum(
            "hqk,khd->qhd", weights, values_heads, preferred_element_type=jnp.float32
        )
        return (
            mixed_rows.reshape(block_rows, head_count * HEAD).astype(jnp.bfloat16),
            (highest + jnp.log(totals))[..., 0],
        )

    mixed_rows, log_norm = lax.map(one_block, jnp.arange(slot_count // block_rows, dtype=jnp.int32))
    return (mixed_rows.reshape(slot_count, head_count * HEAD), log_norm)


def attend_back(query, key, value, segment, log_norm, grad_mixed, block_rows):
    slot_count = query.shape[0]
    head_count = query.shape[1] // HEAD
    keys_heads = key.reshape(slot_count, head_count, HEAD)
    values_heads = value.reshape(slot_count, head_count, HEAD)

    def one_block(carried, block_index):
        grad_keys, grad_values = carried
        offset = block_index * block_rows
        q_rows = lax.dynamic_slice_in_dim(query, offset, block_rows, 0).reshape(
            block_rows, head_count, HEAD
        )
        g_rows = lax.dynamic_slice_in_dim(grad_mixed, offset, block_rows, 0).reshape(
            block_rows, head_count, HEAD
        )
        scores = masked_scores(q_rows, keys_heads, segment, offset, block_rows)
        prob_rows = jnp.exp(scores - log_norm[block_index][..., None])
        grad_values = grad_values + jnp.einsum(
            "hqk,qhd->khd",
            prob_rows.astype(jnp.bfloat16),
            g_rows,
            preferred_element_type=jnp.float32,
        )
        grad_probs = jnp.einsum(
            "qhd,khd->hqk", g_rows, values_heads, preferred_element_type=jnp.float32
        )
        inner_sum = jnp.sum(prob_rows * grad_probs, axis=-1, keepdims=True)
        grad_scores = (prob_rows * (grad_probs - inner_sum) * HEAD ** (-0.5)).astype(jnp.bfloat16)
        grad_query = jnp.einsum(
            "hqk,khd->qhd", grad_scores, keys_heads, preferred_element_type=jnp.float32
        )
        grad_keys = grad_keys + jnp.einsum(
            "hqk,qhd->khd", grad_scores, q_rows, preferred_element_type=jnp.float32
        )
        return (
            (grad_keys, grad_values),
            grad_query.reshape(block_rows, head_count * HEAD).astype(jnp.bfloat16),
        )

    zero_state = jnp.zeros((slot_count, head_count, HEAD), jnp.float32)
    (grad_keys, grad_values), grad_query = lax.scan(
        one_block, (zero_state, zero_state), jnp.arange(slot_count // block_rows, dtype=jnp.int32)
    )
    return (
        grad_query.reshape(slot_count, head_count * HEAD),
        grad_keys.reshape(slot_count, head_count * HEAD).astype(jnp.bfloat16),
        grad_values.reshape(slot_count, head_count * HEAD).astype(jnp.bfloat16),
    )


def on_device_any(
    block_input,
    clip_lengths,
    norm1_gain,
    w_query,
    w_key,
    w_value,
    w_out,
    norm2_gain,
    w_up,
    w_down,
    out_cotangent,
):
    micro_count = block_input.shape[0]
    local_rows = block_input.shape[1]
    tensor_size = lax.axis_size("tensor")
    slot_count = local_rows * tensor_size
    block_rows = min(512, slot_count)
    clip_count = clip_lengths.shape[1]
    row_offset = lax.axis_index("tensor") * local_rows
    places = jnp.arange(slot_count, dtype=jnp.int32)

    def fetch_weights():
        return (
            lax.all_gather(norm1_gain, "dp", axis=0, tiled=True),
            lax.all_gather(norm2_gain, "dp", axis=0, tiled=True),
            lax.all_gather(w_query, "dp", axis=0, tiled=True),
            lax.all_gather(w_key, "dp", axis=0, tiled=True),
            lax.all_gather(w_value, "dp", axis=0, tiled=True),
            lax.all_gather(w_up, "dp", axis=0, tiled=True),
            lax.all_gather(w_out, "dp", axis=1, tiled=True),
            lax.all_gather(w_down, "dp", axis=1, tiled=True),
        )

    def rows_forward(normed):
        return lax.all_gather(normed, "tensor", axis=0, tiled=True)

    def rows_backward(gradients):
        return lax.all_gather(gradients, "tensor", axis=0, tiled=True)

    def sum_forward(term_fn):
        return lax.psum_scatter(
            term_fn(jnp.int32(0), local_rows * lax.axis_size("tensor")),
            "tensor",
            scatter_dimension=0,
            tiled=True,
        )

    def sum_backward(term_fn):
        return lax.psum_scatter(
            term_fn(jnp.int32(0), local_rows * lax.axis_size("tensor")),
            "tensor",
            scatter_dimension=0,
            tiled=True,
        )

    grad_totals = None
    outputs = []
    input_grads = []
    for micro_index in range(micro_count):
        gathered = fetch_weights()
        gain_one = gathered[0].astype(jnp.float32)
        gain_two = gathered[1].astype(jnp.float32)
        query_w, key_w, value_w, up_w, out_w, down_w = (
            gathered[2],
            gathered[3],
            gathered[4],
            gathered[5],
            gathered[6],
            gathered[7],
        )
        tokens = block_input[micro_index].astype(jnp.float32)
        ends = jnp.cumsum(clip_lengths[micro_index])
        segment = jnp.sum((places[:, None] >= ends[None, :]).astype(jnp.int32), axis=1)
        own_segment = lax.dynamic_slice_in_dim(segment, row_offset, local_rows, 0)
        valid_rows = (own_segment < clip_count).astype(jnp.float32)
        normed_one, unit_one, inverse_one = norm_rows(tokens, gain_one)
        features_one = rows_forward(normed_one.astype(jnp.bfloat16))
        query = jnp.dot(features_one, query_w, preferred_element_type=jnp.float32).astype(
            jnp.bfloat16
        )
        key = jnp.dot(features_one, key_w, preferred_element_type=jnp.float32).astype(jnp.bfloat16)
        value = jnp.dot(features_one, value_w, preferred_element_type=jnp.float32).astype(
            jnp.bfloat16
        )
        mixed_rows, log_norm = attend(query, key, value, segment, block_rows)

        def attn_term(offset, row_count):
            return jnp.dot(mixed_rows, out_w, preferred_element_type=jnp.float32)

        hidden = tokens + sum_forward(attn_term)
        normed_two, unit_two, inverse_two = norm_rows(hidden, gain_two)
        features_two = rows_forward(normed_two.astype(jnp.bfloat16))
        pre_act = jnp.dot(features_two, up_w, preferred_element_type=jnp.float32)
        activated = gelu_tanh(pre_act).astype(jnp.bfloat16)

        def mlp_term(offset, row_count):
            return jnp.dot(activated, down_w, preferred_element_type=jnp.float32)

        outputs.append((hidden + sum_forward(mlp_term)).astype(jnp.bfloat16))
        regathered = fetch_weights()
        query_w, key_w, value_w, up_w, out_w, down_w = (
            regathered[2],
            regathered[3],
            regathered[4],
            regathered[5],
            regathered[6],
            regathered[7],
        )
        grad_out = out_cotangent[micro_index].astype(jnp.float32) * valid_rows[:, None]
        grad_branch = rows_backward(grad_out.astype(jnp.bfloat16))
        down_grad = jnp.einsum(
            "sf,sd->fd", activated, grad_branch, preferred_element_type=jnp.float32
        )
        grad_act = jnp.einsum("sd,fd->sf", grad_branch, down_w, preferred_element_type=jnp.float32)
        grad_pre = jax.vjp(gelu_tanh, pre_act)[1](grad_act)[0].astype(jnp.bfloat16)
        up_grad = jnp.einsum(
            "sd,sf->df", features_two, grad_pre, preferred_element_type=jnp.float32
        )

        def up_term(offset, row_count):
            return jnp.einsum("sf,df->sd", grad_pre, up_w, preferred_element_type=jnp.float32)

        grad_normed_two = sum_backward(up_term)
        grad_from_two, gain_two_grad = norm_back(grad_normed_two, unit_two, inverse_two, gain_two)
        grad_hidden = grad_out + grad_from_two
        grad_attn = rows_backward(grad_hidden.astype(jnp.bfloat16))
        out_grad = jnp.einsum(
            "sc,sd->cd", mixed_rows, grad_attn, preferred_element_type=jnp.float32
        )
        grad_mixed = jnp.einsum(
            "sd,cd->sc", grad_attn, out_w, preferred_element_type=jnp.float32
        ).astype(jnp.bfloat16)
        grad_query, grad_key, grad_value = attend_back(
            query, key, value, segment, log_norm, grad_mixed, block_rows
        )
        query_grad = jnp.einsum(
            "sd,sc->dc", features_one, grad_query, preferred_element_type=jnp.float32
        )
        key_grad = jnp.einsum(
            "sd,sc->dc", features_one, grad_key, preferred_element_type=jnp.float32
        )
        value_grad = jnp.einsum(
            "sd,sc->dc", features_one, grad_value, preferred_element_type=jnp.float32
        )

        def qkv_term(offset, row_count):
            part_query = jnp.einsum(
                "sc,dc->sd", grad_query, query_w, preferred_element_type=jnp.float32
            )
            part_key = jnp.einsum("sc,dc->sd", grad_key, key_w, preferred_element_type=jnp.float32)
            part_value = jnp.einsum(
                "sc,dc->sd", grad_value, value_w, preferred_element_type=jnp.float32
            )
            return part_query + part_key + part_value

        grad_normed_one = sum_backward(qkv_term)
        grad_from_one, gain_one_grad = norm_back(grad_normed_one, unit_one, inverse_one, gain_one)
        input_grads.append(grad_hidden + grad_from_one)
        micro_grads = (
            gain_one_grad,
            gain_two_grad,
            query_grad,
            key_grad,
            value_grad,
            up_grad,
            out_grad,
            down_grad,
        )
        if grad_totals is None:
            grad_totals = micro_grads
        else:
            grad_totals = jax.tree.map(jnp.add, grad_totals, micro_grads)
    grad_totals = (
        lax.psum_scatter(
            grad_totals[0].astype(jnp.bfloat16), "dp", scatter_dimension=0, tiled=True
        ).astype(jnp.float32),
        lax.psum_scatter(
            grad_totals[1].astype(jnp.bfloat16), "dp", scatter_dimension=0, tiled=True
        ).astype(jnp.float32),
        lax.psum_scatter(
            grad_totals[2].astype(jnp.bfloat16), "dp", scatter_dimension=0, tiled=True
        ).astype(jnp.float32),
        lax.psum_scatter(
            grad_totals[3].astype(jnp.bfloat16), "dp", scatter_dimension=0, tiled=True
        ).astype(jnp.float32),
        lax.psum_scatter(
            grad_totals[4].astype(jnp.bfloat16), "dp", scatter_dimension=0, tiled=True
        ).astype(jnp.float32),
        lax.psum_scatter(
            grad_totals[5].astype(jnp.bfloat16), "dp", scatter_dimension=0, tiled=True
        ).astype(jnp.float32),
        lax.psum_scatter(
            grad_totals[6].astype(jnp.bfloat16), "dp", scatter_dimension=1, tiled=True
        ).astype(jnp.float32),
        lax.psum_scatter(
            grad_totals[7].astype(jnp.bfloat16), "dp", scatter_dimension=1, tiled=True
        ).astype(jnp.float32),
    )
    gain_sums = lax.psum((grad_totals[0], grad_totals[1]), "tensor")
    return (
        jnp.stack(outputs),
        jnp.stack(input_grads),
        gain_sums[0],
        grad_totals[2],
        grad_totals[3],
        grad_totals[4],
        grad_totals[6],
        gain_sums[1],
        grad_totals[5],
        grad_totals[7],
    )


def chunk_scores(q, k, start, s, c, rows):
    scores = lax.dot_general(
        q, k, (((1,), (1,)), ((), ())), preferred_element_type=f32
    ) * HEAD ** (-0.5)
    k_place = c * rows + lax.broadcasted_iota(jnp.int32, (rows, rows), 1)
    allowed = k_place >= start
    if c == s:
        q_place = s * rows + lax.broadcasted_iota(jnp.int32, (rows, rows), 0)
        allowed = jnp.logical_and(allowed, k_place <= q_place)
    return jnp.where(allowed, scores, masked_fill)


def clip_starts(ends_ref, first, buffer, clip_count, s, rows):
    place = s * rows + lax.broadcasted_iota(jnp.int32, (rows, 1), 0)
    start = jnp.zeros((rows, 1), jnp.int32)
    for clip in range(clip_count):
        end = ends_ref[first + buffer * clip_count + clip]
        start = jnp.where(place >= end, jnp.maximum(start, end), start)
    return start


def window(s, rows):
    back = -(-(LONGEST - 1) // rows)
    return range(max(0, s - back), s + 1)


def chunk_probs(q, keys, start, s, rows):
    cs = list(window(s, rows))
    scores = [chunk_scores(q, keys(c), start, s, c, rows) for c in cs]
    highest = functools.reduce(jnp.maximum, [jnp.max(v, axis=1, keepdims=True) for v in scores])
    shifted = [jnp.exp(v - highest) for v in scores]
    total = functools.reduce(jnp.add, [jnp.sum(v, axis=1, keepdims=True) for v in shifted])
    scale = 1.0 / total
    return cs, [v * scale for v in shifted]


MESH = pl.DeviceIdType.MESH
N_TILE = 1024


class Plane:
    def __init__(self, send_sems, recv_sems, more=()):
        me = lax.axis_index("dp")
        self.core = me % 2
        self.x = (me // 2) % 2
        self.peers = {
            "c": me + 1 - 2 * (me % 2),
            "x": me + 2 - 4 * ((me // 2) % 2),
            "y": me + 4 - 8 * ((me // 4) % 2),
        }
        self.send_sems, self.recv_sems = send_sems, recv_sems
        self.copies = []
        barrier = pltpu.get_barrier_semaphore()
        for peer in self.peers.values():
            pl.semaphore_signal(barrier, inc=1, device_id={"dp": peer}, device_id_type=MESH)
        for place in more:
            pl.semaphore_signal(barrier, inc=1, device_id=at_device(place), device_id_type=MESH)
        pl.semaphore_wait(barrier, 3 + len(more))

    def send(self, src, dst, way):
        return self.send_to(src, dst, {"dp": self.peers[way]})

    def send_to(self, src, dst, device):
        index = len(self.copies)
        copy = pltpu.make_async_remote_copy(
            src_ref=src,
            dst_ref=dst,
            send_sem=self.send_sems.at[index],
            recv_sem=self.recv_sems.at[index],
            device_id=device,
            device_id_type=MESH,
        )
        copy.start()
        self.copies.append(copy)
        return copy

    def finish(self):
        for copy in self.copies:
            copy.wait_send()


class Gather:
    def __init__(self, plane, own, pieces):
        self.plane, self.own, self.pieces = plane, own, pieces
        self.half = own.shape[0] // 2

    def begin(self):
        self.begin_links()
        self.begin_core()

    def begin_links(self):
        self.x = self.plane.send(self.own, self.pieces.at[1], "x")
        self.y = self.plane.send(self.own, self.pieces.at[2], "y")

    def begin_core(self):
        self.c = [self.plane.send(self.own, self.pieces.at[4], "c")]

    def middle(self):
        send, half, pieces = self.plane.send, self.half, self.pieces
        self.x.wait_recv()
        self.fy = send(pieces.at[1, pl.ds(half, half)], pieces.at[3, pl.ds(half, half)], "y")
        self.c.append(send(pieces.at[1], pieces.at[5], "c"))
        self.y.wait_recv()
        self.fx = send(pieces.at[2, pl.ds(0, half)], pieces.at[3, pl.ds(0, half)], "x")
        self.c.append(send(pieces.at[2], pieces.at[6], "c"))

    def end(self):
        self.fx.wait_recv()
        self.fy.wait_recv()
        self.c.append(self.plane.send(self.pieces.at[3], self.pieces.at[7], "c"))

    def core(self, index):
        self.c[index].wait_recv()


class Reduce:
    def __init__(self, plane, pieces, from_core, from_x, from_y):
        self.plane, self.pieces = plane, pieces
        self.from_core, self.from_x, self.from_y = from_core, from_x, from_y
        self.half = pieces.shape[1] // 2
        self.core = {}

    def give(self, m):
        self.core[m] = self.plane.send(self.pieces.at[4 + m], self.from_core.at[m], "c")

    def take(self, m):
        self.core[m].wait_recv()

    def chip_done(self, m):
        send, half, pieces = self.plane.send, self.half, self.pieces
        low, high = pl.ds(0, half), pl.ds(half, half)
        if m == 3:
            self.far_x = send(pieces.at[3, low], self.from_x.at[1], "x")
            self.far_y = send(pieces.at[3, high], self.from_y.at[1], "y")
        elif m == 1:
            self.near_x = send(pieces.at[1, low], self.from_x.at[0], "x")
        elif m == 2:
            self.near_y = send(pieces.at[2, high], self.from_y.at[0], "y")

    def late_x(self):
        high = pl.ds(self.half, self.half)
        self.far_y.wait_recv()
        add_into(self.pieces.at[1, high], self.from_y.at[1])
        self.late_x_copy = self.plane.send(self.pieces.at[1, high], self.from_x.at[2], "x")

    def late_y(self):
        low = pl.ds(0, self.half)
        self.far_x.wait_recv()
        add_into(self.pieces.at[2, low], self.from_x.at[1])
        self.late_y_copy = self.plane.send(self.pieces.at[2, low], self.from_y.at[2], "y")

    def late(self):
        self.late_x()
        self.late_y()

    def total(self, out):
        half = self.half
        self.near_x.wait_recv()
        self.near_y.wait_recv()
        self.late_x_copy.wait_recv()
        self.late_y_copy.wait_recv()
        step = min(64, half)

        for base, x_part, y_part in ((0, 0, 2), (half, 2, 0)):

            def add(index, carry):
                at = pl.ds(pl.multiple_of(index * step, step), step)
                here = pl.ds(pl.multiple_of(base + index * step, step), step)
                out[here] = (
                    self.pieces[0, here].astype(f32)
                    + self.from_x[x_part, at].astype(f32)
                    + self.from_y[y_part, at].astype(f32)
                )
                return carry

            lax.fori_loop(0, half // step, add, 0)


def add_into(ref, other):
    step = min(64, ref.shape[0])

    def add(index, carry):
        at = pl.ds(pl.multiple_of(index * step, step), step)
        ref[at] = (ref[at].astype(f32) + other[at].astype(f32)).astype(bf16)
        return carry

    lax.fori_loop(0, ref.shape[0] // step, add, 0)


ORDER = (3, 1, 2, 0)


def tiles(count, tile, body):
    tile = min(tile, count)

    def step(index, carry):
        body(pl.ds(pl.multiple_of(index * tile, tile), tile))
        return carry

    lax.fori_loop(0, count // tile, step, 0)


def nn(left, right):
    return jnp.dot(left, right, preferred_element_type=f32)


def nt(left, right):
    return lax.dot_general(left, right, (((1,), (1,)), ((), ())), preferred_element_type=f32)


def tn(left, right):
    return lax.dot_general(left, right, (((0,), (0,)), ((), ())), preferred_element_type=f32)


class Feed:
    def __init__(self, source, slots, sems, order):
        self.source, self.slots, self.sems, self.order = source, slots, sems, list(order)

    def copy(self, index):
        slot = index % 2
        return pltpu.make_async_copy(
            self.source(self.order[index]), self.slots.at[slot], self.sems.at[slot]
        )

    def start(self, index):
        if index < len(self.order):
            self.copy(index).start()

    def get(self, index):
        self.copy(index).wait()
        return self.slots.at[index % 2]


def plane_call(kernel, name, collective_id, out_shape, in_spaces, out_spaces, scratch, copies, flops, args):
    spaces = {"any": pl.ANY, "vmem": pltpu.VMEM, "smem": pltpu.SMEM}
    return pl.pallas_call(
        kernel,
        out_shape=out_shape,
        in_specs=[pl.BlockSpec(memory_space=spaces[v]) for v in in_spaces],
        out_specs=[pl.BlockSpec(memory_space=spaces[v]) for v in out_spaces],
        scratch_shapes=list(scratch)
        + [pltpu.SemaphoreType.DMA((copies,)), pltpu.SemaphoreType.DMA((copies,))],
        compiler_params=pltpu.CompilerParams(
            collective_id=collective_id, has_side_effects=True, vmem_limit_bytes=62 << 20
        ),
        cost_estimate=pl.CostEstimate(flops=flops, bytes_accessed=64 << 20, transcendentals=0),
        name=name,
    )(*args)


def row_places():
    me, plane = lax.axis_index("dp"), lax.axis_index("tensor")
    chip, core = 2 * (me // 2), me % 2
    outward = [(chip + 1 - plane // 2, 2 * core + j) for j in range(2)]
    inward = [(chip + plane // 2, 2 * (1 - core) + i) for i in range(2)]
    return outward, inward


def at_device(place):
    return {"dp": place[0], "tensor": place[1]}


class RowMove:
    def __init__(self, src, dst, sems):
        self.src, self.dst, self.sems = src, dst, sems
        self.copies = []

    def copy(self, here, there, place):
        return pltpu.make_async_remote_copy(
            src_ref=self.src.at[here],
            dst_ref=self.dst.at[there],
            send_sem=self.sems.at[0, here],
            recv_sem=self.sems.at[1, there],
            device_id=at_device(place),
            device_id_type=MESH,
        )

    def start(self, places, there):
        for here in range(2):
            copy = self.copy(here, there, places[here])
            copy.start()
            self.copies.append(copy)
        self.arrivals = [self.copy(index, index, places[index]) for index in range(2)]

    def outward(self):
        self.start(row_places()[0], lax.axis_index("tensor") % 2)

    def back(self):
        self.start(row_places()[1], lax.axis_index("tensor") % 2)

    def wait(self):
        for copy in self.copies:
            copy.wait_send()
        for copy in self.arrivals:
            copy.wait_recv()


def start_kernel(
    tokens, w_query, w_key, w_value, w_out, w_up, w_down, small,
    tokens_out, qkv_out, out_out, up_out, down_out, small_out,
    local_sems, row_sems, send_sems, recv_sems,
):
    me, plane = lax.axis_index("dp"), lax.axis_index("tensor")
    chip, core = me // 2, me % 2
    depth = w_query.shape[0]
    part = up_out.shape[1]
    outward, inward = row_places()
    peers = [lax.rem(me + j, 8) for j in range(1, 8)]
    barrier = pltpu.get_barrier_semaphore()
    for peer in peers:
        pl.semaphore_signal(barrier, inc=1, device_id={"dp": peer}, device_id_type=MESH)
    for place in outward + inward:
        pl.semaphore_signal(barrier, inc=1, device_id=at_device(place), device_id_type=MESH)
    pl.semaphore_wait(barrier, 11)
    copies, locals_ = [], []

    def send(src, dst, device):
        copy = pltpu.make_async_remote_copy(
            src_ref=src,
            dst_ref=dst,
            send_sem=send_sems.at[len(copies)],
            recv_sem=recv_sems.at[len(copies)],
            device_id=device,
            device_id_type=MESH,
        )
        copy.start()
        copies.append(copy)

    def keep(src, dst):
        copy = pltpu.make_async_copy(src, dst, local_sems.at[len(locals_)])
        copy.start()
        locals_.append(copy)

    def block(index, size):
        return pl.ds(pl.multiple_of(index * size, size), size)

    rows_move = RowMove(tokens, tokens_out, row_sems)
    rows_move.outward()
    for peer in peers:
        send(small, small_out.at[me], {"dp": peer})
    keep(small, small_out.at[me])
    heads = [(w_query, 0), (w_key, 1), (w_value, 2)]
    for j in range(1, 4):
        other = lax.rem(chip + j, 4)
        device = {"dp": 2 * other + core}
        for weight, which in heads:
            send(weight.at[:, block(other, HEAD)], qkv_out.at[which, chip], device)
    for weight, which in heads:
        keep(weight.at[:, block(chip, HEAD)], qkv_out.at[which, chip])
    for j in range(1, 4):
        other = lax.rem(chip + j, 4)
        send(w_out.at[block(other, HEAD)], out_out.at[chip], {"dp": 2 * other + core})
    keep(w_out.at[block(chip, HEAD)], out_out.at[chip])
    for peer in peers:
        send(w_up.at[:, block(peer, part)], up_out.at[block(me, depth)], {"dp": peer})
        send(w_down.at[block(peer, part)], down_out.at[:, block(me, depth)], {"dp": peer})
    keep(w_up.at[:, block(me, part)], up_out.at[block(me, depth)])
    keep(w_down.at[block(me, part)], down_out.at[:, block(me, depth)])
    for copy in locals_:
        copy.wait()
    for copy in copies:
        copy.wait()
    rows_move.wait()


def gather_kernel(own, rows_in, pieces, rows_out, own_sem, row_sems, send_sems, recv_sems):
    outward, inward = row_places()
    plane = Plane(send_sems, recv_sems, outward + inward)
    streams = own.shape[0]
    rows_move = RowMove(rows_in, rows_out, row_sems)
    rows_move.outward()
    gathers = [Gather(plane, own.at[s], pieces.at[s]) for s in range(streams)]
    keep = [pltpu.make_async_copy(own.at[s], pieces.at[s, 0], own_sem.at[s]) for s in range(streams)]
    for s in range(streams):
        gathers[s].begin()
        keep[s].start()
    for s in range(streams):
        gathers[s].middle()
    for s in range(streams):
        gathers[s].end()
    for s in range(streams):
        keep[s].wait()
        for index in range(4):
            gathers[s].core(index)
    rows_move.wait()
    plane.finish()


def chunk_at(plane, s):
    k = 1 - s // 2
    return s % 2, k + plane.core - 2 * k * plane.core


def chunk_part(plane, qkv, chip, head):
    def part(s, which):
        column = pl.multiple_of((head * 3 + which) * HEAD, HEAD)
        stream, core = chunk_at(plane, s)
        piece = core * (qkv.shape[1] // 2) + chip
        return qkv[stream, piece, :, pl.ds(column, HEAD)]

    return part


def attend_all(plane, qkv, ends_ref, out, clip_count):
    rows = qkv.shape[2]
    heads = qkv.shape[3] // (3 * HEAD)

    def one(index, carry):
        chip, head = index // heads, index % heads
        part = chunk_part(plane, qkv, chip, head)
        column = pl.ds(pl.multiple_of(head * HEAD, HEAD), HEAD)
        for s in range(4):
            start = clip_starts(ends_ref, 0, chip, clip_count, s, rows)
            cs, probs = chunk_probs(part(s, 0), lambda c: part(c, 1), start, s, rows)
            mixed = jnp.zeros((rows, HEAD), f32)
            for c, prob in zip(cs, probs):
                mixed = mixed + nn(prob.astype(bf16), part(c, 2))
            stream, core = chunk_at(plane, s)
            out[stream, core * 4 + chip, :, column] = mixed.astype(bf16)
        return carry

    return one


def attend_back_chip(plane, qkv, grad_mixed, ends_ref, out, key_sum, value_sum, clip_count, chip):
    rows = qkv.shape[2]
    heads = qkv.shape[3] // (3 * HEAD)

    def one(head, carry):
        part = chunk_part(plane, qkv, 0, head)
        column = pl.ds(pl.multiple_of(head * HEAD, HEAD), HEAD)
        key_sum[...] = jnp.zeros_like(key_sum)
        value_sum[...] = jnp.zeros_like(value_sum)

        def put(s, which, value):
            at = pl.ds(pl.multiple_of((head * 3 + which) * HEAD, HEAD), HEAD)
            stream, core = chunk_at(plane, s)
            out[stream, core, :, at] = value.astype(bf16)

        for s in range(4):
            q = part(s, 0)
            stream, core = chunk_at(plane, s)
            g = grad_mixed[stream, core * 4 + chip, :, column]
            start = clip_starts(ends_ref, 0, chip, clip_count, s, rows)
            cs, probs = chunk_probs(q, lambda c: part(c, 1), start, s, rows)
            grad_probs = [nt(g, part(c, 2)) for c in cs]
            inner = functools.reduce(
                jnp.add,
                [jnp.sum(p * v, axis=1, keepdims=True) for p, v in zip(probs, grad_probs)],
            )
            grad_q = jnp.zeros((rows, HEAD), f32)
            for c, prob, grad_prob in zip(cs, probs, grad_probs):
                grad_score = (prob * (grad_prob - inner) * HEAD ** (-0.5)).astype(bf16)
                grad_q = grad_q + nn(grad_score, part(c, 1))
                key_sum[c] += tn(grad_score, q)
                value_sum[c] += tn(prob.astype(bf16), g)
            put(s, 0, grad_q)
        for s in range(4):
            put(s, 1, key_sum[s])
            put(s, 2, value_sum[s])
        return carry

    lax.fori_loop(0, heads, one, 0)


def attention_kernel(
    clip_count, own, rows_in, wide, ends, pieces, qkv, mixed, weight, slots, slot_sems, own_sem, wide_sems, send_sems, recv_sems
):
    plane = Plane(send_sems, recv_sems)
    streams = own.shape[0]
    gathers = [Gather(plane, own.at[s], pieces.at[s]) for s in range(streams)]
    keep = [pltpu.make_async_copy(own.at[s], pieces.at[s, 0], own_sem.at[s]) for s in range(streams)]
    traded, kept = [], []
    for head in range(2):
        for which in range(3):
            column = pl.ds((head * 3 + which) * HEAD, HEAD)
            here = weight.at[:, plane.core, :, column]
            traded.append(plane.send(wide.at[2 * (1 - plane.core) + head, which], here, "c"))
            copy = pltpu.make_async_copy(
                wide.at[2 * plane.core + head, which], here, wide_sems.at[len(kept)]
            )
            copy.start()
            kept.append(copy)
    for s in range(streams):
        gathers[s].begin()
        keep[s].start()
    total = weight.shape[3]
    feed = Feed(
        lambda at: rows_in.at[at[0], at[1]],
        slots,
        slot_sems,
        [(s, p) for s in range(streams) for p in range(8)],
    )
    feed.start(0)

    def project(s):
        for p in range(8):
            feed.start(s * 8 + p + 1)
            piece = feed.get(s * 8 + p)

            def tile(at):
                columns = weight[:, :, :, at].reshape(width, -1)
                qkv[s, p, :, at] = nn(piece[...], columns).astype(bf16)

            tiles(total, N_TILE, tile)

    for copy in traded:
        copy.wait_recv()
    for copy in kept:
        copy.wait()
    width = own.shape[2]

    attend = attend_all(plane, qkv, ends, mixed, clip_count)
    heads = total // (3 * HEAD)
    project(0)
    project(1)
    lax.fori_loop(0, 2 * heads, attend, 0)
    gathers[0].middle()
    gathers[1].middle()
    lax.fori_loop(2 * heads, 4 * heads, attend, 0)
    gathers[0].end()
    gathers[1].end()
    for s in range(streams):
        keep[s].wait()
        for index in range(4):
            gathers[s].core(index)
    plane.finish()


def reduce_scratch(streams, rows, width):
    return [
        pltpu.VMEM((streams, 8, rows, width), bf16),
        pltpu.VMEM((streams, 4, rows, width), bf16),
        pltpu.VMEM((streams, 3, rows // 2, width), bf16),
        pltpu.VMEM((streams, 3, rows // 2, width), bf16),
    ]


def project_kernel(
    mixed, wide, out, weight, parts, from_core, from_x, from_y, wide_sems, send_sems, recv_sems
):
    plane = Plane(send_sems, recv_sems)
    streams = mixed.shape[0]
    width = weight.shape[1]
    depth = wide.shape[3]
    traded, kept = [], []
    for head in range(2):
        for chip in range(4):
            column = pl.ds(pl.multiple_of((2 * chip + plane.core) * depth, depth), depth)
            here = weight.at[pl.ds(head * HEAD, HEAD), column]
            traded.append(plane.send(wide.at[2 * (1 - plane.core) + head, chip], here, "c"))
            copy = pltpu.make_async_copy(
                wide.at[2 * plane.core + head, chip], here, wide_sems.at[len(kept)]
            )
            copy.start()
            kept.append(copy)
    for copy in traded:
        copy.wait_recv()
    for copy in kept:
        copy.wait()
    sums = [
        Reduce(plane, parts.at[s], from_core.at[s], from_x.at[s], from_y.at[s])
        for s in range(streams)
    ]

    for s in range(streams):
        for m in ORDER:

            def other(at):
                parts[s, 4 + m, :, at] = nn(mixed[s, 4 + m], weight[:, at]).astype(bf16)

            tiles(width, N_TILE, other)
            sums[s].give(m)
        for m in ORDER:
            sums[s].take(m)

            def chip(at):
                here = nn(mixed[s, m], weight[:, at])
                parts[s, m, :, at] = (here + from_core[s, m, :, at].astype(f32)).astype(bf16)

            tiles(width, N_TILE, chip)
            sums[s].chip_done(m)
        if s > 0:
            sums[s - 1].late()
    sums[streams - 1].late()
    for s in range(streams):
        sums[s].total(out.at[s])
    plane.finish()


def gelu_pair(v):
    cubic = 0.044715 * (v * v) * v
    inner = (2.0 / np.pi) ** 0.5 * (v + cubic)
    th = jnp.tanh(inner)
    half = 0.5 * (1.0 + th)
    slope = (2.0 / np.pi) ** 0.5 * (1.0 + 3.0 * 0.044715 * (v * v))
    return v * half, half + 0.5 * v * (1.0 - th * th) * slope


def lay_out(wide, flat, sems):
    copies = []
    part = wide.shape[2]
    for plane in range(wide.shape[0]):
        copy = pltpu.make_async_copy(
            wide.at[plane], flat.at[:, pl.ds(plane * part, part)], sems.at[plane]
        )
        copy.start()
        copies.append(copy)
    return copies


def mlp_kernel(
    own, up_wide, down_w, grads, pieces, slope_out, down_grad, out,
    parts, from_core, from_x, from_y, up_w, slots, act, slope, total, grad_slots,
    up_sems, slot_sems, keep_sems, own_sem, grad_sems, send_sems, recv_sems,
):
    plane = Plane(send_sems, recv_sems)
    streams, rows, width = own.shape
    hidden = up_w.shape[1]
    up_copies = lay_out(up_wide, up_w, up_sems)
    gathers = [Gather(plane, own.at[s], pieces.at[s]) for s in range(streams)]
    sums = [
        Reduce(plane, parts.at[s], from_core.at[s], from_x.at[s], from_y.at[s])
        for s in range(streams)
    ]
    keep = [pltpu.make_async_copy(own.at[s], pieces.at[s, 0], own_sem.at[s]) for s in range(streams)]
    stores = []

    def up_piece(s, p, slot):
        if len(stores) >= 2:
            stores[-2].wait()

        def up(at):
            value, grad = gelu_pair(nn(slots[slot], up_w[:, at]))
            act[slot, :, at] = value.astype(bf16)
            slope[slot, :, at] = grad.astype(bf16)

        tiles(hidden, N_TILE, up)
        store = pltpu.make_async_copy(slope.at[slot], slope_out.at[s, p], keep_sems.at[slot])
        store.start()
        stores.append(store)

    def down_piece(s, p, slot):
        def down(at):
            here = nn(act[slot], down_w[:, at])
            if p < 4:
                here = here + from_core[s, p, :, at].astype(f32)
            parts[s, p, :, at] = here.astype(bf16)

        tiles(width, N_TILE, down)

    def pair_up(s, m):
        if m > 0:
            gathers[s].core(m)
        first = not stores
        rows_come = [
            pltpu.make_async_copy(
                own.at[s] if p == 0 else pieces.at[s, p], slots.at[i], slot_sems.at[i]
            )
            for i, p in enumerate((4 + m, m))
        ]
        coming = [
            pltpu.make_async_copy(grads.at[s, p], grad_slots.at[i], grad_sems.at[i])
            for i, p in enumerate((4 + m, m))
        ]
        if m == 0:
            rows_come[1].start()
            gathers[s].core(0)
            rows_come[0].start()
        else:
            rows_come[0].start()
            rows_come[1].start()
        for copy in coming:
            copy.start()
        rows_come[0].wait()
        up_piece(s, 4 + m, 0)
        down_piece(s, 4 + m, 0)
        sums[s].give(m)
        rows_come[1].wait()
        up_piece(s, m, 1)
        for copy in coming:
            copy.wait()
        left = act[...].reshape(2 * rows, hidden)

        def weigh(at):
            term = tn(left, grad_slots[:, :, at].reshape(2 * rows, -1))
            total[:, at] = term if first else total[:, at] + term

        tiles(width, 512, weigh)
        sums[s].take(m)
        down_piece(s, m, 1)
        sums[s].chip_done(m)

    for s in range(streams):
        keep[s].start()
        gathers[s].begin_core()
    gathers[0].begin_links()
    for copy in up_copies:
        copy.wait()
    pair_up(0, 0)
    pair_up(1, 0)
    gathers[0].middle()
    gathers[1].begin_links()
    pair_up(0, 1)
    pair_up(0, 2)
    gathers[0].end()
    pair_up(0, 3)
    gathers[1].middle()
    pair_up(1, 1)
    sums[0].late()
    gathers[1].end()
    pair_up(1, 3)
    pair_up(1, 2)
    sums[1].late()
    for s in range(streams):
        sums[s].total(out.at[s])
        keep[s].wait()
    for store in stores[-2:]:
        store.wait()
    stores = []
    for index in range(hidden // rows):
        if index >= 2:
            stores[index - 2].wait()
        here = pl.ds(index * rows, rows)
        slots[index % 2] = total[here].astype(bf16)
        store = pltpu.make_async_copy(
            slots.at[index % 2], down_grad.at[here], keep_sems.at[index % 2]
        )
        store.start()
        stores.append(store)
    for store in stores[-2:]:
        store.wait()
    plane.finish()


def mlp_back_kernel(
    grads, slope_in, features, up_wide, down_w, up_grad, out,
    parts, from_core, from_x, from_y, up_w, slots, slopes, pre, rows_two, total,
    up_sems, slot_sems, slope_sems, row_sems, keep_sems, send_sems, recv_sems,
):
    plane = Plane(send_sems, recv_sems)
    streams, _, rows, width = grads.shape
    hidden = up_w.shape[1]
    part = up_wide.shape[2]
    up_copies = lay_out(up_wide, up_w, up_sems)
    sums = [
        Reduce(plane, parts.at[s], from_core.at[s], from_x.at[s], from_y.at[s])
        for s in range(streams)
    ]
    order = [(s, p) for s in range(streams) for m in ORDER for p in (4 + m, m)]
    feed = Feed(lambda at: grads.at[at[0], at[1]], slots, slot_sems, order)
    feed_slope = Feed(lambda at: slope_in.at[at[0], at[1]], slopes, slope_sems, order)
    feed_rows = Feed(lambda at: features.at[at[0], at[1]], rows_two, row_sems, order)
    feed.start(0)
    feed_slope.start(0)
    def back_piece(index):
        feed.start(index + 1)
        feed_slope.start(index + 1)
        feed_rows.start(index)
        grad = feed.get(index)
        slope = feed_slope.get(index)

        def back(at):
            value = nt(grad[...], down_w[at]) * slope[:, at].astype(f32)
            pre[index % 2, :, at] = value.astype(bf16)

        tiles(hidden, N_TILE, back)

    def through_piece(index, s, p):
        def through(at):
            here = nt(pre[index % 2], up_w[at])
            if p < 4:
                here = here + from_core[s, p, :, at].astype(f32)
            parts[s, p, :, at] = here.astype(bf16)

        tiles(width, N_TILE, through)

    for index, (s, p) in enumerate(order):
        back_piece(index)
        if index == 0:
            for copy in up_copies:
                copy.wait()
        if p >= 4:
            through_piece(index, s, p)
            sums[s].give(p - 4)
            continue
        feed_rows.get(index - 1)
        feed_rows.get(index)
        right = pre[...].reshape(2 * rows, hidden)

        def weigh(at):
            term = tn(rows_two[:, :, at].reshape(2 * rows, -1), right)
            total[at] = term if index == 1 else total[at] + term

        tiles(width, 512, weigh)
        sums[s].take(p)
        through_piece(index, s, p)
        sums[s].chip_done(p)
        if p == 2:
            sums[s].late_x()
        if p == 0:
            sums[s].late_y()
    stores = []
    for index in range(width // rows):
        slot = index % 2
        for store in stores[index - 2] if index >= 2 else []:
            store.wait()
        here = pl.ds(index * rows, rows)
        pre[slot] = total[here].astype(bf16)
        stores.append([])
        for at in range(hidden // part):
            store = pltpu.make_async_copy(
                pre.at[slot, :, pl.ds(at * part, part)], up_grad.at[at, here], keep_sems.at[slot, at]
            )
            store.start()
            stores[-1].append(store)
    for s in range(streams):
        sums[s].total(out.at[s])
    for pair in stores[-2:]:
        for store in pair:
            store.wait()
    plane.finish()


MIX_ORDER = ((0, (0,)), (1, (0,)), (0, (1, 2, 3)), (1, (1, 2, 3)))


def attention_back_kernel(
    clip_count, own, qkv, mixed, features, rows_in, qkv_w, out_w, ends,
    pieces, qkv_grad, out_grad, rows_out, out,
    parts, from_core, from_x, from_y, slots, mixed_slots, grad_mixed, qkv_chip, grad_chip, key_sum, value_sum,
    qkv_sum, out_sum, slot_sems, mixed_sems, chip_sems, store_sems, row_sems, own_sem, send_sems, recv_sems,
):
    outward, inward = row_places()
    plane = Plane(send_sems, recv_sems, outward + inward)
    rows_move = RowMove(rows_in, rows_out, row_sems)
    rows_move.back()
    streams, rows, width = own.shape
    gathers = [Gather(plane, own.at[s], pieces.at[s]) for s in range(streams)]
    sums = [
        Reduce(plane, parts.at[s], from_core.at[s], from_x.at[s], from_y.at[s])
        for s in range(streams)
    ]
    keep = [pltpu.make_async_copy(own.at[s], pieces.at[s, 0], own_sem.at[s]) for s in range(streams)]
    order = [(s, p) for s, ms in MIX_ORDER for m in ms for p in (m, 4 + m)]
    feed_mixed = Feed(lambda at: mixed.at[at[0], at[1]], mixed_slots, mixed_sems, order)
    feed_mixed.start(0)
    done = [0]

    def mix(s, p):
        index = done[0]
        done[0] += 1
        feed_mixed.start(index + 1)
        slot = index % 2
        source = own.at[s] if p == 0 else pieces.at[s, p]
        copy = pltpu.make_async_copy(source, slots.at[slot], slot_sems.at[slot])
        copy.start()
        left = feed_mixed.get(index)
        copy.wait()
        grad_mixed[s, p] = nt(slots[slot], out_w[...]).astype(bf16)

        def weigh(at):
            term = tn(left[...], slots[slot, :, at])
            out_sum[:, at] = term if index == 0 else out_sum[:, at] + term

        tiles(width, N_TILE, weigh)

    def load_chip(m):
        copies = [
            pltpu.make_async_copy(
                qkv.at[s, core * 4 + m], qkv_chip.at[s, core], chip_sems.at[s * 2 + core]
            )
            for s in range(streams)
            for core in range(2)
        ]
        for copy in copies:
            copy.start()
        return copies

    def load_rows(m):
        copies = [
            pltpu.make_async_copy(
                features.at[s, core * 4 + m], slots.at[s * 2 + core], slot_sems.at[s * 2 + core]
            )
            for s in range(streams)
            for core in range(2)
        ]
        for copy in copies:
            copy.start()
        return copies

    def weigh_chip(place, copies):
        for copy in copies:
            copy.wait()
        right = grad_chip[place % 2].reshape(4 * rows, -1)

        def weigh(at):
            term = tn(slots[:, :, at].reshape(4 * rows, -1), right)
            qkv_sum[at] = term if place == 0 else qkv_sum[at] + term

        tiles(width, 512, weigh)

    def mix_pair(s, m):
        mix(s, m)
        gathers[s].core(m)
        mix(s, 4 + m)

    def attend_chip(place, m, coming, following):
        for copy in coming:
            copy.wait()
        grad_here = grad_chip.at[place % 2]
        attend_back_chip(
            plane, qkv_chip, grad_mixed, ends, grad_here, key_sum, value_sum, clip_count, m
        )
        coming = load_chip(following) if following is not None else []
        for s in range(streams):

            def other(at):
                parts[s, 4 + m, :, at] = nt(grad_here[s, 1], qkv_w[at]).astype(bf16)

            tiles(width, N_TILE, other)
            sums[s].give(m)
        for s in range(streams):
            sums[s].take(m)

            def chip(at):
                here = nt(grad_here[s, 0], qkv_w[at])
                parts[s, m, :, at] = (here + from_core[s, m, :, at].astype(f32)).astype(bf16)

            tiles(width, N_TILE, chip)
            sums[s].chip_done(m)
        return coming

    for s in range(streams):
        keep[s].start()
        gathers[s].begin_core()
    gathers[0].begin_links()
    coming = load_chip(0)
    mix_pair(0, 0)
    mix_pair(1, 0)
    coming = attend_chip(0, 0, coming, 1)
    gathers[0].middle()
    gathers[1].begin_links()
    mix_pair(0, 1)
    mix_pair(0, 2)
    weigh_chip(0, load_rows(0))
    gathers[0].end()
    mix_pair(0, 3)
    gathers[1].middle()
    mix_pair(1, 1)
    mix_pair(1, 2)
    coming = attend_chip(1, 1, coming, 3)
    gathers[1].end()
    mix_pair(1, 3)
    coming_rows = load_rows(1)
    coming = attend_chip(2, 3, coming, 2)
    weigh_chip(1, coming_rows)
    coming_rows = load_rows(3)
    attend_chip(3, 2, coming, None)
    for s in range(streams):
        sums[s].late_x()
    for s in range(streams):
        sums[s].late_y()
    weigh_chip(2, coming_rows)
    weigh_chip(3, load_rows(2))
    for index in range(out_sum.shape[0] // rows):
        here = pl.ds(index * rows, rows)
        slots[0] = out_sum[here].astype(bf16)
        out_store = pltpu.make_async_copy(slots.at[0], out_grad.at[here], slot_sems.at[0])
        out_store.start()
        out_store.wait()
    stores = []
    for index in range(width // rows):
        if index >= 4:
            stores[index - 4].wait()
        here = pl.ds(index * rows, rows)
        stage = grad_chip.at[0, index // 2 % 2, index % 2]
        stage[...] = qkv_sum[here].astype(bf16)
        store = pltpu.make_async_copy(stage, qkv_grad.at[here], store_sems.at[index % 4])
        store.start()
        stores.append(store)
    for s in range(streams):
        sums[s].total(out.at[s])
        keep[s].wait()
    for store in stores[-4:]:
        store.wait()
    rows_move.wait()
    plane.finish()


def end_kernel(
    rows_in, qkv_grad, out_grad, up_sum, down_sum, gains,
    rows_out, qkv_out, out_out, up_out, down_out, gains_out,
    qkv_part, out_part, qkv_come, out_come, gain_come, gain_sum, gain_all,
    local_sems, row_sems, send_sems, recv_sems,
):
    me, z = lax.axis_index("dp"), lax.axis_index("tensor")
    chip, core = me // 2, me % 2
    depth = qkv_grad.shape[2]
    outward, inward = row_places()
    peers = [lax.rem(me + j, 8) for j in range(1, 8)]
    planes = [lax.rem(z + j, 4) for j in range(1, 4)]
    barrier = pltpu.get_barrier_semaphore()
    for peer in peers:
        pl.semaphore_signal(barrier, inc=1, device_id={"dp": peer}, device_id_type=MESH)
    for plane in planes:
        pl.semaphore_signal(barrier, inc=1, device_id={"tensor": plane}, device_id_type=MESH)
    for place in outward + inward:
        pl.semaphore_signal(barrier, inc=1, device_id=at_device(place), device_id_type=MESH)
    pl.semaphore_wait(barrier, 14)
    copies, locals_ = [], []

    def send(src, dst, device):
        copy = pltpu.make_async_remote_copy(
            src_ref=src,
            dst_ref=dst,
            send_sem=send_sems.at[len(copies)],
            recv_sem=recv_sems.at[len(copies)],
            device_id=device,
            device_id_type=MESH,
        )
        copy.start()
        copies.append(copy)
        return copy

    def keep(src, dst):
        copy = pltpu.make_async_copy(src, dst, local_sems.at[len(locals_)])
        copy.start()
        locals_.append(copy)

    def block(index, size):
        return pl.ds(pl.multiple_of(index * size, size), size)

    other = {"dp": me + 1 - 2 * core}
    traded = []
    for head in range(2):
        mine = 2 * core + head
        for which in range(3):
            column = pl.ds((head * 3 + which) * HEAD, HEAD)
            traded.append(
                send(qkv_grad.at[:, 1 - core, :, column], qkv_part.at[mine, which], other)
            )
            keep(qkv_grad.at[:, core, :, column], qkv_part.at[mine, which])
        here = pl.ds(head * HEAD, HEAD)
        for c in range(4):
            theirs = pl.ds(pl.multiple_of((2 * c + 1 - core) * depth, depth), depth)
            own = pl.ds(pl.multiple_of((2 * c + core) * depth, depth), depth)
            traded.append(send(out_grad.at[here, theirs], out_part.at[mine, c], other))
            keep(out_grad.at[here, own], out_part.at[mine, c])
    gain_first = [send(gains.at[peer], gain_come.at[me], {"dp": peer}) for peer in peers]
    gain_come[me] = gains[me]
    begun = len(locals_)
    part = up_sum.shape[1]
    shards = []
    for peer in peers:
        shards.append(send(up_sum.at[block(peer, depth)], up_out.at[:, block(me, part)], {"dp": peer}))
        shards.append(send(down_sum.at[:, block(peer, depth)], down_out.at[block(me, part)], {"dp": peer}))
    keep(up_sum.at[block(me, depth)], up_out.at[:, block(me, part)])
    keep(down_sum.at[:, block(me, depth)], down_out.at[block(me, part)])
    for copy in traded:
        copy.wait_recv()
    for copy in locals_[:begun]:
        copy.wait()
    after = {"tensor": planes[0]}
    for step in range(3):
        part = lax.rem(z + 3 - step, 4)
        ring = [
            send(qkv_part.at[part], qkv_come.at[step], after),
            send(out_part.at[part], out_come.at[step], after),
        ]
        if step == 0:
            rows_move = RowMove(rows_in, rows_out, row_sems)
            rows_move.back()
            for copy in gain_first:
                copy.wait_recv()
            gain_sum[...] = functools.reduce(jnp.add, [gain_come[i] for i in range(8)])
            gain_second = [
                send(gain_sum, gain_all.at[z], {"tensor": plane}) for plane in planes
            ]
            gain_all[z] = gain_sum[...]
        for copy in ring:
            copy.wait_recv()
        part = lax.rem(z + 2 - step, 4) if step < 2 else z
        for which in range(3):
            for c in range(4):
                here = qkv_part.at[part, which, c]
                here[...] = (
                    here[...].astype(f32) + qkv_come[step, which, c].astype(f32)
                ).astype(bf16)
        for c in range(4):
            here = out_part.at[part, c]
            here[...] = (here[...].astype(f32) + out_come[step, c].astype(f32)).astype(bf16)
    last = []
    for j in range(1, 4):
        to = lax.rem(chip + j, 4)
        device = {"dp": 2 * to + core}
        last.append(send(qkv_part.at[z, :, to], qkv_out.at[:, :, block(chip, HEAD)], device))
        last.append(send(out_part.at[z, to], out_out.at[block(chip, HEAD)], device))
    keep(qkv_part.at[z, :, chip], qkv_out.at[:, :, block(chip, HEAD)])
    keep(out_part.at[z, chip], out_out.at[block(chip, HEAD)])
    for copy in gain_second:
        copy.wait_recv()
    gains_out[...] = functools.reduce(jnp.add, [gain_all[i] for i in range(4)])
    for copy in last + shards:
        copy.wait_recv()
    for copy in locals_[begun:]:
        copy.wait()
    rows_move.wait()
    for copy in copies:
        copy.wait_send()


def on_device(
    block_input,
    clip_lengths,
    norm1_gain,
    w_query,
    w_key,
    w_value,
    w_out,
    norm2_gain,
    w_up,
    w_down,
    out_cotangent,
):
    streams, rows, width = block_input.shape
    planes = lax.axis_size("tensor")
    lanes = lax.axis_size("dp")
    clip_count = clip_lengths.shape[1]
    own = lax.axis_index("dp")
    own_plane = lax.axis_index("tensor")
    own_core = own % 2
    heads = w_query.shape[1] * planes // (HEAD * lanes)
    depth = w_query.shape[0]
    hidden_part = w_up.shape[1] // lanes
    hidden_own = planes * hidden_part
    inner = heads * HEAD

    small = jnp.zeros((8, depth), f32)
    small = small.at[0].set(norm1_gain.astype(f32)).at[1].set(norm2_gain.astype(f32))
    small = small.at[2, : streams * clip_count].set(clip_lengths.reshape(-1).astype(f32))
    tokens_in, qkv_part, out_part, up_part, down_part, small = plane_call(
        start_kernel,
        "start",
        6,
        [
            jax.ShapeDtypeStruct(block_input.shape, bf16),
            jax.ShapeDtypeStruct((3, 4, depth, HEAD), bf16),
            jax.ShapeDtypeStruct((4, HEAD, depth), bf16),
            jax.ShapeDtypeStruct((width, hidden_part), bf16),
            jax.ShapeDtypeStruct((hidden_part, width), bf16),
            jax.ShapeDtypeStruct((lanes, 8, depth), f32),
        ],
        ["any"] * 8,
        ["any"] * 6,
        [pltpu.SemaphoreType.DMA((7,)), pltpu.SemaphoreType.DMA((2, 2))],
        33,
        0,
        (block_input, w_query, w_key, w_value, w_out, w_up, w_down, small),
    )
    gain_one = small[:, 0].reshape(-1)
    gain_two = small[:, 1].reshape(-1)
    lengths = small[:, 2, : streams * clip_count].reshape(-1, clip_count).astype(jnp.int32)

    qkv_wide = lax.all_gather(qkv_part, "tensor", axis=0, tiled=False)
    out_wide = lax.all_gather(out_part, "tensor", axis=0, tiled=False)
    up_wide = lax.all_gather(up_part, "tensor", axis=0, tiled=False)
    down_w = lax.all_gather(down_part, "tensor", axis=0, tiled=True)

    all_ends = jnp.cumsum(lengths, axis=1)
    buffers = 4 * (own // 2 ^ jnp.arange(4, dtype=jnp.int32)) + own_plane
    ends = jnp.take(all_ends, buffers, axis=0)
    chunks = 2 * (1 - own_core) + jnp.arange(streams, dtype=jnp.int32)
    places = chunks[:, None] * rows + jnp.arange(rows, dtype=jnp.int32)
    valid = (places < ends[0, -1]).astype(f32)
    ends = ends.reshape(-1).astype(jnp.int32)

    pieces = jax.ShapeDtypeStruct((streams, 8, rows, width), bf16)
    sums = jax.ShapeDtypeStruct((streams, rows, width), f32)
    row_count = streams * 8 * rows
    slots = pltpu.VMEM((2, rows, width), bf16)
    dma = pltpu.SemaphoreType.DMA

    def piece_shape(columns):
        return jax.ShapeDtypeStruct((streams, 8, rows, columns), bf16)

    tokens = tokens_in.astype(f32)
    normed_one, unit_one, inverse_one = norm_rows(tokens, gain_one)
    features_one, cotangent = plane_call(
        gather_kernel,
        "gather",
        0,
        [pieces, jax.ShapeDtypeStruct(block_input.shape, bf16)],
        ["any", "any"],
        ["any", "any"],
        [dma((streams,)), dma((2, 2))],
        8 * streams,
        0,
        (normed_one.astype(bf16), out_cotangent),
    )
    grad_out = cotangent.astype(f32) * valid[:, :, None]
    grad_branch, qkv, mixed, qkv_w = plane_call(
        functools.partial(attention_kernel, clip_count),
        "attention",
        1,
        [
            pieces,
            piece_shape(3 * inner),
            piece_shape(inner),
            jax.ShapeDtypeStruct((4, 2, depth, 3 * inner), bf16),
        ],
        ["any", "any", "any", "smem"],
        ["any", "vmem", "vmem", "vmem"],
        [slots, dma((2,)), dma((streams,)), dma((6,))],
        8 * streams + 6,
        2 * row_count * width * 3 * inner,
        (grad_out.astype(bf16), features_one, qkv_wide, ends),
    )
    attn_sum, out_w = plane_call(
        project_kernel,
        "project",
        2,
        [sums, jax.ShapeDtypeStruct((inner, width), bf16)],
        ["vmem", "any"],
        ["vmem", "vmem"],
        reduce_scratch(streams, rows, width) + [dma((8,))],
        10 * streams + 8,
        2 * row_count * width * inner,
        (mixed, out_wide),
    )
    hidden = tokens + attn_sum
    normed_two, unit_two, inverse_two = norm_rows(hidden, gain_two)
    part = pltpu.VMEM((2, rows, hidden_own), bf16)
    up_flat = pltpu.VMEM((width, hidden_own), bf16)
    features_two, slope, down_dot, mlp_sum = plane_call(
        mlp_kernel,
        "mlp",
        3,
        [
            pieces,
            piece_shape(hidden_own),
            jax.ShapeDtypeStruct((hidden_own, width), bf16),
            sums,
        ],
        ["any", "any", "vmem", "any"],
        ["any", "any", "any", "vmem"],
        reduce_scratch(streams, rows, width)
        + [up_flat, slots, part, part, pltpu.VMEM((hidden_own, width), f32), slots]
        + [dma((planes,)), dma((2,)), dma((2,)), dma((streams,)), dma((2,))],
        18 * streams,
        6 * row_count * width * hidden_own,
        (normed_two.astype(bf16), up_wide, down_w, grad_branch),
    )

    up_dot, back_sum = plane_call(
        mlp_back_kernel,
        "mlp_back",
        4,
        [jax.ShapeDtypeStruct((planes, width, hidden_part), bf16), sums],
        ["any", "any", "any", "any", "vmem"],
        ["any", "vmem"],
        reduce_scratch(streams, rows, width)
        + [up_flat, slots, part, part, slots, pltpu.VMEM((width, hidden_own), f32)]
        + [dma((planes,)), dma((2,)), dma((2,)), dma((2,)), dma((2, planes))],
        10 * streams,
        6 * row_count * width * hidden_own,
        (grad_branch, slope, features_two, up_wide, down_w),
    )
    from_two, gain_two_grad = norm_back(back_sum, unit_two, inverse_two, gain_two)
    grad_hidden = grad_out + from_two
    down_sum = lax.psum_scatter(down_dot, "tensor", scatter_dimension=0, tiled=True)
    up_sum = lax.psum_scatter(up_dot, "tensor", scatter_dimension=0, tiled=False)
    chunk = pltpu.VMEM((4, rows, HEAD), f32)
    chip_rows = pltpu.VMEM((streams, 2, rows, 3 * inner), bf16)
    _, qkv_dot, out_dot, output, input_sum = plane_call(
        functools.partial(attention_back_kernel, clip_count),
        "attention_back",
        5,
        [
            pieces,
            jax.ShapeDtypeStruct((width, 3 * inner), bf16),
            jax.ShapeDtypeStruct((inner, width), bf16),
            jax.ShapeDtypeStruct(block_input.shape, bf16),
            sums,
        ],
        ["any", "any", "any", "any", "any", "vmem", "vmem", "smem"],
        ["any", "any", "any", "any", "vmem"],
        reduce_scratch(streams, rows, width)
        + [pltpu.VMEM((4, rows, width), bf16), pltpu.VMEM((2, rows, inner), bf16)]
        + [pltpu.VMEM((streams, 8, rows, inner), bf16), chip_rows]
        + [pltpu.VMEM((2, streams, 2, rows, 3 * inner), bf16), chunk, chunk]
        + [pltpu.VMEM((width, 3 * inner), f32), pltpu.VMEM((inner, width), f32)]
        + [dma((4,)), dma((2,)), dma((4,)), dma((4,)), dma((2, 2)), dma((streams,))],
        18 * streams,
        2 * row_count * width * 8 * inner,
        (
            grad_hidden.astype(bf16),
            qkv,
            mixed,
            features_one,
            (hidden + mlp_sum).astype(bf16),
            qkv_w.reshape(width, 3 * inner),
            out_w,
            ends,
        ),
    )
    input_sum, down_sum, up_sum = lax.optimization_barrier((input_sum, down_sum, up_sum))
    from_one, gain_one_grad = norm_back(input_sum, unit_one, inverse_one, gain_one)
    gains = jnp.stack([gain_one_grad.sum(0), gain_two_grad.sum(0)]).reshape(2, lanes, depth)
    gains = jnp.zeros((lanes, 8, depth), f32).at[:, :2].set(gains.swapaxes(0, 1))
    small_sum = pltpu.VMEM((8, depth), f32)
    input_grad, qkv_grad, out_grad, up_grad, down_grad, gains = plane_call(
        end_kernel,
        "end",
        7,
        [
            jax.ShapeDtypeStruct(block_input.shape, bf16),
            jax.ShapeDtypeStruct((3, depth, 4 * HEAD), bf16),
            jax.ShapeDtypeStruct((4 * HEAD, depth), bf16),
            jax.ShapeDtypeStruct(w_up.shape, bf16),
            jax.ShapeDtypeStruct(w_down.shape, bf16),
            jax.ShapeDtypeStruct((8, depth), f32),
        ],
        ["any", "any", "any", "any", "any", "vmem"],
        ["any", "any", "any", "any", "any", "vmem"],
        [
            pltpu.VMEM((4, 3, 4, depth, HEAD), bf16),
            pltpu.VMEM((4, 4, HEAD, depth), bf16),
            pltpu.VMEM((3, 3, 4, depth, HEAD), bf16),
            pltpu.VMEM((3, 4, HEAD, depth), bf16),
            pltpu.VMEM((8, 8, depth), f32),
            small_sum,
            pltpu.VMEM((4, 8, depth), f32),
            dma((18,)),
            dma((2, 2)),
        ],
        50,
        0,
        (
            (grad_hidden + from_one).astype(bf16),
            qkv_dot.reshape(4, 2, depth, 3 * inner),
            out_dot,
            up_sum,
            down_sum,
            gains,
        ),
    )
    qkv_grad = qkv_grad.astype(f32)
    return (
        output,
        input_grad.astype(f32),
        gains[0],
        qkv_grad[0],
        qkv_grad[1],
        qkv_grad[2],
        out_grad.astype(f32),
        gains[1],
        up_grad.astype(f32),
        down_grad.astype(f32),
    )


def solution(mesh):
    in_specs = (
        P("dp", "tensor", None),
        P("dp", None),
        P("dp"),
        P("dp", "tensor"),
        P("dp", "tensor"),
        P("dp", "tensor"),
        P("tensor", "dp"),
        P("dp"),
        P("dp", "tensor"),
        P("tensor", "dp"),
        P("dp", "tensor", None),
    )
    out_specs = (
        P("dp", "tensor", None),
        P("dp", "tensor", None),
        P("dp"),
        P("dp", "tensor"),
        P("dp", "tensor"),
        P("dp", "tensor"),
        P("tensor", "dp"),
        P("dp"),
        P("dp", "tensor"),
        P("tensor", "dp"),
    )
    own_form = mesh.shape["dp"] == 8 and mesh.shape["tensor"] == 4
    return jax.shard_map(
        on_device if own_form else on_device_any, mesh=mesh, in_specs=in_specs, out_specs=out_specs, check_vma=False
    )
```

```python
import functools

import jax
import jax.numpy as jnp
import numpy as np
from jax import lax
from jax.experimental import pallas as pl
from jax.experimental.pallas import tpu as pltpu
from jax.sharding import PartitionSpec as P

HEAD = 128
LONGEST = 512
epsilon = 1e-05
masked_fill = -1000000000.0
bf16 = jnp.bfloat16
f32 = jnp.float32


def norm_rows(tokens, gain):
    centred = tokens - jnp.mean(tokens, axis=-1, keepdims=True)
    inverse = lax.rsqrt(jnp.mean(centred * centred, axis=-1, keepdims=True) + epsilon)
    unit_rows = centred * inverse
    return (unit_rows * gain, unit_rows, inverse)


def norm_back(grad_normed, unit_rows, inverse, gain):
    scaled = grad_normed * gain
    inner_sum = (
        scaled
        - jnp.mean(scaled, axis=-1, keepdims=True)
        - unit_rows * jnp.mean(scaled * unit_rows, axis=-1, keepdims=True)
    )
    return (inverse * inner_sum, jnp.sum(grad_normed * unit_rows, axis=0))


def gelu_tanh(values):
    return jax.nn.gelu(values, approximate=True)


def masked_scores(q_rows, keys_heads, segment, offset, block_rows):
    slot_count = keys_heads.shape[0]
    raw_scores = jnp.einsum(
        "qhd,khd->hqk", q_rows, keys_heads, preferred_element_type=jnp.float32
    ) * HEAD ** (-0.5)
    q_segment = lax.dynamic_slice_in_dim(segment, offset, block_rows, 0)
    q_place = offset + jnp.arange(block_rows, dtype=jnp.int32)
    places = jnp.arange(slot_count, dtype=jnp.int32)
    allowed = (q_segment[:, None] == segment[None, :]) & (places[None, :] <= q_place[:, None])
    return jnp.where(allowed[None], raw_scores, masked_fill)


def attend(query, key, value, segment, block_rows):
    slot_count = query.shape[0]
    head_count = query.shape[1] // HEAD
    keys_heads = key.reshape(slot_count, head_count, HEAD)
    values_heads = value.reshape(slot_count, head_count, HEAD)

    def one_block(block_index):
        offset = block_index * block_rows
        q_rows = lax.dynamic_slice_in_dim(query, offset, block_rows, 0).reshape(
            block_rows, head_count, HEAD
        )
        scores = masked_scores(q_rows, keys_heads, segment, offset, block_rows)
        highest = jnp.max(scores, axis=-1, keepdims=True)
        shifted = jnp.exp(scores - highest)
        totals = jnp.sum(shifted, axis=-1, keepdims=True)
        weights = (shifted / totals).astype(jnp.bfloat16)
        mixed_rows = jnp.einsum(
            "hqk,khd->qhd", weights, values_heads, preferred_element_type=jnp.float32
        )
        return (
            mixed_rows.reshape(block_rows, head_count * HEAD).astype(jnp.bfloat16),
            (highest + jnp.log(totals))[..., 0],
        )

    mixed_rows, log_norm = lax.map(one_block, jnp.arange(slot_count // block_rows, dtype=jnp.int32))
    return (mixed_rows.reshape(slot_count, head_count * HEAD), log_norm)


def attend_back(query, key, value, segment, log_norm, grad_mixed, block_rows):
    slot_count = query.shape[0]
    head_count = query.shape[1] // HEAD
    keys_heads = key.reshape(slot_count, head_count, HEAD)
    values_heads = value.reshape(slot_count, head_count, HEAD)

    def one_block(carried, block_index):
        grad_keys, grad_values = carried
        offset = block_index * block_rows
        q_rows = lax.dynamic_slice_in_dim(query, offset, block_rows, 0).reshape(
            block_rows, head_count, HEAD
        )
        g_rows = lax.dynamic_slice_in_dim(grad_mixed, offset, block_rows, 0).reshape(
            block_rows, head_count, HEAD
        )
        scores = masked_scores(q_rows, keys_heads, segment, offset, block_rows)
        prob_rows = jnp.exp(scores - log_norm[block_index][..., None])
        grad_values = grad_values + jnp.einsum(
            "hqk,qhd->khd",
            prob_rows.astype(jnp.bfloat16),
            g_rows,
            preferred_element_type=jnp.float32,
        )
        grad_probs = jnp.einsum(
            "qhd,khd->hqk", g_rows, values_heads, preferred_element_type=jnp.float32
        )
        inner_sum = jnp.sum(prob_rows * grad_probs, axis=-1, keepdims=True)
        grad_scores = (prob_rows * (grad_probs - inner_sum) * HEAD ** (-0.5)).astype(jnp.bfloat16)
        grad_query = jnp.einsum(
            "hqk,khd->qhd", grad_scores, keys_heads, preferred_element_type=jnp.float32
        )
        grad_keys = grad_keys + jnp.einsum(
            "hqk,qhd->khd", grad_scores, q_rows, preferred_element_type=jnp.float32
        )
        return (
            (grad_keys, grad_values),
            grad_query.reshape(block_rows, head_count * HEAD).astype(jnp.bfloat16),
        )

    zero_state = jnp.zeros((slot_count, head_count, HEAD), jnp.float32)
    (grad_keys, grad_values), grad_query = lax.scan(
        one_block, (zero_state, zero_state), jnp.arange(slot_count // block_rows, dtype=jnp.int32)
    )
    return (
        grad_query.reshape(slot_count, head_count * HEAD),
        grad_keys.reshape(slot_count, head_count * HEAD).astype(jnp.bfloat16),
        grad_values.reshape(slot_count, head_count * HEAD).astype(jnp.bfloat16),
    )


def on_device_any(
    block_input,
    clip_lengths,
    norm1_gain,
    w_query,
    w_key,
    w_value,
    w_out,
    norm2_gain,
    w_up,
    w_down,
    out_cotangent,
):
    micro_count = block_input.shape[0]
    local_rows = block_input.shape[1]
    tensor_size = lax.axis_size("tensor")
    slot_count = local_rows * tensor_size
    block_rows = min(512, slot_count)
    clip_count = clip_lengths.shape[1]
    row_offset = lax.axis_index("tensor") * local_rows
    places = jnp.arange(slot_count, dtype=jnp.int32)

    def fetch_weights():
        return (
            lax.all_gather(norm1_gain, "dp", axis=0, tiled=True),
            lax.all_gather(norm2_gain, "dp", axis=0, tiled=True),
            lax.all_gather(w_query, "dp", axis=0, tiled=True),
            lax.all_gather(w_key, "dp", axis=0, tiled=True),
            lax.all_gather(w_value, "dp", axis=0, tiled=True),
            lax.all_gather(w_up, "dp", axis=0, tiled=True),
            lax.all_gather(w_out, "dp", axis=1, tiled=True),
            lax.all_gather(w_down, "dp", axis=1, tiled=True),
        )

    def rows_forward(normed):
        return lax.all_gather(normed, "tensor", axis=0, tiled=True)

    def rows_backward(gradients):
        return lax.all_gather(gradients, "tensor", axis=0, tiled=True)

    def sum_forward(term_fn):
        return lax.psum_scatter(
            term_fn(jnp.int32(0), local_rows * lax.axis_size("tensor")),
            "tensor",
            scatter_dimension=0,
            tiled=True,
        )

    def sum_backward(term_fn):
        return lax.psum_scatter(
            term_fn(jnp.int32(0), local_rows * lax.axis_size("tensor")),
            "tensor",
            scatter_dimension=0,
            tiled=True,
        )

    grad_totals = None
    outputs = []
    input_grads = []
    for micro_index in range(micro_count):
        gathered = fetch_weights()
        gain_one = gathered[0].astype(jnp.float32)
        gain_two = gathered[1].astype(jnp.float32)
        query_w, key_w, value_w, up_w, out_w, down_w = (
            gathered[2],
            gathered[3],
            gathered[4],
            gathered[5],
            gathered[6],
            gathered[7],
        )
        tokens = block_input[micro_index].astype(jnp.float32)
        ends = jnp.cumsum(clip_lengths[micro_index])
        segment = jnp.sum((places[:, None] >= ends[None, :]).astype(jnp.int32), axis=1)
        own_segment = lax.dynamic_slice_in_dim(segment, row_offset, local_rows, 0)
        valid_rows = (own_segment < clip_count).astype(jnp.float32)
        normed_one, unit_one, inverse_one = norm_rows(tokens, gain_one)
        features_one = rows_forward(normed_one.astype(jnp.bfloat16))
        query = jnp.dot(features_one, query_w, preferred_element_type=jnp.float32).astype(
            jnp.bfloat16
        )
        key = jnp.dot(features_one, key_w, preferred_element_type=jnp.float32).astype(jnp.bfloat16)
        value = jnp.dot(features_one, value_w, preferred_element_type=jnp.float32).astype(
            jnp.bfloat16
        )
        mixed_rows, log_norm = attend(query, key, value, segment, block_rows)

        def attn_term(offset, row_count):
            return jnp.dot(mixed_rows, out_w, preferred_element_type=jnp.float32)

        hidden = tokens + sum_forward(attn_term)
        normed_two, unit_two, inverse_two = norm_rows(hidden, gain_two)
        features_two = rows_forward(normed_two.astype(jnp.bfloat16))
        pre_act = jnp.dot(features_two, up_w, preferred_element_type=jnp.float32)
        activated = gelu_tanh(pre_act).astype(jnp.bfloat16)

        def mlp_term(offset, row_count):
            return jnp.dot(activated, down_w, preferred_element_type=jnp.float32)

        outputs.append((hidden + sum_forward(mlp_term)).astype(jnp.bfloat16))
        regathered = fetch_weights()
        query_w, key_w, value_w, up_w, out_w, down_w = (
            regathered[2],
            regathered[3],
            regathered[4],
            regathered[5],
            regathered[6],
            regathered[7],
        )
        grad_out = out_cotangent[micro_index].astype(jnp.float32) * valid_rows[:, None]
        grad_branch = rows_backward(grad_out.astype(jnp.bfloat16))
        down_grad = jnp.einsum(
            "sf,sd->fd", activated, grad_branch, preferred_element_type=jnp.float32
        )
        grad_act = jnp.einsum("sd,fd->sf", grad_branch, down_w, preferred_element_type=jnp.float32)
        grad_pre = jax.vjp(gelu_tanh, pre_act)[1](grad_act)[0].astype(jnp.bfloat16)
        up_grad = jnp.einsum(
            "sd,sf->df", features_two, grad_pre, preferred_element_type=jnp.float32
        )

        def up_term(offset, row_count):
            return jnp.einsum("sf,df->sd", grad_pre, up_w, preferred_element_type=jnp.float32)

        grad_normed_two = sum_backward(up_term)
        grad_from_two, gain_two_grad = norm_back(grad_normed_two, unit_two, inverse_two, gain_two)
        grad_hidden = grad_out + grad_from_two
        grad_attn = rows_backward(grad_hidden.astype(jnp.bfloat16))
        out_grad = jnp.einsum(
            "sc,sd->cd", mixed_rows, grad_attn, preferred_element_type=jnp.float32
        )
        grad_mixed = jnp.einsum(
            "sd,cd->sc", grad_attn, out_w, preferred_element_type=jnp.float32
        ).astype(jnp.bfloat16)
        grad_query, grad_key, grad_value = attend_back(
            query, key, value, segment, log_norm, grad_mixed, block_rows
        )
        query_grad = jnp.einsum(
            "sd,sc->dc", features_one, grad_query, preferred_element_type=jnp.float32
        )
        key_grad = jnp.einsum(
            "sd,sc->dc", features_one, grad_key, preferred_element_type=jnp.float32
        )
        value_grad = jnp.einsum(
            "sd,sc->dc", features_one, grad_value, preferred_element_type=jnp.float32
        )

        def qkv_term(offset, row_count):
            part_query = jnp.einsum(
                "sc,dc->sd", grad_query, query_w, preferred_element_type=jnp.float32
            )
            part_key = jnp.einsum("sc,dc->sd", grad_key, key_w, preferred_element_type=jnp.float32)
            part_value = jnp.einsum(
                "sc,dc->sd", grad_value, value_w, preferred_element_type=jnp.float32
            )
            return part_query + part_key + part_value

        grad_normed_one = sum_backward(qkv_term)
        grad_from_one, gain_one_grad = norm_back(grad_normed_one, unit_one, inverse_one, gain_one)
        input_grads.append(grad_hidden + grad_from_one)
        micro_grads = (
            gain_one_grad,
            gain_two_grad,
            query_grad,
            key_grad,
            value_grad,
            up_grad,
            out_grad,
            down_grad,
        )
        if grad_totals is None:
            grad_totals = micro_grads
        else:
            grad_totals = jax.tree.map(jnp.add, grad_totals, micro_grads)
    grad_totals = (
        lax.psum_scatter(
            grad_totals[0].astype(jnp.bfloat16), "dp", scatter_dimension=0, tiled=True
        ).astype(jnp.float32),
        lax.psum_scatter(
            grad_totals[1].astype(jnp.bfloat16), "dp", scatter_dimension=0, tiled=True
        ).astype(jnp.float32),
        lax.psum_scatter(
            grad_totals[2].astype(jnp.bfloat16), "dp", scatter_dimension=0, tiled=True
        ).astype(jnp.float32),
        lax.psum_scatter(
            grad_totals[3].astype(jnp.bfloat16), "dp", scatter_dimension=0, tiled=True
        ).astype(jnp.float32),
        lax.psum_scatter(
            grad_totals[4].astype(jnp.bfloat16), "dp", scatter_dimension=0, tiled=True
        ).astype(jnp.float32),
        lax.psum_scatter(
            grad_totals[5].astype(jnp.bfloat16), "dp", scatter_dimension=0, tiled=True
        ).astype(jnp.float32),
        lax.psum_scatter(
            grad_totals[6].astype(jnp.bfloat16), "dp", scatter_dimension=1, tiled=True
        ).astype(jnp.float32),
        lax.psum_scatter(
            grad_totals[7].astype(jnp.bfloat16), "dp", scatter_dimension=1, tiled=True
        ).astype(jnp.float32),
    )
    gain_sums = lax.psum((grad_totals[0], grad_totals[1]), "tensor")
    return (
        jnp.stack(outputs),
        jnp.stack(input_grads),
        gain_sums[0],
        grad_totals[2],
        grad_totals[3],
        grad_totals[4],
        grad_totals[6],
        gain_sums[1],
        grad_totals[5],
        grad_totals[7],
    )


def chunk_scores(q, k, start, s, c, rows):
    scores = lax.dot_general(
        q, k, (((1,), (1,)), ((), ())), preferred_element_type=f32
    ) * HEAD ** (-0.5)
    k_place = c * rows + lax.broadcasted_iota(jnp.int32, (rows, rows), 1)
    allowed = k_place >= start
    if c == s:
        q_place = s * rows + lax.broadcasted_iota(jnp.int32, (rows, rows), 0)
        allowed = jnp.logical_and(allowed, k_place <= q_place)
    return jnp.where(allowed, scores, masked_fill)


def clip_starts(ends_ref, first, buffer, clip_count, s, rows):
    place = s * rows + lax.broadcasted_iota(jnp.int32, (rows, 1), 0)
    start = jnp.zeros((rows, 1), jnp.int32)
    for clip in range(clip_count):
        end = ends_ref[first + buffer * clip_count + clip]
        start = jnp.where(place >= end, jnp.maximum(start, end), start)
    return start


def window(s, rows):
    back = -(-(LONGEST - 1) // rows)
    return range(max(0, s - back), s + 1)


def chunk_probs(q, keys, start, s, rows):
    cs = list(window(s, rows))
    scores = [chunk_scores(q, keys(c), start, s, c, rows) for c in cs]
    highest = functools.reduce(jnp.maximum, [jnp.max(v, axis=1, keepdims=True) for v in scores])
    shifted = [jnp.exp(v - highest) for v in scores]
    total = functools.reduce(jnp.add, [jnp.sum(v, axis=1, keepdims=True) for v in shifted])
    scale = 1.0 / total
    return cs, [v * scale for v in shifted]


MESH = pl.DeviceIdType.MESH
N_TILE = 1024


class Plane:
    def __init__(self, send_sems, recv_sems, more=()):
        me = lax.axis_index("dp")
        self.core = me % 2
        self.x = (me // 2) % 2
        self.peers = {
            "c": me + 1 - 2 * (me % 2),
            "x": me + 2 - 4 * ((me // 2) % 2),
            "y": me + 4 - 8 * ((me // 4) % 2),
        }
        self.send_sems, self.recv_sems = send_sems, recv_sems
        self.copies = []
        barrier = pltpu.get_barrier_semaphore()
        for peer in self.peers.values():
            pl.semaphore_signal(barrier, inc=1, device_id={"dp": peer}, device_id_type=MESH)
        for place in more:
            pl.semaphore_signal(barrier, inc=1, device_id=at_device(place), device_id_type=MESH)
        pl.semaphore_wait(barrier, 3 + len(more))

    def send(self, src, dst, way):
        return self.send_to(src, dst, {"dp": self.peers[way]})

    def send_to(self, src, dst, device):
        index = len(self.copies)
        copy = pltpu.make_async_remote_copy(
            src_ref=src,
            dst_ref=dst,
            send_sem=self.send_sems.at[index],
            recv_sem=self.recv_sems.at[index],
            device_id=device,
            device_id_type=MESH,
        )
        copy.start()
        self.copies.append(copy)
        return copy

    def finish(self):
        for copy in self.copies:
            copy.wait_send()


class Gather:
    def __init__(self, plane, own, pieces):
        self.plane, self.own, self.pieces = plane, own, pieces
        self.half = own.shape[0] // 2

    def begin(self):
        self.begin_links()
        self.begin_core()

    def begin_links(self):
        self.x = self.plane.send(self.own, self.pieces.at[1], "x")
        self.y = self.plane.send(self.own, self.pieces.at[2], "y")

    def begin_core(self):
        self.c = [self.plane.send(self.own, self.pieces.at[4], "c")]

    def middle(self):
        send, half, pieces = self.plane.send, self.half, self.pieces
        self.x.wait_recv()
        self.fy = send(pieces.at[1, pl.ds(half, half)], pieces.at[3, pl.ds(half, half)], "y")
        self.c.append(send(pieces.at[1], pieces.at[5], "c"))
        self.y.wait_recv()
        self.fx = send(pieces.at[2, pl.ds(0, half)], pieces.at[3, pl.ds(0, half)], "x")
        self.c.append(send(pieces.at[2], pieces.at[6], "c"))

    def end(self):
        self.fx.wait_recv()
        self.fy.wait_recv()
        self.c.append(self.plane.send(self.pieces.at[3], self.pieces.at[7], "c"))

    def core(self, index):
        self.c[index].wait_recv()


class Reduce:
    def __init__(self, plane, pieces, from_core, from_x, from_y):
        self.plane, self.pieces = plane, pieces
        self.from_core, self.from_x, self.from_y = from_core, from_x, from_y
        self.half = pieces.shape[1] // 2
        self.core = {}

    def give(self, m):
        self.core[m] = self.plane.send(self.pieces.at[4 + m], self.from_core.at[m], "c")

    def take(self, m):
        self.core[m].wait_recv()

    def chip_done(self, m):
        send, half, pieces = self.plane.send, self.half, self.pieces
        low, high = pl.ds(0, half), pl.ds(half, half)
        if m == 3:
            self.far_x = send(pieces.at[3, low], self.from_x.at[1], "x")
            self.far_y = send(pieces.at[3, high], self.from_y.at[1], "y")
        elif m == 1:
            self.near_x = send(pieces.at[1, low], self.from_x.at[0], "x")
        elif m == 2:
            self.near_y = send(pieces.at[2, high], self.from_y.at[0], "y")

    def late_x(self):
        high = pl.ds(self.half, self.half)
        self.far_y.wait_recv()
        add_into(self.pieces.at[1, high], self.from_y.at[1])
        self.late_x_copy = self.plane.send(self.pieces.at[1, high], self.from_x.at[2], "x")

    def late_y(self):
        low = pl.ds(0, self.half)
        self.far_x.wait_recv()
        add_into(self.pieces.at[2, low], self.from_x.at[1])
        self.late_y_copy = self.plane.send(self.pieces.at[2, low], self.from_y.at[2], "y")

    def late(self):
        self.late_x()
        self.late_y()

    def total(self, out):
        half = self.half
        self.near_x.wait_recv()
        self.near_y.wait_recv()
        self.late_x_copy.wait_recv()
        self.late_y_copy.wait_recv()
        step = min(64, half)

        for base, x_part, y_part in ((0, 0, 2), (half, 2, 0)):

            def add(index, carry):
                at = pl.ds(pl.multiple_of(index * step, step), step)
                here = pl.ds(pl.multiple_of(base + index * step, step), step)
                out[here] = (
                    self.pieces[0, here].astype(f32)
                    + self.from_x[x_part, at].astype(f32)
                    + self.from_y[y_part, at].astype(f32)
                )
                return carry

            lax.fori_loop(0, half // step, add, 0)


def add_into(ref, other):
    step = min(64, ref.shape[0])

    def add(index, carry):
        at = pl.ds(pl.multiple_of(index * step, step), step)
        ref[at] = (ref[at].astype(f32) + other[at].astype(f32)).astype(bf16)
        return carry

    lax.fori_loop(0, ref.shape[0] // step, add, 0)


class Ring:
    def __init__(self, plane, own, blocks):
        self.plane, self.own, self.blocks = plane, own, blocks
        self.z = lax.axis_index("tensor")
        self.came = None

    @staticmethod
    def places():
        me, z = lax.axis_index("dp"), lax.axis_index("tensor")
        return [(me, lax.rem(z + 1, 4)), (me, lax.rem(z + 3, 4))]

    def step(self, index):
        if self.came is not None:
            self.came.wait_recv()
        if index < 3:
            block = self.blocks(lax.rem(self.z + 4 - index, 4))
            source = self.own if index == 0 else block
            self.came = self.plane.send_to(source, block, {"tensor": lax.rem(self.z + 1, 4)})


ORDER = (3, 1, 2, 0)


def tiles(count, tile, body):
    tile = min(tile, count)

    def step(index, carry):
        body(pl.ds(pl.multiple_of(index * tile, tile), tile))
        return carry

    lax.fori_loop(0, count // tile, step, 0)


def nn(left, right):
    return jnp.dot(left, right, preferred_element_type=f32)


def nt(left, right):
    return lax.dot_general(left, right, (((1,), (1,)), ((), ())), preferred_element_type=f32)


def tn(left, right):
    return lax.dot_general(left, right, (((0,), (0,)), ((), ())), preferred_element_type=f32)


class Feed:
    def __init__(self, source, slots, sems, order):
        self.source, self.slots, self.sems, self.order = source, slots, sems, list(order)

    def copy(self, index):
        slot = index % 2
        return pltpu.make_async_copy(
            self.source(self.order[index]), self.slots.at[slot], self.sems.at[slot]
        )

    def start(self, index):
        if index < len(self.order):
            self.copy(index).start()

    def get(self, index):
        self.copy(index).wait()
        return self.slots.at[index % 2]


def plane_call(kernel, name, collective_id, out_shape, in_spaces, out_spaces, scratch, copies, flops, args):
    spaces = {"any": pl.ANY, "vmem": pltpu.VMEM, "smem": pltpu.SMEM}
    return pl.pallas_call(
        kernel,
        out_shape=out_shape,
        in_specs=[pl.BlockSpec(memory_space=spaces[v]) for v in in_spaces],
        out_specs=[pl.BlockSpec(memory_space=spaces[v]) for v in out_spaces],
        scratch_shapes=list(scratch)
        + [pltpu.SemaphoreType.DMA((copies,)), pltpu.SemaphoreType.DMA((copies,))],
        compiler_params=pltpu.CompilerParams(
            collective_id=collective_id, has_side_effects=True, vmem_limit_bytes=62 << 20
        ),
        cost_estimate=pl.CostEstimate(flops=flops, bytes_accessed=64 << 20, transcendentals=0),
        name=name,
    )(*args)


def row_places():
    me, plane = lax.axis_index("dp"), lax.axis_index("tensor")
    chip, core = 2 * (me // 2), me % 2
    outward = [(chip + 1 - plane // 2, 2 * core + j) for j in range(2)]
    inward = [(chip + plane // 2, 2 * (1 - core) + i) for i in range(2)]
    return outward, inward


def at_device(place):
    return {"dp": place[0], "tensor": place[1]}


class RowMove:
    def __init__(self, src, dst, sems):
        self.src, self.dst, self.sems = src, dst, sems
        self.copies = []

    def copy(self, here, there, place):
        return pltpu.make_async_remote_copy(
            src_ref=self.src.at[here],
            dst_ref=self.dst.at[there],
            send_sem=self.sems.at[0, here],
            recv_sem=self.sems.at[1, there],
            device_id=at_device(place),
            device_id_type=MESH,
        )

    def start(self, places, there):
        for here in range(2):
            copy = self.copy(here, there, places[here])
            copy.start()
            self.copies.append(copy)
        self.arrivals = [self.copy(index, index, places[index]) for index in range(2)]

    def outward(self):
        self.start(row_places()[0], lax.axis_index("tensor") % 2)

    def back(self):
        self.start(row_places()[1], lax.axis_index("tensor") % 2)

    def wait(self):
        for copy in self.copies:
            copy.wait_send()
        for copy in self.arrivals:
            copy.wait_recv()


def start_kernel(
    tokens, w_query, w_key, w_value, w_out, w_up, w_down, small,
    tokens_out, qkv_out, out_out, up_out, down_out, small_out,
    local_sems, row_sems, send_sems, recv_sems,
):
    me, plane = lax.axis_index("dp"), lax.axis_index("tensor")
    chip, core = me // 2, me % 2
    depth = w_query.shape[0]
    part = up_out.shape[1]
    outward, inward = row_places()
    peers = [lax.rem(me + j, 8) for j in range(1, 8)]
    barrier = pltpu.get_barrier_semaphore()
    for peer in peers:
        pl.semaphore_signal(barrier, inc=1, device_id={"dp": peer}, device_id_type=MESH)
    for place in outward + inward:
        pl.semaphore_signal(barrier, inc=1, device_id=at_device(place), device_id_type=MESH)
    pl.semaphore_wait(barrier, 11)
    copies, locals_ = [], []

    def send(src, dst, device):
        copy = pltpu.make_async_remote_copy(
            src_ref=src,
            dst_ref=dst,
            send_sem=send_sems.at[len(copies)],
            recv_sem=recv_sems.at[len(copies)],
            device_id=device,
            device_id_type=MESH,
        )
        copy.start()
        copies.append(copy)

    def keep(src, dst):
        copy = pltpu.make_async_copy(src, dst, local_sems.at[len(locals_)])
        copy.start()
        locals_.append(copy)

    def block(index, size):
        return pl.ds(pl.multiple_of(index * size, size), size)

    rows_move = RowMove(tokens, tokens_out, row_sems)
    rows_move.outward()
    for peer in peers:
        send(small, small_out.at[me], {"dp": peer})
    keep(small, small_out.at[me])
    heads = [(w_query, 0), (w_key, 1), (w_value, 2)]
    for j in range(1, 4):
        other = lax.rem(chip + j, 4)
        device = {"dp": 2 * other + core}
        for weight, which in heads:
            send(weight.at[:, block(other, HEAD)], qkv_out.at[which, chip], device)
    for weight, which in heads:
        keep(weight.at[:, block(chip, HEAD)], qkv_out.at[which, chip])
    for j in range(1, 4):
        other = lax.rem(chip + j, 4)
        send(w_out.at[block(other, HEAD)], out_out.at[chip], {"dp": 2 * other + core})
    keep(w_out.at[block(chip, HEAD)], out_out.at[chip])
    for peer in peers:
        send(w_up.at[:, block(peer, part)], up_out.at[block(me, depth)], {"dp": peer})
        send(w_down.at[block(peer, part)], down_out.at[:, block(me, depth)], {"dp": peer})
    keep(w_up.at[:, block(me, part)], up_out.at[block(me, depth)])
    keep(w_down.at[block(me, part)], down_out.at[:, block(me, depth)])
    for copy in locals_:
        copy.wait()
    for copy in copies:
        copy.wait()
    rows_move.wait()


def gather_kernel(own, rows_in, pieces, rows_out, own_sem, row_sems, send_sems, recv_sems):
    outward, inward = row_places()
    plane = Plane(send_sems, recv_sems, outward + inward)
    streams = own.shape[0]
    rows_move = RowMove(rows_in, rows_out, row_sems)
    rows_move.outward()
    gathers = [Gather(plane, own.at[s], pieces.at[s]) for s in range(streams)]
    keep = [pltpu.make_async_copy(own.at[s], pieces.at[s, 0], own_sem.at[s]) for s in range(streams)]
    for s in range(streams):
        gathers[s].begin()
        keep[s].start()
    for s in range(streams):
        gathers[s].middle()
    for s in range(streams):
        gathers[s].end()
    for s in range(streams):
        keep[s].wait()
        for index in range(4):
            gathers[s].core(index)
    rows_move.wait()
    plane.finish()


def chunk_at(plane, s):
    k = 1 - s // 2
    return s % 2, k + plane.core - 2 * k * plane.core


def chunk_part(plane, qkv, chip, head):
    def part(s, which):
        column = pl.multiple_of((head * 3 + which) * HEAD, HEAD)
        stream, core = chunk_at(plane, s)
        piece = core * (qkv.shape[1] // 2) + chip
        return qkv[stream, piece, :, pl.ds(column, HEAD)]

    return part


def attend_all(plane, qkv, ends_ref, out, clip_count):
    rows = qkv.shape[2]
    heads = qkv.shape[3] // (3 * HEAD)

    def one(index, carry):
        chip, head = index // heads, index % heads
        part = chunk_part(plane, qkv, chip, head)
        column = pl.ds(pl.multiple_of(head * HEAD, HEAD), HEAD)
        for s in range(4):
            start = clip_starts(ends_ref, 0, chip, clip_count, s, rows)
            cs, probs = chunk_probs(part(s, 0), lambda c: part(c, 1), start, s, rows)
            mixed = jnp.zeros((rows, HEAD), f32)
            for c, prob in zip(cs, probs):
                mixed = mixed + nn(prob.astype(bf16), part(c, 2))
            stream, core = chunk_at(plane, s)
            out[stream, core * 4 + chip, :, column] = mixed.astype(bf16)
        return carry

    return one


def attend_back_chip(plane, qkv, grad_mixed, ends_ref, out, key_sum, value_sum, clip_count, chip):
    rows = qkv.shape[2]
    heads = qkv.shape[3] // (3 * HEAD)

    def one(head, carry):
        part = chunk_part(plane, qkv, 0, head)
        column = pl.ds(pl.multiple_of(head * HEAD, HEAD), HEAD)
        key_sum[...] = jnp.zeros_like(key_sum)
        value_sum[...] = jnp.zeros_like(value_sum)

        def put(s, which, value):
            at = pl.ds(pl.multiple_of((head * 3 + which) * HEAD, HEAD), HEAD)
            stream, core = chunk_at(plane, s)
            out[stream, core, :, at] = value.astype(bf16)

        for s in range(4):
            q = part(s, 0)
            stream, core = chunk_at(plane, s)
            g = grad_mixed[stream, core * 4 + chip, :, column]
            start = clip_starts(ends_ref, 0, chip, clip_count, s, rows)
            cs, probs = chunk_probs(q, lambda c: part(c, 1), start, s, rows)
            grad_probs = [nt(g, part(c, 2)) for c in cs]
            inner = functools.reduce(
                jnp.add,
                [jnp.sum(p * v, axis=1, keepdims=True) for p, v in zip(probs, grad_probs)],
            )
            grad_q = jnp.zeros((rows, HEAD), f32)
            for c, prob, grad_prob in zip(cs, probs, grad_probs):
                grad_score = (prob * (grad_prob - inner) * HEAD ** (-0.5)).astype(bf16)
                grad_q = grad_q + nn(grad_score, part(c, 1))
                key_sum[c] += tn(grad_score, q)
                value_sum[c] += tn(prob.astype(bf16), g)
            put(s, 0, grad_q)
        for s in range(4):
            put(s, 1, key_sum[s])
            put(s, 2, value_sum[s])
        return carry

    lax.fori_loop(0, heads, one, 0)


def attention_kernel(
    clip_count, own, rows_in, wide, ends, pieces, qkv, mixed, weight, slots, slot_sems, own_sem, wide_sems, send_sems, recv_sems
):
    plane = Plane(send_sems, recv_sems)
    streams = own.shape[0]
    gathers = [Gather(plane, own.at[s], pieces.at[s]) for s in range(streams)]
    keep = [pltpu.make_async_copy(own.at[s], pieces.at[s, 0], own_sem.at[s]) for s in range(streams)]
    traded, kept = [], []
    for head in range(2):
        for which in range(3):
            column = pl.ds((head * 3 + which) * HEAD, HEAD)
            here = weight.at[:, plane.core, :, column]
            traded.append(plane.send(wide.at[2 * (1 - plane.core) + head, which], here, "c"))
            copy = pltpu.make_async_copy(
                wide.at[2 * plane.core + head, which], here, wide_sems.at[len(kept)]
            )
            copy.start()
            kept.append(copy)
    for s in range(streams):
        gathers[s].begin()
        keep[s].start()
    total = weight.shape[3]
    feed = Feed(
        lambda at: rows_in.at[at[0], at[1]],
        slots,
        slot_sems,
        [(s, p) for s in range(streams) for p in range(8)],
    )
    feed.start(0)

    def project(s):
        for p in range(8):
            feed.start(s * 8 + p + 1)
            piece = feed.get(s * 8 + p)

            def tile(at):
                columns = weight[:, :, :, at].reshape(width, -1)
                qkv[s, p, :, at] = nn(piece[...], columns).astype(bf16)

            tiles(total, N_TILE, tile)

    for copy in traded:
        copy.wait_recv()
    for copy in kept:
        copy.wait()
    width = own.shape[2]

    attend = attend_all(plane, qkv, ends, mixed, clip_count)
    heads = total // (3 * HEAD)
    project(0)
    project(1)
    lax.fori_loop(0, 2 * heads, attend, 0)
    gathers[0].middle()
    gathers[1].middle()
    lax.fori_loop(2 * heads, 4 * heads, attend, 0)
    gathers[0].end()
    gathers[1].end()
    for s in range(streams):
        keep[s].wait()
        for index in range(4):
            gathers[s].core(index)
    plane.finish()


def reduce_scratch(streams, rows, width):
    return [
        pltpu.VMEM((streams, 8, rows, width), bf16),
        pltpu.VMEM((streams, 4, rows, width), bf16),
        pltpu.VMEM((streams, 3, rows // 2, width), bf16),
        pltpu.VMEM((streams, 3, rows // 2, width), bf16),
    ]


def project_kernel(
    mixed, wide, down_part, out, weight, down_w,
    parts, from_core, from_x, from_y, wide_sems, send_sems, recv_sems,
):
    plane = Plane(send_sems, recv_sems, Ring.places())
    size = down_part.shape[0]

    def down_block(index):
        return down_w.at[pl.ds(pl.multiple_of(index * size, size), size)]

    ring = Ring(plane, down_part, down_block)
    own_down = pltpu.make_async_copy(down_part, down_block(ring.z), wide_sems.at[8])
    own_down.start()
    ring.step(0)
    streams = mixed.shape[0]
    width = weight.shape[1]
    depth = wide.shape[3]
    traded, kept = [], []
    for head in range(2):
        for chip in range(4):
            column = pl.ds(pl.multiple_of((2 * chip + plane.core) * depth, depth), depth)
            here = weight.at[pl.ds(head * HEAD, HEAD), column]
            traded.append(plane.send(wide.at[2 * (1 - plane.core) + head, chip], here, "c"))
            copy = pltpu.make_async_copy(
                wide.at[2 * plane.core + head, chip], here, wide_sems.at[len(kept)]
            )
            copy.start()
            kept.append(copy)
    for copy in traded:
        copy.wait_recv()
    for copy in kept:
        copy.wait()
    sums = [
        Reduce(plane, parts.at[s], from_core.at[s], from_x.at[s], from_y.at[s])
        for s in range(streams)
    ]

    for s in range(streams):
        for m in ORDER:

            def other(at):
                parts[s, 4 + m, :, at] = nn(mixed[s, 4 + m], weight[:, at]).astype(bf16)

            tiles(width, N_TILE, other)
            sums[s].give(m)
        for m in ORDER:
            sums[s].take(m)

            def chip(at):
                here = nn(mixed[s, m], weight[:, at])
                parts[s, m, :, at] = (here + from_core[s, m, :, at].astype(f32)).astype(bf16)

            tiles(width, N_TILE, chip)
            sums[s].chip_done(m)
    ring.step(1)
    for s in range(streams):
        sums[s].late()
    ring.step(2)
    for s in range(streams):
        sums[s].total(out.at[s])
    ring.step(3)
    own_down.wait()
    plane.finish()


def gelu_pair(v):
    cubic = 0.044715 * (v * v) * v
    inner = (2.0 / np.pi) ** 0.5 * (v + cubic)
    th = jnp.tanh(inner)
    half = 0.5 * (1.0 + th)
    slope = (2.0 / np.pi) ** 0.5 * (1.0 + 3.0 * 0.044715 * (v * v))
    return v * half, half + 0.5 * v * (1.0 - th * th) * slope


def lay_out(wide, flat, sems):
    copies = []
    part = wide.shape[2]
    for plane in range(wide.shape[0]):
        copy = pltpu.make_async_copy(
            wide.at[plane], flat.at[:, pl.ds(plane * part, part)], sems.at[plane]
        )
        copy.start()
        copies.append(copy)
    return copies


def mlp_kernel(
    own, up_wide, down_w, grads, pieces, slope_out, down_grad, out,
    parts, from_core, from_x, from_y, up_w, slots, act, slope, total, grad_slots,
    up_sems, slot_sems, keep_sems, own_sem, grad_sems, send_sems, recv_sems,
):
    plane = Plane(send_sems, recv_sems)
    streams, rows, width = own.shape
    hidden = up_w.shape[1]
    up_copies = lay_out(up_wide, up_w, up_sems)
    gathers = [Gather(plane, own.at[s], pieces.at[s]) for s in range(streams)]
    sums = [
        Reduce(plane, parts.at[s], from_core.at[s], from_x.at[s], from_y.at[s])
        for s in range(streams)
    ]
    keep = [pltpu.make_async_copy(own.at[s], pieces.at[s, 0], own_sem.at[s]) for s in range(streams)]
    stores = []

    def up_piece(s, p, slot):
        if len(stores) >= 2:
            stores[-2].wait()

        def up(at):
            value, grad = gelu_pair(nn(slots[slot], up_w[:, at]))
            act[slot, :, at] = value.astype(bf16)
            slope[slot, :, at] = grad.astype(bf16)

        tiles(hidden, N_TILE, up)
        store = pltpu.make_async_copy(slope.at[slot], slope_out.at[s, p], keep_sems.at[slot])
        store.start()
        stores.append(store)

    def down_piece(s, p, slot):
        def down(at):
            here = nn(act[slot], down_w[:, at])
            if p < 4:
                here = here + from_core[s, p, :, at].astype(f32)
            parts[s, p, :, at] = here.astype(bf16)

        tiles(width, N_TILE, down)

    def pair_up(s, m):
        if m > 0:
            gathers[s].core(m)
        first = not stores
        rows_come = [
            pltpu.make_async_copy(
                own.at[s] if p == 0 else pieces.at[s, p], slots.at[i], slot_sems.at[i]
            )
            for i, p in enumerate((4 + m, m))
        ]
        coming = [
            pltpu.make_async_copy(grads.at[s, p], grad_slots.at[i], grad_sems.at[i])
            for i, p in enumerate((4 + m, m))
        ]
        if m == 0:
            rows_come[1].start()
            gathers[s].core(0)
            rows_come[0].start()
        else:
            rows_come[0].start()
            rows_come[1].start()
        for copy in coming:
            copy.start()
        rows_come[0].wait()
        up_piece(s, 4 + m, 0)
        down_piece(s, 4 + m, 0)
        sums[s].give(m)
        rows_come[1].wait()
        up_piece(s, m, 1)
        for copy in coming:
            copy.wait()
        left = act[...].reshape(2 * rows, hidden)

        def weigh(at):
            term = tn(left, grad_slots[:, :, at].reshape(2 * rows, -1))
            total[:, at] = term if first else total[:, at] + term

        tiles(width, 512, weigh)
        sums[s].take(m)
        down_piece(s, m, 1)
        sums[s].chip_done(m)

    for s in range(streams):
        keep[s].start()
        gathers[s].begin_core()
    gathers[0].begin_links()
    for copy in up_copies:
        copy.wait()
    pair_up(0, 0)
    pair_up(1, 0)
    gathers[0].middle()
    gathers[1].begin_links()
    pair_up(0, 1)
    pair_up(0, 2)
    gathers[0].end()
    pair_up(0, 3)
    gathers[1].middle()
    pair_up(1, 1)
    sums[0].late()
    gathers[1].end()
    pair_up(1, 3)
    pair_up(1, 2)
    sums[1].late()
    for s in range(streams):
        sums[s].total(out.at[s])
        keep[s].wait()
    for store in stores[-2:]:
        store.wait()
    stores = []
    for index in range(hidden // rows):
        if index >= 2:
            stores[index - 2].wait()
        here = pl.ds(index * rows, rows)
        slots[index % 2] = total[here].astype(bf16)
        store = pltpu.make_async_copy(
            slots.at[index % 2], down_grad.at[here], keep_sems.at[index % 2]
        )
        store.start()
        stores.append(store)
    for store in stores[-2:]:
        store.wait()
    plane.finish()


def mlp_back_kernel(
    grads, slope_in, features, up_wide, down_w, up_grad, out,
    parts, from_core, from_x, from_y, up_w, slots, slopes, pre, rows_two, total,
    up_sems, slot_sems, slope_sems, row_sems, keep_sems, send_sems, recv_sems,
):
    plane = Plane(send_sems, recv_sems)
    streams, _, rows, width = grads.shape
    hidden = up_w.shape[1]
    part = up_wide.shape[2]
    up_copies = lay_out(up_wide, up_w, up_sems)
    sums = [
        Reduce(plane, parts.at[s], from_core.at[s], from_x.at[s], from_y.at[s])
        for s in range(streams)
    ]
    order = [(s, p) for s in range(streams) for m in ORDER for p in (4 + m, m)]
    feed = Feed(lambda at: grads.at[at[0], at[1]], slots, slot_sems, order)
    feed_slope = Feed(lambda at: slope_in.at[at[0], at[1]], slopes, slope_sems, order)
    feed_rows = Feed(lambda at: features.at[at[0], at[1]], rows_two, row_sems, order)
    feed.start(0)
    feed_slope.start(0)
    def back_piece(index):
        feed.start(index + 1)
        feed_slope.start(index + 1)
        feed_rows.start(index)
        grad = feed.get(index)
        slope = feed_slope.get(index)

        def back(at):
            value = nt(grad[...], down_w[at]) * slope[:, at].astype(f32)
            pre[index % 2, :, at] = value.astype(bf16)

        tiles(hidden, N_TILE, back)

    def through_piece(index, s, p):
        def through(at):
            here = nt(pre[index % 2], up_w[at])
            if p < 4:
                here = here + from_core[s, p, :, at].astype(f32)
            parts[s, p, :, at] = here.astype(bf16)

        tiles(width, N_TILE, through)

    for index, (s, p) in enumerate(order):
        back_piece(index)
        if index == 0:
            for copy in up_copies:
                copy.wait()
        if p >= 4:
            through_piece(index, s, p)
            sums[s].give(p - 4)
            continue
        feed_rows.get(index - 1)
        feed_rows.get(index)
        right = pre[...].reshape(2 * rows, hidden)

        def weigh(at):
            term = tn(rows_two[:, :, at].reshape(2 * rows, -1), right)
            total[at] = term if index == 1 else total[at] + term

        tiles(width, 512, weigh)
        sums[s].take(p)
        through_piece(index, s, p)
        sums[s].chip_done(p)
        if p == 2:
            sums[s].late_x()
        if p == 0:
            sums[s].late_y()
    stores = []
    for index in range(width // rows):
        slot = index % 2
        for store in stores[index - 2] if index >= 2 else []:
            store.wait()
        here = pl.ds(index * rows, rows)
        pre[slot] = total[here].astype(bf16)
        stores.append([])
        for at in range(hidden // part):
            store = pltpu.make_async_copy(
                pre.at[slot, :, pl.ds(at * part, part)], up_grad.at[at, here], keep_sems.at[slot, at]
            )
            store.start()
            stores[-1].append(store)
    for s in range(streams):
        sums[s].total(out.at[s])
    for pair in stores[-2:]:
        for store in pair:
            store.wait()
    plane.finish()


def attention_back_kernel(
    clip_count, own, qkv, mixed, features, rows_in, qkv_w, out_w, ends,
    pieces, qkv_grad, out_grad, rows_out, out,
    parts, from_core, from_x, from_y, slots, mixed_slots, grad_mixed, qkv_chip, grad_chip, key_sum, value_sum,
    qkv_sum, out_sum, slot_sems, mixed_sems, chip_sems, store_sems, row_sems, own_sem, send_sems, recv_sems,
):
    outward, inward = row_places()
    plane = Plane(send_sems, recv_sems, outward + inward)
    rows_move = RowMove(rows_in, rows_out, row_sems)
    rows_move.back()
    streams, rows, width = own.shape
    gathers = [Gather(plane, own.at[s], pieces.at[s]) for s in range(streams)]
    sums = [
        Reduce(plane, parts.at[s], from_core.at[s], from_x.at[s], from_y.at[s])
        for s in range(streams)
    ]
    keep = [pltpu.make_async_copy(own.at[s], pieces.at[s, 0], own_sem.at[s]) for s in range(streams)]
    def load_chip(m):
        copies = [
            pltpu.make_async_copy(
                qkv.at[s, core * 4 + m], qkv_chip.at[s, core], chip_sems.at[s * 2 + core]
            )
            for s in range(streams)
            for core in range(2)
        ]
        for copy in copies:
            copy.start()
        return copies

    def load_rows(m):
        copies = [
            pltpu.make_async_copy(
                features.at[s, core * 4 + m], slots.at[s * 2 + core], slot_sems.at[s * 2 + core]
            )
            for s in range(streams)
            for core in range(2)
        ]
        for copy in copies:
            copy.start()
        return copies

    def weigh_chip(place, copies):
        for copy in copies:
            copy.wait()
        right = grad_chip[place % 2].reshape(4 * rows, -1)

        def weigh(at):
            term = tn(slots[:, :, at].reshape(4 * rows, -1), right)
            qkv_sum[at] = term if place == 0 else qkv_sum[at] + term

        tiles(width, 512, weigh)

    mixed_before = []

    def mix_pair(s, m):
        pair = (m, 4 + m)
        rows_come = [
            pltpu.make_async_copy(
                own.at[s] if p == 0 else pieces.at[s, p], slots.at[i], slot_sems.at[i]
            )
            for i, p in enumerate(pair)
        ]
        left_come = [
            pltpu.make_async_copy(mixed.at[s, p], mixed_slots.at[i], mixed_sems.at[i])
            for i, p in enumerate(pair)
        ]
        rows_come[0].start()
        for copy in left_come:
            copy.start()
        gathers[s].core(m)
        rows_come[1].start()
        for i, p in enumerate(pair):
            rows_come[i].wait()
            grad_mixed[s, p] = nt(slots[i], out_w[...]).astype(bf16)
        for copy in left_come:
            copy.wait()
        left = mixed_slots[...].reshape(2 * rows, -1)
        first = not mixed_before
        mixed_before.append(m)

        def weigh(at):
            term = tn(left, slots[pl.ds(0, 2), :, at].reshape(2 * rows, -1))
            out_sum[:, at] = term if first else out_sum[:, at] + term

        tiles(width, N_TILE, weigh)

    def attend_chip(place, m, coming, following):
        for copy in coming:
            copy.wait()
        grad_here = grad_chip.at[place % 2]
        attend_back_chip(
            plane, qkv_chip, grad_mixed, ends, grad_here, key_sum, value_sum, clip_count, m
        )
        coming = load_chip(following) if following is not None else []
        for s in range(streams):

            def other(at):
                parts[s, 4 + m, :, at] = nt(grad_here[s, 1], qkv_w[at]).astype(bf16)

            tiles(width, N_TILE, other)
            sums[s].give(m)
        for s in range(streams):
            sums[s].take(m)

            def chip(at):
                here = nt(grad_here[s, 0], qkv_w[at])
                parts[s, m, :, at] = (here + from_core[s, m, :, at].astype(f32)).astype(bf16)

            tiles(width, N_TILE, chip)
            sums[s].chip_done(m)
        return coming

    for s in range(streams):
        keep[s].start()
        gathers[s].begin_core()
    gathers[0].begin_links()
    coming = load_chip(0)
    mix_pair(0, 0)
    mix_pair(1, 0)
    coming = attend_chip(0, 0, coming, 1)
    gathers[0].middle()
    gathers[1].begin_links()
    mix_pair(0, 1)
    mix_pair(0, 2)
    weigh_chip(0, load_rows(0))
    gathers[0].end()
    mix_pair(0, 3)
    gathers[1].middle()
    mix_pair(1, 1)
    mix_pair(1, 2)
    coming = attend_chip(1, 1, coming, 3)
    gathers[1].end()
    mix_pair(1, 3)
    coming_rows = load_rows(1)
    coming = attend_chip(2, 3, coming, 2)
    weigh_chip(1, coming_rows)
    coming_rows = load_rows(3)
    attend_chip(3, 2, coming, None)
    for s in range(streams):
        sums[s].late_x()
    for s in range(streams):
        sums[s].late_y()
    weigh_chip(2, coming_rows)
    weigh_chip(3, load_rows(2))
    for index in range(out_sum.shape[0] // rows):
        here = pl.ds(index * rows, rows)
        slots[0] = out_sum[here].astype(bf16)
        out_store = pltpu.make_async_copy(slots.at[0], out_grad.at[here], slot_sems.at[0])
        out_store.start()
        out_store.wait()
    stores = []
    for index in range(width // rows):
        if index >= 4:
            stores[index - 4].wait()
        here = pl.ds(index * rows, rows)
        stage = grad_chip.at[0, index // 2 % 2, index % 2]
        stage[...] = qkv_sum[here].astype(bf16)
        store = pltpu.make_async_copy(stage, qkv_grad.at[here], store_sems.at[index % 4])
        store.start()
        stores.append(store)
    for s in range(streams):
        sums[s].total(out.at[s])
        keep[s].wait()
    for store in stores[-4:]:
        store.wait()
    rows_move.wait()
    plane.finish()


def end_kernel(
    rows_in, qkv_grad, out_grad, up_sum, down_sum, gains,
    rows_out, qkv_out, out_out, up_out, down_out, gains_out,
    qkv_part, out_part, qkv_come, out_come, gain_come, gain_sum, gain_all,
    rows_got, qkv_got, out_got, up_got, down_got, local_sems, row_sems, send_sems, recv_sems,
):
    me, z = lax.axis_index("dp"), lax.axis_index("tensor")
    chip, core = me // 2, me % 2
    depth = qkv_grad.shape[2]
    outward, inward = row_places()
    peers = [lax.rem(me + j, 8) for j in range(1, 8)]
    planes = [lax.rem(z + j, 4) for j in range(1, 4)]
    barrier = pltpu.get_barrier_semaphore()
    for peer in peers:
        pl.semaphore_signal(barrier, inc=1, device_id={"dp": peer}, device_id_type=MESH)
    for plane in planes:
        pl.semaphore_signal(barrier, inc=1, device_id={"tensor": plane}, device_id_type=MESH)
    for place in outward + inward:
        pl.semaphore_signal(barrier, inc=1, device_id=at_device(place), device_id_type=MESH)
    pl.semaphore_wait(barrier, 14)
    copies, locals_ = [], []

    def send(src, dst, device):
        copy = pltpu.make_async_remote_copy(
            src_ref=src,
            dst_ref=dst,
            send_sem=send_sems.at[len(copies)],
            recv_sem=recv_sems.at[len(copies)],
            device_id=device,
            device_id_type=MESH,
        )
        copy.start()
        copies.append(copy)
        return copy

    def keep(src, dst):
        copy = pltpu.make_async_copy(src, dst, local_sems.at[len(locals_)])
        copy.start()
        locals_.append(copy)

    def block(index, size):
        return pl.ds(pl.multiple_of(index * size, size), size)

    other = {"dp": me + 1 - 2 * core}
    traded = []
    for head in range(2):
        mine = 2 * core + head
        for which in range(3):
            column = pl.ds((head * 3 + which) * HEAD, HEAD)
            traded.append(
                send(qkv_grad.at[:, 1 - core, :, column], qkv_part.at[mine, which], other)
            )
            keep(qkv_grad.at[:, core, :, column], qkv_part.at[mine, which])
        here = pl.ds(head * HEAD, HEAD)
        for c in range(4):
            theirs = pl.ds(pl.multiple_of((2 * c + 1 - core) * depth, depth), depth)
            own = pl.ds(pl.multiple_of((2 * c + core) * depth, depth), depth)
            traded.append(send(out_grad.at[here, theirs], out_part.at[mine, c], other))
            keep(out_grad.at[here, own], out_part.at[mine, c])
    gain_first = [send(gains.at[peer], gain_come.at[me], {"dp": peer}) for peer in peers]
    gain_come[me] = gains[me]
    begun = len(locals_)
    part = up_sum.shape[1]
    shards = []
    for peer in peers:
        shards.append(send(up_sum.at[block(peer, depth)], up_got.at[:, block(me, part)], {"dp": peer}))
        shards.append(send(down_sum.at[:, block(peer, depth)], down_got.at[block(me, part)], {"dp": peer}))
    keep(up_sum.at[block(me, depth)], up_got.at[:, block(me, part)])
    keep(down_sum.at[:, block(me, depth)], down_got.at[block(me, part)])
    for copy in traded:
        copy.wait_recv()
    for copy in locals_[:begun]:
        copy.wait()
    after = {"tensor": planes[0]}
    for step in range(3):
        part = lax.rem(z + 3 - step, 4)
        ring = [
            send(qkv_part.at[part], qkv_come.at[step], after),
            send(out_part.at[part], out_come.at[step], after),
        ]
        if step == 0:
            rows_move = RowMove(rows_in, rows_got, row_sems)
            rows_move.back()
            for copy in gain_first:
                copy.wait_recv()
            gain_sum[...] = functools.reduce(jnp.add, [gain_come[i] for i in range(8)])
            gain_second = [
                send(gain_sum, gain_all.at[z], {"tensor": plane}) for plane in planes
            ]
            gain_all[z] = gain_sum[...]
        for copy in ring:
            copy.wait_recv()
        part = lax.rem(z + 2 - step, 4) if step < 2 else z
        for which in range(3):
            for c in range(4):
                here = qkv_part.at[part, which, c]
                here[...] = (
                    here[...].astype(f32) + qkv_come[step, which, c].astype(f32)
                ).astype(bf16)
        for c in range(4):
            here = out_part.at[part, c]
            here[...] = (here[...].astype(f32) + out_come[step, c].astype(f32)).astype(bf16)
    last = []
    for j in range(1, 4):
        to = lax.rem(chip + j, 4)
        device = {"dp": 2 * to + core}
        last.append(send(qkv_part.at[z, :, to], qkv_got.at[:, :, block(chip, HEAD)], device))
        last.append(send(out_part.at[z, to], out_got.at[block(chip, HEAD)], device))
    keep(qkv_part.at[z, :, chip], qkv_got.at[:, :, block(chip, HEAD)])
    keep(out_part.at[z, chip], out_got.at[block(chip, HEAD)])
    for copy in gain_second:
        copy.wait_recv()
    gains_out[...] = functools.reduce(jnp.add, [gain_all[i] for i in range(4)])
    for copy in shards:
        copy.wait_recv()
    for copy in locals_[begun:]:
        copy.wait()
    up_out[...] = up_got[...].astype(f32)
    down_out[...] = down_got[...].astype(f32)
    for copy in last:
        copy.wait_recv()
    qkv_out[...] = qkv_got[...].astype(f32)
    out_out[...] = out_got[...].astype(f32)
    rows_move.wait()
    rows_out[...] = rows_got[...].astype(f32)
    for copy in copies:
        copy.wait_send()


def on_device(
    block_input,
    clip_lengths,
    norm1_gain,
    w_query,
    w_key,
    w_value,
    w_out,
    norm2_gain,
    w_up,
    w_down,
    out_cotangent,
):
    streams, rows, width = block_input.shape
    planes = lax.axis_size("tensor")
    lanes = lax.axis_size("dp")
    clip_count = clip_lengths.shape[1]
    own = lax.axis_index("dp")
    own_plane = lax.axis_index("tensor")
    own_core = own % 2
    heads = w_query.shape[1] * planes // (HEAD * lanes)
    depth = w_query.shape[0]
    hidden_part = w_up.shape[1] // lanes
    hidden_own = planes * hidden_part
    inner = heads * HEAD

    small = jnp.zeros((8, depth), f32)
    small = small.at[0].set(norm1_gain.astype(f32)).at[1].set(norm2_gain.astype(f32))
    small = small.at[2, : streams * clip_count].set(clip_lengths.reshape(-1).astype(f32))
    tokens_in, qkv_part, out_part, up_part, down_part, small = plane_call(
        start_kernel,
        "start",
        6,
        [
            jax.ShapeDtypeStruct(block_input.shape, bf16),
            jax.ShapeDtypeStruct((3, 4, depth, HEAD), bf16),
            jax.ShapeDtypeStruct((4, HEAD, depth), bf16),
            jax.ShapeDtypeStruct((width, hidden_part), bf16),
            jax.ShapeDtypeStruct((hidden_part, width), bf16),
            jax.ShapeDtypeStruct((lanes, 8, depth), f32),
        ],
        ["any"] * 8,
        ["any"] * 6,
        [pltpu.SemaphoreType.DMA((7,)), pltpu.SemaphoreType.DMA((2, 2))],
        33,
        0,
        (block_input, w_query, w_key, w_value, w_out, w_up, w_down, small),
    )
    gain_one = small[:, 0].reshape(-1)
    gain_two = small[:, 1].reshape(-1)
    lengths = small[:, 2, : streams * clip_count].reshape(-1, clip_count).astype(jnp.int32)

    qkv_wide = lax.all_gather(qkv_part, "tensor", axis=0, tiled=False)
    out_wide = lax.all_gather(out_part, "tensor", axis=0, tiled=False)
    up_wide = lax.all_gather(up_part, "tensor", axis=0, tiled=False)

    all_ends = jnp.cumsum(lengths, axis=1)
    buffers = 4 * (own // 2 ^ jnp.arange(4, dtype=jnp.int32)) + own_plane
    ends = jnp.take(all_ends, buffers, axis=0)
    chunks = 2 * (1 - own_core) + jnp.arange(streams, dtype=jnp.int32)
    places = chunks[:, None] * rows + jnp.arange(rows, dtype=jnp.int32)
    valid = (places < ends[0, -1]).astype(f32)
    ends = ends.reshape(-1).astype(jnp.int32)

    pieces = jax.ShapeDtypeStruct((streams, 8, rows, width), bf16)
    sums = jax.ShapeDtypeStruct((streams, rows, width), f32)
    row_count = streams * 8 * rows
    slots = pltpu.VMEM((2, rows, width), bf16)
    dma = pltpu.SemaphoreType.DMA

    def piece_shape(columns):
        return jax.ShapeDtypeStruct((streams, 8, rows, columns), bf16)

    tokens = tokens_in.astype(f32)
    normed_one, unit_one, inverse_one = norm_rows(tokens, gain_one)
    features_one, cotangent = plane_call(
        gather_kernel,
        "gather",
        0,
        [pieces, jax.ShapeDtypeStruct(block_input.shape, bf16)],
        ["any", "any"],
        ["any", "any"],
        [dma((streams,)), dma((2, 2))],
        8 * streams,
        0,
        (normed_one.astype(bf16), out_cotangent),
    )
    grad_out = cotangent.astype(f32) * valid[:, :, None]
    grad_branch, qkv, mixed, qkv_w = plane_call(
        functools.partial(attention_kernel, clip_count),
        "attention",
        1,
        [
            pieces,
            piece_shape(3 * inner),
            piece_shape(inner),
            jax.ShapeDtypeStruct((4, 2, depth, 3 * inner), bf16),
        ],
        ["any", "any", "any", "smem"],
        ["any", "vmem", "vmem", "vmem"],
        [slots, dma((2,)), dma((streams,)), dma((6,))],
        8 * streams + 6,
        2 * row_count * width * 3 * inner,
        (grad_out.astype(bf16), features_one, qkv_wide, ends),
    )
    attn_sum, out_w, down_w = plane_call(
        project_kernel,
        "project",
        2,
        [
            sums,
            jax.ShapeDtypeStruct((inner, width), bf16),
            jax.ShapeDtypeStruct((hidden_own, width), bf16),
        ],
        ["vmem", "any", "any"],
        ["vmem", "vmem", "any"],
        reduce_scratch(streams, rows, width) + [dma((9,))],
        10 * streams + 11,
        2 * row_count * width * inner,
        (mixed, out_wide, down_part),
    )
    hidden = tokens + attn_sum
    normed_two, unit_two, inverse_two = norm_rows(hidden, gain_two)
    part = pltpu.VMEM((2, rows, hidden_own), bf16)
    up_flat = pltpu.VMEM((width, hidden_own), bf16)
    features_two, slope, down_dot, mlp_sum = plane_call(
        mlp_kernel,
        "mlp",
        3,
        [
            pieces,
            piece_shape(hidden_own),
            jax.ShapeDtypeStruct((hidden_own, width), bf16),
            sums,
        ],
        ["any", "any", "vmem", "any"],
        ["any", "any", "any", "vmem"],
        reduce_scratch(streams, rows, width)
        + [up_flat, slots, part, part, pltpu.VMEM((hidden_own, width), f32), slots]
        + [dma((planes,)), dma((2,)), dma((2,)), dma((streams,)), dma((2,))],
        18 * streams,
        6 * row_count * width * hidden_own,
        (normed_two.astype(bf16), up_wide, down_w, grad_branch),
    )

    up_dot, back_sum = plane_call(
        mlp_back_kernel,
        "mlp_back",
        4,
        [jax.ShapeDtypeStruct((planes, width, hidden_part), bf16), sums],
        ["any", "any", "any", "any", "vmem"],
        ["any", "vmem"],
        reduce_scratch(streams, rows, width)
        + [up_flat, slots, part, part, slots, pltpu.VMEM((width, hidden_own), f32)]
        + [dma((planes,)), dma((2,)), dma((2,)), dma((2,)), dma((2, planes))],
        10 * streams,
        6 * row_count * width * hidden_own,
        (grad_branch, slope, features_two, up_wide, down_w),
    )
    from_two, gain_two_grad = norm_back(back_sum, unit_two, inverse_two, gain_two)
    grad_hidden = grad_out + from_two
    down_sum = lax.psum_scatter(down_dot, "tensor", scatter_dimension=0, tiled=True)
    up_sum = lax.psum_scatter(up_dot, "tensor", scatter_dimension=0, tiled=False)
    chunk = pltpu.VMEM((4, rows, HEAD), f32)
    chip_rows = pltpu.VMEM((streams, 2, rows, 3 * inner), bf16)
    _, qkv_dot, out_dot, output, input_sum = plane_call(
        functools.partial(attention_back_kernel, clip_count),
        "attention_back",
        5,
        [
            pieces,
            jax.ShapeDtypeStruct((width, 3 * inner), bf16),
            jax.ShapeDtypeStruct((inner, width), bf16),
            jax.ShapeDtypeStruct(block_input.shape, bf16),
            sums,
        ],
        ["any", "any", "any", "any", "any", "vmem", "vmem", "smem"],
        ["any", "any", "any", "any", "vmem"],
        reduce_scratch(streams, rows, width)
        + [pltpu.VMEM((4, rows, width), bf16), pltpu.VMEM((2, rows, inner), bf16)]
        + [pltpu.VMEM((streams, 8, rows, inner), bf16), chip_rows]
        + [pltpu.VMEM((2, streams, 2, rows, 3 * inner), bf16), chunk, chunk]
        + [pltpu.VMEM((width, 3 * inner), f32), pltpu.VMEM((inner, width), f32)]
        + [dma((4,)), dma((2,)), dma((4,)), dma((4,)), dma((2, 2)), dma((streams,))],
        18 * streams,
        2 * row_count * width * 8 * inner,
        (
            grad_hidden.astype(bf16),
            qkv,
            mixed,
            features_one,
            (hidden + mlp_sum).astype(bf16),
            qkv_w.reshape(width, 3 * inner),
            out_w,
            ends,
        ),
    )
    input_sum, down_sum, up_sum = lax.optimization_barrier((input_sum, down_sum, up_sum))
    from_one, gain_one_grad = norm_back(input_sum, unit_one, inverse_one, gain_one)
    gains = jnp.stack([gain_one_grad.sum(0), gain_two_grad.sum(0)]).reshape(2, lanes, depth)
    gains = jnp.zeros((lanes, 8, depth), f32).at[:, :2].set(gains.swapaxes(0, 1))
    small_sum = pltpu.VMEM((8, depth), f32)
    input_grad, qkv_grad, out_grad, up_grad, down_grad, gains = plane_call(
        end_kernel,
        "end",
        7,
        [
            sums,
            jax.ShapeDtypeStruct((3, depth, 4 * HEAD), f32),
            jax.ShapeDtypeStruct((4 * HEAD, depth), f32),
            jax.ShapeDtypeStruct(w_up.shape, f32),
            jax.ShapeDtypeStruct(w_down.shape, f32),
            jax.ShapeDtypeStruct((8, depth), f32),
        ],
        ["any", "any", "any", "any", "any", "vmem"],
        ["vmem"] * 6,
        [
            pltpu.VMEM((4, 3, 4, depth, HEAD), bf16),
            pltpu.VMEM((4, 4, HEAD, depth), bf16),
            pltpu.VMEM((3, 3, 4, depth, HEAD), bf16),
            pltpu.VMEM((3, 4, HEAD, depth), bf16),
            pltpu.VMEM((8, 8, depth), f32),
            small_sum,
            pltpu.VMEM((4, 8, depth), f32),
            pltpu.VMEM(block_input.shape, bf16),
            pltpu.VMEM((3, depth, 4 * HEAD), bf16),
            pltpu.VMEM((4 * HEAD, depth), bf16),
            pltpu.VMEM(w_up.shape, bf16),
            pltpu.VMEM(w_down.shape, bf16),
            dma((18,)),
            dma((2, 2)),
        ],
        50,
        0,
        (
            (grad_hidden + from_one).astype(bf16),
            qkv_dot.reshape(4, 2, depth, 3 * inner),
            out_dot,
            up_sum,
            down_sum,
            gains,
        ),
    )
    return (
        output,
        input_grad,
        gains[0],
        qkv_grad[0],
        qkv_grad[1],
        qkv_grad[2],
        out_grad,
        gains[1],
        up_grad,
        down_grad,
    )


def solution(mesh):
    in_specs = (
        P("dp", "tensor", None),
        P("dp", None),
        P("dp"),
        P("dp", "tensor"),
        P("dp", "tensor"),
        P("dp", "tensor"),
        P("tensor", "dp"),
        P("dp"),
        P("dp", "tensor"),
        P("tensor", "dp"),
        P("dp", "tensor", None),
    )
    out_specs = (
        P("dp", "tensor", None),
        P("dp", "tensor", None),
        P("dp"),
        P("dp", "tensor"),
        P("dp", "tensor"),
        P("dp", "tensor"),
        P("tensor", "dp"),
        P("dp"),
        P("dp", "tensor"),
        P("tensor", "dp"),
    )
    own_form = mesh.shape["dp"] == 8 and mesh.shape["tensor"] == 4
    return jax.shard_map(
        on_device if own_form else on_device_any, mesh=mesh, in_specs=in_specs, out_specs=out_specs, check_vma=False
    )
```

```python
import functools

import jax
import jax.numpy as jnp
import numpy as np
from jax import lax
from jax.experimental import pallas as pl
from jax.experimental.pallas import tpu as pltpu
from jax.sharding import PartitionSpec as P

HEAD = 128
LONGEST = 512
epsilon = 1e-05
masked_fill = -1000000000.0
bf16 = jnp.bfloat16
f32 = jnp.float32


def norm_rows(tokens, gain):
    centred = tokens - jnp.mean(tokens, axis=-1, keepdims=True)
    inverse = lax.rsqrt(jnp.mean(centred * centred, axis=-1, keepdims=True) + epsilon)
    unit_rows = centred * inverse
    return (unit_rows * gain, unit_rows, inverse)


def norm_back(grad_normed, unit_rows, inverse, gain):
    scaled = grad_normed * gain
    inner_sum = (
        scaled
        - jnp.mean(scaled, axis=-1, keepdims=True)
        - unit_rows * jnp.mean(scaled * unit_rows, axis=-1, keepdims=True)
    )
    return (inverse * inner_sum, jnp.sum(grad_normed * unit_rows, axis=0))


def gelu_tanh(values):
    return jax.nn.gelu(values, approximate=True)


def masked_scores(q_rows, keys_heads, segment, offset, block_rows):
    slot_count = keys_heads.shape[0]
    raw_scores = jnp.einsum(
        "qhd,khd->hqk", q_rows, keys_heads, preferred_element_type=jnp.float32
    ) * HEAD ** (-0.5)
    q_segment = lax.dynamic_slice_in_dim(segment, offset, block_rows, 0)
    q_place = offset + jnp.arange(block_rows, dtype=jnp.int32)
    places = jnp.arange(slot_count, dtype=jnp.int32)
    allowed = (q_segment[:, None] == segment[None, :]) & (places[None, :] <= q_place[:, None])
    return jnp.where(allowed[None], raw_scores, masked_fill)


def attend(query, key, value, segment, block_rows):
    slot_count = query.shape[0]
    head_count = query.shape[1] // HEAD
    keys_heads = key.reshape(slot_count, head_count, HEAD)
    values_heads = value.reshape(slot_count, head_count, HEAD)

    def one_block(block_index):
        offset = block_index * block_rows
        q_rows = lax.dynamic_slice_in_dim(query, offset, block_rows, 0).reshape(
            block_rows, head_count, HEAD
        )
        scores = masked_scores(q_rows, keys_heads, segment, offset, block_rows)
        highest = jnp.max(scores, axis=-1, keepdims=True)
        shifted = jnp.exp(scores - highest)
        totals = jnp.sum(shifted, axis=-1, keepdims=True)
        weights = (shifted / totals).astype(jnp.bfloat16)
        mixed_rows = jnp.einsum(
            "hqk,khd->qhd", weights, values_heads, preferred_element_type=jnp.float32
        )
        return (
            mixed_rows.reshape(block_rows, head_count * HEAD).astype(jnp.bfloat16),
            (highest + jnp.log(totals))[..., 0],
        )

    mixed_rows, log_norm = lax.map(one_block, jnp.arange(slot_count // block_rows, dtype=jnp.int32))
    return (mixed_rows.reshape(slot_count, head_count * HEAD), log_norm)


def attend_back(query, key, value, segment, log_norm, grad_mixed, block_rows):
    slot_count = query.shape[0]
    head_count = query.shape[1] // HEAD
    keys_heads = key.reshape(slot_count, head_count, HEAD)
    values_heads = value.reshape(slot_count, head_count, HEAD)

    def one_block(carried, block_index):
        grad_keys, grad_values = carried
        offset = block_index * block_rows
        q_rows = lax.dynamic_slice_in_dim(query, offset, block_rows, 0).reshape(
            block_rows, head_count, HEAD
        )
        g_rows = lax.dynamic_slice_in_dim(grad_mixed, offset, block_rows, 0).reshape(
            block_rows, head_count, HEAD
        )
        scores = masked_scores(q_rows, keys_heads, segment, offset, block_rows)
        prob_rows = jnp.exp(scores - log_norm[block_index][..., None])
        grad_values = grad_values + jnp.einsum(
            "hqk,qhd->khd",
            prob_rows.astype(jnp.bfloat16),
            g_rows,
            preferred_element_type=jnp.float32,
        )
        grad_probs = jnp.einsum(
            "qhd,khd->hqk", g_rows, values_heads, preferred_element_type=jnp.float32
        )
        inner_sum = jnp.sum(prob_rows * grad_probs, axis=-1, keepdims=True)
        grad_scores = (prob_rows * (grad_probs - inner_sum) * HEAD ** (-0.5)).astype(jnp.bfloat16)
        grad_query = jnp.einsum(
            "hqk,khd->qhd", grad_scores, keys_heads, preferred_element_type=jnp.float32
        )
        grad_keys = grad_keys + jnp.einsum(
            "hqk,qhd->khd", grad_scores, q_rows, preferred_element_type=jnp.float32
        )
        return (
            (grad_keys, grad_values),
            grad_query.reshape(block_rows, head_count * HEAD).astype(jnp.bfloat16),
        )

    zero_state = jnp.zeros((slot_count, head_count, HEAD), jnp.float32)
    (grad_keys, grad_values), grad_query = lax.scan(
        one_block, (zero_state, zero_state), jnp.arange(slot_count // block_rows, dtype=jnp.int32)
    )
    return (
        grad_query.reshape(slot_count, head_count * HEAD),
        grad_keys.reshape(slot_count, head_count * HEAD).astype(jnp.bfloat16),
        grad_values.reshape(slot_count, head_count * HEAD).astype(jnp.bfloat16),
    )


def on_device_any(
    block_input,
    clip_lengths,
    norm1_gain,
    w_query,
    w_key,
    w_value,
    w_out,
    norm2_gain,
    w_up,
    w_down,
    out_cotangent,
):
    micro_count = block_input.shape[0]
    local_rows = block_input.shape[1]
    tensor_size = lax.axis_size("tensor")
    slot_count = local_rows * tensor_size
    block_rows = min(512, slot_count)
    clip_count = clip_lengths.shape[1]
    row_offset = lax.axis_index("tensor") * local_rows
    places = jnp.arange(slot_count, dtype=jnp.int32)

    def fetch_weights():
        return (
            lax.all_gather(norm1_gain, "dp", axis=0, tiled=True),
            lax.all_gather(norm2_gain, "dp", axis=0, tiled=True),
            lax.all_gather(w_query, "dp", axis=0, tiled=True),
            lax.all_gather(w_key, "dp", axis=0, tiled=True),
            lax.all_gather(w_value, "dp", axis=0, tiled=True),
            lax.all_gather(w_up, "dp", axis=0, tiled=True),
            lax.all_gather(w_out, "dp", axis=1, tiled=True),
            lax.all_gather(w_down, "dp", axis=1, tiled=True),
        )

    def rows_forward(normed):
        return lax.all_gather(normed, "tensor", axis=0, tiled=True)

    def rows_backward(gradients):
        return lax.all_gather(gradients, "tensor", axis=0, tiled=True)

    def sum_forward(term_fn):
        return lax.psum_scatter(
            term_fn(jnp.int32(0), local_rows * lax.axis_size("tensor")),
            "tensor",
            scatter_dimension=0,
            tiled=True,
        )

    def sum_backward(term_fn):
        return lax.psum_scatter(
            term_fn(jnp.int32(0), local_rows * lax.axis_size("tensor")),
            "tensor",
            scatter_dimension=0,
            tiled=True,
        )

    grad_totals = None
    outputs = []
    input_grads = []
    for micro_index in range(micro_count):
        gathered = fetch_weights()
        gain_one = gathered[0].astype(jnp.float32)
        gain_two = gathered[1].astype(jnp.float32)
        query_w, key_w, value_w, up_w, out_w, down_w = (
            gathered[2],
            gathered[3],
            gathered[4],
            gathered[5],
            gathered[6],
            gathered[7],
        )
        tokens = block_input[micro_index].astype(jnp.float32)
        ends = jnp.cumsum(clip_lengths[micro_index])
        segment = jnp.sum((places[:, None] >= ends[None, :]).astype(jnp.int32), axis=1)
        own_segment = lax.dynamic_slice_in_dim(segment, row_offset, local_rows, 0)
        valid_rows = (own_segment < clip_count).astype(jnp.float32)
        normed_one, unit_one, inverse_one = norm_rows(tokens, gain_one)
        features_one = rows_forward(normed_one.astype(jnp.bfloat16))
        query = jnp.dot(features_one, query_w, preferred_element_type=jnp.float32).astype(
            jnp.bfloat16
        )
        key = jnp.dot(features_one, key_w, preferred_element_type=jnp.float32).astype(jnp.bfloat16)
        value = jnp.dot(features_one, value_w, preferred_element_type=jnp.float32).astype(
            jnp.bfloat16
        )
        mixed_rows, log_norm = attend(query, key, value, segment, block_rows)

        def attn_term(offset, row_count):
            return jnp.dot(mixed_rows, out_w, preferred_element_type=jnp.float32)

        hidden = tokens + sum_forward(attn_term)
        normed_two, unit_two, inverse_two = norm_rows(hidden, gain_two)
        features_two = rows_forward(normed_two.astype(jnp.bfloat16))
        pre_act = jnp.dot(features_two, up_w, preferred_element_type=jnp.float32)
        activated = gelu_tanh(pre_act).astype(jnp.bfloat16)

        def mlp_term(offset, row_count):
            return jnp.dot(activated, down_w, preferred_element_type=jnp.float32)

        outputs.append((hidden + sum_forward(mlp_term)).astype(jnp.bfloat16))
        regathered = fetch_weights()
        query_w, key_w, value_w, up_w, out_w, down_w = (
            regathered[2],
            regathered[3],
            regathered[4],
            regathered[5],
            regathered[6],
            regathered[7],
        )
        grad_out = out_cotangent[micro_index].astype(jnp.float32) * valid_rows[:, None]
        grad_branch = rows_backward(grad_out.astype(jnp.bfloat16))
        down_grad = jnp.einsum(
            "sf,sd->fd", activated, grad_branch, preferred_element_type=jnp.float32
        )
        grad_act = jnp.einsum("sd,fd->sf", grad_branch, down_w, preferred_element_type=jnp.float32)
        grad_pre = jax.vjp(gelu_tanh, pre_act)[1](grad_act)[0].astype(jnp.bfloat16)
        up_grad = jnp.einsum(
            "sd,sf->df", features_two, grad_pre, preferred_element_type=jnp.float32
        )

        def up_term(offset, row_count):
            return jnp.einsum("sf,df->sd", grad_pre, up_w, preferred_element_type=jnp.float32)

        grad_normed_two = sum_backward(up_term)
        grad_from_two, gain_two_grad = norm_back(grad_normed_two, unit_two, inverse_two, gain_two)
        grad_hidden = grad_out + grad_from_two
        grad_attn = rows_backward(grad_hidden.astype(jnp.bfloat16))
        out_grad = jnp.einsum(
            "sc,sd->cd", mixed_rows, grad_attn, preferred_element_type=jnp.float32
        )
        grad_mixed = jnp.einsum(
            "sd,cd->sc", grad_attn, out_w, preferred_element_type=jnp.float32
        ).astype(jnp.bfloat16)
        grad_query, grad_key, grad_value = attend_back(
            query, key, value, segment, log_norm, grad_mixed, block_rows
        )
        query_grad = jnp.einsum(
            "sd,sc->dc", features_one, grad_query, preferred_element_type=jnp.float32
        )
        key_grad = jnp.einsum(
            "sd,sc->dc", features_one, grad_key, preferred_element_type=jnp.float32
        )
        value_grad = jnp.einsum(
            "sd,sc->dc", features_one, grad_value, preferred_element_type=jnp.float32
        )

        def qkv_term(offset, row_count):
            part_query = jnp.einsum(
                "sc,dc->sd", grad_query, query_w, preferred_element_type=jnp.float32
            )
            part_key = jnp.einsum("sc,dc->sd", grad_key, key_w, preferred_element_type=jnp.float32)
            part_value = jnp.einsum(
                "sc,dc->sd", grad_value, value_w, preferred_element_type=jnp.float32
            )
            return part_query + part_key + part_value

        grad_normed_one = sum_backward(qkv_term)
        grad_from_one, gain_one_grad = norm_back(grad_normed_one, unit_one, inverse_one, gain_one)
        input_grads.append(grad_hidden + grad_from_one)
        micro_grads = (
            gain_one_grad,
            gain_two_grad,
            query_grad,
            key_grad,
            value_grad,
            up_grad,
            out_grad,
            down_grad,
        )
        if grad_totals is None:
            grad_totals = micro_grads
        else:
            grad_totals = jax.tree.map(jnp.add, grad_totals, micro_grads)
    grad_totals = (
        lax.psum_scatter(
            grad_totals[0].astype(jnp.bfloat16), "dp", scatter_dimension=0, tiled=True
        ).astype(jnp.float32),
        lax.psum_scatter(
            grad_totals[1].astype(jnp.bfloat16), "dp", scatter_dimension=0, tiled=True
        ).astype(jnp.float32),
        lax.psum_scatter(
            grad_totals[2].astype(jnp.bfloat16), "dp", scatter_dimension=0, tiled=True
        ).astype(jnp.float32),
        lax.psum_scatter(
            grad_totals[3].astype(jnp.bfloat16), "dp", scatter_dimension=0, tiled=True
        ).astype(jnp.float32),
        lax.psum_scatter(
            grad_totals[4].astype(jnp.bfloat16), "dp", scatter_dimension=0, tiled=True
        ).astype(jnp.float32),
        lax.psum_scatter(
            grad_totals[5].astype(jnp.bfloat16), "dp", scatter_dimension=0, tiled=True
        ).astype(jnp.float32),
        lax.psum_scatter(
            grad_totals[6].astype(jnp.bfloat16), "dp", scatter_dimension=1, tiled=True
        ).astype(jnp.float32),
        lax.psum_scatter(
            grad_totals[7].astype(jnp.bfloat16), "dp", scatter_dimension=1, tiled=True
        ).astype(jnp.float32),
    )
    gain_sums = lax.psum((grad_totals[0], grad_totals[1]), "tensor")
    return (
        jnp.stack(outputs),
        jnp.stack(input_grads),
        gain_sums[0],
        grad_totals[2],
        grad_totals[3],
        grad_totals[4],
        grad_totals[6],
        gain_sums[1],
        grad_totals[5],
        grad_totals[7],
    )


def chunk_scores(q, k, start, s, c, rows):
    scores = lax.dot_general(
        q, k, (((1,), (1,)), ((), ())), preferred_element_type=f32
    ) * HEAD ** (-0.5)
    k_place = c * rows + lax.broadcasted_iota(jnp.int32, (rows, rows), 1)
    allowed = k_place >= start
    if c == s:
        q_place = s * rows + lax.broadcasted_iota(jnp.int32, (rows, rows), 0)
        allowed = jnp.logical_and(allowed, k_place <= q_place)
    return jnp.where(allowed, scores, masked_fill)


def clip_starts(ends_ref, first, buffer, clip_count, s, rows):
    place = s * rows + lax.broadcasted_iota(jnp.int32, (rows, 1), 0)
    start = jnp.zeros((rows, 1), jnp.int32)
    for clip in range(clip_count):
        end = ends_ref[first + buffer * clip_count + clip]
        start = jnp.where(place >= end, jnp.maximum(start, end), start)
    return start


def window(s, rows):
    back = -(-(LONGEST - 1) // rows)
    return range(max(0, s - back), s + 1)


def chunk_probs(q, keys, start, s, rows):
    cs = list(window(s, rows))
    scores = [chunk_scores(q, keys(c), start, s, c, rows) for c in cs]
    highest = functools.reduce(jnp.maximum, [jnp.max(v, axis=1, keepdims=True) for v in scores])
    shifted = [jnp.exp(v - highest) for v in scores]
    total = functools.reduce(jnp.add, [jnp.sum(v, axis=1, keepdims=True) for v in shifted])
    scale = 1.0 / total
    return cs, [v * scale for v in shifted]


MESH = pl.DeviceIdType.MESH
N_TILE = 1024


class Plane:
    def __init__(self, send_sems, recv_sems, more=()):
        me = lax.axis_index("dp")
        self.core = me % 2
        self.x = (me // 2) % 2
        self.peers = {
            "c": me + 1 - 2 * (me % 2),
            "x": me + 2 - 4 * ((me // 2) % 2),
            "y": me + 4 - 8 * ((me // 4) % 2),
        }
        self.send_sems, self.recv_sems = send_sems, recv_sems
        self.copies = []
        barrier = pltpu.get_barrier_semaphore()
        for peer in self.peers.values():
            pl.semaphore_signal(barrier, inc=1, device_id={"dp": peer}, device_id_type=MESH)
        for place in more:
            pl.semaphore_signal(barrier, inc=1, device_id=at_device(place), device_id_type=MESH)
        pl.semaphore_wait(barrier, 3 + len(more))

    def send(self, src, dst, way):
        return self.send_to(src, dst, {"dp": self.peers[way]})

    def send_to(self, src, dst, device):
        index = len(self.copies)
        copy = pltpu.make_async_remote_copy(
            src_ref=src,
            dst_ref=dst,
            send_sem=self.send_sems.at[index],
            recv_sem=self.recv_sems.at[index],
            device_id=device,
            device_id_type=MESH,
        )
        copy.start()
        self.copies.append(copy)
        return copy

    def finish(self):
        for copy in self.copies:
            copy.wait_send()


class Gather:
    def __init__(self, plane, own, pieces):
        self.plane, self.own, self.pieces = plane, own, pieces
        self.half = own.shape[0] // 2

    def begin(self):
        self.begin_links()
        self.begin_core()

    def begin_links(self):
        self.x = self.plane.send(self.own, self.pieces.at[1], "x")
        self.y = self.plane.send(self.own, self.pieces.at[2], "y")

    def begin_core(self):
        self.c = [self.plane.send(self.own, self.pieces.at[4], "c")]

    def middle(self):
        send, half, pieces = self.plane.send, self.half, self.pieces
        self.x.wait_recv()
        self.fy = send(pieces.at[1, pl.ds(half, half)], pieces.at[3, pl.ds(half, half)], "y")
        self.c.append(send(pieces.at[1], pieces.at[5], "c"))
        self.y.wait_recv()
        self.fx = send(pieces.at[2, pl.ds(0, half)], pieces.at[3, pl.ds(0, half)], "x")
        self.c.append(send(pieces.at[2], pieces.at[6], "c"))

    def end(self):
        self.fx.wait_recv()
        self.fy.wait_recv()
        self.c.append(self.plane.send(self.pieces.at[3], self.pieces.at[7], "c"))

    def core(self, index):
        self.c[index].wait_recv()


class Reduce:
    def __init__(self, plane, pieces, from_core, from_x, from_y):
        self.plane, self.pieces = plane, pieces
        self.from_core, self.from_x, self.from_y = from_core, from_x, from_y
        self.half = pieces.shape[1] // 2
        self.core = {}

    def give(self, m):
        self.core[m] = self.plane.send(self.pieces.at[4 + m], self.from_core.at[m], "c")

    def take(self, m):
        self.core[m].wait_recv()

    def chip_done(self, m):
        send, half, pieces = self.plane.send, self.half, self.pieces
        low, high = pl.ds(0, half), pl.ds(half, half)
        if m == 3:
            self.far_x = send(pieces.at[3, low], self.from_x.at[1], "x")
            self.far_y = send(pieces.at[3, high], self.from_y.at[1], "y")
        elif m == 1:
            self.near_x = send(pieces.at[1, low], self.from_x.at[0], "x")
        elif m == 2:
            self.near_y = send(pieces.at[2, high], self.from_y.at[0], "y")

    def late_x(self):
        high = pl.ds(self.half, self.half)
        self.far_y.wait_recv()
        add_into(self.pieces.at[1, high], self.from_y.at[1])
        self.late_x_copy = self.plane.send(self.pieces.at[1, high], self.from_x.at[2], "x")

    def late_y(self):
        low = pl.ds(0, self.half)
        self.far_x.wait_recv()
        add_into(self.pieces.at[2, low], self.from_x.at[1])
        self.late_y_copy = self.plane.send(self.pieces.at[2, low], self.from_y.at[2], "y")

    def late(self):
        self.late_x()
        self.late_y()

    def total(self, out):
        half = self.half
        self.near_x.wait_recv()
        self.near_y.wait_recv()
        self.late_x_copy.wait_recv()
        self.late_y_copy.wait_recv()
        step = min(64, half)

        for base, x_part, y_part in ((0, 0, 2), (half, 2, 0)):

            def add(index, carry):
                at = pl.ds(pl.multiple_of(index * step, step), step)
                here = pl.ds(pl.multiple_of(base + index * step, step), step)
                out[here] = (
                    self.pieces[0, here].astype(f32)
                    + self.from_x[x_part, at].astype(f32)
                    + self.from_y[y_part, at].astype(f32)
                )
                return carry

            lax.fori_loop(0, half // step, add, 0)


def add_into(ref, other):
    step = min(64, ref.shape[0])

    def add(index, carry):
        at = pl.ds(pl.multiple_of(index * step, step), step)
        ref[at] = (ref[at].astype(f32) + other[at].astype(f32)).astype(bf16)
        return carry

    lax.fori_loop(0, ref.shape[0] // step, add, 0)


class Ring:
    def __init__(self, plane, own, blocks):
        self.plane, self.own, self.blocks = plane, own, blocks
        self.z = lax.axis_index("tensor")
        self.came = None

    @staticmethod
    def places():
        me, z = lax.axis_index("dp"), lax.axis_index("tensor")
        return [(me, lax.rem(z + 1, 4)), (me, lax.rem(z + 3, 4))]

    def step(self, index):
        if self.came is not None:
            self.came.wait_recv()
        if index < 3:
            block = self.blocks(lax.rem(self.z + 4 - index, 4))
            source = self.own if index == 0 else block
            self.came = self.plane.send_to(source, block, {"tensor": lax.rem(self.z + 1, 4)})


ORDER = (3, 1, 2, 0)


def tiles(count, tile, body):
    tile = min(tile, count)

    def step(index, carry):
        body(pl.ds(pl.multiple_of(index * tile, tile), tile))
        return carry

    lax.fori_loop(0, count // tile, step, 0)


def nn(left, right):
    return jnp.dot(left, right, preferred_element_type=f32)


def nt(left, right):
    return lax.dot_general(left, right, (((1,), (1,)), ((), ())), preferred_element_type=f32)


def tn(left, right):
    return lax.dot_general(left, right, (((0,), (0,)), ((), ())), preferred_element_type=f32)


class Feed:
    def __init__(self, source, slots, sems, order):
        self.source, self.slots, self.sems, self.order = source, slots, sems, list(order)

    def copy(self, index):
        slot = index % 2
        return pltpu.make_async_copy(
            self.source(self.order[index]), self.slots.at[slot], self.sems.at[slot]
        )

    def start(self, index):
        if index < len(self.order):
            self.copy(index).start()

    def get(self, index):
        self.copy(index).wait()
        return self.slots.at[index % 2]


def plane_call(kernel, name, collective_id, out_shape, in_spaces, out_spaces, scratch, copies, flops, args):
    spaces = {"any": pl.ANY, "vmem": pltpu.VMEM, "smem": pltpu.SMEM}
    return pl.pallas_call(
        kernel,
        out_shape=out_shape,
        in_specs=[pl.BlockSpec(memory_space=spaces[v]) for v in in_spaces],
        out_specs=[pl.BlockSpec(memory_space=spaces[v]) for v in out_spaces],
        scratch_shapes=list(scratch)
        + [pltpu.SemaphoreType.DMA((copies,)), pltpu.SemaphoreType.DMA((copies,))],
        compiler_params=pltpu.CompilerParams(
            collective_id=collective_id, has_side_effects=True, vmem_limit_bytes=62 << 20
        ),
        cost_estimate=pl.CostEstimate(flops=flops, bytes_accessed=64 << 20, transcendentals=0),
        name=name,
    )(*args)


def row_places():
    me, plane = lax.axis_index("dp"), lax.axis_index("tensor")
    chip, core = 2 * (me // 2), me % 2
    outward = [(chip + 1 - plane // 2, 2 * core + j) for j in range(2)]
    inward = [(chip + plane // 2, 2 * (1 - core) + i) for i in range(2)]
    return outward, inward


def at_device(place):
    return {"dp": place[0], "tensor": place[1]}


class RowMove:
    def __init__(self, src, dst, sems):
        self.src, self.dst, self.sems = src, dst, sems
        self.copies = []

    def copy(self, here, there, place):
        return pltpu.make_async_remote_copy(
            src_ref=self.src.at[here],
            dst_ref=self.dst.at[there],
            send_sem=self.sems.at[0, here],
            recv_sem=self.sems.at[1, there],
            device_id=at_device(place),
            device_id_type=MESH,
        )

    def start(self, places, there):
        for here in range(2):
            copy = self.copy(here, there, places[here])
            copy.start()
            self.copies.append(copy)
        self.arrivals = [self.copy(index, index, places[index]) for index in range(2)]

    def outward(self):
        self.start(row_places()[0], lax.axis_index("tensor") % 2)

    def back(self):
        self.start(row_places()[1], lax.axis_index("tensor") % 2)

    def wait(self):
        for copy in self.copies:
            copy.wait_send()
        for copy in self.arrivals:
            copy.wait_recv()


def start_kernel(
    tokens, w_query, w_key, w_value, w_out, w_up, w_down, small,
    tokens_out, qkv_out, out_out, up_out, down_out, small_out,
    local_sems, row_sems, send_sems, recv_sems,
):
    me, plane = lax.axis_index("dp"), lax.axis_index("tensor")
    chip, core = me // 2, me % 2
    depth = w_query.shape[0]
    part = up_out.shape[1]
    outward, inward = row_places()
    peers = [lax.rem(me + j, 8) for j in range(1, 8)]
    barrier = pltpu.get_barrier_semaphore()
    for peer in peers:
        pl.semaphore_signal(barrier, inc=1, device_id={"dp": peer}, device_id_type=MESH)
    for place in outward + inward:
        pl.semaphore_signal(barrier, inc=1, device_id=at_device(place), device_id_type=MESH)
    pl.semaphore_wait(barrier, 11)
    copies, locals_ = [], []

    def send(src, dst, device):
        copy = pltpu.make_async_remote_copy(
            src_ref=src,
            dst_ref=dst,
            send_sem=send_sems.at[len(copies)],
            recv_sem=recv_sems.at[len(copies)],
            device_id=device,
            device_id_type=MESH,
        )
        copy.start()
        copies.append(copy)

    def keep(src, dst):
        copy = pltpu.make_async_copy(src, dst, local_sems.at[len(locals_)])
        copy.start()
        locals_.append(copy)

    def block(index, size):
        return pl.ds(pl.multiple_of(index * size, size), size)

    rows_move = RowMove(tokens, tokens_out, row_sems)
    rows_move.outward()
    for peer in peers:
        send(small, small_out.at[me], {"dp": peer})
    keep(small, small_out.at[me])
    heads = [(w_query, 0), (w_key, 1), (w_value, 2)]
    for j in range(1, 4):
        other = lax.rem(chip + j, 4)
        device = {"dp": 2 * other + core}
        for weight, which in heads:
            send(weight.at[:, block(other, HEAD)], qkv_out.at[which, chip], device)
    for weight, which in heads:
        keep(weight.at[:, block(chip, HEAD)], qkv_out.at[which, chip])
    for j in range(1, 4):
        other = lax.rem(chip + j, 4)
        send(w_out.at[block(other, HEAD)], out_out.at[chip], {"dp": 2 * other + core})
    keep(w_out.at[block(chip, HEAD)], out_out.at[chip])
    for peer in peers:
        send(w_up.at[:, block(peer, part)], up_out.at[block(me, depth)], {"dp": peer})
        send(w_down.at[block(peer, part)], down_out.at[:, block(me, depth)], {"dp": peer})
    keep(w_up.at[:, block(me, part)], up_out.at[block(me, depth)])
    keep(w_down.at[block(me, part)], down_out.at[:, block(me, depth)])
    for copy in locals_:
        copy.wait()
    for copy in copies:
        copy.wait()
    rows_move.wait()


def gather_kernel(own, rows_in, pieces, rows_out, own_sem, row_sems, send_sems, recv_sems):
    outward, inward = row_places()
    plane = Plane(send_sems, recv_sems, outward + inward)
    streams = own.shape[0]
    rows_move = RowMove(rows_in, rows_out, row_sems)
    rows_move.outward()
    gathers = [Gather(plane, own.at[s], pieces.at[s]) for s in range(streams)]
    keep = [pltpu.make_async_copy(own.at[s], pieces.at[s, 0], own_sem.at[s]) for s in range(streams)]
    for s in range(streams):
        gathers[s].begin()
        keep[s].start()
    for s in range(streams):
        gathers[s].middle()
    for s in range(streams):
        gathers[s].end()
    for s in range(streams):
        keep[s].wait()
        for index in range(4):
            gathers[s].core(index)
    rows_move.wait()
    plane.finish()


def chunk_at(plane, s):
    k = 1 - s // 2
    return s % 2, k + plane.core - 2 * k * plane.core


def chunk_part(plane, qkv, chip, head):
    def part(s, which):
        column = pl.multiple_of((head * 3 + which) * HEAD, HEAD)
        stream, core = chunk_at(plane, s)
        piece = core * (qkv.shape[1] // 2) + chip
        return qkv[stream, piece, :, pl.ds(column, HEAD)]

    return part


def attend_all(plane, qkv, ends_ref, out, clip_count):
    rows = qkv.shape[2]
    heads = qkv.shape[3] // (3 * HEAD)

    def one(index, carry):
        chip, head = index // heads, index % heads
        part = chunk_part(plane, qkv, chip, head)
        column = pl.ds(pl.multiple_of(head * HEAD, HEAD), HEAD)
        for s in range(4):
            start = clip_starts(ends_ref, 0, chip, clip_count, s, rows)
            cs, probs = chunk_probs(part(s, 0), lambda c: part(c, 1), start, s, rows)
            mixed = jnp.zeros((rows, HEAD), f32)
            for c, prob in zip(cs, probs):
                mixed = mixed + nn(prob.astype(bf16), part(c, 2))
            stream, core = chunk_at(plane, s)
            out[stream, core * 4 + chip, :, column] = mixed.astype(bf16)
        return carry

    return one


def attend_back_chip(plane, qkv, grad_mixed, ends_ref, out, key_sum, value_sum, clip_count, chip):
    rows = qkv.shape[2]
    heads = qkv.shape[3] // (3 * HEAD)

    def one(head, carry):
        part = chunk_part(plane, qkv, 0, head)
        column = pl.ds(pl.multiple_of(head * HEAD, HEAD), HEAD)
        key_sum[...] = jnp.zeros_like(key_sum)
        value_sum[...] = jnp.zeros_like(value_sum)

        def put(s, which, value):
            at = pl.ds(pl.multiple_of((head * 3 + which) * HEAD, HEAD), HEAD)
            stream, core = chunk_at(plane, s)
            out[stream, core, :, at] = value.astype(bf16)

        for s in range(4):
            q = part(s, 0)
            stream, core = chunk_at(plane, s)
            g = grad_mixed[stream, core * 4 + chip, :, column]
            start = clip_starts(ends_ref, 0, chip, clip_count, s, rows)
            cs, probs = chunk_probs(q, lambda c: part(c, 1), start, s, rows)
            grad_probs = [nt(g, part(c, 2)) for c in cs]
            inner = functools.reduce(
                jnp.add,
                [jnp.sum(p * v, axis=1, keepdims=True) for p, v in zip(probs, grad_probs)],
            )
            grad_q = jnp.zeros((rows, HEAD), f32)
            for c, prob, grad_prob in zip(cs, probs, grad_probs):
                grad_score = (prob * (grad_prob - inner) * HEAD ** (-0.5)).astype(bf16)
                grad_q = grad_q + nn(grad_score, part(c, 1))
                key_sum[c] += tn(grad_score, q)
                value_sum[c] += tn(prob.astype(bf16), g)
            put(s, 0, grad_q)
        for s in range(4):
            put(s, 1, key_sum[s])
            put(s, 2, value_sum[s])
        return carry

    lax.fori_loop(0, heads, one, 0)


def attention_kernel(
    clip_count, own, rows_in, wide, up_part, ends, pieces, qkv, mixed, weight, up_wide,
    slots, slot_sems, own_sem, wide_sems, send_sems, recv_sems,
):
    plane = Plane(send_sems, recv_sems, Ring.places())
    ring = Ring(plane, up_part, lambda index: up_wide.at[index])
    own_up = pltpu.make_async_copy(up_part, up_wide.at[ring.z], wide_sems.at[6])
    own_up.start()
    streams = own.shape[0]
    gathers = [Gather(plane, own.at[s], pieces.at[s]) for s in range(streams)]
    keep = [pltpu.make_async_copy(own.at[s], pieces.at[s, 0], own_sem.at[s]) for s in range(streams)]
    traded, kept = [], []
    for head in range(2):
        for which in range(3):
            column = pl.ds((head * 3 + which) * HEAD, HEAD)
            here = weight.at[:, plane.core, :, column]
            traded.append(plane.send(wide.at[2 * (1 - plane.core) + head, which], here, "c"))
            copy = pltpu.make_async_copy(
                wide.at[2 * plane.core + head, which], here, wide_sems.at[len(kept)]
            )
            copy.start()
            kept.append(copy)
    for s in range(streams):
        gathers[s].begin()
        keep[s].start()
    ring.step(0)
    total = weight.shape[3]
    feed = Feed(
        lambda at: rows_in.at[at[0], at[1]],
        slots,
        slot_sems,
        [(s, p) for s in range(streams) for p in range(8)],
    )
    feed.start(0)

    def project(s):
        for p in range(8):
            feed.start(s * 8 + p + 1)
            piece = feed.get(s * 8 + p)

            def tile(at):
                columns = weight[:, :, :, at].reshape(width, -1)
                qkv[s, p, :, at] = nn(piece[...], columns).astype(bf16)

            tiles(total, N_TILE, tile)

    for copy in traded:
        copy.wait_recv()
    for copy in kept:
        copy.wait()
    width = own.shape[2]

    attend = attend_all(plane, qkv, ends, mixed, clip_count)
    heads = total // (3 * HEAD)
    project(0)
    project(1)
    lax.fori_loop(0, 2 * heads, attend, 0)
    ring.step(1)
    gathers[0].middle()
    gathers[1].middle()
    lax.fori_loop(2 * heads, 4 * heads, attend, 0)
    ring.step(2)
    gathers[0].end()
    gathers[1].end()
    for s in range(streams):
        keep[s].wait()
        for index in range(4):
            gathers[s].core(index)
    ring.step(3)
    own_up.wait()
    plane.finish()


def reduce_scratch(streams, rows, width):
    return [
        pltpu.VMEM((streams, 8, rows, width), bf16),
        pltpu.VMEM((streams, 4, rows, width), bf16),
        pltpu.VMEM((streams, 3, rows // 2, width), bf16),
        pltpu.VMEM((streams, 3, rows // 2, width), bf16),
    ]


def project_kernel(
    mixed, wide, down_part, out, weight, down_w,
    parts, from_core, from_x, from_y, wide_sems, send_sems, recv_sems,
):
    plane = Plane(send_sems, recv_sems, Ring.places())
    size = down_part.shape[0]

    def down_block(index):
        return down_w.at[pl.ds(pl.multiple_of(index * size, size), size)]

    ring = Ring(plane, down_part, down_block)
    own_down = pltpu.make_async_copy(down_part, down_block(ring.z), wide_sems.at[8])
    own_down.start()
    ring.step(0)
    streams = mixed.shape[0]
    width = weight.shape[1]
    depth = wide.shape[3]
    traded, kept = [], []
    for head in range(2):
        for chip in range(4):
            column = pl.ds(pl.multiple_of((2 * chip + plane.core) * depth, depth), depth)
            here = weight.at[pl.ds(head * HEAD, HEAD), column]
            traded.append(plane.send(wide.at[2 * (1 - plane.core) + head, chip], here, "c"))
            copy = pltpu.make_async_copy(
                wide.at[2 * plane.core + head, chip], here, wide_sems.at[len(kept)]
            )
            copy.start()
            kept.append(copy)
    for copy in traded:
        copy.wait_recv()
    for copy in kept:
        copy.wait()
    sums = [
        Reduce(plane, parts.at[s], from_core.at[s], from_x.at[s], from_y.at[s])
        for s in range(streams)
    ]

    for s in range(streams):
        for m in ORDER:

            def other(at):
                parts[s, 4 + m, :, at] = nn(mixed[s, 4 + m], weight[:, at]).astype(bf16)

            tiles(width, N_TILE, other)
            sums[s].give(m)
        for m in ORDER:
            sums[s].take(m)

            def chip(at):
                here = nn(mixed[s, m], weight[:, at])
                parts[s, m, :, at] = (here + from_core[s, m, :, at].astype(f32)).astype(bf16)

            tiles(width, N_TILE, chip)
            sums[s].chip_done(m)
    ring.step(1)
    sums[0].late()
    ring.step(2)
    sums[1].late()
    for s in range(streams):
        sums[s].total(out.at[s])
    ring.step(3)
    own_down.wait()
    plane.finish()


def gelu_pair(v):
    cubic = 0.044715 * (v * v) * v
    inner = (2.0 / np.pi) ** 0.5 * (v + cubic)
    th = jnp.tanh(inner)
    half = 0.5 * (1.0 + th)
    slope = (2.0 / np.pi) ** 0.5 * (1.0 + 3.0 * 0.044715 * (v * v))
    return v * half, half + 0.5 * v * (1.0 - th * th) * slope


def lay_out(wide, flat, sems):
    copies = []
    part = wide.shape[2]
    for plane in range(wide.shape[0]):
        copy = pltpu.make_async_copy(
            wide.at[plane], flat.at[:, pl.ds(plane * part, part)], sems.at[plane]
        )
        copy.start()
        copies.append(copy)
    return copies


def mlp_kernel(
    own, up_wide, down_w, grads, pieces, slope_out, down_grad, out,
    parts, from_core, from_x, from_y, up_w, slots, act, slope, total, grad_slots,
    up_sems, slot_sems, keep_sems, own_sem, grad_sems, send_sems, recv_sems,
):
    plane = Plane(send_sems, recv_sems)
    streams, rows, width = own.shape
    hidden = up_w.shape[1]
    up_copies = lay_out(up_wide, up_w, up_sems)
    gathers = [Gather(plane, own.at[s], pieces.at[s]) for s in range(streams)]
    sums = [
        Reduce(plane, parts.at[s], from_core.at[s], from_x.at[s], from_y.at[s])
        for s in range(streams)
    ]
    keep = [pltpu.make_async_copy(own.at[s], pieces.at[s, 0], own_sem.at[s]) for s in range(streams)]
    stores = []

    def up_piece(s, p, slot):
        if len(stores) >= 2:
            stores[-2].wait()

        def up(at):
            value, grad = gelu_pair(nn(slots[slot], up_w[:, at]))
            act[slot, :, at] = value.astype(bf16)
            slope[slot, :, at] = grad.astype(bf16)

        tiles(hidden, N_TILE, up)
        store = pltpu.make_async_copy(slope.at[slot], slope_out.at[s, p], keep_sems.at[slot])
        store.start()
        stores.append(store)

    def down_piece(s, p, slot):
        def down(at):
            here = nn(act[slot], down_w[:, at])
            if p < 4:
                here = here + from_core[s, p, :, at].astype(f32)
            parts[s, p, :, at] = here.astype(bf16)

        tiles(width, N_TILE, down)

    def pair_up(s, m):
        if m > 0:
            gathers[s].core(m)
        first = not stores
        rows_come = [
            pltpu.make_async_copy(
                own.at[s] if p == 0 else pieces.at[s, p], slots.at[i], slot_sems.at[i]
            )
            for i, p in enumerate((4 + m, m))
        ]
        coming = [
            pltpu.make_async_copy(grads.at[s, p], grad_slots.at[i], grad_sems.at[i])
            for i, p in enumerate((4 + m, m))
        ]
        if m == 0:
            rows_come[1].start()
            gathers[s].core(0)
            rows_come[0].start()
        else:
            rows_come[0].start()
            rows_come[1].start()
        for copy in coming:
            copy.start()
        rows_come[0].wait()
        up_piece(s, 4 + m, 0)
        down_piece(s, 4 + m, 0)
        sums[s].give(m)
        rows_come[1].wait()
        up_piece(s, m, 1)
        for copy in coming:
            copy.wait()
        left = act[...].reshape(2 * rows, hidden)

        def weigh(at):
            term = tn(left, grad_slots[:, :, at].reshape(2 * rows, -1))
            total[:, at] = term if first else total[:, at] + term

        tiles(width, 512, weigh)
        sums[s].take(m)
        down_piece(s, m, 1)
        sums[s].chip_done(m)

    for s in range(streams):
        keep[s].start()
        gathers[s].begin_core()
    gathers[0].begin_links()
    for copy in up_copies:
        copy.wait()
    pair_up(0, 0)
    pair_up(1, 0)
    gathers[0].middle()
    gathers[1].begin_links()
    pair_up(0, 1)
    pair_up(0, 2)
    gathers[0].end()
    pair_up(0, 3)
    gathers[1].middle()
    pair_up(1, 1)
    sums[0].late()
    gathers[1].end()
    pair_up(1, 3)
    pair_up(1, 2)
    sums[1].late()
    for s in range(streams):
        sums[s].total(out.at[s])
        keep[s].wait()
    for store in stores[-2:]:
        store.wait()
    stores = []
    for index in range(hidden // rows):
        if index >= 2:
            stores[index - 2].wait()
        here = pl.ds(index * rows, rows)
        slots[index % 2] = total[here].astype(bf16)
        store = pltpu.make_async_copy(
            slots.at[index % 2], down_grad.at[here], keep_sems.at[index % 2]
        )
        store.start()
        stores.append(store)
    for store in stores[-2:]:
        store.wait()
    plane.finish()


def mlp_back_kernel(
    grads, slope_in, features, up_wide, down_w, up_grad, out,
    parts, from_core, from_x, from_y, up_w, slots, slopes, pre, rows_two, total,
    up_sems, slot_sems, slope_sems, row_sems, keep_sems, send_sems, recv_sems,
):
    plane = Plane(send_sems, recv_sems)
    streams, _, rows, width = grads.shape
    hidden = up_w.shape[1]
    part = up_wide.shape[2]
    up_copies = lay_out(up_wide, up_w, up_sems)
    sums = [
        Reduce(plane, parts.at[s], from_core.at[s], from_x.at[s], from_y.at[s])
        for s in range(streams)
    ]
    order = [(s, p) for s in range(streams) for m in ORDER for p in (4 + m, m)]
    feed = Feed(lambda at: grads.at[at[0], at[1]], slots, slot_sems, order)
    feed_slope = Feed(lambda at: slope_in.at[at[0], at[1]], slopes, slope_sems, order)
    feed_rows = Feed(lambda at: features.at[at[0], at[1]], rows_two, row_sems, order)
    feed.start(0)
    feed_slope.start(0)
    def back_piece(index):
        feed.start(index + 1)
        feed_slope.start(index + 1)
        feed_rows.start(index)
        grad = feed.get(index)
        slope = feed_slope.get(index)

        def back(at):
            value = nt(grad[...], down_w[at]) * slope[:, at].astype(f32)
            pre[index % 2, :, at] = value.astype(bf16)

        tiles(hidden, N_TILE, back)

    def through_piece(index, s, p):
        def through(at):
            here = nt(pre[index % 2], up_w[at])
            if p < 4:
                here = here + from_core[s, p, :, at].astype(f32)
            parts[s, p, :, at] = here.astype(bf16)

        tiles(width, N_TILE, through)

    for index, (s, p) in enumerate(order):
        back_piece(index)
        if index == 0:
            for copy in up_copies:
                copy.wait()
        if p >= 4:
            through_piece(index, s, p)
            sums[s].give(p - 4)
            continue
        feed_rows.get(index - 1)
        feed_rows.get(index)
        right = pre[...].reshape(2 * rows, hidden)

        def weigh(at):
            term = tn(rows_two[:, :, at].reshape(2 * rows, -1), right)
            total[at] = term if index == 1 else total[at] + term

        tiles(width, 512, weigh)
        sums[s].take(p)
        through_piece(index, s, p)
        sums[s].chip_done(p)
        if p == 2:
            sums[s].late_x()
        if p == 0:
            sums[s].late_y()
    stores = []
    for index in range(width // rows):
        slot = index % 2
        for store in stores[index - 2] if index >= 2 else []:
            store.wait()
        here = pl.ds(index * rows, rows)
        pre[slot] = total[here].astype(bf16)
        stores.append([])
        for at in range(hidden // part):
            store = pltpu.make_async_copy(
                pre.at[slot, :, pl.ds(at * part, part)], up_grad.at[at, here], keep_sems.at[slot, at]
            )
            store.start()
            stores[-1].append(store)
    for s in range(streams):
        sums[s].total(out.at[s])
    for pair in stores[-2:]:
        for store in pair:
            store.wait()
    plane.finish()


def attention_back_kernel(
    clip_count, own, qkv, mixed, features, rows_in, qkv_w, out_w, ends,
    pieces, qkv_grad, out_grad, rows_out, out,
    parts, from_core, from_x, from_y, slots, mixed_slots, grad_mixed, qkv_chip, grad_chip, key_sum, value_sum,
    qkv_sum, out_sum, slot_sems, mixed_sems, chip_sems, store_sems, row_sems, own_sem, send_sems, recv_sems,
):
    outward, inward = row_places()
    plane = Plane(send_sems, recv_sems, outward + inward)
    rows_move = RowMove(rows_in, rows_out, row_sems)
    rows_move.back()
    streams, rows, width = own.shape
    gathers = [Gather(plane, own.at[s], pieces.at[s]) for s in range(streams)]
    sums = [
        Reduce(plane, parts.at[s], from_core.at[s], from_x.at[s], from_y.at[s])
        for s in range(streams)
    ]
    keep = [pltpu.make_async_copy(own.at[s], pieces.at[s, 0], own_sem.at[s]) for s in range(streams)]
    def load_chip(m):
        copies = [
            pltpu.make_async_copy(
                qkv.at[s, core * 4 + m], qkv_chip.at[s, core], chip_sems.at[s * 2 + core]
            )
            for s in range(streams)
            for core in range(2)
        ]
        for copy in copies:
            copy.start()
        return copies

    def load_rows(m):
        copies = [
            pltpu.make_async_copy(
                features.at[s, core * 4 + m], slots.at[s * 2 + core], slot_sems.at[s * 2 + core]
            )
            for s in range(streams)
            for core in range(2)
        ]
        for copy in copies:
            copy.start()
        return copies

    def weigh_chip(place, copies):
        for copy in copies:
            copy.wait()
        right = grad_chip[place % 2].reshape(4 * rows, -1)

        def weigh(at):
            term = tn(slots[:, :, at].reshape(4 * rows, -1), right)
            qkv_sum[at] = term if place == 0 else qkv_sum[at] + term

        tiles(width, 512, weigh)

    mixed_before = []

    def mix_pair(s, m):
        pair = (m, 4 + m)
        rows_come = [
            pltpu.make_async_copy(
                own.at[s] if p == 0 else pieces.at[s, p], slots.at[i], slot_sems.at[i]
            )
            for i, p in enumerate(pair)
        ]
        left_come = [
            pltpu.make_async_copy(mixed.at[s, p], mixed_slots.at[i], mixed_sems.at[i])
            for i, p in enumerate(pair)
        ]
        rows_come[0].start()
        for copy in left_come:
            copy.start()
        gathers[s].core(m)
        rows_come[1].start()
        for i, p in enumerate(pair):
            rows_come[i].wait()
            grad_mixed[s, p] = nt(slots[i], out_w[...]).astype(bf16)
        for copy in left_come:
            copy.wait()
        left = mixed_slots[...].reshape(2 * rows, -1)
        first = not mixed_before
        mixed_before.append(m)

        def weigh(at):
            term = tn(left, slots[pl.ds(0, 2), :, at].reshape(2 * rows, -1))
            out_sum[:, at] = term if first else out_sum[:, at] + term

        tiles(width, N_TILE, weigh)

    def attend_chip(place, m, coming, following):
        for copy in coming:
            copy.wait()
        grad_here = grad_chip.at[place % 2]
        attend_back_chip(
            plane, qkv_chip, grad_mixed, ends, grad_here, key_sum, value_sum, clip_count, m
        )
        coming = load_chip(following) if following is not None else []
        for s in range(streams):

            def other(at):
                parts[s, 4 + m, :, at] = nt(grad_here[s, 1], qkv_w[at]).astype(bf16)

            tiles(width, N_TILE, other)
            sums[s].give(m)
        for s in range(streams):
            sums[s].take(m)

            def chip(at):
                here = nt(grad_here[s, 0], qkv_w[at])
                parts[s, m, :, at] = (here + from_core[s, m, :, at].astype(f32)).astype(bf16)

            tiles(width, N_TILE, chip)
            sums[s].chip_done(m)
        return coming

    for s in range(streams):
        keep[s].start()
        gathers[s].begin_core()
    gathers[0].begin_links()
    coming = load_chip(0)
    mix_pair(0, 0)
    mix_pair(1, 0)
    coming = attend_chip(0, 0, coming, 1)
    gathers[0].middle()
    gathers[1].begin_links()
    mix_pair(0, 1)
    mix_pair(0, 2)
    weigh_chip(0, load_rows(0))
    gathers[0].end()
    mix_pair(0, 3)
    gathers[1].middle()
    mix_pair(1, 1)
    mix_pair(1, 2)
    coming = attend_chip(1, 1, coming, 3)
    gathers[1].end()
    mix_pair(1, 3)
    coming_rows = load_rows(1)
    coming = attend_chip(2, 3, coming, 2)
    weigh_chip(1, coming_rows)
    coming_rows = load_rows(3)
    attend_chip(3, 2, coming, None)
    for s in range(streams):
        sums[s].late_x()
    for s in range(streams):
        sums[s].late_y()
    weigh_chip(2, coming_rows)
    weigh_chip(3, load_rows(2))
    for index in range(out_sum.shape[0] // rows):
        here = pl.ds(index * rows, rows)
        slots[0] = out_sum[here].astype(bf16)
        out_store = pltpu.make_async_copy(slots.at[0], out_grad.at[here], slot_sems.at[0])
        out_store.start()
        out_store.wait()
    stores = []
    for index in range(width // rows):
        if index >= 4:
            stores[index - 4].wait()
        here = pl.ds(index * rows, rows)
        stage = grad_chip.at[0, index // 2 % 2, index % 2]
        stage[...] = qkv_sum[here].astype(bf16)
        store = pltpu.make_async_copy(stage, qkv_grad.at[here], store_sems.at[index % 4])
        store.start()
        stores.append(store)
    for s in range(streams):
        sums[s].total(out.at[s])
        keep[s].wait()
    for store in stores[-4:]:
        store.wait()
    rows_move.wait()
    plane.finish()


def end_kernel(
    rows_in, qkv_grad, out_grad, up_sum, down_sum, gains,
    rows_out, qkv_out, out_out, up_out, down_out, gains_out,
    qkv_part, out_part, qkv_come, out_come, gain_come, gain_sum, gain_all,
    rows_got, qkv_got, out_got, up_got, down_got, local_sems, row_sems, send_sems, recv_sems,
):
    me, z = lax.axis_index("dp"), lax.axis_index("tensor")
    chip, core = me // 2, me % 2
    depth = qkv_grad.shape[2]
    outward, inward = row_places()
    peers = [lax.rem(me + j, 8) for j in range(1, 8)]
    planes = [lax.rem(z + j, 4) for j in range(1, 4)]
    barrier = pltpu.get_barrier_semaphore()
    for peer in peers:
        pl.semaphore_signal(barrier, inc=1, device_id={"dp": peer}, device_id_type=MESH)
    for plane in planes:
        pl.semaphore_signal(barrier, inc=1, device_id={"tensor": plane}, device_id_type=MESH)
    for place in outward + inward:
        pl.semaphore_signal(barrier, inc=1, device_id=at_device(place), device_id_type=MESH)
    pl.semaphore_wait(barrier, 14)
    copies, locals_ = [], []

    def send(src, dst, device):
        copy = pltpu.make_async_remote_copy(
            src_ref=src,
            dst_ref=dst,
            send_sem=send_sems.at[len(copies)],
            recv_sem=recv_sems.at[len(copies)],
            device_id=device,
            device_id_type=MESH,
        )
        copy.start()
        copies.append(copy)
        return copy

    def keep(src, dst):
        copy = pltpu.make_async_copy(src, dst, local_sems.at[len(locals_)])
        copy.start()
        locals_.append(copy)

    def block(index, size):
        return pl.ds(pl.multiple_of(index * size, size), size)

    other = {"dp": me + 1 - 2 * core}
    traded = []
    for head in range(2):
        mine = 2 * core + head
        for which in range(3):
            column = pl.ds((head * 3 + which) * HEAD, HEAD)
            traded.append(
                send(qkv_grad.at[:, 1 - core, :, column], qkv_part.at[mine, which], other)
            )
            keep(qkv_grad.at[:, core, :, column], qkv_part.at[mine, which])
        here = pl.ds(head * HEAD, HEAD)
        for c in range(4):
            theirs = pl.ds(pl.multiple_of((2 * c + 1 - core) * depth, depth), depth)
            own = pl.ds(pl.multiple_of((2 * c + core) * depth, depth), depth)
            traded.append(send(out_grad.at[here, theirs], out_part.at[mine, c], other))
            keep(out_grad.at[here, own], out_part.at[mine, c])
    gain_first = [send(gains.at[peer], gain_come.at[me], {"dp": peer}) for peer in peers]
    gain_come[me] = gains[me]
    begun = len(locals_)
    part = up_sum.shape[1]
    shards = []
    for peer in peers:
        shards.append(send(up_sum.at[block(peer, depth)], up_got.at[:, block(me, part)], {"dp": peer}))
        shards.append(send(down_sum.at[:, block(peer, depth)], down_got.at[block(me, part)], {"dp": peer}))
    keep(up_sum.at[block(me, depth)], up_got.at[:, block(me, part)])
    keep(down_sum.at[:, block(me, depth)], down_got.at[block(me, part)])
    for copy in traded:
        copy.wait_recv()
    for copy in locals_[:begun]:
        copy.wait()
    after = {"tensor": planes[0]}
    for step in range(3):
        part = lax.rem(z + 3 - step, 4)
        ring = [
            send(qkv_part.at[part], qkv_come.at[step], after),
            send(out_part.at[part], out_come.at[step], after),
        ]
        if step == 0:
            rows_move = RowMove(rows_in, rows_got, row_sems)
            rows_move.back()
            for copy in gain_first:
                copy.wait_recv()
            gain_sum[...] = functools.reduce(jnp.add, [gain_come[i] for i in range(8)])
            gain_second = [
                send(gain_sum, gain_all.at[z], {"tensor": plane}) for plane in planes
            ]
            gain_all[z] = gain_sum[...]
        for copy in ring:
            copy.wait_recv()
        part = lax.rem(z + 2 - step, 4) if step < 2 else z
        for which in range(3):
            for c in range(4):
                here = qkv_part.at[part, which, c]
                here[...] = (
                    here[...].astype(f32) + qkv_come[step, which, c].astype(f32)
                ).astype(bf16)
        for c in range(4):
            here = out_part.at[part, c]
            here[...] = (here[...].astype(f32) + out_come[step, c].astype(f32)).astype(bf16)
    last = []
    for j in range(1, 4):
        to = lax.rem(chip + j, 4)
        device = {"dp": 2 * to + core}
        last.append(send(qkv_part.at[z, :, to], qkv_got.at[:, :, block(chip, HEAD)], device))
        last.append(send(out_part.at[z, to], out_got.at[block(chip, HEAD)], device))
    keep(qkv_part.at[z, :, chip], qkv_got.at[:, :, block(chip, HEAD)])
    keep(out_part.at[z, chip], out_got.at[block(chip, HEAD)])
    for copy in gain_second:
        copy.wait_recv()
    gains_out[...] = functools.reduce(jnp.add, [gain_all[i] for i in range(4)])
    for copy in shards:
        copy.wait_recv()
    for copy in locals_[begun:]:
        copy.wait()
    up_out[...] = up_got[...].astype(f32)
    down_out[...] = down_got[...].astype(f32)
    for copy in last:
        copy.wait_recv()
    qkv_out[...] = qkv_got[...].astype(f32)
    out_out[...] = out_got[...].astype(f32)
    rows_move.wait()
    rows_out[...] = rows_got[...].astype(f32)
    for copy in copies:
        copy.wait_send()


def on_device(
    block_input,
    clip_lengths,
    norm1_gain,
    w_query,
    w_key,
    w_value,
    w_out,
    norm2_gain,
    w_up,
    w_down,
    out_cotangent,
):
    streams, rows, width = block_input.shape
    planes = lax.axis_size("tensor")
    lanes = lax.axis_size("dp")
    clip_count = clip_lengths.shape[1]
    own = lax.axis_index("dp")
    own_plane = lax.axis_index("tensor")
    own_core = own % 2
    heads = w_query.shape[1] * planes // (HEAD * lanes)
    depth = w_query.shape[0]
    hidden_part = w_up.shape[1] // lanes
    hidden_own = planes * hidden_part
    inner = heads * HEAD

    small = jnp.zeros((8, depth), f32)
    small = small.at[0].set(norm1_gain.astype(f32)).at[1].set(norm2_gain.astype(f32))
    small = small.at[2, : streams * clip_count].set(clip_lengths.reshape(-1).astype(f32))
    tokens_in, qkv_part, out_part, up_part, down_part, small = plane_call(
        start_kernel,
        "start",
        6,
        [
            jax.ShapeDtypeStruct(block_input.shape, bf16),
            jax.ShapeDtypeStruct((3, 4, depth, HEAD), bf16),
            jax.ShapeDtypeStruct((4, HEAD, depth), bf16),
            jax.ShapeDtypeStruct((width, hidden_part), bf16),
            jax.ShapeDtypeStruct((hidden_part, width), bf16),
            jax.ShapeDtypeStruct((lanes, 8, depth), f32),
        ],
        ["any"] * 8,
        ["any"] * 6,
        [pltpu.SemaphoreType.DMA((7,)), pltpu.SemaphoreType.DMA((2, 2))],
        33,
        0,
        (block_input, w_query, w_key, w_value, w_out, w_up, w_down, small),
    )
    gain_one = small[:, 0].reshape(-1)
    gain_two = small[:, 1].reshape(-1)
    lengths = small[:, 2, : streams * clip_count].reshape(-1, clip_count).astype(jnp.int32)

    qkv_wide = lax.all_gather(qkv_part, "tensor", axis=0, tiled=False)
    out_wide = lax.all_gather(out_part, "tensor", axis=0, tiled=False)

    all_ends = jnp.cumsum(lengths, axis=1)
    buffers = 4 * (own // 2 ^ jnp.arange(4, dtype=jnp.int32)) + own_plane
    ends = jnp.take(all_ends, buffers, axis=0)
    chunks = 2 * (1 - own_core) + jnp.arange(streams, dtype=jnp.int32)
    places = chunks[:, None] * rows + jnp.arange(rows, dtype=jnp.int32)
    valid = (places < ends[0, -1]).astype(f32)
    ends = ends.reshape(-1).astype(jnp.int32)

    pieces = jax.ShapeDtypeStruct((streams, 8, rows, width), bf16)
    sums = jax.ShapeDtypeStruct((streams, rows, width), f32)
    row_count = streams * 8 * rows
    slots = pltpu.VMEM((2, rows, width), bf16)
    dma = pltpu.SemaphoreType.DMA

    def piece_shape(columns):
        return jax.ShapeDtypeStruct((streams, 8, rows, columns), bf16)

    tokens = tokens_in.astype(f32)
    normed_one, unit_one, inverse_one = norm_rows(tokens, gain_one)
    features_one, cotangent = plane_call(
        gather_kernel,
        "gather",
        0,
        [pieces, jax.ShapeDtypeStruct(block_input.shape, bf16)],
        ["any", "any"],
        ["any", "any"],
        [dma((streams,)), dma((2, 2))],
        8 * streams,
        0,
        (normed_one.astype(bf16), out_cotangent),
    )
    grad_out = cotangent.astype(f32) * valid[:, :, None]
    grad_branch, qkv, mixed, qkv_w, up_wide = plane_call(
        functools.partial(attention_kernel, clip_count),
        "attention",
        1,
        [
            pieces,
            piece_shape(3 * inner),
            piece_shape(inner),
            jax.ShapeDtypeStruct((4, 2, depth, 3 * inner), bf16),
            jax.ShapeDtypeStruct((planes, width, hidden_part), bf16),
        ],
        ["any", "any", "any", "any", "smem"],
        ["any", "vmem", "vmem", "vmem", "any"],
        [slots, dma((2,)), dma((streams,)), dma((7,))],
        8 * streams + 9,
        2 * row_count * width * 3 * inner,
        (grad_out.astype(bf16), features_one, qkv_wide, up_part, ends),
    )
    attn_sum, out_w, down_w = plane_call(
        project_kernel,
        "project",
        2,
        [
            sums,
            jax.ShapeDtypeStruct((inner, width), bf16),
            jax.ShapeDtypeStruct((hidden_own, width), bf16),
        ],
        ["vmem", "any", "any"],
        ["vmem", "vmem", "any"],
        reduce_scratch(streams, rows, width) + [dma((9,))],
        10 * streams + 11,
        2 * row_count * width * inner,
        (mixed, out_wide, down_part),
    )
    hidden = tokens + attn_sum
    normed_two, unit_two, inverse_two = norm_rows(hidden, gain_two)
    part = pltpu.VMEM((2, rows, hidden_own), bf16)
    up_flat = pltpu.VMEM((width, hidden_own), bf16)
    features_two, slope, down_dot, mlp_sum = plane_call(
        mlp_kernel,
        "mlp",
        3,
        [
            pieces,
            piece_shape(hidden_own),
            jax.ShapeDtypeStruct((hidden_own, width), bf16),
            sums,
        ],
        ["any", "any", "vmem", "any"],
        ["any", "any", "any", "vmem"],
        reduce_scratch(streams, rows, width)
        + [up_flat, slots, part, part, pltpu.VMEM((hidden_own, width), f32), slots]
        + [dma((planes,)), dma((2,)), dma((2,)), dma((streams,)), dma((2,))],
        18 * streams,
        6 * row_count * width * hidden_own,
        (normed_two.astype(bf16), up_wide, down_w, grad_branch),
    )

    up_dot, back_sum = plane_call(
        mlp_back_kernel,
        "mlp_back",
        4,
        [jax.ShapeDtypeStruct((planes, width, hidden_part), bf16), sums],
        ["any", "any", "any", "any", "vmem"],
        ["any", "vmem"],
        reduce_scratch(streams, rows, width)
        + [up_flat, slots, part, part, slots, pltpu.VMEM((width, hidden_own), f32)]
        + [dma((planes,)), dma((2,)), dma((2,)), dma((2,)), dma((2, planes))],
        10 * streams,
        6 * row_count * width * hidden_own,
        (grad_branch, slope, features_two, up_wide, down_w),
    )
    from_two, gain_two_grad = norm_back(back_sum, unit_two, inverse_two, gain_two)
    grad_hidden = grad_out + from_two
    down_sum = lax.psum_scatter(down_dot, "tensor", scatter_dimension=0, tiled=True)
    grad_hidden, down_sum = lax.optimization_barrier((grad_hidden, down_sum))
    up_sum = lax.psum_scatter(up_dot, "tensor", scatter_dimension=0, tiled=False)
    chunk = pltpu.VMEM((4, rows, HEAD), f32)
    chip_rows = pltpu.VMEM((streams, 2, rows, 3 * inner), bf16)
    _, qkv_dot, out_dot, output, input_sum = plane_call(
        functools.partial(attention_back_kernel, clip_count),
        "attention_back",
        5,
        [
            pieces,
            jax.ShapeDtypeStruct((width, 3 * inner), bf16),
            jax.ShapeDtypeStruct((inner, width), bf16),
            jax.ShapeDtypeStruct(block_input.shape, bf16),
            sums,
        ],
        ["any", "any", "any", "any", "any", "vmem", "vmem", "smem"],
        ["any", "any", "any", "any", "vmem"],
        reduce_scratch(streams, rows, width)
        + [pltpu.VMEM((4, rows, width), bf16), pltpu.VMEM((2, rows, inner), bf16)]
        + [pltpu.VMEM((streams, 8, rows, inner), bf16), chip_rows]
        + [pltpu.VMEM((2, streams, 2, rows, 3 * inner), bf16), chunk, chunk]
        + [pltpu.VMEM((width, 3 * inner), f32), pltpu.VMEM((inner, width), f32)]
        + [dma((4,)), dma((2,)), dma((4,)), dma((4,)), dma((2, 2)), dma((streams,))],
        18 * streams,
        2 * row_count * width * 8 * inner,
        (
            grad_hidden.astype(bf16),
            qkv,
            mixed,
            features_one,
            (hidden + mlp_sum).astype(bf16),
            qkv_w.reshape(width, 3 * inner),
            out_w,
            ends,
        ),
    )
    input_sum, up_sum = lax.optimization_barrier((input_sum, up_sum))
    from_one, gain_one_grad = norm_back(input_sum, unit_one, inverse_one, gain_one)
    gains = jnp.stack([gain_one_grad.sum(0), gain_two_grad.sum(0)]).reshape(2, lanes, depth)
    gains = jnp.zeros((lanes, 8, depth), f32).at[:, :2].set(gains.swapaxes(0, 1))
    small_sum = pltpu.VMEM((8, depth), f32)
    input_grad, qkv_grad, out_grad, up_grad, down_grad, gains = plane_call(
        end_kernel,
        "end",
        7,
        [
            sums,
            jax.ShapeDtypeStruct((3, depth, 4 * HEAD), f32),
            jax.ShapeDtypeStruct((4 * HEAD, depth), f32),
            jax.ShapeDtypeStruct(w_up.shape, f32),
            jax.ShapeDtypeStruct(w_down.shape, f32),
            jax.ShapeDtypeStruct((8, depth), f32),
        ],
        ["any", "any", "any", "any", "any", "vmem"],
        ["vmem"] * 6,
        [
            pltpu.VMEM((4, 3, 4, depth, HEAD), bf16),
            pltpu.VMEM((4, 4, HEAD, depth), bf16),
            pltpu.VMEM((3, 3, 4, depth, HEAD), bf16),
            pltpu.VMEM((3, 4, HEAD, depth), bf16),
            pltpu.VMEM((8, 8, depth), f32),
            small_sum,
            pltpu.VMEM((4, 8, depth), f32),
            pltpu.VMEM(block_input.shape, bf16),
            pltpu.VMEM((3, depth, 4 * HEAD), bf16),
            pltpu.VMEM((4 * HEAD, depth), bf16),
            pltpu.VMEM(w_up.shape, bf16),
            pltpu.VMEM(w_down.shape, bf16),
            dma((18,)),
            dma((2, 2)),
        ],
        50,
        0,
        (
            (grad_hidden + from_one).astype(bf16),
            qkv_dot.reshape(4, 2, depth, 3 * inner),
            out_dot,
            up_sum,
            down_sum,
            gains,
        ),
    )
    return (
        output,
        input_grad,
        gains[0],
        qkv_grad[0],
        qkv_grad[1],
        qkv_grad[2],
        out_grad,
        gains[1],
        up_grad,
        down_grad,
    )


def solution(mesh):
    in_specs = (
        P("dp", "tensor", None),
        P("dp", None),
        P("dp"),
        P("dp", "tensor"),
        P("dp", "tensor"),
        P("dp", "tensor"),
        P("tensor", "dp"),
        P("dp"),
        P("dp", "tensor"),
        P("tensor", "dp"),
        P("dp", "tensor", None),
    )
    out_specs = (
        P("dp", "tensor", None),
        P("dp", "tensor", None),
        P("dp"),
        P("dp", "tensor"),
        P("dp", "tensor"),
        P("dp", "tensor"),
        P("tensor", "dp"),
        P("dp"),
        P("dp", "tensor"),
        P("tensor", "dp"),
    )
    own_form = mesh.shape["dp"] == 8 and mesh.shape["tensor"] == 4
    return jax.shard_map(
        on_device if own_form else on_device_any, mesh=mesh, in_specs=in_specs, out_specs=out_specs, check_vma=False
    )
```

```python
import functools

import jax
import jax.numpy as jnp
import numpy as np
from jax import lax
from jax.experimental import pallas as pl
from jax.experimental.pallas import tpu as pltpu
from jax.sharding import PartitionSpec as P

HEAD = 128
LONGEST = 512
epsilon = 1e-05
masked_fill = -1000000000.0
bf16 = jnp.bfloat16
f32 = jnp.float32


def norm_rows(tokens, gain):
    centred = tokens - jnp.mean(tokens, axis=-1, keepdims=True)
    inverse = lax.rsqrt(jnp.mean(centred * centred, axis=-1, keepdims=True) + epsilon)
    unit_rows = centred * inverse
    return (unit_rows * gain, unit_rows, inverse)


def norm_back(grad_normed, unit_rows, inverse, gain):
    scaled = grad_normed * gain
    inner_sum = (
        scaled
        - jnp.mean(scaled, axis=-1, keepdims=True)
        - unit_rows * jnp.mean(scaled * unit_rows, axis=-1, keepdims=True)
    )
    return (inverse * inner_sum, jnp.sum(grad_normed * unit_rows, axis=0))


def gelu_tanh(values):
    return jax.nn.gelu(values, approximate=True)


def masked_scores(q_rows, keys_heads, segment, offset, block_rows):
    slot_count = keys_heads.shape[0]
    raw_scores = jnp.einsum(
        "qhd,khd->hqk", q_rows, keys_heads, preferred_element_type=jnp.float32
    ) * HEAD ** (-0.5)
    q_segment = lax.dynamic_slice_in_dim(segment, offset, block_rows, 0)
    q_place = offset + jnp.arange(block_rows, dtype=jnp.int32)
    places = jnp.arange(slot_count, dtype=jnp.int32)
    allowed = (q_segment[:, None] == segment[None, :]) & (places[None, :] <= q_place[:, None])
    return jnp.where(allowed[None], raw_scores, masked_fill)


def attend(query, key, value, segment, block_rows):
    slot_count = query.shape[0]
    head_count = query.shape[1] // HEAD
    keys_heads = key.reshape(slot_count, head_count, HEAD)
    values_heads = value.reshape(slot_count, head_count, HEAD)

    def one_block(block_index):
        offset = block_index * block_rows
        q_rows = lax.dynamic_slice_in_dim(query, offset, block_rows, 0).reshape(
            block_rows, head_count, HEAD
        )
        scores = masked_scores(q_rows, keys_heads, segment, offset, block_rows)
        highest = jnp.max(scores, axis=-1, keepdims=True)
        shifted = jnp.exp(scores - highest)
        totals = jnp.sum(shifted, axis=-1, keepdims=True)
        weights = (shifted / totals).astype(jnp.bfloat16)
        mixed_rows = jnp.einsum(
            "hqk,khd->qhd", weights, values_heads, preferred_element_type=jnp.float32
        )
        return (
            mixed_rows.reshape(block_rows, head_count * HEAD).astype(jnp.bfloat16),
            (highest + jnp.log(totals))[..., 0],
        )

    mixed_rows, log_norm = lax.map(one_block, jnp.arange(slot_count // block_rows, dtype=jnp.int32))
    return (mixed_rows.reshape(slot_count, head_count * HEAD), log_norm)


def attend_back(query, key, value, segment, log_norm, grad_mixed, block_rows):
    slot_count = query.shape[0]
    head_count = query.shape[1] // HEAD
    keys_heads = key.reshape(slot_count, head_count, HEAD)
    values_heads = value.reshape(slot_count, head_count, HEAD)

    def one_block(carried, block_index):
        grad_keys, grad_values = carried
        offset = block_index * block_rows
        q_rows = lax.dynamic_slice_in_dim(query, offset, block_rows, 0).reshape(
            block_rows, head_count, HEAD
        )
        g_rows = lax.dynamic_slice_in_dim(grad_mixed, offset, block_rows, 0).reshape(
            block_rows, head_count, HEAD
        )
        scores = masked_scores(q_rows, keys_heads, segment, offset, block_rows)
        prob_rows = jnp.exp(scores - log_norm[block_index][..., None])
        grad_values = grad_values + jnp.einsum(
            "hqk,qhd->khd",
            prob_rows.astype(jnp.bfloat16),
            g_rows,
            preferred_element_type=jnp.float32,
        )
        grad_probs = jnp.einsum(
            "qhd,khd->hqk", g_rows, values_heads, preferred_element_type=jnp.float32
        )
        inner_sum = jnp.sum(prob_rows * grad_probs, axis=-1, keepdims=True)
        grad_scores = (prob_rows * (grad_probs - inner_sum) * HEAD ** (-0.5)).astype(jnp.bfloat16)
        grad_query = jnp.einsum(
            "hqk,khd->qhd", grad_scores, keys_heads, preferred_element_type=jnp.float32
        )
        grad_keys = grad_keys + jnp.einsum(
            "hqk,qhd->khd", grad_scores, q_rows, preferred_element_type=jnp.float32
        )
        return (
            (grad_keys, grad_values),
            grad_query.reshape(block_rows, head_count * HEAD).astype(jnp.bfloat16),
        )

    zero_state = jnp.zeros((slot_count, head_count, HEAD), jnp.float32)
    (grad_keys, grad_values), grad_query = lax.scan(
        one_block, (zero_state, zero_state), jnp.arange(slot_count // block_rows, dtype=jnp.int32)
    )
    return (
        grad_query.reshape(slot_count, head_count * HEAD),
        grad_keys.reshape(slot_count, head_count * HEAD).astype(jnp.bfloat16),
        grad_values.reshape(slot_count, head_count * HEAD).astype(jnp.bfloat16),
    )


def on_device_any(
    block_input,
    clip_lengths,
    norm1_gain,
    w_query,
    w_key,
    w_value,
    w_out,
    norm2_gain,
    w_up,
    w_down,
    out_cotangent,
):
    micro_count = block_input.shape[0]
    local_rows = block_input.shape[1]
    tensor_size = lax.axis_size("tensor")
    slot_count = local_rows * tensor_size
    block_rows = min(512, slot_count)
    clip_count = clip_lengths.shape[1]
    row_offset = lax.axis_index("tensor") * local_rows
    places = jnp.arange(slot_count, dtype=jnp.int32)

    def fetch_weights():
        return (
            lax.all_gather(norm1_gain, "dp", axis=0, tiled=True),
            lax.all_gather(norm2_gain, "dp", axis=0, tiled=True),
            lax.all_gather(w_query, "dp", axis=0, tiled=True),
            lax.all_gather(w_key, "dp", axis=0, tiled=True),
            lax.all_gather(w_value, "dp", axis=0, tiled=True),
            lax.all_gather(w_up, "dp", axis=0, tiled=True),
            lax.all_gather(w_out, "dp", axis=1, tiled=True),
            lax.all_gather(w_down, "dp", axis=1, tiled=True),
        )

    def rows_forward(normed):
        return lax.all_gather(normed, "tensor", axis=0, tiled=True)

    def rows_backward(gradients):
        return lax.all_gather(gradients, "tensor", axis=0, tiled=True)

    def sum_forward(term_fn):
        return lax.psum_scatter(
            term_fn(jnp.int32(0), local_rows * lax.axis_size("tensor")),
            "tensor",
            scatter_dimension=0,
            tiled=True,
        )

    def sum_backward(term_fn):
        return lax.psum_scatter(
            term_fn(jnp.int32(0), local_rows * lax.axis_size("tensor")),
            "tensor",
            scatter_dimension=0,
            tiled=True,
        )

    grad_totals = None
    outputs = []
    input_grads = []
    for micro_index in range(micro_count):
        gathered = fetch_weights()
        gain_one = gathered[0].astype(jnp.float32)
        gain_two = gathered[1].astype(jnp.float32)
        query_w, key_w, value_w, up_w, out_w, down_w = (
            gathered[2],
            gathered[3],
            gathered[4],
            gathered[5],
            gathered[6],
            gathered[7],
        )
        tokens = block_input[micro_index].astype(jnp.float32)
        ends = jnp.cumsum(clip_lengths[micro_index])
        segment = jnp.sum((places[:, None] >= ends[None, :]).astype(jnp.int32), axis=1)
        own_segment = lax.dynamic_slice_in_dim(segment, row_offset, local_rows, 0)
        valid_rows = (own_segment < clip_count).astype(jnp.float32)
        normed_one, unit_one, inverse_one = norm_rows(tokens, gain_one)
        features_one = rows_forward(normed_one.astype(jnp.bfloat16))
        query = jnp.dot(features_one, query_w, preferred_element_type=jnp.float32).astype(
            jnp.bfloat16
        )
        key = jnp.dot(features_one, key_w, preferred_element_type=jnp.float32).astype(jnp.bfloat16)
        value = jnp.dot(features_one, value_w, preferred_element_type=jnp.float32).astype(
            jnp.bfloat16
        )
        mixed_rows, log_norm = attend(query, key, value, segment, block_rows)

        def attn_term(offset, row_count):
            return jnp.dot(mixed_rows, out_w, preferred_element_type=jnp.float32)

        hidden = tokens + sum_forward(attn_term)
        normed_two, unit_two, inverse_two = norm_rows(hidden, gain_two)
        features_two = rows_forward(normed_two.astype(jnp.bfloat16))
        pre_act = jnp.dot(features_two, up_w, preferred_element_type=jnp.float32)
        activated = gelu_tanh(pre_act).astype(jnp.bfloat16)

        def mlp_term(offset, row_count):
            return jnp.dot(activated, down_w, preferred_element_type=jnp.float32)

        outputs.append((hidden + sum_forward(mlp_term)).astype(jnp.bfloat16))
        regathered = fetch_weights()
        query_w, key_w, value_w, up_w, out_w, down_w = (
            regathered[2],
            regathered[3],
            regathered[4],
            regathered[5],
            regathered[6],
            regathered[7],
        )
        grad_out = out_cotangent[micro_index].astype(jnp.float32) * valid_rows[:, None]
        grad_branch = rows_backward(grad_out.astype(jnp.bfloat16))
        down_grad = jnp.einsum(
            "sf,sd->fd", activated, grad_branch, preferred_element_type=jnp.float32
        )
        grad_act = jnp.einsum("sd,fd->sf", grad_branch, down_w, preferred_element_type=jnp.float32)
        grad_pre = jax.vjp(gelu_tanh, pre_act)[1](grad_act)[0].astype(jnp.bfloat16)
        up_grad = jnp.einsum(
            "sd,sf->df", features_two, grad_pre, preferred_element_type=jnp.float32
        )

        def up_term(offset, row_count):
            return jnp.einsum("sf,df->sd", grad_pre, up_w, preferred_element_type=jnp.float32)

        grad_normed_two = sum_backward(up_term)
        grad_from_two, gain_two_grad = norm_back(grad_normed_two, unit_two, inverse_two, gain_two)
        grad_hidden = grad_out + grad_from_two
        grad_attn = rows_backward(grad_hidden.astype(jnp.bfloat16))
        out_grad = jnp.einsum(
            "sc,sd->cd", mixed_rows, grad_attn, preferred_element_type=jnp.float32
        )
        grad_mixed = jnp.einsum(
            "sd,cd->sc", grad_attn, out_w, preferred_element_type=jnp.float32
        ).astype(jnp.bfloat16)
        grad_query, grad_key, grad_value = attend_back(
            query, key, value, segment, log_norm, grad_mixed, block_rows
        )
        query_grad = jnp.einsum(
            "sd,sc->dc", features_one, grad_query, preferred_element_type=jnp.float32
        )
        key_grad = jnp.einsum(
            "sd,sc->dc", features_one, grad_key, preferred_element_type=jnp.float32
        )
        value_grad = jnp.einsum(
            "sd,sc->dc", features_one, grad_value, preferred_element_type=jnp.float32
        )

        def qkv_term(offset, row_count):
            part_query = jnp.einsum(
                "sc,dc->sd", grad_query, query_w, preferred_element_type=jnp.float32
            )
            part_key = jnp.einsum("sc,dc->sd", grad_key, key_w, preferred_element_type=jnp.float32)
            part_value = jnp.einsum(
                "sc,dc->sd", grad_value, value_w, preferred_element_type=jnp.float32
            )
            return part_query + part_key + part_value

        grad_normed_one = sum_backward(qkv_term)
        grad_from_one, gain_one_grad = norm_back(grad_normed_one, unit_one, inverse_one, gain_one)
        input_grads.append(grad_hidden + grad_from_one)
        micro_grads = (
            gain_one_grad,
            gain_two_grad,
            query_grad,
            key_grad,
            value_grad,
            up_grad,
            out_grad,
            down_grad,
        )
        if grad_totals is None:
            grad_totals = micro_grads
        else:
            grad_totals = jax.tree.map(jnp.add, grad_totals, micro_grads)
    grad_totals = (
        lax.psum_scatter(
            grad_totals[0].astype(jnp.bfloat16), "dp", scatter_dimension=0, tiled=True
        ).astype(jnp.float32),
        lax.psum_scatter(
            grad_totals[1].astype(jnp.bfloat16), "dp", scatter_dimension=0, tiled=True
        ).astype(jnp.float32),
        lax.psum_scatter(
            grad_totals[2].astype(jnp.bfloat16), "dp", scatter_dimension=0, tiled=True
        ).astype(jnp.float32),
        lax.psum_scatter(
            grad_totals[3].astype(jnp.bfloat16), "dp", scatter_dimension=0, tiled=True
        ).astype(jnp.float32),
        lax.psum_scatter(
            grad_totals[4].astype(jnp.bfloat16), "dp", scatter_dimension=0, tiled=True
        ).astype(jnp.float32),
        lax.psum_scatter(
            grad_totals[5].astype(jnp.bfloat16), "dp", scatter_dimension=0, tiled=True
        ).astype(jnp.float32),
        lax.psum_scatter(
            grad_totals[6].astype(jnp.bfloat16), "dp", scatter_dimension=1, tiled=True
        ).astype(jnp.float32),
        lax.psum_scatter(
            grad_totals[7].astype(jnp.bfloat16), "dp", scatter_dimension=1, tiled=True
        ).astype(jnp.float32),
    )
    gain_sums = lax.psum((grad_totals[0], grad_totals[1]), "tensor")
    return (
        jnp.stack(outputs),
        jnp.stack(input_grads),
        gain_sums[0],
        grad_totals[2],
        grad_totals[3],
        grad_totals[4],
        grad_totals[6],
        gain_sums[1],
        grad_totals[5],
        grad_totals[7],
    )


def chunk_scores(q, k, start, s, c, rows):
    scores = lax.dot_general(
        q, k, (((1,), (1,)), ((), ())), preferred_element_type=f32
    ) * HEAD ** (-0.5)
    k_place = c * rows + lax.broadcasted_iota(jnp.int32, (rows, rows), 1)
    allowed = k_place >= start
    if c == s:
        q_place = s * rows + lax.broadcasted_iota(jnp.int32, (rows, rows), 0)
        allowed = jnp.logical_and(allowed, k_place <= q_place)
    return jnp.where(allowed, scores, masked_fill)


def clip_starts(ends_ref, first, buffer, clip_count, s, rows):
    place = s * rows + lax.broadcasted_iota(jnp.int32, (rows, 1), 0)
    start = jnp.zeros((rows, 1), jnp.int32)
    for clip in range(clip_count):
        end = ends_ref[first + buffer * clip_count + clip]
        start = jnp.where(place >= end, jnp.maximum(start, end), start)
    return start


def window(s, rows):
    back = -(-(LONGEST - 1) // rows)
    return range(max(0, s - back), s + 1)


def chunk_probs(q, keys, start, s, rows):
    cs = list(window(s, rows))
    scores = [chunk_scores(q, keys(c), start, s, c, rows) for c in cs]
    highest = functools.reduce(jnp.maximum, [jnp.max(v, axis=1, keepdims=True) for v in scores])
    shifted = [jnp.exp(v - highest) for v in scores]
    total = functools.reduce(jnp.add, [jnp.sum(v, axis=1, keepdims=True) for v in shifted])
    scale = 1.0 / total
    return cs, [v * scale for v in shifted]


MESH = pl.DeviceIdType.MESH
N_TILE = 1024


class Plane:
    def __init__(self, send_sems, recv_sems, more=()):
        me = lax.axis_index("dp")
        self.core = me % 2
        self.x = (me // 2) % 2
        self.peers = {
            "c": me + 1 - 2 * (me % 2),
            "x": me + 2 - 4 * ((me // 2) % 2),
            "y": me + 4 - 8 * ((me // 4) % 2),
        }
        self.send_sems, self.recv_sems = send_sems, recv_sems
        self.copies = []
        barrier = pltpu.get_barrier_semaphore()
        for peer in self.peers.values():
            pl.semaphore_signal(barrier, inc=1, device_id={"dp": peer}, device_id_type=MESH)
        for place in more:
            pl.semaphore_signal(barrier, inc=1, device_id=at_device(place), device_id_type=MESH)
        pl.semaphore_wait(barrier, 3 + len(more))

    def send(self, src, dst, way):
        return self.send_to(src, dst, {"dp": self.peers[way]})

    def send_to(self, src, dst, device):
        index = len(self.copies)
        copy = pltpu.make_async_remote_copy(
            src_ref=src,
            dst_ref=dst,
            send_sem=self.send_sems.at[index],
            recv_sem=self.recv_sems.at[index],
            device_id=device,
            device_id_type=MESH,
        )
        copy.start()
        self.copies.append(copy)
        return copy

    def finish(self):
        for copy in self.copies:
            copy.wait_send()


class Gather:
    def __init__(self, plane, own, pieces):
        self.plane, self.own, self.pieces = plane, own, pieces
        self.half = own.shape[0] // 2

    def begin(self):
        self.begin_links()
        self.begin_core()

    def begin_links(self):
        self.x = self.plane.send(self.own, self.pieces.at[1], "x")
        self.y = self.plane.send(self.own, self.pieces.at[2], "y")

    def begin_core(self):
        self.c = [self.plane.send(self.own, self.pieces.at[4], "c")]

    def middle(self):
        send, half, pieces = self.plane.send, self.half, self.pieces
        self.x.wait_recv()
        self.fy = send(pieces.at[1, pl.ds(half, half)], pieces.at[3, pl.ds(half, half)], "y")
        self.c.append(send(pieces.at[1], pieces.at[5], "c"))
        self.y.wait_recv()
        self.fx = send(pieces.at[2, pl.ds(0, half)], pieces.at[3, pl.ds(0, half)], "x")
        self.c.append(send(pieces.at[2], pieces.at[6], "c"))

    def end(self):
        self.fx.wait_recv()
        self.fy.wait_recv()
        self.c.append(self.plane.send(self.pieces.at[3], self.pieces.at[7], "c"))

    def core(self, index):
        self.c[index].wait_recv()


class Reduce:
    def __init__(self, plane, pieces, from_core, from_x, from_y):
        self.plane, self.pieces = plane, pieces
        self.from_core, self.from_x, self.from_y = from_core, from_x, from_y
        self.half = pieces.shape[1] // 2
        self.core = {}

    def give(self, m):
        self.core[m] = self.plane.send(self.pieces.at[4 + m], self.from_core.at[m], "c")

    def take(self, m):
        self.core[m].wait_recv()

    def chip_done(self, m):
        send, half, pieces = self.plane.send, self.half, self.pieces
        low, high = pl.ds(0, half), pl.ds(half, half)
        if m == 3:
            self.far_x = send(pieces.at[3, low], self.from_x.at[1], "x")
            self.far_y = send(pieces.at[3, high], self.from_y.at[1], "y")
        elif m == 1:
            self.near_x = send(pieces.at[1, low], self.from_x.at[0], "x")
        elif m == 2:
            self.near_y = send(pieces.at[2, high], self.from_y.at[0], "y")

    def late_x(self):
        high = pl.ds(self.half, self.half)
        self.far_y.wait_recv()
        add_into(self.pieces.at[1, high], self.from_y.at[1])
        self.late_x_copy = self.plane.send(self.pieces.at[1, high], self.from_x.at[2], "x")

    def late_y(self):
        low = pl.ds(0, self.half)
        self.far_x.wait_recv()
        add_into(self.pieces.at[2, low], self.from_x.at[1])
        self.late_y_copy = self.plane.send(self.pieces.at[2, low], self.from_y.at[2], "y")

    def late(self):
        self.late_x()
        self.late_y()

    def total(self, out):
        half = self.half
        self.near_x.wait_recv()
        self.near_y.wait_recv()
        self.late_x_copy.wait_recv()
        self.late_y_copy.wait_recv()
        step = min(64, half)

        for base, x_part, y_part in ((0, 0, 2), (half, 2, 0)):

            def add(index, carry):
                at = pl.ds(pl.multiple_of(index * step, step), step)
                here = pl.ds(pl.multiple_of(base + index * step, step), step)
                out[here] = (
                    self.pieces[0, here].astype(f32)
                    + self.from_x[x_part, at].astype(f32)
                    + self.from_y[y_part, at].astype(f32)
                )
                return carry

            lax.fori_loop(0, half // step, add, 0)


def add_into(ref, other):
    step = min(64, ref.shape[0])

    def add(index, carry):
        at = pl.ds(pl.multiple_of(index * step, step), step)
        ref[at] = (ref[at].astype(f32) + other[at].astype(f32)).astype(bf16)
        return carry

    lax.fori_loop(0, ref.shape[0] // step, add, 0)


class Ring:
    def __init__(self, plane, own, blocks):
        self.plane, self.own, self.blocks = plane, own, blocks
        self.z = lax.axis_index("tensor")
        self.came = None

    @staticmethod
    def places():
        me, z = lax.axis_index("dp"), lax.axis_index("tensor")
        return [(me, lax.rem(z + 1, 4)), (me, lax.rem(z + 3, 4))]

    def step(self, index):
        if self.came is not None:
            self.came.wait_recv()
        if index < 3:
            block = self.blocks(lax.rem(self.z + 4 - index, 4))
            source = self.own if index == 0 else block
            self.came = self.plane.send_to(source, block, {"tensor": lax.rem(self.z + 1, 4)})


ORDER = (3, 1, 2, 0)


def tiles(count, tile, body):
    tile = min(tile, count)

    def step(index, carry):
        body(pl.ds(pl.multiple_of(index * tile, tile), tile))
        return carry

    lax.fori_loop(0, count // tile, step, 0)


def nn(left, right):
    return jnp.dot(left, right, preferred_element_type=f32)


def nt(left, right):
    return lax.dot_general(left, right, (((1,), (1,)), ((), ())), preferred_element_type=f32)


def tn(left, right):
    return lax.dot_general(left, right, (((0,), (0,)), ((), ())), preferred_element_type=f32)


class Feed:
    def __init__(self, source, slots, sems, order):
        self.source, self.slots, self.sems, self.order = source, slots, sems, list(order)

    def copy(self, index):
        slot = index % 2
        return pltpu.make_async_copy(
            self.source(self.order[index]), self.slots.at[slot], self.sems.at[slot]
        )

    def start(self, index):
        if index < len(self.order):
            self.copy(index).start()

    def get(self, index):
        self.copy(index).wait()
        return self.slots.at[index % 2]


def plane_call(kernel, name, collective_id, out_shape, in_spaces, out_spaces, scratch, copies, flops, args):
    spaces = {"any": pl.ANY, "vmem": pltpu.VMEM, "smem": pltpu.SMEM}
    return pl.pallas_call(
        kernel,
        out_shape=out_shape,
        in_specs=[pl.BlockSpec(memory_space=spaces[v]) for v in in_spaces],
        out_specs=[pl.BlockSpec(memory_space=spaces[v]) for v in out_spaces],
        scratch_shapes=list(scratch)
        + [pltpu.SemaphoreType.DMA((copies,)), pltpu.SemaphoreType.DMA((copies,))],
        compiler_params=pltpu.CompilerParams(
            collective_id=collective_id, has_side_effects=True, vmem_limit_bytes=62 << 20
        ),
        cost_estimate=pl.CostEstimate(flops=flops, bytes_accessed=64 << 20, transcendentals=0),
        name=name,
    )(*args)


def row_places():
    me, plane = lax.axis_index("dp"), lax.axis_index("tensor")
    chip, core = 2 * (me // 2), me % 2
    outward = [(chip + 1 - plane // 2, 2 * core + j) for j in range(2)]
    inward = [(chip + plane // 2, 2 * (1 - core) + i) for i in range(2)]
    return outward, inward


def at_device(place):
    return {"dp": place[0], "tensor": place[1]}


class RowMove:
    def __init__(self, src, dst, sems):
        self.src, self.dst, self.sems = src, dst, sems
        self.copies = []

    def copy(self, here, there, place):
        return pltpu.make_async_remote_copy(
            src_ref=self.src.at[here],
            dst_ref=self.dst.at[there],
            send_sem=self.sems.at[0, here],
            recv_sem=self.sems.at[1, there],
            device_id=at_device(place),
            device_id_type=MESH,
        )

    def start(self, places, there):
        for here in range(2):
            copy = self.copy(here, there, places[here])
            copy.start()
            self.copies.append(copy)
        self.arrivals = [self.copy(index, index, places[index]) for index in range(2)]

    def outward(self):
        self.start(row_places()[0], lax.axis_index("tensor") % 2)

    def back(self):
        self.start(row_places()[1], lax.axis_index("tensor") % 2)

    def wait(self):
        for copy in self.copies:
            copy.wait_send()
        for copy in self.arrivals:
            copy.wait_recv()


def start_kernel(
    tokens, w_query, w_key, w_value, w_out, w_up, w_down, small,
    tokens_out, qkv_out, out_out, up_out, down_out, small_out,
    local_sems, row_sems, send_sems, recv_sems,
):
    me, plane = lax.axis_index("dp"), lax.axis_index("tensor")
    chip, core = me // 2, me % 2
    depth = w_query.shape[0]
    part = up_out.shape[1]
    outward, inward = row_places()
    peers = [lax.rem(me + j, 8) for j in range(1, 8)]
    barrier = pltpu.get_barrier_semaphore()
    for peer in peers:
        pl.semaphore_signal(barrier, inc=1, device_id={"dp": peer}, device_id_type=MESH)
    for place in outward + inward:
        pl.semaphore_signal(barrier, inc=1, device_id=at_device(place), device_id_type=MESH)
    pl.semaphore_wait(barrier, 11)
    copies, locals_ = [], []

    def send(src, dst, device):
        copy = pltpu.make_async_remote_copy(
            src_ref=src,
            dst_ref=dst,
            send_sem=send_sems.at[len(copies)],
            recv_sem=recv_sems.at[len(copies)],
            device_id=device,
            device_id_type=MESH,
        )
        copy.start()
        copies.append(copy)

    def keep(src, dst):
        copy = pltpu.make_async_copy(src, dst, local_sems.at[len(locals_)])
        copy.start()
        locals_.append(copy)

    def block(index, size):
        return pl.ds(pl.multiple_of(index * size, size), size)

    rows_move = RowMove(tokens, tokens_out, row_sems)
    rows_move.outward()
    for peer in peers:
        send(small, small_out.at[me], {"dp": peer})
    keep(small, small_out.at[me])
    heads = [(w_query, 0), (w_key, 1), (w_value, 2)]
    for j in range(1, 4):
        other = lax.rem(chip + j, 4)
        device = {"dp": 2 * other + core}
        for weight, which in heads:
            send(weight.at[:, block(other, HEAD)], qkv_out.at[which, chip], device)
    for weight, which in heads:
        keep(weight.at[:, block(chip, HEAD)], qkv_out.at[which, chip])
    for j in range(1, 4):
        other = lax.rem(chip + j, 4)
        send(w_out.at[block(other, HEAD)], out_out.at[chip], {"dp": 2 * other + core})
    keep(w_out.at[block(chip, HEAD)], out_out.at[chip])
    for peer in peers:
        send(w_up.at[:, block(peer, part)], up_out.at[block(me, depth)], {"dp": peer})
        send(w_down.at[block(peer, part)], down_out.at[:, block(me, depth)], {"dp": peer})
    keep(w_up.at[:, block(me, part)], up_out.at[block(me, depth)])
    keep(w_down.at[block(me, part)], down_out.at[:, block(me, depth)])
    for copy in locals_:
        copy.wait()
    for copy in copies:
        copy.wait()
    rows_move.wait()


def gather_kernel(
    own, rows_in, weights, pieces, rows_out, wide, own_sem, row_sems, send_sems, recv_sems
):
    outward, inward = row_places()
    plane = Plane(send_sems, recv_sems, outward + inward + Ring.places())
    ring = Ring(plane, weights, lambda index: wide.at[index])
    ring.step(0)
    own_weights = pltpu.make_async_copy(weights, wide.at[ring.z], own_sem.at[own.shape[0]])
    own_weights.start()
    streams = own.shape[0]
    rows_move = RowMove(rows_in, rows_out, row_sems)
    rows_move.outward()
    gathers = [Gather(plane, own.at[s], pieces.at[s]) for s in range(streams)]
    keep = [pltpu.make_async_copy(own.at[s], pieces.at[s, 0], own_sem.at[s]) for s in range(streams)]
    for s in range(streams):
        gathers[s].begin()
        keep[s].start()
    ring.step(1)
    for s in range(streams):
        gathers[s].middle()
    ring.step(2)
    for s in range(streams):
        gathers[s].end()
    for s in range(streams):
        keep[s].wait()
        for index in range(4):
            gathers[s].core(index)
    ring.step(3)
    own_weights.wait()
    rows_move.wait()
    plane.finish()


def chunk_at(plane, s):
    k = 1 - s // 2
    return s % 2, k + plane.core - 2 * k * plane.core


def chunk_part(plane, qkv, chip, head):
    def part(s, which):
        column = pl.multiple_of((head * 3 + which) * HEAD, HEAD)
        stream, core = chunk_at(plane, s)
        piece = core * (qkv.shape[1] // 2) + chip
        return qkv[stream, piece, :, pl.ds(column, HEAD)]

    return part


def attend_all(plane, qkv, ends_ref, out, clip_count):
    rows = qkv.shape[2]
    heads = qkv.shape[3] // (3 * HEAD)

    def one(index, carry):
        chip, head = index // heads, index % heads
        part = chunk_part(plane, qkv, chip, head)
        column = pl.ds(pl.multiple_of(head * HEAD, HEAD), HEAD)
        for s in range(4):
            start = clip_starts(ends_ref, 0, chip, clip_count, s, rows)
            cs, probs = chunk_probs(part(s, 0), lambda c: part(c, 1), start, s, rows)
            mixed = jnp.zeros((rows, HEAD), f32)
            for c, prob in zip(cs, probs):
                mixed = mixed + nn(prob.astype(bf16), part(c, 2))
            stream, core = chunk_at(plane, s)
            out[stream, core * 4 + chip, :, column] = mixed.astype(bf16)
        return carry

    return one


def attend_back_chip(plane, qkv, grad_mixed, ends_ref, out, key_sum, value_sum, clip_count, chip):
    rows = qkv.shape[2]
    heads = qkv.shape[3] // (3 * HEAD)

    def one(head, carry):
        part = chunk_part(plane, qkv, 0, head)
        column = pl.ds(pl.multiple_of(head * HEAD, HEAD), HEAD)
        key_sum[...] = jnp.zeros_like(key_sum)
        value_sum[...] = jnp.zeros_like(value_sum)

        def put(s, which, value):
            at = pl.ds(pl.multiple_of((head * 3 + which) * HEAD, HEAD), HEAD)
            stream, core = chunk_at(plane, s)
            out[stream, core, :, at] = value.astype(bf16)

        for s in range(4):
            q = part(s, 0)
            stream, core = chunk_at(plane, s)
            g = grad_mixed[stream, core * 4 + chip, :, column]
            start = clip_starts(ends_ref, 0, chip, clip_count, s, rows)
            cs, probs = chunk_probs(q, lambda c: part(c, 1), start, s, rows)
            grad_probs = [nt(g, part(c, 2)) for c in cs]
            inner = functools.reduce(
                jnp.add,
                [jnp.sum(p * v, axis=1, keepdims=True) for p, v in zip(probs, grad_probs)],
            )
            grad_q = jnp.zeros((rows, HEAD), f32)
            for c, prob, grad_prob in zip(cs, probs, grad_probs):
                grad_score = (prob * (grad_prob - inner) * HEAD ** (-0.5)).astype(bf16)
                grad_q = grad_q + nn(grad_score, part(c, 1))
                key_sum[c] += tn(grad_score, q)
                value_sum[c] += tn(prob.astype(bf16), g)
            put(s, 0, grad_q)
        for s in range(4):
            put(s, 1, key_sum[s])
            put(s, 2, value_sum[s])
        return carry

    lax.fori_loop(0, heads, one, 0)


def attention_kernel(
    clip_count, own, rows_in, wide, ends, pieces, qkv, mixed, weight, slots, slot_sems, own_sem, wide_sems, send_sems, recv_sems
):
    plane = Plane(send_sems, recv_sems)
    streams = own.shape[0]
    gathers = [Gather(plane, own.at[s], pieces.at[s]) for s in range(streams)]
    keep = [pltpu.make_async_copy(own.at[s], pieces.at[s, 0], own_sem.at[s]) for s in range(streams)]
    traded, kept = [], []
    for head in range(2):
        for which in range(3):
            column = pl.ds((head * 3 + which) * HEAD, HEAD)
            here = weight.at[:, plane.core, :, column]
            traded.append(plane.send(wide.at[2 * (1 - plane.core) + head, which], here, "c"))
            copy = pltpu.make_async_copy(
                wide.at[2 * plane.core + head, which], here, wide_sems.at[len(kept)]
            )
            copy.start()
            kept.append(copy)
    for s in range(streams):
        gathers[s].begin()
        keep[s].start()
    total = weight.shape[3]
    feed = Feed(
        lambda at: rows_in.at[at[0], at[1]],
        slots,
        slot_sems,
        [(s, p) for s in range(streams) for p in range(8)],
    )
    feed.start(0)

    def project(s):
        for p in range(8):
            feed.start(s * 8 + p + 1)
            piece = feed.get(s * 8 + p)

            def tile(at):
                columns = weight[:, :, :, at].reshape(width, -1)
                qkv[s, p, :, at] = nn(piece[...], columns).astype(bf16)

            tiles(total, N_TILE, tile)

    for copy in traded:
        copy.wait_recv()
    for copy in kept:
        copy.wait()
    width = own.shape[2]

    attend = attend_all(plane, qkv, ends, mixed, clip_count)
    heads = total // (3 * HEAD)
    project(0)
    project(1)
    lax.fori_loop(0, 2 * heads, attend, 0)
    gathers[0].middle()
    gathers[1].middle()
    lax.fori_loop(2 * heads, 4 * heads, attend, 0)
    gathers[0].end()
    gathers[1].end()
    for s in range(streams):
        keep[s].wait()
        for index in range(4):
            gathers[s].core(index)
    plane.finish()


def reduce_scratch(streams, rows, width):
    return [
        pltpu.VMEM((streams, 8, rows, width), bf16),
        pltpu.VMEM((streams, 4, rows, width), bf16),
        pltpu.VMEM((streams, 3, rows // 2, width), bf16),
        pltpu.VMEM((streams, 3, rows // 2, width), bf16),
    ]


def project_kernel(
    mixed, wide, down_part, out, weight, down_w,
    parts, from_core, from_x, from_y, wide_sems, send_sems, recv_sems,
):
    plane = Plane(send_sems, recv_sems, Ring.places())
    size = down_part.shape[0]

    def down_block(index):
        return down_w.at[pl.ds(pl.multiple_of(index * size, size), size)]

    ring = Ring(plane, down_part, down_block)
    own_down = pltpu.make_async_copy(down_part, down_block(ring.z), wide_sems.at[8])
    own_down.start()
    ring.step(0)
    streams = mixed.shape[0]
    width = weight.shape[1]
    depth = wide.shape[3]
    traded, kept = [], []
    for head in range(2):
        for chip in range(4):
            column = pl.ds(pl.multiple_of((2 * chip + plane.core) * depth, depth), depth)
            here = weight.at[pl.ds(head * HEAD, HEAD), column]
            traded.append(plane.send(wide.at[2 * (1 - plane.core) + head, chip], here, "c"))
            copy = pltpu.make_async_copy(
                wide.at[2 * plane.core + head, chip], here, wide_sems.at[len(kept)]
            )
            copy.start()
            kept.append(copy)
    for copy in traded:
        copy.wait_recv()
    for copy in kept:
        copy.wait()
    sums = [
        Reduce(plane, parts.at[s], from_core.at[s], from_x.at[s], from_y.at[s])
        for s in range(streams)
    ]

    for s in range(streams):
        for m in ORDER:

            def other(at):
                parts[s, 4 + m, :, at] = nn(mixed[s, 4 + m], weight[:, at]).astype(bf16)

            tiles(width, N_TILE, other)
            sums[s].give(m)
        for m in ORDER:
            sums[s].take(m)

            def chip(at):
                here = nn(mixed[s, m], weight[:, at])
                parts[s, m, :, at] = (here + from_core[s, m, :, at].astype(f32)).astype(bf16)

            tiles(width, N_TILE, chip)
            sums[s].chip_done(m)
    ring.step(1)
    sums[0].late()
    ring.step(2)
    sums[1].late()
    for s in range(streams):
        sums[s].total(out.at[s])
    ring.step(3)
    own_down.wait()
    plane.finish()


def gelu_pair(v):
    cubic = 0.044715 * (v * v) * v
    inner = (2.0 / np.pi) ** 0.5 * (v + cubic)
    th = jnp.tanh(inner)
    half = 0.5 * (1.0 + th)
    slope = (2.0 / np.pi) ** 0.5 * (1.0 + 3.0 * 0.044715 * (v * v))
    return v * half, half + 0.5 * v * (1.0 - th * th) * slope


def lay_out(wide, flat, sems):
    copies = []
    part = wide.shape[2]
    for plane in range(wide.shape[0]):
        copy = pltpu.make_async_copy(
            wide.at[plane], flat.at[:, pl.ds(plane * part, part)], sems.at[plane]
        )
        copy.start()
        copies.append(copy)
    return copies


def mlp_kernel(
    own, up_wide, down_w, grads, pieces, slope_out, down_grad, out,
    parts, from_core, from_x, from_y, up_w, slots, act, slope, total, grad_slots,
    up_sems, slot_sems, keep_sems, own_sem, grad_sems, send_sems, recv_sems,
):
    plane = Plane(send_sems, recv_sems)
    streams, rows, width = own.shape
    hidden = up_w.shape[1]
    up_copies = lay_out(up_wide, up_w, up_sems)
    gathers = [Gather(plane, own.at[s], pieces.at[s]) for s in range(streams)]
    sums = [
        Reduce(plane, parts.at[s], from_core.at[s], from_x.at[s], from_y.at[s])
        for s in range(streams)
    ]
    keep = [pltpu.make_async_copy(own.at[s], pieces.at[s, 0], own_sem.at[s]) for s in range(streams)]
    stores = []

    def up_piece(s, p, slot):
        if len(stores) >= 2:
            stores[-2].wait()

        def up(at):
            value, grad = gelu_pair(nn(slots[slot], up_w[:, at]))
            act[slot, :, at] = value.astype(bf16)
            slope[slot, :, at] = grad.astype(bf16)

        tiles(hidden, N_TILE, up)
        store = pltpu.make_async_copy(slope.at[slot], slope_out.at[s, p], keep_sems.at[slot])
        store.start()
        stores.append(store)

    def down_piece(s, p, slot):
        def down(at):
            here = nn(act[slot], down_w[:, at])
            if p < 4:
                here = here + from_core[s, p, :, at].astype(f32)
            parts[s, p, :, at] = here.astype(bf16)

        tiles(width, N_TILE, down)

    def pair_up(s, m):
        if m > 0:
            gathers[s].core(m)
        first = not stores
        rows_come = [
            pltpu.make_async_copy(
                own.at[s] if p == 0 else pieces.at[s, p], slots.at[i], slot_sems.at[i]
            )
            for i, p in enumerate((4 + m, m))
        ]
        coming = [
            pltpu.make_async_copy(grads.at[s, p], grad_slots.at[i], grad_sems.at[i])
            for i, p in enumerate((4 + m, m))
        ]
        if m == 0:
            rows_come[1].start()
            gathers[s].core(0)
            rows_come[0].start()
        else:
            rows_come[0].start()
            rows_come[1].start()
        for copy in coming:
            copy.start()
        rows_come[0].wait()
        up_piece(s, 4 + m, 0)
        down_piece(s, 4 + m, 0)
        sums[s].give(m)
        rows_come[1].wait()
        up_piece(s, m, 1)
        for copy in coming:
            copy.wait()
        left = act[...].reshape(2 * rows, hidden)

        def weigh(at):
            term = tn(left, grad_slots[:, :, at].reshape(2 * rows, -1))
            total[:, at] = term if first else total[:, at] + term

        tiles(width, 512, weigh)
        sums[s].take(m)
        down_piece(s, m, 1)
        sums[s].chip_done(m)

    for s in range(streams):
        keep[s].start()
        gathers[s].begin_core()
    gathers[0].begin_links()
    for copy in up_copies:
        copy.wait()
    pair_up(0, 0)
    pair_up(1, 0)
    gathers[0].middle()
    gathers[1].begin_links()
    pair_up(0, 1)
    pair_up(0, 2)
    gathers[0].end()
    pair_up(0, 3)
    gathers[1].middle()
    pair_up(1, 1)
    sums[0].late()
    gathers[1].end()
    pair_up(1, 3)
    pair_up(1, 2)
    sums[1].late()
    for s in range(streams):
        sums[s].total(out.at[s])
        keep[s].wait()
    for store in stores[-2:]:
        store.wait()
    stores = []
    for index in range(hidden // rows):
        if index >= 2:
            stores[index - 2].wait()
        here = pl.ds(index * rows, rows)
        slots[index % 2] = total[here].astype(bf16)
        store = pltpu.make_async_copy(
            slots.at[index % 2], down_grad.at[here], keep_sems.at[index % 2]
        )
        store.start()
        stores.append(store)
    for store in stores[-2:]:
        store.wait()
    plane.finish()


def mlp_back_kernel(
    grads, slope_in, features, up_wide, down_w, up_grad, out,
    parts, from_core, from_x, from_y, up_w, slots, slopes, pre, rows_two, total,
    up_sems, slot_sems, slope_sems, row_sems, keep_sems, send_sems, recv_sems,
):
    plane = Plane(send_sems, recv_sems)
    streams, _, rows, width = grads.shape
    hidden = up_w.shape[1]
    part = up_wide.shape[2]
    up_copies = lay_out(up_wide, up_w, up_sems)
    sums = [
        Reduce(plane, parts.at[s], from_core.at[s], from_x.at[s], from_y.at[s])
        for s in range(streams)
    ]
    order = [(s, p) for s in range(streams) for m in ORDER for p in (4 + m, m)]
    feed = Feed(lambda at: grads.at[at[0], at[1]], slots, slot_sems, order)
    feed_slope = Feed(lambda at: slope_in.at[at[0], at[1]], slopes, slope_sems, order)
    feed_rows = Feed(lambda at: features.at[at[0], at[1]], rows_two, row_sems, order)
    feed.start(0)
    feed_slope.start(0)
    def back_piece(index):
        feed.start(index + 1)
        feed_slope.start(index + 1)
        feed_rows.start(index)
        grad = feed.get(index)
        slope = feed_slope.get(index)

        def back(at):
            value = nt(grad[...], down_w[at]) * slope[:, at].astype(f32)
            pre[index % 2, :, at] = value.astype(bf16)

        tiles(hidden, N_TILE, back)

    def through_piece(index, s, p):
        def through(at):
            here = nt(pre[index % 2], up_w[at])
            if p < 4:
                here = here + from_core[s, p, :, at].astype(f32)
            parts[s, p, :, at] = here.astype(bf16)

        tiles(width, N_TILE, through)

    for index, (s, p) in enumerate(order):
        back_piece(index)
        if index == 0:
            for copy in up_copies:
                copy.wait()
        if p >= 4:
            through_piece(index, s, p)
            sums[s].give(p - 4)
            continue
        feed_rows.get(index - 1)
        feed_rows.get(index)
        right = pre[...].reshape(2 * rows, hidden)

        def weigh(at):
            term = tn(rows_two[:, :, at].reshape(2 * rows, -1), right)
            total[at] = term if index == 1 else total[at] + term

        tiles(width, 512, weigh)
        sums[s].take(p)
        through_piece(index, s, p)
        sums[s].chip_done(p)
        if p == 2:
            sums[s].late_x()
        if p == 0:
            sums[s].late_y()
    stores = []
    for index in range(width // rows):
        slot = index % 2
        for store in stores[index - 2] if index >= 2 else []:
            store.wait()
        here = pl.ds(index * rows, rows)
        pre[slot] = total[here].astype(bf16)
        stores.append([])
        for at in range(hidden // part):
            store = pltpu.make_async_copy(
                pre.at[slot, :, pl.ds(at * part, part)], up_grad.at[at, here], keep_sems.at[slot, at]
            )
            store.start()
            stores[-1].append(store)
    for s in range(streams):
        sums[s].total(out.at[s])
    for pair in stores[-2:]:
        for store in pair:
            store.wait()
    plane.finish()


def attention_back_kernel(
    clip_count, own, qkv, mixed, features, rows_in, qkv_w, out_w, ends,
    pieces, qkv_grad, out_grad, rows_out, out,
    parts, from_core, from_x, from_y, slots, mixed_slots, grad_mixed, qkv_chip, grad_chip, key_sum, value_sum,
    qkv_sum, out_sum, slot_sems, mixed_sems, chip_sems, store_sems, row_sems, own_sem, send_sems, recv_sems,
):
    outward, inward = row_places()
    plane = Plane(send_sems, recv_sems, outward + inward)
    rows_move = RowMove(rows_in, rows_out, row_sems)
    rows_move.back()
    streams, rows, width = own.shape
    gathers = [Gather(plane, own.at[s], pieces.at[s]) for s in range(streams)]
    sums = [
        Reduce(plane, parts.at[s], from_core.at[s], from_x.at[s], from_y.at[s])
        for s in range(streams)
    ]
    keep = [pltpu.make_async_copy(own.at[s], pieces.at[s, 0], own_sem.at[s]) for s in range(streams)]
    def load_chip(m):
        copies = [
            pltpu.make_async_copy(
                qkv.at[s, core * 4 + m], qkv_chip.at[s, core], chip_sems.at[s * 2 + core]
            )
            for s in range(streams)
            for core in range(2)
        ]
        for copy in copies:
            copy.start()
        return copies

    def load_rows(m):
        copies = [
            pltpu.make_async_copy(
                features.at[s, core * 4 + m], slots.at[s * 2 + core], slot_sems.at[s * 2 + core]
            )
            for s in range(streams)
            for core in range(2)
        ]
        for copy in copies:
            copy.start()
        return copies

    def weigh_chip(place, copies):
        for copy in copies:
            copy.wait()
        right = grad_chip[place % 2].reshape(4 * rows, -1)

        def weigh(at):
            term = tn(slots[:, :, at].reshape(4 * rows, -1), right)
            qkv_sum[at] = term if place == 0 else qkv_sum[at] + term

        tiles(width, 512, weigh)

    mixed_before = []

    def mix_pair(s, m):
        pair = (m, 4 + m)
        rows_come = [
            pltpu.make_async_copy(
                own.at[s] if p == 0 else pieces.at[s, p], slots.at[i], slot_sems.at[i]
            )
            for i, p in enumerate(pair)
        ]
        left_come = [
            pltpu.make_async_copy(mixed.at[s, p], mixed_slots.at[i], mixed_sems.at[i])
            for i, p in enumerate(pair)
        ]
        rows_come[0].start()
        for copy in left_come:
            copy.start()
        gathers[s].core(m)
        rows_come[1].start()
        for i, p in enumerate(pair):
            rows_come[i].wait()
            grad_mixed[s, p] = nt(slots[i], out_w[...]).astype(bf16)
        for copy in left_come:
            copy.wait()
        left = mixed_slots[...].reshape(2 * rows, -1)
        first = not mixed_before
        mixed_before.append(m)

        def weigh(at):
            term = tn(left, slots[pl.ds(0, 2), :, at].reshape(2 * rows, -1))
            out_sum[:, at] = term if first else out_sum[:, at] + term

        tiles(width, N_TILE, weigh)

    def attend_chip(place, m, coming, following):
        for copy in coming:
            copy.wait()
        grad_here = grad_chip.at[place % 2]
        attend_back_chip(
            plane, qkv_chip, grad_mixed, ends, grad_here, key_sum, value_sum, clip_count, m
        )
        coming = load_chip(following) if following is not None else []
        for s in range(streams):

            def other(at):
                parts[s, 4 + m, :, at] = nt(grad_here[s, 1], qkv_w[at]).astype(bf16)

            tiles(width, N_TILE, other)
            sums[s].give(m)
        for s in range(streams):
            sums[s].take(m)

            def chip(at):
                here = nt(grad_here[s, 0], qkv_w[at])
                parts[s, m, :, at] = (here + from_core[s, m, :, at].astype(f32)).astype(bf16)

            tiles(width, N_TILE, chip)
            sums[s].chip_done(m)
        return coming

    for s in range(streams):
        keep[s].start()
        gathers[s].begin_core()
    gathers[0].begin_links()
    coming = load_chip(0)
    mix_pair(0, 0)
    mix_pair(1, 0)
    coming = attend_chip(0, 0, coming, 1)
    gathers[0].middle()
    gathers[1].begin_links()
    mix_pair(0, 1)
    mix_pair(0, 2)
    weigh_chip(0, load_rows(0))
    gathers[0].end()
    mix_pair(0, 3)
    gathers[1].middle()
    mix_pair(1, 1)
    mix_pair(1, 2)
    coming = attend_chip(1, 1, coming, 3)
    gathers[1].end()
    mix_pair(1, 3)
    coming_rows = load_rows(1)
    coming = attend_chip(2, 3, coming, 2)
    weigh_chip(1, coming_rows)
    coming_rows = load_rows(3)
    attend_chip(3, 2, coming, None)
    for s in range(streams):
        sums[s].late_x()
    for s in range(streams):
        sums[s].late_y()
    weigh_chip(2, coming_rows)
    weigh_chip(3, load_rows(2))
    for index in range(out_sum.shape[0] // rows):
        here = pl.ds(index * rows, rows)
        slots[0] = out_sum[here].astype(bf16)
        out_store = pltpu.make_async_copy(slots.at[0], out_grad.at[here], slot_sems.at[0])
        out_store.start()
        out_store.wait()
    stores = []
    for index in range(width // rows):
        if index >= 4:
            stores[index - 4].wait()
        here = pl.ds(index * rows, rows)
        stage = grad_chip.at[0, index // 2 % 2, index % 2]
        stage[...] = qkv_sum[here].astype(bf16)
        store = pltpu.make_async_copy(stage, qkv_grad.at[here], store_sems.at[index % 4])
        store.start()
        stores.append(store)
    for s in range(streams):
        sums[s].total(out.at[s])
        keep[s].wait()
    for store in stores[-4:]:
        store.wait()
    rows_move.wait()
    plane.finish()


def end_kernel(
    rows_in, qkv_grad, out_grad, up_sum, down_sum, gains,
    rows_out, qkv_out, out_out, up_out, down_out, gains_out,
    qkv_part, out_part, qkv_come, out_come, gain_come, gain_sum, gain_all,
    rows_got, qkv_got, out_got, up_got, down_got, local_sems, row_sems, send_sems, recv_sems,
):
    me, z = lax.axis_index("dp"), lax.axis_index("tensor")
    chip, core = me // 2, me % 2
    depth = qkv_grad.shape[2]
    outward, inward = row_places()
    peers = [lax.rem(me + j, 8) for j in range(1, 8)]
    planes = [lax.rem(z + j, 4) for j in range(1, 4)]
    barrier = pltpu.get_barrier_semaphore()
    for peer in peers:
        pl.semaphore_signal(barrier, inc=1, device_id={"dp": peer}, device_id_type=MESH)
    for plane in planes:
        pl.semaphore_signal(barrier, inc=1, device_id={"tensor": plane}, device_id_type=MESH)
    for place in outward + inward:
        pl.semaphore_signal(barrier, inc=1, device_id=at_device(place), device_id_type=MESH)
    pl.semaphore_wait(barrier, 14)
    copies, locals_ = [], []

    def send(src, dst, device):
        copy = pltpu.make_async_remote_copy(
            src_ref=src,
            dst_ref=dst,
            send_sem=send_sems.at[len(copies)],
            recv_sem=recv_sems.at[len(copies)],
            device_id=device,
            device_id_type=MESH,
        )
        copy.start()
        copies.append(copy)
        return copy

    def keep(src, dst):
        copy = pltpu.make_async_copy(src, dst, local_sems.at[len(locals_)])
        copy.start()
        locals_.append(copy)

    def block(index, size):
        return pl.ds(pl.multiple_of(index * size, size), size)

    other = {"dp": me + 1 - 2 * core}
    traded = []
    for head in range(2):
        mine = 2 * core + head
        for which in range(3):
            column = pl.ds((head * 3 + which) * HEAD, HEAD)
            traded.append(
                send(qkv_grad.at[:, 1 - core, :, column], qkv_part.at[mine, which], other)
            )
            keep(qkv_grad.at[:, core, :, column], qkv_part.at[mine, which])
        here = pl.ds(head * HEAD, HEAD)
        for c in range(4):
            theirs = pl.ds(pl.multiple_of((2 * c + 1 - core) * depth, depth), depth)
            own = pl.ds(pl.multiple_of((2 * c + core) * depth, depth), depth)
            traded.append(send(out_grad.at[here, theirs], out_part.at[mine, c], other))
            keep(out_grad.at[here, own], out_part.at[mine, c])
    gain_first = [send(gains.at[peer], gain_come.at[me], {"dp": peer}) for peer in peers]
    gain_come[me] = gains[me]
    begun = len(locals_)
    part = up_sum.shape[1]
    shards = []
    for peer in peers:
        shards.append(send(up_sum.at[block(peer, depth)], up_got.at[:, block(me, part)], {"dp": peer}))
        shards.append(send(down_sum.at[:, block(peer, depth)], down_got.at[block(me, part)], {"dp": peer}))
    keep(up_sum.at[block(me, depth)], up_got.at[:, block(me, part)])
    keep(down_sum.at[:, block(me, depth)], down_got.at[block(me, part)])
    for copy in traded:
        copy.wait_recv()
    for copy in locals_[:begun]:
        copy.wait()
    after = {"tensor": planes[0]}
    for step in range(3):
        part = lax.rem(z + 3 - step, 4)
        ring = [
            send(qkv_part.at[part], qkv_come.at[step], after),
            send(out_part.at[part], out_come.at[step], after),
        ]
        if step == 0:
            rows_move = RowMove(rows_in, rows_got, row_sems)
            rows_move.back()
            for copy in gain_first:
                copy.wait_recv()
            gain_sum[...] = functools.reduce(jnp.add, [gain_come[i] for i in range(8)])
            gain_second = [
                send(gain_sum, gain_all.at[z], {"tensor": plane}) for plane in planes
            ]
            gain_all[z] = gain_sum[...]
        for copy in ring:
            copy.wait_recv()
        part = lax.rem(z + 2 - step, 4) if step < 2 else z
        for which in range(3):
            for c in range(4):
                here = qkv_part.at[part, which, c]
                here[...] = (
                    here[...].astype(f32) + qkv_come[step, which, c].astype(f32)
                ).astype(bf16)
        for c in range(4):
            here = out_part.at[part, c]
            here[...] = (here[...].astype(f32) + out_come[step, c].astype(f32)).astype(bf16)
    last = []
    for j in range(1, 4):
        to = lax.rem(chip + j, 4)
        device = {"dp": 2 * to + core}
        last.append(send(qkv_part.at[z, :, to], qkv_got.at[:, :, block(chip, HEAD)], device))
        last.append(send(out_part.at[z, to], out_got.at[block(chip, HEAD)], device))
    keep(qkv_part.at[z, :, chip], qkv_got.at[:, :, block(chip, HEAD)])
    keep(out_part.at[z, chip], out_got.at[block(chip, HEAD)])
    for copy in gain_second:
        copy.wait_recv()
    gains_out[...] = functools.reduce(jnp.add, [gain_all[i] for i in range(4)])
    for copy in shards:
        copy.wait_recv()
    for copy in locals_[begun:]:
        copy.wait()
    up_out[...] = up_got[...].astype(f32)
    down_out[...] = down_got[...].astype(f32)
    for copy in last:
        copy.wait_recv()
    qkv_out[...] = qkv_got[...].astype(f32)
    out_out[...] = out_got[...].astype(f32)
    rows_move.wait()
    rows_out[...] = rows_got[...].astype(f32)
    for copy in copies:
        copy.wait_send()


def on_device(
    block_input,
    clip_lengths,
    norm1_gain,
    w_query,
    w_key,
    w_value,
    w_out,
    norm2_gain,
    w_up,
    w_down,
    out_cotangent,
):
    streams, rows, width = block_input.shape
    planes = lax.axis_size("tensor")
    lanes = lax.axis_size("dp")
    clip_count = clip_lengths.shape[1]
    own = lax.axis_index("dp")
    own_plane = lax.axis_index("tensor")
    own_core = own % 2
    heads = w_query.shape[1] * planes // (HEAD * lanes)
    depth = w_query.shape[0]
    hidden_part = w_up.shape[1] // lanes
    hidden_own = planes * hidden_part
    inner = heads * HEAD

    small = jnp.zeros((8, depth), f32)
    small = small.at[0].set(norm1_gain.astype(f32)).at[1].set(norm2_gain.astype(f32))
    small = small.at[2, : streams * clip_count].set(clip_lengths.reshape(-1).astype(f32))
    tokens_in, qkv_part, out_part, up_part, down_part, small = plane_call(
        start_kernel,
        "start",
        6,
        [
            jax.ShapeDtypeStruct(block_input.shape, bf16),
            jax.ShapeDtypeStruct((3, 4, depth, HEAD), bf16),
            jax.ShapeDtypeStruct((4, HEAD, depth), bf16),
            jax.ShapeDtypeStruct((width, hidden_part), bf16),
            jax.ShapeDtypeStruct((hidden_part, width), bf16),
            jax.ShapeDtypeStruct((lanes, 8, depth), f32),
        ],
        ["any"] * 8,
        ["any"] * 6,
        [pltpu.SemaphoreType.DMA((7,)), pltpu.SemaphoreType.DMA((2, 2))],
        33,
        0,
        (block_input, w_query, w_key, w_value, w_out, w_up, w_down, small),
    )
    gain_one = small[:, 0].reshape(-1)
    gain_two = small[:, 1].reshape(-1)
    lengths = small[:, 2, : streams * clip_count].reshape(-1, clip_count).astype(jnp.int32)


    all_ends = jnp.cumsum(lengths, axis=1)
    buffers = 4 * (own // 2 ^ jnp.arange(4, dtype=jnp.int32)) + own_plane
    ends = jnp.take(all_ends, buffers, axis=0)
    chunks = 2 * (1 - own_core) + jnp.arange(streams, dtype=jnp.int32)
    places = chunks[:, None] * rows + jnp.arange(rows, dtype=jnp.int32)
    valid = (places < ends[0, -1]).astype(f32)
    ends = ends.reshape(-1).astype(jnp.int32)

    pieces = jax.ShapeDtypeStruct((streams, 8, rows, width), bf16)
    sums = jax.ShapeDtypeStruct((streams, rows, width), f32)
    row_count = streams * 8 * rows
    slots = pltpu.VMEM((2, rows, width), bf16)
    dma = pltpu.SemaphoreType.DMA

    def piece_shape(columns):
        return jax.ShapeDtypeStruct((streams, 8, rows, columns), bf16)

    tokens = tokens_in.astype(f32)
    normed_one, unit_one, inverse_one = norm_rows(tokens, gain_one)
    features_one, cotangent, qkv_wide = plane_call(
        gather_kernel,
        "gather",
        0,
        [
            pieces,
            jax.ShapeDtypeStruct(block_input.shape, bf16),
            jax.ShapeDtypeStruct((planes,) + qkv_part.shape, bf16),
        ],
        ["any", "any", "any"],
        ["any", "any", "any"],
        [dma((streams + 1,)), dma((2, 2))],
        8 * streams + 3,
        0,
        (normed_one.astype(bf16), out_cotangent, qkv_part),
    )
    out_part, up_part, qkv_wide = lax.optimization_barrier((out_part, up_part, qkv_wide))
    out_wide = lax.all_gather(out_part, "tensor", axis=0, tiled=False)
    up_wide = lax.all_gather(up_part, "tensor", axis=0, tiled=False)
    grad_out = cotangent.astype(f32) * valid[:, :, None]
    grad_branch, qkv, mixed, qkv_w = plane_call(
        functools.partial(attention_kernel, clip_count),
        "attention",
        1,
        [
            pieces,
            piece_shape(3 * inner),
            piece_shape(inner),
            jax.ShapeDtypeStruct((4, 2, depth, 3 * inner), bf16),
        ],
        ["any", "any", "any", "smem"],
        ["any", "vmem", "vmem", "vmem"],
        [slots, dma((2,)), dma((streams,)), dma((6,))],
        8 * streams + 6,
        2 * row_count * width * 3 * inner,
        (grad_out.astype(bf16), features_one, qkv_wide, ends),
    )
    attn_sum, out_w, down_w = plane_call(
        project_kernel,
        "project",
        2,
        [
            sums,
            jax.ShapeDtypeStruct((inner, width), bf16),
            jax.ShapeDtypeStruct((hidden_own, width), bf16),
        ],
        ["vmem", "any", "any"],
        ["vmem", "vmem", "any"],
        reduce_scratch(streams, rows, width) + [dma((9,))],
        10 * streams + 11,
        2 * row_count * width * inner,
        (mixed, out_wide, down_part),
    )
    hidden = tokens + attn_sum
    normed_two, unit_two, inverse_two = norm_rows(hidden, gain_two)
    part = pltpu.VMEM((2, rows, hidden_own), bf16)
    up_flat = pltpu.VMEM((width, hidden_own), bf16)
    features_two, slope, down_dot, mlp_sum = plane_call(
        mlp_kernel,
        "mlp",
        3,
        [
            pieces,
            piece_shape(hidden_own),
            jax.ShapeDtypeStruct((hidden_own, width), bf16),
            sums,
        ],
        ["any", "any", "vmem", "any"],
        ["any", "any", "any", "vmem"],
        reduce_scratch(streams, rows, width)
        + [up_flat, slots, part, part, pltpu.VMEM((hidden_own, width), f32), slots]
        + [dma((planes,)), dma((2,)), dma((2,)), dma((streams,)), dma((2,))],
        18 * streams,
        6 * row_count * width * hidden_own,
        (normed_two.astype(bf16), up_wide, down_w, grad_branch),
    )

    up_dot, back_sum = plane_call(
        mlp_back_kernel,
        "mlp_back",
        4,
        [jax.ShapeDtypeStruct((planes, width, hidden_part), bf16), sums],
        ["any", "any", "any", "any", "vmem"],
        ["any", "vmem"],
        reduce_scratch(streams, rows, width)
        + [up_flat, slots, part, part, slots, pltpu.VMEM((width, hidden_own), f32)]
        + [dma((planes,)), dma((2,)), dma((2,)), dma((2,)), dma((2, planes))],
        10 * streams,
        6 * row_count * width * hidden_own,
        (grad_branch, slope, features_two, up_wide, down_w),
    )
    from_two, gain_two_grad = norm_back(back_sum, unit_two, inverse_two, gain_two)
    grad_hidden = grad_out + from_two
    down_sum = lax.psum_scatter(down_dot, "tensor", scatter_dimension=0, tiled=True)
    up_sum = lax.psum_scatter(up_dot, "tensor", scatter_dimension=0, tiled=False)
    chunk = pltpu.VMEM((4, rows, HEAD), f32)
    chip_rows = pltpu.VMEM((streams, 2, rows, 3 * inner), bf16)
    _, qkv_dot, out_dot, output, input_sum = plane_call(
        functools.partial(attention_back_kernel, clip_count),
        "attention_back",
        5,
        [
            pieces,
            jax.ShapeDtypeStruct((width, 3 * inner), bf16),
            jax.ShapeDtypeStruct((inner, width), bf16),
            jax.ShapeDtypeStruct(block_input.shape, bf16),
            sums,
        ],
        ["any", "any", "any", "any", "any", "vmem", "vmem", "smem"],
        ["any", "any", "any", "any", "vmem"],
        reduce_scratch(streams, rows, width)
        + [pltpu.VMEM((4, rows, width), bf16), pltpu.VMEM((2, rows, inner), bf16)]
        + [pltpu.VMEM((streams, 8, rows, inner), bf16), chip_rows]
        + [pltpu.VMEM((2, streams, 2, rows, 3 * inner), bf16), chunk, chunk]
        + [pltpu.VMEM((width, 3 * inner), f32), pltpu.VMEM((inner, width), f32)]
        + [dma((4,)), dma((2,)), dma((4,)), dma((4,)), dma((2, 2)), dma((streams,))],
        18 * streams,
        2 * row_count * width * 8 * inner,
        (
            grad_hidden.astype(bf16),
            qkv,
            mixed,
            features_one,
            (hidden + mlp_sum).astype(bf16),
            qkv_w.reshape(width, 3 * inner),
            out_w,
            ends,
        ),
    )
    input_sum, down_sum, up_sum = lax.optimization_barrier((input_sum, down_sum, up_sum))
    from_one, gain_one_grad = norm_back(input_sum, unit_one, inverse_one, gain_one)
    gains = jnp.stack([gain_one_grad.sum(0), gain_two_grad.sum(0)]).reshape(2, lanes, depth)
    gains = jnp.zeros((lanes, 8, depth), f32).at[:, :2].set(gains.swapaxes(0, 1))
    small_sum = pltpu.VMEM((8, depth), f32)
    input_grad, qkv_grad, out_grad, up_grad, down_grad, gains = plane_call(
        end_kernel,
        "end",
        7,
        [
            sums,
            jax.ShapeDtypeStruct((3, depth, 4 * HEAD), f32),
            jax.ShapeDtypeStruct((4 * HEAD, depth), f32),
            jax.ShapeDtypeStruct(w_up.shape, f32),
            jax.ShapeDtypeStruct(w_down.shape, f32),
            jax.ShapeDtypeStruct((8, depth), f32),
        ],
        ["any", "any", "any", "any", "any", "vmem"],
        ["vmem"] * 6,
        [
            pltpu.VMEM((4, 3, 4, depth, HEAD), bf16),
            pltpu.VMEM((4, 4, HEAD, depth), bf16),
            pltpu.VMEM((3, 3, 4, depth, HEAD), bf16),
            pltpu.VMEM((3, 4, HEAD, depth), bf16),
            pltpu.VMEM((8, 8, depth), f32),
            small_sum,
            pltpu.VMEM((4, 8, depth), f32),
            pltpu.VMEM(block_input.shape, bf16),
            pltpu.VMEM((3, depth, 4 * HEAD), bf16),
            pltpu.VMEM((4 * HEAD, depth), bf16),
            pltpu.VMEM(w_up.shape, bf16),
            pltpu.VMEM(w_down.shape, bf16),
            dma((18,)),
            dma((2, 2)),
        ],
        50,
        0,
        (
            (grad_hidden + from_one).astype(bf16),
            qkv_dot.reshape(4, 2, depth, 3 * inner),
            out_dot,
            up_sum,
            down_sum,
            gains,
        ),
    )
    return (
        output,
        input_grad,
        gains[0],
        qkv_grad[0],
        qkv_grad[1],
        qkv_grad[2],
        out_grad,
        gains[1],
        up_grad,
        down_grad,
    )


def solution(mesh):
    in_specs = (
        P("dp", "tensor", None),
        P("dp", None),
        P("dp"),
        P("dp", "tensor"),
        P("dp", "tensor"),
        P("dp", "tensor"),
        P("tensor", "dp"),
        P("dp"),
        P("dp", "tensor"),
        P("tensor", "dp"),
        P("dp", "tensor", None),
    )
    out_specs = (
        P("dp", "tensor", None),
        P("dp", "tensor", None),
        P("dp"),
        P("dp", "tensor"),
        P("dp", "tensor"),
        P("dp", "tensor"),
        P("tensor", "dp"),
        P("dp"),
        P("dp", "tensor"),
        P("tensor", "dp"),
    )
    own_form = mesh.shape["dp"] == 8 and mesh.shape["tensor"] == 4
    return jax.shard_map(
        on_device if own_form else on_device_any, mesh=mesh, in_specs=in_specs, out_specs=out_specs, check_vma=False
    )
```

```python
import functools

import jax
import jax.numpy as jnp
import numpy as np
from jax import lax
from jax.experimental import pallas as pl
from jax.experimental.pallas import tpu as pltpu
from jax.sharding import PartitionSpec as P

HEAD = 128
LONGEST = 512
epsilon = 1e-05
masked_fill = -1000000000.0
bf16 = jnp.bfloat16
f32 = jnp.float32


def norm_rows(tokens, gain):
    centred = tokens - jnp.mean(tokens, axis=-1, keepdims=True)
    inverse = lax.rsqrt(jnp.mean(centred * centred, axis=-1, keepdims=True) + epsilon)
    unit_rows = centred * inverse
    return (unit_rows * gain, unit_rows, inverse)


def norm_back(grad_normed, unit_rows, inverse, gain):
    scaled = grad_normed * gain
    inner_sum = (
        scaled
        - jnp.mean(scaled, axis=-1, keepdims=True)
        - unit_rows * jnp.mean(scaled * unit_rows, axis=-1, keepdims=True)
    )
    return (inverse * inner_sum, jnp.sum(grad_normed * unit_rows, axis=0))


def gelu_tanh(values):
    return jax.nn.gelu(values, approximate=True)


def masked_scores(q_rows, keys_heads, segment, offset, block_rows):
    slot_count = keys_heads.shape[0]
    raw_scores = jnp.einsum(
        "qhd,khd->hqk", q_rows, keys_heads, preferred_element_type=jnp.float32
    ) * HEAD ** (-0.5)
    q_segment = lax.dynamic_slice_in_dim(segment, offset, block_rows, 0)
    q_place = offset + jnp.arange(block_rows, dtype=jnp.int32)
    places = jnp.arange(slot_count, dtype=jnp.int32)
    allowed = (q_segment[:, None] == segment[None, :]) & (places[None, :] <= q_place[:, None])
    return jnp.where(allowed[None], raw_scores, masked_fill)


def attend(query, key, value, segment, block_rows):
    slot_count = query.shape[0]
    head_count = query.shape[1] // HEAD
    keys_heads = key.reshape(slot_count, head_count, HEAD)
    values_heads = value.reshape(slot_count, head_count, HEAD)

    def one_block(block_index):
        offset = block_index * block_rows
        q_rows = lax.dynamic_slice_in_dim(query, offset, block_rows, 0).reshape(
            block_rows, head_count, HEAD
        )
        scores = masked_scores(q_rows, keys_heads, segment, offset, block_rows)
        highest = jnp.max(scores, axis=-1, keepdims=True)
        shifted = jnp.exp(scores - highest)
        totals = jnp.sum(shifted, axis=-1, keepdims=True)
        weights = (shifted / totals).astype(jnp.bfloat16)
        mixed_rows = jnp.einsum(
            "hqk,khd->qhd", weights, values_heads, preferred_element_type=jnp.float32
        )
        return (
            mixed_rows.reshape(block_rows, head_count * HEAD).astype(jnp.bfloat16),
            (highest + jnp.log(totals))[..., 0],
        )

    mixed_rows, log_norm = lax.map(one_block, jnp.arange(slot_count // block_rows, dtype=jnp.int32))
    return (mixed_rows.reshape(slot_count, head_count * HEAD), log_norm)


def attend_back(query, key, value, segment, log_norm, grad_mixed, block_rows):
    slot_count = query.shape[0]
    head_count = query.shape[1] // HEAD
    keys_heads = key.reshape(slot_count, head_count, HEAD)
    values_heads = value.reshape(slot_count, head_count, HEAD)

    def one_block(carried, block_index):
        grad_keys, grad_values = carried
        offset = block_index * block_rows
        q_rows = lax.dynamic_slice_in_dim(query, offset, block_rows, 0).reshape(
            block_rows, head_count, HEAD
        )
        g_rows = lax.dynamic_slice_in_dim(grad_mixed, offset, block_rows, 0).reshape(
            block_rows, head_count, HEAD
        )
        scores = masked_scores(q_rows, keys_heads, segment, offset, block_rows)
        prob_rows = jnp.exp(scores - log_norm[block_index][..., None])
        grad_values = grad_values + jnp.einsum(
            "hqk,qhd->khd",
            prob_rows.astype(jnp.bfloat16),
            g_rows,
            preferred_element_type=jnp.float32,
        )
        grad_probs = jnp.einsum(
            "qhd,khd->hqk", g_rows, values_heads, preferred_element_type=jnp.float32
        )
        inner_sum = jnp.sum(prob_rows * grad_probs, axis=-1, keepdims=True)
        grad_scores = (prob_rows * (grad_probs - inner_sum) * HEAD ** (-0.5)).astype(jnp.bfloat16)
        grad_query = jnp.einsum(
            "hqk,khd->qhd", grad_scores, keys_heads, preferred_element_type=jnp.float32
        )
        grad_keys = grad_keys + jnp.einsum(
            "hqk,qhd->khd", grad_scores, q_rows, preferred_element_type=jnp.float32
        )
        return (
            (grad_keys, grad_values),
            grad_query.reshape(block_rows, head_count * HEAD).astype(jnp.bfloat16),
        )

    zero_state = jnp.zeros((slot_count, head_count, HEAD), jnp.float32)
    (grad_keys, grad_values), grad_query = lax.scan(
        one_block, (zero_state, zero_state), jnp.arange(slot_count // block_rows, dtype=jnp.int32)
    )
    return (
        grad_query.reshape(slot_count, head_count * HEAD),
        grad_keys.reshape(slot_count, head_count * HEAD).astype(jnp.bfloat16),
        grad_values.reshape(slot_count, head_count * HEAD).astype(jnp.bfloat16),
    )


def on_device_any(
    block_input,
    clip_lengths,
    norm1_gain,
    w_query,
    w_key,
    w_value,
    w_out,
    norm2_gain,
    w_up,
    w_down,
    out_cotangent,
):
    micro_count = block_input.shape[0]
    local_rows = block_input.shape[1]
    tensor_size = lax.axis_size("tensor")
    slot_count = local_rows * tensor_size
    block_rows = min(512, slot_count)
    clip_count = clip_lengths.shape[1]
    row_offset = lax.axis_index("tensor") * local_rows
    places = jnp.arange(slot_count, dtype=jnp.int32)

    def fetch_weights():
        return (
            lax.all_gather(norm1_gain, "dp", axis=0, tiled=True),
            lax.all_gather(norm2_gain, "dp", axis=0, tiled=True),
            lax.all_gather(w_query, "dp", axis=0, tiled=True),
            lax.all_gather(w_key, "dp", axis=0, tiled=True),
            lax.all_gather(w_value, "dp", axis=0, tiled=True),
            lax.all_gather(w_up, "dp", axis=0, tiled=True),
            lax.all_gather(w_out, "dp", axis=1, tiled=True),
            lax.all_gather(w_down, "dp", axis=1, tiled=True),
        )

    def rows_forward(normed):
        return lax.all_gather(normed, "tensor", axis=0, tiled=True)

    def rows_backward(gradients):
        return lax.all_gather(gradients, "tensor", axis=0, tiled=True)

    def sum_forward(term_fn):
        return lax.psum_scatter(
            term_fn(jnp.int32(0), local_rows * lax.axis_size("tensor")),
            "tensor",
            scatter_dimension=0,
            tiled=True,
        )

    def sum_backward(term_fn):
        return lax.psum_scatter(
            term_fn(jnp.int32(0), local_rows * lax.axis_size("tensor")),
            "tensor",
            scatter_dimension=0,
            tiled=True,
        )

    grad_totals = None
    outputs = []
    input_grads = []
    for micro_index in range(micro_count):
        gathered = fetch_weights()
        gain_one = gathered[0].astype(jnp.float32)
        gain_two = gathered[1].astype(jnp.float32)
        query_w, key_w, value_w, up_w, out_w, down_w = (
            gathered[2],
            gathered[3],
            gathered[4],
            gathered[5],
            gathered[6],
            gathered[7],
        )
        tokens = block_input[micro_index].astype(jnp.float32)
        ends = jnp.cumsum(clip_lengths[micro_index])
        segment = jnp.sum((places[:, None] >= ends[None, :]).astype(jnp.int32), axis=1)
        own_segment = lax.dynamic_slice_in_dim(segment, row_offset, local_rows, 0)
        valid_rows = (own_segment < clip_count).astype(jnp.float32)
        normed_one, unit_one, inverse_one = norm_rows(tokens, gain_one)
        features_one = rows_forward(normed_one.astype(jnp.bfloat16))
        query = jnp.dot(features_one, query_w, preferred_element_type=jnp.float32).astype(
            jnp.bfloat16
        )
        key = jnp.dot(features_one, key_w, preferred_element_type=jnp.float32).astype(jnp.bfloat16)
        value = jnp.dot(features_one, value_w, preferred_element_type=jnp.float32).astype(
            jnp.bfloat16
        )
        mixed_rows, log_norm = attend(query, key, value, segment, block_rows)

        def attn_term(offset, row_count):
            return jnp.dot(mixed_rows, out_w, preferred_element_type=jnp.float32)

        hidden = tokens + sum_forward(attn_term)
        normed_two, unit_two, inverse_two = norm_rows(hidden, gain_two)
        features_two = rows_forward(normed_two.astype(jnp.bfloat16))
        pre_act = jnp.dot(features_two, up_w, preferred_element_type=jnp.float32)
        activated = gelu_tanh(pre_act).astype(jnp.bfloat16)

        def mlp_term(offset, row_count):
            return jnp.dot(activated, down_w, preferred_element_type=jnp.float32)

        outputs.append((hidden + sum_forward(mlp_term)).astype(jnp.bfloat16))
        regathered = fetch_weights()
        query_w, key_w, value_w, up_w, out_w, down_w = (
            regathered[2],
            regathered[3],
            regathered[4],
            regathered[5],
            regathered[6],
            regathered[7],
        )
        grad_out = out_cotangent[micro_index].astype(jnp.float32) * valid_rows[:, None]
        grad_branch = rows_backward(grad_out.astype(jnp.bfloat16))
        down_grad = jnp.einsum(
            "sf,sd->fd", activated, grad_branch, preferred_element_type=jnp.float32
        )
        grad_act = jnp.einsum("sd,fd->sf", grad_branch, down_w, preferred_element_type=jnp.float32)
        grad_pre = jax.vjp(gelu_tanh, pre_act)[1](grad_act)[0].astype(jnp.bfloat16)
        up_grad = jnp.einsum(
            "sd,sf->df", features_two, grad_pre, preferred_element_type=jnp.float32
        )

        def up_term(offset, row_count):
            return jnp.einsum("sf,df->sd", grad_pre, up_w, preferred_element_type=jnp.float32)

        grad_normed_two = sum_backward(up_term)
        grad_from_two, gain_two_grad = norm_back(grad_normed_two, unit_two, inverse_two, gain_two)
        grad_hidden = grad_out + grad_from_two
        grad_attn = rows_backward(grad_hidden.astype(jnp.bfloat16))
        out_grad = jnp.einsum(
            "sc,sd->cd", mixed_rows, grad_attn, preferred_element_type=jnp.float32
        )
        grad_mixed = jnp.einsum(
            "sd,cd->sc", grad_attn, out_w, preferred_element_type=jnp.float32
        ).astype(jnp.bfloat16)
        grad_query, grad_key, grad_value = attend_back(
            query, key, value, segment, log_norm, grad_mixed, block_rows
        )
        query_grad = jnp.einsum(
            "sd,sc->dc", features_one, grad_query, preferred_element_type=jnp.float32
        )
        key_grad = jnp.einsum(
            "sd,sc->dc", features_one, grad_key, preferred_element_type=jnp.float32
        )
        value_grad = jnp.einsum(
            "sd,sc->dc", features_one, grad_value, preferred_element_type=jnp.float32
        )

        def qkv_term(offset, row_count):
            part_query = jnp.einsum(
                "sc,dc->sd", grad_query, query_w, preferred_element_type=jnp.float32
            )
            part_key = jnp.einsum("sc,dc->sd", grad_key, key_w, preferred_element_type=jnp.float32)
            part_value = jnp.einsum(
                "sc,dc->sd", grad_value, value_w, preferred_element_type=jnp.float32
            )
            return part_query + part_key + part_value

        grad_normed_one = sum_backward(qkv_term)
        grad_from_one, gain_one_grad = norm_back(grad_normed_one, unit_one, inverse_one, gain_one)
        input_grads.append(grad_hidden + grad_from_one)
        micro_grads = (
            gain_one_grad,
            gain_two_grad,
            query_grad,
            key_grad,
            value_grad,
            up_grad,
            out_grad,
            down_grad,
        )
        if grad_totals is None:
            grad_totals = micro_grads
        else:
            grad_totals = jax.tree.map(jnp.add, grad_totals, micro_grads)
    grad_totals = (
        lax.psum_scatter(
            grad_totals[0].astype(jnp.bfloat16), "dp", scatter_dimension=0, tiled=True
        ).astype(jnp.float32),
        lax.psum_scatter(
            grad_totals[1].astype(jnp.bfloat16), "dp", scatter_dimension=0, tiled=True
        ).astype(jnp.float32),
        lax.psum_scatter(
            grad_totals[2].astype(jnp.bfloat16), "dp", scatter_dimension=0, tiled=True
        ).astype(jnp.float32),
        lax.psum_scatter(
            grad_totals[3].astype(jnp.bfloat16), "dp", scatter_dimension=0, tiled=True
        ).astype(jnp.float32),
        lax.psum_scatter(
            grad_totals[4].astype(jnp.bfloat16), "dp", scatter_dimension=0, tiled=True
        ).astype(jnp.float32),
        lax.psum_scatter(
            grad_totals[5].astype(jnp.bfloat16), "dp", scatter_dimension=0, tiled=True
        ).astype(jnp.float32),
        lax.psum_scatter(
            grad_totals[6].astype(jnp.bfloat16), "dp", scatter_dimension=1, tiled=True
        ).astype(jnp.float32),
        lax.psum_scatter(
            grad_totals[7].astype(jnp.bfloat16), "dp", scatter_dimension=1, tiled=True
        ).astype(jnp.float32),
    )
    gain_sums = lax.psum((grad_totals[0], grad_totals[1]), "tensor")
    return (
        jnp.stack(outputs),
        jnp.stack(input_grads),
        gain_sums[0],
        grad_totals[2],
        grad_totals[3],
        grad_totals[4],
        grad_totals[6],
        gain_sums[1],
        grad_totals[5],
        grad_totals[7],
    )


def chunk_scores(q, k, start, s, c, rows):
    scores = lax.dot_general(
        q, k, (((1,), (1,)), ((), ())), preferred_element_type=f32
    ) * HEAD ** (-0.5)
    k_place = c * rows + lax.broadcasted_iota(jnp.int32, (rows, rows), 1)
    allowed = k_place >= start
    if c == s:
        q_place = s * rows + lax.broadcasted_iota(jnp.int32, (rows, rows), 0)
        allowed = jnp.logical_and(allowed, k_place <= q_place)
    return jnp.where(allowed, scores, masked_fill)


def clip_starts(ends_ref, first, buffer, clip_count, s, rows):
    place = s * rows + lax.broadcasted_iota(jnp.int32, (rows, 1), 0)
    start = jnp.zeros((rows, 1), jnp.int32)
    for clip in range(clip_count):
        end = ends_ref[first + buffer * clip_count + clip]
        start = jnp.where(place >= end, jnp.maximum(start, end), start)
    return start


def window(s, rows):
    back = -(-(LONGEST - 1) // rows)
    return range(max(0, s - back), s + 1)


def chunk_probs(q, keys, start, s, rows):
    cs = list(window(s, rows))
    scores = [chunk_scores(q, keys(c), start, s, c, rows) for c in cs]
    highest = functools.reduce(jnp.maximum, [jnp.max(v, axis=1, keepdims=True) for v in scores])
    shifted = [jnp.exp(v - highest) for v in scores]
    total = functools.reduce(jnp.add, [jnp.sum(v, axis=1, keepdims=True) for v in shifted])
    scale = 1.0 / total
    return cs, [v * scale for v in shifted]


MESH = pl.DeviceIdType.MESH
N_TILE = 1024


class Plane:
    def __init__(self, send_sems, recv_sems, more=()):
        me = lax.axis_index("dp")
        self.core = me % 2
        self.x = (me // 2) % 2
        self.peers = {
            "c": me + 1 - 2 * (me % 2),
            "x": me + 2 - 4 * ((me // 2) % 2),
            "y": me + 4 - 8 * ((me // 4) % 2),
        }
        self.send_sems, self.recv_sems = send_sems, recv_sems
        self.copies = []
        barrier = pltpu.get_barrier_semaphore()
        for peer in self.peers.values():
            pl.semaphore_signal(barrier, inc=1, device_id={"dp": peer}, device_id_type=MESH)
        for place in more:
            pl.semaphore_signal(barrier, inc=1, device_id=at_device(place), device_id_type=MESH)
        pl.semaphore_wait(barrier, 3 + len(more))

    def send(self, src, dst, way):
        return self.send_to(src, dst, {"dp": self.peers[way]})

    def send_to(self, src, dst, device):
        index = len(self.copies)
        copy = pltpu.make_async_remote_copy(
            src_ref=src,
            dst_ref=dst,
            send_sem=self.send_sems.at[index],
            recv_sem=self.recv_sems.at[index],
            device_id=device,
            device_id_type=MESH,
        )
        copy.start()
        self.copies.append(copy)
        return copy

    def finish(self):
        for copy in self.copies:
            copy.wait_send()


class Gather:
    def __init__(self, plane, own, pieces):
        self.plane, self.own, self.pieces = plane, own, pieces
        self.half = own.shape[0] // 2

    def begin(self):
        self.begin_links()
        self.begin_core()

    def begin_links(self):
        self.x = self.plane.send(self.own, self.pieces.at[1], "x")
        self.y = self.plane.send(self.own, self.pieces.at[2], "y")

    def begin_core(self):
        self.c = [self.plane.send(self.own, self.pieces.at[4], "c")]

    def middle(self):
        send, half, pieces = self.plane.send, self.half, self.pieces
        self.x.wait_recv()
        self.fy = send(pieces.at[1, pl.ds(half, half)], pieces.at[3, pl.ds(half, half)], "y")
        self.c.append(send(pieces.at[1], pieces.at[5], "c"))
        self.y.wait_recv()
        self.fx = send(pieces.at[2, pl.ds(0, half)], pieces.at[3, pl.ds(0, half)], "x")
        self.c.append(send(pieces.at[2], pieces.at[6], "c"))

    def end(self):
        self.fx.wait_recv()
        self.fy.wait_recv()
        self.c.append(self.plane.send(self.pieces.at[3], self.pieces.at[7], "c"))

    def core(self, index):
        self.c[index].wait_recv()


class Reduce:
    def __init__(self, plane, pieces, from_core, from_x, from_y):
        self.plane, self.pieces = plane, pieces
        self.from_core, self.from_x, self.from_y = from_core, from_x, from_y
        self.half = pieces.shape[1] // 2
        self.core = {}

    def give(self, m):
        self.core[m] = self.plane.send(self.pieces.at[4 + m], self.from_core.at[m], "c")

    def take(self, m):
        self.core[m].wait_recv()

    def chip_done(self, m):
        send, half, pieces = self.plane.send, self.half, self.pieces
        low, high = pl.ds(0, half), pl.ds(half, half)
        if m == 3:
            self.far_x = send(pieces.at[3, low], self.from_x.at[1], "x")
            self.far_y = send(pieces.at[3, high], self.from_y.at[1], "y")
        elif m == 1:
            self.near_x = send(pieces.at[1, low], self.from_x.at[0], "x")
        elif m == 2:
            self.near_y = send(pieces.at[2, high], self.from_y.at[0], "y")

    def late_x(self):
        high = pl.ds(self.half, self.half)
        self.far_y.wait_recv()
        add_into(self.pieces.at[1, high], self.from_y.at[1])
        self.late_x_copy = self.plane.send(self.pieces.at[1, high], self.from_x.at[2], "x")

    def late_y(self):
        low = pl.ds(0, self.half)
        self.far_x.wait_recv()
        add_into(self.pieces.at[2, low], self.from_x.at[1])
        self.late_y_copy = self.plane.send(self.pieces.at[2, low], self.from_y.at[2], "y")

    def late(self):
        self.late_x()
        self.late_y()

    def total(self, out):
        half = self.half
        self.near_x.wait_recv()
        self.near_y.wait_recv()
        self.late_x_copy.wait_recv()
        self.late_y_copy.wait_recv()
        step = min(64, half)

        for base, x_part, y_part in ((0, 0, 2), (half, 2, 0)):

            def add(index, carry):
                at = pl.ds(pl.multiple_of(index * step, step), step)
                here = pl.ds(pl.multiple_of(base + index * step, step), step)
                out[here] = (
                    self.pieces[0, here].astype(f32)
                    + self.from_x[x_part, at].astype(f32)
                    + self.from_y[y_part, at].astype(f32)
                )
                return carry

            lax.fori_loop(0, half // step, add, 0)


def add_into(ref, other):
    step = min(64, ref.shape[0])

    def add(index, carry):
        at = pl.ds(pl.multiple_of(index * step, step), step)
        ref[at] = (ref[at].astype(f32) + other[at].astype(f32)).astype(bf16)
        return carry

    lax.fori_loop(0, ref.shape[0] // step, add, 0)


ORDER = (3, 1, 2, 0)


def tiles(count, tile, body):
    tile = min(tile, count)

    def step(index, carry):
        body(pl.ds(pl.multiple_of(index * tile, tile), tile))
        return carry

    lax.fori_loop(0, count // tile, step, 0)


def nn(left, right):
    return jnp.dot(left, right, preferred_element_type=f32)


def nt(left, right):
    return lax.dot_general(left, right, (((1,), (1,)), ((), ())), preferred_element_type=f32)


def tn(left, right):
    return lax.dot_general(left, right, (((0,), (0,)), ((), ())), preferred_element_type=f32)


class Feed:
    def __init__(self, source, slots, sems, order):
        self.source, self.slots, self.sems, self.order = source, slots, sems, list(order)

    def copy(self, index):
        slot = index % 2
        return pltpu.make_async_copy(
            self.source(self.order[index]), self.slots.at[slot], self.sems.at[slot]
        )

    def start(self, index):
        if index < len(self.order):
            self.copy(index).start()

    def get(self, index):
        self.copy(index).wait()
        return self.slots.at[index % 2]


def plane_call(kernel, name, collective_id, out_shape, in_spaces, out_spaces, scratch, copies, flops, args):
    spaces = {"any": pl.ANY, "vmem": pltpu.VMEM, "smem": pltpu.SMEM}
    return pl.pallas_call(
        kernel,
        out_shape=out_shape,
        in_specs=[pl.BlockSpec(memory_space=spaces[v]) for v in in_spaces],
        out_specs=[pl.BlockSpec(memory_space=spaces[v]) for v in out_spaces],
        scratch_shapes=list(scratch)
        + [pltpu.SemaphoreType.DMA((copies,)), pltpu.SemaphoreType.DMA((copies,))],
        compiler_params=pltpu.CompilerParams(
            collective_id=collective_id, has_side_effects=True, vmem_limit_bytes=62 << 20
        ),
        cost_estimate=pl.CostEstimate(flops=flops, bytes_accessed=64 << 20, transcendentals=0),
        name=name,
    )(*args)


def row_places():
    me, plane = lax.axis_index("dp"), lax.axis_index("tensor")
    chip, core = 2 * (me // 2), me % 2
    outward = [(chip + 1 - plane // 2, 2 * core + j) for j in range(2)]
    inward = [(chip + plane // 2, 2 * (1 - core) + i) for i in range(2)]
    return outward, inward


def at_device(place):
    return {"dp": place[0], "tensor": place[1]}


class RowMove:
    def __init__(self, src, dst, sems):
        self.src, self.dst, self.sems = src, dst, sems
        self.copies = []

    def copy(self, here, there, place):
        return pltpu.make_async_remote_copy(
            src_ref=self.src.at[here],
            dst_ref=self.dst.at[there],
            send_sem=self.sems.at[0, here],
            recv_sem=self.sems.at[1, there],
            device_id=at_device(place),
            device_id_type=MESH,
        )

    def start(self, places, there):
        for here in range(2):
            copy = self.copy(here, there, places[here])
            copy.start()
            self.copies.append(copy)
        self.arrivals = [self.copy(index, index, places[index]) for index in range(2)]

    def outward(self):
        self.start(row_places()[0], lax.axis_index("tensor") % 2)

    def back(self):
        self.start(row_places()[1], lax.axis_index("tensor") % 2)

    def wait(self):
        for copy in self.copies:
            copy.wait_send()
        for copy in self.arrivals:
            copy.wait_recv()


def start_kernel(
    tokens, w_query, w_key, w_value, w_out, w_up, w_down, small,
    tokens_out, qkv_out, out_out, up_out, down_out, small_out,
    local_sems, row_sems, send_sems, recv_sems,
):
    me, plane = lax.axis_index("dp"), lax.axis_index("tensor")
    chip, core = me // 2, me % 2
    depth = w_query.shape[0]
    part = up_out.shape[1]
    outward, inward = row_places()
    peers = [lax.rem(me + j, 8) for j in range(1, 8)]
    barrier = pltpu.get_barrier_semaphore()
    for peer in peers:
        pl.semaphore_signal(barrier, inc=1, device_id={"dp": peer}, device_id_type=MESH)
    for place in outward + inward:
        pl.semaphore_signal(barrier, inc=1, device_id=at_device(place), device_id_type=MESH)
    pl.semaphore_wait(barrier, 11)
    copies, locals_ = [], []

    def send(src, dst, device):
        copy = pltpu.make_async_remote_copy(
            src_ref=src,
            dst_ref=dst,
            send_sem=send_sems.at[len(copies)],
            recv_sem=recv_sems.at[len(copies)],
            device_id=device,
            device_id_type=MESH,
        )
        copy.start()
        copies.append(copy)

    def keep(src, dst):
        copy = pltpu.make_async_copy(src, dst, local_sems.at[len(locals_)])
        copy.start()
        locals_.append(copy)

    def block(index, size):
        return pl.ds(pl.multiple_of(index * size, size), size)

    rows_move = RowMove(tokens, tokens_out, row_sems)
    rows_move.outward()
    for peer in peers:
        send(small, small_out.at[me], {"dp": peer})
    keep(small, small_out.at[me])
    heads = [(w_query, 0), (w_key, 1), (w_value, 2)]
    for j in range(1, 4):
        other = lax.rem(chip + j, 4)
        device = {"dp": 2 * other + core}
        for weight, which in heads:
            send(weight.at[:, block(other, HEAD)], qkv_out.at[which, chip], device)
    for weight, which in heads:
        keep(weight.at[:, block(chip, HEAD)], qkv_out.at[which, chip])
    for j in range(1, 4):
        other = lax.rem(chip + j, 4)
        send(w_out.at[block(other, HEAD)], out_out.at[chip], {"dp": 2 * other + core})
    keep(w_out.at[block(chip, HEAD)], out_out.at[chip])
    for peer in peers:
        send(w_up.at[:, block(peer, part)], up_out.at[block(me, depth)], {"dp": peer})
        send(w_down.at[block(peer, part)], down_out.at[:, block(me, depth)], {"dp": peer})
    keep(w_up.at[:, block(me, part)], up_out.at[block(me, depth)])
    keep(w_down.at[block(me, part)], down_out.at[:, block(me, depth)])
    for copy in locals_:
        copy.wait()
    for copy in copies:
        copy.wait()
    rows_move.wait()


def gather_kernel(own, rows_in, pieces, rows_out, own_sem, row_sems, send_sems, recv_sems):
    outward, inward = row_places()
    plane = Plane(send_sems, recv_sems, outward + inward)
    streams = own.shape[0]
    rows_move = RowMove(rows_in, rows_out, row_sems)
    rows_move.outward()
    gathers = [Gather(plane, own.at[s], pieces.at[s]) for s in range(streams)]
    keep = [pltpu.make_async_copy(own.at[s], pieces.at[s, 0], own_sem.at[s]) for s in range(streams)]
    for s in range(streams):
        gathers[s].begin()
        keep[s].start()
    for s in range(streams):
        gathers[s].middle()
    for s in range(streams):
        gathers[s].end()
    for s in range(streams):
        keep[s].wait()
        for index in range(4):
            gathers[s].core(index)
    rows_move.wait()
    plane.finish()


def chunk_at(plane, s):
    k = 1 - s // 2
    return s % 2, k + plane.core - 2 * k * plane.core


def chunk_part(plane, qkv, chip, head):
    def part(s, which):
        column = pl.multiple_of((head * 3 + which) * HEAD, HEAD)
        stream, core = chunk_at(plane, s)
        piece = core * (qkv.shape[1] // 2) + chip
        return qkv[stream, piece, :, pl.ds(column, HEAD)]

    return part


def attend_all(plane, qkv, ends_ref, out, clip_count):
    rows = qkv.shape[2]
    heads = qkv.shape[3] // (3 * HEAD)

    def one(index, carry):
        chip, head = index // heads, index % heads
        part = chunk_part(plane, qkv, chip, head)
        column = pl.ds(pl.multiple_of(head * HEAD, HEAD), HEAD)
        for s in range(4):
            start = clip_starts(ends_ref, 0, chip, clip_count, s, rows)
            cs, probs = chunk_probs(part(s, 0), lambda c: part(c, 1), start, s, rows)
            mixed = jnp.zeros((rows, HEAD), f32)
            for c, prob in zip(cs, probs):
                mixed = mixed + nn(prob.astype(bf16), part(c, 2))
            stream, core = chunk_at(plane, s)
            out[stream, core * 4 + chip, :, column] = mixed.astype(bf16)
        return carry

    return one


def attend_back_chip(plane, qkv, grad_mixed, ends_ref, out, key_sum, value_sum, clip_count, chip):
    rows = qkv.shape[2]
    heads = qkv.shape[3] // (3 * HEAD)

    def one(head, carry):
        part = chunk_part(plane, qkv, 0, head)
        column = pl.ds(pl.multiple_of(head * HEAD, HEAD), HEAD)
        key_sum[...] = jnp.zeros_like(key_sum)
        value_sum[...] = jnp.zeros_like(value_sum)

        def put(s, which, value):
            at = pl.ds(pl.multiple_of((head * 3 + which) * HEAD, HEAD), HEAD)
            stream, core = chunk_at(plane, s)
            out[stream, core, :, at] = value.astype(bf16)

        for s in range(4):
            q = part(s, 0)
            stream, core = chunk_at(plane, s)
            g = grad_mixed[stream, core * 4 + chip, :, column]
            start = clip_starts(ends_ref, 0, chip, clip_count, s, rows)
            cs, probs = chunk_probs(q, lambda c: part(c, 1), start, s, rows)
            grad_probs = [nt(g, part(c, 2)) for c in cs]
            inner = functools.reduce(
                jnp.add,
                [jnp.sum(p * v, axis=1, keepdims=True) for p, v in zip(probs, grad_probs)],
            )
            grad_q = jnp.zeros((rows, HEAD), f32)
            for c, prob, grad_prob in zip(cs, probs, grad_probs):
                grad_score = (prob * (grad_prob - inner) * HEAD ** (-0.5)).astype(bf16)
                grad_q = grad_q + nn(grad_score, part(c, 1))
                key_sum[c] += tn(grad_score, q)
                value_sum[c] += tn(prob.astype(bf16), g)
            put(s, 0, grad_q)
        for s in range(4):
            put(s, 1, key_sum[s])
            put(s, 2, value_sum[s])
        return carry

    lax.fori_loop(0, heads, one, 0)


def attention_kernel(
    clip_count, own, rows_in, wide, ends, pieces, qkv, mixed, weight, slots, slot_sems, own_sem, wide_sems, send_sems, recv_sems
):
    plane = Plane(send_sems, recv_sems)
    streams = own.shape[0]
    gathers = [Gather(plane, own.at[s], pieces.at[s]) for s in range(streams)]
    keep = [pltpu.make_async_copy(own.at[s], pieces.at[s, 0], own_sem.at[s]) for s in range(streams)]
    traded, kept = [], []
    for head in range(2):
        for which in range(3):
            column = pl.ds((head * 3 + which) * HEAD, HEAD)
            here = weight.at[:, plane.core, :, column]
            traded.append(plane.send(wide.at[2 * (1 - plane.core) + head, which], here, "c"))
            copy = pltpu.make_async_copy(
                wide.at[2 * plane.core + head, which], here, wide_sems.at[len(kept)]
            )
            copy.start()
            kept.append(copy)
    for s in range(streams):
        gathers[s].begin()
        keep[s].start()
    total = weight.shape[3]
    feed = Feed(
        lambda at: rows_in.at[at[0], at[1]],
        slots,
        slot_sems,
        [(s, p) for s in range(streams) for p in range(8)],
    )
    feed.start(0)

    def project(s):
        for p in range(8):
            feed.start(s * 8 + p + 1)
            piece = feed.get(s * 8 + p)

            def tile(at):
                columns = weight[:, :, :, at].reshape(width, -1)
                qkv[s, p, :, at] = nn(piece[...], columns).astype(bf16)

            tiles(total, N_TILE, tile)

    for copy in traded:
        copy.wait_recv()
    for copy in kept:
        copy.wait()
    width = own.shape[2]

    attend = attend_all(plane, qkv, ends, mixed, clip_count)
    heads = total // (3 * HEAD)
    project(0)
    project(1)
    lax.fori_loop(0, 2 * heads, attend, 0)
    gathers[0].middle()
    gathers[1].middle()
    lax.fori_loop(2 * heads, 4 * heads, attend, 0)
    gathers[0].end()
    gathers[1].end()
    for s in range(streams):
        keep[s].wait()
        for index in range(4):
            gathers[s].core(index)
    plane.finish()


def reduce_scratch(streams, rows, width):
    return [
        pltpu.VMEM((streams, 8, rows, width), bf16),
        pltpu.VMEM((streams, 4, rows, width), bf16),
        pltpu.VMEM((streams, 3, rows // 2, width), bf16),
        pltpu.VMEM((streams, 3, rows // 2, width), bf16),
    ]


def project_kernel(
    mixed, wide, out, weight, parts, from_core, from_x, from_y, wide_sems, send_sems, recv_sems
):
    plane = Plane(send_sems, recv_sems)
    streams = mixed.shape[0]
    width = weight.shape[1]
    depth = wide.shape[3]
    traded, kept = [], []
    for head in range(2):
        for chip in range(4):
            column = pl.ds(pl.multiple_of((2 * chip + plane.core) * depth, depth), depth)
            here = weight.at[pl.ds(head * HEAD, HEAD), column]
            traded.append(plane.send(wide.at[2 * (1 - plane.core) + head, chip], here, "c"))
            copy = pltpu.make_async_copy(
                wide.at[2 * plane.core + head, chip], here, wide_sems.at[len(kept)]
            )
            copy.start()
            kept.append(copy)
    for copy in traded:
        copy.wait_recv()
    for copy in kept:
        copy.wait()
    sums = [
        Reduce(plane, parts.at[s], from_core.at[s], from_x.at[s], from_y.at[s])
        for s in range(streams)
    ]

    for s in range(streams):
        for m in ORDER:

            def other(at):
                parts[s, 4 + m, :, at] = nn(mixed[s, 4 + m], weight[:, at]).astype(bf16)

            tiles(width, N_TILE, other)
            sums[s].give(m)
        for m in ORDER:
            sums[s].take(m)

            def chip(at):
                here = nn(mixed[s, m], weight[:, at])
                parts[s, m, :, at] = (here + from_core[s, m, :, at].astype(f32)).astype(bf16)

            tiles(width, N_TILE, chip)
            sums[s].chip_done(m)
        if s > 0:
            sums[s - 1].late()
    sums[streams - 1].late()
    for s in range(streams):
        sums[s].total(out.at[s])
    plane.finish()


def gelu_pair(v):
    cubic = 0.044715 * (v * v) * v
    inner = (2.0 / np.pi) ** 0.5 * (v + cubic)
    th = jnp.tanh(inner)
    half = 0.5 * (1.0 + th)
    slope = (2.0 / np.pi) ** 0.5 * (1.0 + 3.0 * 0.044715 * (v * v))
    return v * half, half + 0.5 * v * (1.0 - th * th) * slope


def lay_out(wide, flat, sems):
    copies = []
    part = wide.shape[2]
    for plane in range(wide.shape[0]):
        copy = pltpu.make_async_copy(
            wide.at[plane], flat.at[:, pl.ds(plane * part, part)], sems.at[plane]
        )
        copy.start()
        copies.append(copy)
    return copies


def mlp_kernel(
    own, up_wide, down_w, grads, pieces, slope_out, down_grad, out,
    parts, from_core, from_x, from_y, up_w, slots, act, slope, total, grad_slots,
    up_sems, slot_sems, keep_sems, own_sem, grad_sems, send_sems, recv_sems,
):
    plane = Plane(send_sems, recv_sems)
    streams, rows, width = own.shape
    hidden = up_w.shape[1]
    up_copies = lay_out(up_wide, up_w, up_sems)
    gathers = [Gather(plane, own.at[s], pieces.at[s]) for s in range(streams)]
    sums = [
        Reduce(plane, parts.at[s], from_core.at[s], from_x.at[s], from_y.at[s])
        for s in range(streams)
    ]
    keep = [pltpu.make_async_copy(own.at[s], pieces.at[s, 0], own_sem.at[s]) for s in range(streams)]
    stores = []

    def up_piece(s, p, slot):
        if len(stores) >= 2:
            stores[-2].wait()

        def up(at):
            value, grad = gelu_pair(nn(slots[slot], up_w[:, at]))
            act[slot, :, at] = value.astype(bf16)
            slope[slot, :, at] = grad.astype(bf16)

        tiles(hidden, N_TILE, up)
        store = pltpu.make_async_copy(slope.at[slot], slope_out.at[s, p], keep_sems.at[slot])
        store.start()
        stores.append(store)

    def down_piece(s, p, slot):
        def down(at):
            here = nn(act[slot], down_w[:, at])
            if p < 4:
                here = here + from_core[s, p, :, at].astype(f32)
            parts[s, p, :, at] = here.astype(bf16)

        tiles(width, N_TILE, down)

    def pair_up(s, m):
        if m > 0:
            gathers[s].core(m)
        first = not stores
        rows_come = [
            pltpu.make_async_copy(
                own.at[s] if p == 0 else pieces.at[s, p], slots.at[i], slot_sems.at[i]
            )
            for i, p in enumerate((4 + m, m))
        ]
        coming = [
            pltpu.make_async_copy(grads.at[s, p], grad_slots.at[i], grad_sems.at[i])
            for i, p in enumerate((4 + m, m))
        ]
        if m == 0:
            rows_come[1].start()
            gathers[s].core(0)
            rows_come[0].start()
        else:
            rows_come[0].start()
            rows_come[1].start()
        for copy in coming:
            copy.start()
        rows_come[0].wait()
        up_piece(s, 4 + m, 0)
        down_piece(s, 4 + m, 0)
        sums[s].give(m)
        rows_come[1].wait()
        up_piece(s, m, 1)
        for copy in coming:
            copy.wait()
        left = act[...].reshape(2 * rows, hidden)

        def weigh(at):
            term = tn(left, grad_slots[:, :, at].reshape(2 * rows, -1))
            total[:, at] = term if first else total[:, at] + term

        tiles(width, 512, weigh)
        sums[s].take(m)
        down_piece(s, m, 1)
        sums[s].chip_done(m)

    for s in range(streams):
        keep[s].start()
        gathers[s].begin_core()
    gathers[0].begin_links()
    for copy in up_copies:
        copy.wait()
    pair_up(0, 0)
    pair_up(1, 0)
    gathers[0].middle()
    gathers[1].begin_links()
    pair_up(0, 1)
    pair_up(0, 2)
    gathers[0].end()
    pair_up(0, 3)
    gathers[1].middle()
    pair_up(1, 1)
    sums[0].late()
    gathers[1].end()
    pair_up(1, 3)
    pair_up(1, 2)
    sums[1].late()
    for s in range(streams):
        sums[s].total(out.at[s])
        keep[s].wait()
    for store in stores[-2:]:
        store.wait()
    stores = []
    for index in range(hidden // rows):
        if index >= 2:
            stores[index - 2].wait()
        here = pl.ds(index * rows, rows)
        slots[index % 2] = total[here].astype(bf16)
        store = pltpu.make_async_copy(
            slots.at[index % 2], down_grad.at[here], keep_sems.at[index % 2]
        )
        store.start()
        stores.append(store)
    for store in stores[-2:]:
        store.wait()
    plane.finish()


def mlp_back_kernel(
    grads, slope_in, features, up_wide, down_w, up_grad, out,
    parts, from_core, from_x, from_y, up_w, slots, slopes, pre, rows_two, total,
    up_sems, slot_sems, slope_sems, row_sems, keep_sems, send_sems, recv_sems,
):
    plane = Plane(send_sems, recv_sems)
    streams, _, rows, width = grads.shape
    hidden = up_w.shape[1]
    part = up_wide.shape[2]
    up_copies = lay_out(up_wide, up_w, up_sems)
    sums = [
        Reduce(plane, parts.at[s], from_core.at[s], from_x.at[s], from_y.at[s])
        for s in range(streams)
    ]
    order = [(s, p) for s in range(streams) for m in ORDER for p in (4 + m, m)]
    feed = Feed(lambda at: grads.at[at[0], at[1]], slots, slot_sems, order)
    feed_slope = Feed(lambda at: slope_in.at[at[0], at[1]], slopes, slope_sems, order)
    feed_rows = Feed(lambda at: features.at[at[0], at[1]], rows_two, row_sems, order)
    feed.start(0)
    feed_slope.start(0)
    def back_piece(index):
        feed.start(index + 1)
        feed_slope.start(index + 1)
        feed_rows.start(index)
        grad = feed.get(index)
        slope = feed_slope.get(index)

        def back(at):
            value = nt(grad[...], down_w[at]) * slope[:, at].astype(f32)
            pre[index % 2, :, at] = value.astype(bf16)

        tiles(hidden, N_TILE, back)

    def through_piece(index, s, p):
        def through(at):
            here = nt(pre[index % 2], up_w[at])
            if p < 4:
                here = here + from_core[s, p, :, at].astype(f32)
            parts[s, p, :, at] = here.astype(bf16)

        tiles(width, N_TILE, through)

    for index, (s, p) in enumerate(order):
        back_piece(index)
        if index == 0:
            for copy in up_copies:
                copy.wait()
        if p >= 4:
            through_piece(index, s, p)
            sums[s].give(p - 4)
            continue
        feed_rows.get(index - 1)
        feed_rows.get(index)
        right = pre[...].reshape(2 * rows, hidden)

        def weigh(at):
            term = tn(rows_two[:, :, at].reshape(2 * rows, -1), right)
            total[at] = term if index == 1 else total[at] + term

        tiles(width, 512, weigh)
        sums[s].take(p)
        through_piece(index, s, p)
        sums[s].chip_done(p)
        if p == 2:
            sums[s].late_x()
        if p == 0:
            sums[s].late_y()
    stores = []
    for index in range(width // rows):
        slot = index % 2
        for store in stores[index - 2] if index >= 2 else []:
            store.wait()
        here = pl.ds(index * rows, rows)
        pre[slot] = total[here].astype(bf16)
        stores.append([])
        for at in range(hidden // part):
            store = pltpu.make_async_copy(
                pre.at[slot, :, pl.ds(at * part, part)], up_grad.at[at, here], keep_sems.at[slot, at]
            )
            store.start()
            stores[-1].append(store)
    for s in range(streams):
        sums[s].total(out.at[s])
    for pair in stores[-2:]:
        for store in pair:
            store.wait()
    plane.finish()


def attention_back_kernel(
    clip_count, own, qkv, mixed, features, rows_in, qkv_w, out_w, ends,
    pieces, qkv_grad, out_grad, rows_out, out,
    parts, from_core, from_x, from_y, slots, mixed_slots, grad_mixed, qkv_chip, grad_chip, key_sum, value_sum,
    qkv_sum, out_sum, slot_sems, mixed_sems, chip_sems, store_sems, row_sems, own_sem, send_sems, recv_sems,
):
    outward, inward = row_places()
    plane = Plane(send_sems, recv_sems, outward + inward)
    rows_move = RowMove(rows_in, rows_out, row_sems)
    rows_move.back()
    streams, rows, width = own.shape
    gathers = [Gather(plane, own.at[s], pieces.at[s]) for s in range(streams)]
    sums = [
        Reduce(plane, parts.at[s], from_core.at[s], from_x.at[s], from_y.at[s])
        for s in range(streams)
    ]
    keep = [pltpu.make_async_copy(own.at[s], pieces.at[s, 0], own_sem.at[s]) for s in range(streams)]
    def load_chip(m):
        copies = [
            pltpu.make_async_copy(
                qkv.at[s, core * 4 + m], qkv_chip.at[s, core], chip_sems.at[s * 2 + core]
            )
            for s in range(streams)
            for core in range(2)
        ]
        for copy in copies:
            copy.start()
        return copies

    def load_rows(m):
        copies = [
            pltpu.make_async_copy(
                features.at[s, core * 4 + m], slots.at[s * 2 + core], slot_sems.at[s * 2 + core]
            )
            for s in range(streams)
            for core in range(2)
        ]
        for copy in copies:
            copy.start()
        return copies

    def weigh_chip(place, copies):
        for copy in copies:
            copy.wait()
        right = grad_chip[place % 2].reshape(4 * rows, -1)

        def weigh(at):
            term = tn(slots[:, :, at].reshape(4 * rows, -1), right)
            qkv_sum[at] = term if place == 0 else qkv_sum[at] + term

        tiles(width, 512, weigh)

    mixed_before = []

    def mix_pair(s, m):
        pair = (m, 4 + m)
        rows_come = [
            pltpu.make_async_copy(
                own.at[s] if p == 0 else pieces.at[s, p], slots.at[i], slot_sems.at[i]
            )
            for i, p in enumerate(pair)
        ]
        left_come = [
            pltpu.make_async_copy(mixed.at[s, p], mixed_slots.at[i], mixed_sems.at[i])
            for i, p in enumerate(pair)
        ]
        rows_come[0].start()
        for copy in left_come:
            copy.start()
        gathers[s].core(m)
        rows_come[1].start()
        for i, p in enumerate(pair):
            rows_come[i].wait()
            grad_mixed[s, p] = nt(slots[i], out_w[...]).astype(bf16)
        for copy in left_come:
            copy.wait()
        left = mixed_slots[...].reshape(2 * rows, -1)
        first = not mixed_before
        mixed_before.append(m)

        def weigh(at):
            term = tn(left, slots[pl.ds(0, 2), :, at].reshape(2 * rows, -1))
            out_sum[:, at] = term if first else out_sum[:, at] + term

        tiles(width, N_TILE, weigh)

    def attend_chip(place, m, coming, following):
        for copy in coming:
            copy.wait()
        grad_here = grad_chip.at[place % 2]
        attend_back_chip(
            plane, qkv_chip, grad_mixed, ends, grad_here, key_sum, value_sum, clip_count, m
        )
        coming = load_chip(following) if following is not None else []
        for s in range(streams):

            def other(at):
                parts[s, 4 + m, :, at] = nt(grad_here[s, 1], qkv_w[at]).astype(bf16)

            tiles(width, N_TILE, other)
            sums[s].give(m)
        for s in range(streams):
            sums[s].take(m)

            def chip(at):
                here = nt(grad_here[s, 0], qkv_w[at])
                parts[s, m, :, at] = (here + from_core[s, m, :, at].astype(f32)).astype(bf16)

            tiles(width, N_TILE, chip)
            sums[s].chip_done(m)
        return coming

    for s in range(streams):
        keep[s].start()
        gathers[s].begin_core()
    gathers[0].begin_links()
    coming = load_chip(0)
    mix_pair(0, 0)
    mix_pair(1, 0)
    coming = attend_chip(0, 0, coming, 1)
    gathers[0].middle()
    gathers[1].begin_links()
    mix_pair(0, 1)
    mix_pair(0, 2)
    weigh_chip(0, load_rows(0))
    gathers[0].end()
    mix_pair(0, 3)
    gathers[1].middle()
    mix_pair(1, 1)
    mix_pair(1, 2)
    coming = attend_chip(1, 1, coming, 3)
    gathers[1].end()
    mix_pair(1, 3)
    coming_rows = load_rows(1)
    coming = attend_chip(2, 3, coming, 2)
    weigh_chip(1, coming_rows)
    coming_rows = load_rows(3)
    attend_chip(3, 2, coming, None)
    for s in range(streams):
        sums[s].late_x()
    for s in range(streams):
        sums[s].late_y()
    weigh_chip(2, coming_rows)
    weigh_chip(3, load_rows(2))
    for index in range(out_sum.shape[0] // rows):
        here = pl.ds(index * rows, rows)
        slots[0] = out_sum[here].astype(bf16)
        out_store = pltpu.make_async_copy(slots.at[0], out_grad.at[here], slot_sems.at[0])
        out_store.start()
        out_store.wait()
    stores = []
    for index in range(width // rows):
        if index >= 4:
            stores[index - 4].wait()
        here = pl.ds(index * rows, rows)
        stage = grad_chip.at[0, index // 2 % 2, index % 2]
        stage[...] = qkv_sum[here].astype(bf16)
        store = pltpu.make_async_copy(stage, qkv_grad.at[here], store_sems.at[index % 4])
        store.start()
        stores.append(store)
    for s in range(streams):
        sums[s].total(out.at[s])
        keep[s].wait()
    for store in stores[-4:]:
        store.wait()
    rows_move.wait()
    plane.finish()


def end_kernel(
    rows_in, qkv_grad, out_grad, up_sum, down_sum, gains,
    rows_out, qkv_out, out_out, up_out, down_out, gains_out,
    qkv_part, out_part, qkv_come, out_come, gain_come, gain_sum, gain_all,
    local_sems, row_sems, send_sems, recv_sems,
):
    me, z = lax.axis_index("dp"), lax.axis_index("tensor")
    chip, core = me // 2, me % 2
    depth = qkv_grad.shape[2]
    outward, inward = row_places()
    peers = [lax.rem(me + j, 8) for j in range(1, 8)]
    planes = [lax.rem(z + j, 4) for j in range(1, 4)]
    barrier = pltpu.get_barrier_semaphore()
    for peer in peers:
        pl.semaphore_signal(barrier, inc=1, device_id={"dp": peer}, device_id_type=MESH)
    for plane in planes:
        pl.semaphore_signal(barrier, inc=1, device_id={"tensor": plane}, device_id_type=MESH)
    for place in outward + inward:
        pl.semaphore_signal(barrier, inc=1, device_id=at_device(place), device_id_type=MESH)
    pl.semaphore_wait(barrier, 14)
    copies, locals_ = [], []

    def send(src, dst, device):
        copy = pltpu.make_async_remote_copy(
            src_ref=src,
            dst_ref=dst,
            send_sem=send_sems.at[len(copies)],
            recv_sem=recv_sems.at[len(copies)],
            device_id=device,
            device_id_type=MESH,
        )
        copy.start()
        copies.append(copy)
        return copy

    def keep(src, dst):
        copy = pltpu.make_async_copy(src, dst, local_sems.at[len(locals_)])
        copy.start()
        locals_.append(copy)

    def block(index, size):
        return pl.ds(pl.multiple_of(index * size, size), size)

    other = {"dp": me + 1 - 2 * core}
    traded = []
    for head in range(2):
        mine = 2 * core + head
        for which in range(3):
            column = pl.ds((head * 3 + which) * HEAD, HEAD)
            traded.append(
                send(qkv_grad.at[:, 1 - core, :, column], qkv_part.at[mine, which], other)
            )
            keep(qkv_grad.at[:, core, :, column], qkv_part.at[mine, which])
        here = pl.ds(head * HEAD, HEAD)
        for c in range(4):
            theirs = pl.ds(pl.multiple_of((2 * c + 1 - core) * depth, depth), depth)
            own = pl.ds(pl.multiple_of((2 * c + core) * depth, depth), depth)
            traded.append(send(out_grad.at[here, theirs], out_part.at[mine, c], other))
            keep(out_grad.at[here, own], out_part.at[mine, c])
    gain_first = [send(gains.at[peer], gain_come.at[me], {"dp": peer}) for peer in peers]
    gain_come[me] = gains[me]
    begun = len(locals_)
    part = up_sum.shape[1]
    shards = []
    for peer in peers:
        shards.append(send(up_sum.at[block(peer, depth)], up_out.at[:, block(me, part)], {"dp": peer}))
        shards.append(send(down_sum.at[:, block(peer, depth)], down_out.at[block(me, part)], {"dp": peer}))
    keep(up_sum.at[block(me, depth)], up_out.at[:, block(me, part)])
    keep(down_sum.at[:, block(me, depth)], down_out.at[block(me, part)])
    for copy in traded:
        copy.wait_recv()
    for copy in locals_[:begun]:
        copy.wait()
    after = {"tensor": planes[0]}
    for step in range(3):
        part = lax.rem(z + 3 - step, 4)
        ring = [
            send(qkv_part.at[part], qkv_come.at[step], after),
            send(out_part.at[part], out_come.at[step], after),
        ]
        if step == 0:
            rows_move = RowMove(rows_in, rows_out, row_sems)
            rows_move.back()
            for copy in gain_first:
                copy.wait_recv()
            gain_sum[...] = functools.reduce(jnp.add, [gain_come[i] for i in range(8)])
            gain_second = [
                send(gain_sum, gain_all.at[z], {"tensor": plane}) for plane in planes
            ]
            gain_all[z] = gain_sum[...]
        for copy in ring:
            copy.wait_recv()
        part = lax.rem(z + 2 - step, 4) if step < 2 else z
        for which in range(3):
            for c in range(4):
                here = qkv_part.at[part, which, c]
                here[...] = (
                    here[...].astype(f32) + qkv_come[step, which, c].astype(f32)
                ).astype(bf16)
        for c in range(4):
            here = out_part.at[part, c]
            here[...] = (here[...].astype(f32) + out_come[step, c].astype(f32)).astype(bf16)
    last = []
    for j in range(1, 4):
        to = lax.rem(chip + j, 4)
        device = {"dp": 2 * to + core}
        last.append(send(qkv_part.at[z, :, to], qkv_out.at[:, :, block(chip, HEAD)], device))
        last.append(send(out_part.at[z, to], out_out.at[block(chip, HEAD)], device))
    keep(qkv_part.at[z, :, chip], qkv_out.at[:, :, block(chip, HEAD)])
    keep(out_part.at[z, chip], out_out.at[block(chip, HEAD)])
    for copy in gain_second:
        copy.wait_recv()
    gains_out[...] = functools.reduce(jnp.add, [gain_all[i] for i in range(4)])
    for copy in last + shards:
        copy.wait_recv()
    for copy in locals_[begun:]:
        copy.wait()
    rows_move.wait()
    for copy in copies:
        copy.wait_send()


def on_device(
    block_input,
    clip_lengths,
    norm1_gain,
    w_query,
    w_key,
    w_value,
    w_out,
    norm2_gain,
    w_up,
    w_down,
    out_cotangent,
):
    streams, rows, width = block_input.shape
    planes = lax.axis_size("tensor")
    lanes = lax.axis_size("dp")
    clip_count = clip_lengths.shape[1]
    own = lax.axis_index("dp")
    own_plane = lax.axis_index("tensor")
    own_core = own % 2
    heads = w_query.shape[1] * planes // (HEAD * lanes)
    depth = w_query.shape[0]
    hidden_part = w_up.shape[1] // lanes
    hidden_own = planes * hidden_part
    inner = heads * HEAD

    small = jnp.zeros((8, depth), f32)
    small = small.at[0].set(norm1_gain.astype(f32)).at[1].set(norm2_gain.astype(f32))
    small = small.at[2, : streams * clip_count].set(clip_lengths.reshape(-1).astype(f32))
    tokens_in, qkv_part, out_part, up_part, down_part, small = plane_call(
        start_kernel,
        "start",
        6,
        [
            jax.ShapeDtypeStruct(block_input.shape, bf16),
            jax.ShapeDtypeStruct((3, 4, depth, HEAD), bf16),
            jax.ShapeDtypeStruct((4, HEAD, depth), bf16),
            jax.ShapeDtypeStruct((width, hidden_part), bf16),
            jax.ShapeDtypeStruct((hidden_part, width), bf16),
            jax.ShapeDtypeStruct((lanes, 8, depth), f32),
        ],
        ["any"] * 8,
        ["any"] * 6,
        [pltpu.SemaphoreType.DMA((7,)), pltpu.SemaphoreType.DMA((2, 2))],
        33,
        0,
        (block_input, w_query, w_key, w_value, w_out, w_up, w_down, small),
    )
    gain_one = small[:, 0].reshape(-1)
    gain_two = small[:, 1].reshape(-1)
    lengths = small[:, 2, : streams * clip_count].reshape(-1, clip_count).astype(jnp.int32)

    qkv_wide = lax.all_gather(qkv_part, "tensor", axis=0, tiled=False)
    out_wide = lax.all_gather(out_part, "tensor", axis=0, tiled=False)
    up_wide = lax.all_gather(up_part, "tensor", axis=0, tiled=False)
    down_w = lax.all_gather(down_part, "tensor", axis=0, tiled=True)

    all_ends = jnp.cumsum(lengths, axis=1)
    buffers = 4 * (own // 2 ^ jnp.arange(4, dtype=jnp.int32)) + own_plane
    ends = jnp.take(all_ends, buffers, axis=0)
    chunks = 2 * (1 - own_core) + jnp.arange(streams, dtype=jnp.int32)
    places = chunks[:, None] * rows + jnp.arange(rows, dtype=jnp.int32)
    valid = (places < ends[0, -1]).astype(f32)
    ends = ends.reshape(-1).astype(jnp.int32)

    pieces = jax.ShapeDtypeStruct((streams, 8, rows, width), bf16)
    sums = jax.ShapeDtypeStruct((streams, rows, width), f32)
    row_count = streams * 8 * rows
    slots = pltpu.VMEM((2, rows, width), bf16)
    dma = pltpu.SemaphoreType.DMA

    def piece_shape(columns):
        return jax.ShapeDtypeStruct((streams, 8, rows, columns), bf16)

    tokens = tokens_in.astype(f32)
    normed_one, unit_one, inverse_one = norm_rows(tokens, gain_one)
    features_one, cotangent = plane_call(
        gather_kernel,
        "gather",
        0,
        [pieces, jax.ShapeDtypeStruct(block_input.shape, bf16)],
        ["any", "any"],
        ["any", "any"],
        [dma((streams,)), dma((2, 2))],
        8 * streams,
        0,
        (normed_one.astype(bf16), out_cotangent),
    )
    grad_out = cotangent.astype(f32) * valid[:, :, None]
    grad_branch, qkv, mixed, qkv_w = plane_call(
        functools.partial(attention_kernel, clip_count),
        "attention",
        1,
        [
            pieces,
            piece_shape(3 * inner),
            piece_shape(inner),
            jax.ShapeDtypeStruct((4, 2, depth, 3 * inner), bf16),
        ],
        ["any", "any", "any", "smem"],
        ["any", "vmem", "vmem", "vmem"],
        [slots, dma((2,)), dma((streams,)), dma((6,))],
        8 * streams + 6,
        2 * row_count * width * 3 * inner,
        (grad_out.astype(bf16), features_one, qkv_wide, ends),
    )
    attn_sum, out_w = plane_call(
        project_kernel,
        "project",
        2,
        [sums, jax.ShapeDtypeStruct((inner, width), bf16)],
        ["vmem", "any"],
        ["vmem", "vmem"],
        reduce_scratch(streams, rows, width) + [dma((8,))],
        10 * streams + 8,
        2 * row_count * width * inner,
        (mixed, out_wide),
    )
    hidden = tokens + attn_sum
    normed_two, unit_two, inverse_two = norm_rows(hidden, gain_two)
    part = pltpu.VMEM((2, rows, hidden_own), bf16)
    up_flat = pltpu.VMEM((width, hidden_own), bf16)
    features_two, slope, down_dot, mlp_sum = plane_call(
        mlp_kernel,
        "mlp",
        3,
        [
            pieces,
            piece_shape(hidden_own),
            jax.ShapeDtypeStruct((hidden_own, width), bf16),
            sums,
        ],
        ["any", "any", "vmem", "any"],
        ["any", "any", "any", "vmem"],
        reduce_scratch(streams, rows, width)
        + [up_flat, slots, part, part, pltpu.VMEM((hidden_own, width), f32), slots]
        + [dma((planes,)), dma((2,)), dma((2,)), dma((streams,)), dma((2,))],
        18 * streams,
        6 * row_count * width * hidden_own,
        (normed_two.astype(bf16), up_wide, down_w, grad_branch),
    )

    up_dot, back_sum = plane_call(
        mlp_back_kernel,
        "mlp_back",
        4,
        [jax.ShapeDtypeStruct((planes, width, hidden_part), bf16), sums],
        ["any", "any", "any", "any", "vmem"],
        ["any", "vmem"],
        reduce_scratch(streams, rows, width)
        + [up_flat, slots, part, part, slots, pltpu.VMEM((width, hidden_own), f32)]
        + [dma((planes,)), dma((2,)), dma((2,)), dma((2,)), dma((2, planes))],
        10 * streams,
        6 * row_count * width * hidden_own,
        (grad_branch, slope, features_two, up_wide, down_w),
    )
    from_two, gain_two_grad = norm_back(back_sum, unit_two, inverse_two, gain_two)
    grad_hidden = grad_out + from_two
    down_sum = lax.psum_scatter(down_dot, "tensor", scatter_dimension=0, tiled=True)
    up_sum = lax.psum_scatter(up_dot, "tensor", scatter_dimension=0, tiled=False)
    chunk = pltpu.VMEM((4, rows, HEAD), f32)
    chip_rows = pltpu.VMEM((streams, 2, rows, 3 * inner), bf16)
    _, qkv_dot, out_dot, output, input_sum = plane_call(
        functools.partial(attention_back_kernel, clip_count),
        "attention_back",
        5,
        [
            pieces,
            jax.ShapeDtypeStruct((width, 3 * inner), bf16),
            jax.ShapeDtypeStruct((inner, width), bf16),
            jax.ShapeDtypeStruct(block_input.shape, bf16),
            sums,
        ],
        ["any", "any", "any", "any", "any", "vmem", "vmem", "smem"],
        ["any", "any", "any", "any", "vmem"],
        reduce_scratch(streams, rows, width)
        + [pltpu.VMEM((4, rows, width), bf16), pltpu.VMEM((2, rows, inner), bf16)]
        + [pltpu.VMEM((streams, 8, rows, inner), bf16), chip_rows]
        + [pltpu.VMEM((2, streams, 2, rows, 3 * inner), bf16), chunk, chunk]
        + [pltpu.VMEM((width, 3 * inner), f32), pltpu.VMEM((inner, width), f32)]
        + [dma((4,)), dma((2,)), dma((4,)), dma((4,)), dma((2, 2)), dma((streams,))],
        18 * streams,
        2 * row_count * width * 8 * inner,
        (
            grad_hidden.astype(bf16),
            qkv,
            mixed,
            features_one,
            (hidden + mlp_sum).astype(bf16),
            qkv_w.reshape(width, 3 * inner),
            out_w,
            ends,
        ),
    )
    input_sum, down_sum, up_sum = lax.optimization_barrier((input_sum, down_sum, up_sum))
    from_one, gain_one_grad = norm_back(input_sum, unit_one, inverse_one, gain_one)
    gains = jnp.stack([gain_one_grad.sum(0), gain_two_grad.sum(0)]).reshape(2, lanes, depth)
    gains = jnp.zeros((lanes, 8, depth), f32).at[:, :2].set(gains.swapaxes(0, 1))
    small_sum = pltpu.VMEM((8, depth), f32)
    input_grad, qkv_grad, out_grad, up_grad, down_grad, gains = plane_call(
        end_kernel,
        "end",
        7,
        [
            jax.ShapeDtypeStruct(block_input.shape, bf16),
            jax.ShapeDtypeStruct((3, depth, 4 * HEAD), bf16),
            jax.ShapeDtypeStruct((4 * HEAD, depth), bf16),
            jax.ShapeDtypeStruct(w_up.shape, bf16),
            jax.ShapeDtypeStruct(w_down.shape, bf16),
            jax.ShapeDtypeStruct((8, depth), f32),
        ],
        ["any", "any", "any", "any", "any", "vmem"],
        ["any", "any", "any", "any", "any", "vmem"],
        [
            pltpu.VMEM((4, 3, 4, depth, HEAD), bf16),
            pltpu.VMEM((4, 4, HEAD, depth), bf16),
            pltpu.VMEM((3, 3, 4, depth, HEAD), bf16),
            pltpu.VMEM((3, 4, HEAD, depth), bf16),
            pltpu.VMEM((8, 8, depth), f32),
            small_sum,
            pltpu.VMEM((4, 8, depth), f32),
            dma((18,)),
            dma((2, 2)),
        ],
        50,
        0,
        (
            (grad_hidden + from_one).astype(bf16),
            qkv_dot.reshape(4, 2, depth, 3 * inner),
            out_dot,
            up_sum,
            down_sum,
            gains,
        ),
    )
    qkv_grad = qkv_grad.astype(f32)
    return (
        output,
        input_grad.astype(f32),
        gains[0],
        qkv_grad[0],
        qkv_grad[1],
        qkv_grad[2],
        out_grad.astype(f32),
        gains[1],
        up_grad.astype(f32),
        down_grad.astype(f32),
    )


def solution(mesh):
    in_specs = (
        P("dp", "tensor", None),
        P("dp", None),
        P("dp"),
        P("dp", "tensor"),
        P("dp", "tensor"),
        P("dp", "tensor"),
        P("tensor", "dp"),
        P("dp"),
        P("dp", "tensor"),
        P("tensor", "dp"),
        P("dp", "tensor", None),
    )
    out_specs = (
        P("dp", "tensor", None),
        P("dp", "tensor", None),
        P("dp"),
        P("dp", "tensor"),
        P("dp", "tensor"),
        P("dp", "tensor"),
        P("tensor", "dp"),
        P("dp"),
        P("dp", "tensor"),
        P("tensor", "dp"),
    )
    own_form = mesh.shape["dp"] == 8 and mesh.shape["tensor"] == 4
    return jax.shard_map(
        on_device if own_form else on_device_any, mesh=mesh, in_specs=in_specs, out_specs=out_specs, check_vma=False
    )
```
